32 devices in a mesh: dp: 4 (over x, core), seq: 8 (over z, y).
Axes of the slice: x: 2, y: 2, z: 4, core: 2. Of those that a mesh axis runs over, the one named last changes fastest.
Arguments:
- tokens: bfloat16 [8, 1024, 1024], P('dp', 'seq'), may hold values from -6 to 6
- attn_gain: bfloat16 [1024], P(('dp', 'seq')), may hold values from 0.25 to 1.75
- w_query: bfloat16 [1024, 2048], P(('dp', 'seq')), may hold values from -0.1875 to 0.1875
- key_projection: bfloat16 [1024, 1024], P(('dp', 'seq')), may hold values from -0.1875 to 0.1875
- value_projection: bfloat16 [1024, 1024], P(('dp', 'seq')), may hold values from -0.1875 to 0.1875
- query_head_gain: bfloat16 [128], replicated, may hold values from 1.3984375 to 2.59375
- key_gain: bfloat16 [128], replicated, may hold values from 0.25 to 1.75
- w_out: bfloat16 [2048, 1024], P(('dp', 'seq')), may hold values from -0.75 to 0.75
- mlp_gain: bfloat16 [1024], P(('dp', 'seq')), may hold values from 0.25 to 1.75
- w_gate: bfloat16 [1024, 3072], P(('dp', 'seq')), may hold values from -0.1875 to 0.1875
- w_up: bfloat16 [1024, 3072], P(('dp', 'seq')), may hold values from -0.1875 to 0.1875
- w_down: bfloat16 [3072, 1024], P(('dp', 'seq')), may hold values from -0.21875 to 0.21875
- cotangent: bfloat16 [8, 1024, 1024], P('dp', 'seq'), may hold values from -6 to 6
- span_order: int32 [8, 16], P('dp'), may hold values from 0 to 15, each once within a row
Outputs:
- output: bfloat16 [8, 1024, 1024], P('dp', 'seq')
- input_grad: bfloat16 [8, 1024, 1024], P('dp', 'seq')
- grad_attn_gain: float32 [1024], P(('dp', 'seq'))
- grad_query: float32 [1024, 2048], P(('dp', 'seq'))
- grad_key: float32 [1024, 1024], P(('dp', 'seq'))
- grad_value: float32 [1024, 1024], P(('dp', 'seq'))
- grad_query_gain: float32 [128], replicated
- grad_key_gain: float32 [128], replicated
- grad_out: float32 [2048, 1024], P(('dp', 'seq'))
- grad_mlp_gain: float32 [1024], P(('dp', 'seq'))
- grad_gate: float32 [1024, 3072], P(('dp', 'seq'))
- grad_up: float32 [1024, 3072], P(('dp', 'seq'))
- grad_down: float32 [3072, 1024], P(('dp', 'seq'))
The draws below stay inside these ranges and needn't reach their ends.
Inputs may be any that keep to these rules, and one draw needn't show every extreme that they name: Each row is a permutation of the numbers 0 to 15: stored block b of sequence s holds its tokens span_order[s, b] * 64 to span_order[s, b] * 64 + 63.
All inputs are finite; a program needn't handle non-finite values.
Results may differ from the reference program's by a relative error of at most 0.02.
Values may be sent and summed in bfloat16 or wider, within the bound.
A program may use at most 192 MiB of HBM per device.

```python
import jax
import jax.numpy as jnp
from jax import lax

MODEL_WIDTH = 1024
QUERY_HEADS = 16
KEY_VALUE_HEADS = 8
HEAD_SIZE = 128
FF = 3072
BLK = 64
BLOCKS = 16
SEQ_LEN = 1024
SEQS = 8


def steps_of(own_key, dims, pieces, least, top_value):
    level = 1.0
    for axis_at, shards_of in pieces:
        draws = jax.random.uniform(jax.random.fold_in(jax.random.fold_in(own_key, 6), axis_at), (shards_of,), jnp.float32, least / len(pieces), top_value / len(pieces))
        level = level * jnp.repeat(jnp.exp(draws), dims[axis_at] // shards_of).reshape((-1,) + (1,) * (len(dims) - 1 - axis_at))
    return level


def centred(stream_key, extent, deviation, limit, shards=(), held_as=jnp.bfloat16):
    entries = deviation * jax.random.normal(stream_key, extent, jnp.float32)
    if shards:
        entries = entries * steps_of(stream_key, extent, shards, -0.22, 0.18)
    return jnp.clip(entries, -limit, limit).astype(held_as)


def setup_inputs(seed: int = 0) -> dict:
    seeds = jax.random.split(jax.random.key(seed), 15)
    return {
        "tokens": centred(seeds[0], (SEQS, SEQ_LEN, MODEL_WIDTH), 1.0, 6.0, ((0, 4), (1, 8))),
        "attn_gain": jnp.clip(1.0 + 0.15 * jax.random.normal(seeds[1], (MODEL_WIDTH,), jnp.float32), 0.25, 1.75).astype(jnp.bfloat16),
        "w_query": centred(seeds[2], (MODEL_WIDTH, QUERY_HEADS * HEAD_SIZE), MODEL_WIDTH ** -0.5, 0.1875, ((0, 32),)),
        "key_projection": centred(seeds[3], (MODEL_WIDTH, KEY_VALUE_HEADS * HEAD_SIZE), MODEL_WIDTH ** -0.5, 0.1875, ((0, 32),)),
        "value_projection": centred(seeds[4], (MODEL_WIDTH, KEY_VALUE_HEADS * HEAD_SIZE), MODEL_WIDTH ** -0.5, 0.1875, ((0, 32),)),
        "query_head_gain": jnp.clip(jax.random.uniform(seeds[5], (HEAD_SIZE,), jnp.float32, 1.3984375, 2.59375), 1.3984375, 2.59375).astype(jnp.bfloat16),
        "key_gain": jnp.clip(1.0 + 0.15 * jax.random.normal(seeds[6], (HEAD_SIZE,), jnp.float32), 0.25, 1.75).astype(jnp.bfloat16),
        "w_out": centred(seeds[7], (QUERY_HEADS * HEAD_SIZE, MODEL_WIDTH), (QUERY_HEADS * HEAD_SIZE // 32) ** -0.5, 0.75, ((0, 32),)),
        "mlp_gain": jnp.clip(1.0 + 0.15 * jax.random.normal(seeds[8], (MODEL_WIDTH,), jnp.float32), 0.25, 1.75).astype(jnp.bfloat16),
        "w_gate": centred(seeds[9], (MODEL_WIDTH, FF), MODEL_WIDTH ** -0.5, 0.1875, ((0, 32),)),
        "w_up": centred(seeds[10], (MODEL_WIDTH, FF), MODEL_WIDTH ** -0.5, 0.1875, ((0, 32),)),
        "w_down": centred(seeds[11], (FF, MODEL_WIDTH), (FF // 4) ** -0.5, 0.21875, ((0, 32),)),
        "cotangent": centred(seeds[12], (SEQS, SEQ_LEN, MODEL_WIDTH), 1.0, 6.0, ((0, 4), (1, 8))),
        "span_order": jax.vmap(lambda own: jax.random.permutation(own, BLOCKS))(jax.random.split(seeds[13], SEQS)).reshape((SEQS, BLOCKS)).astype(jnp.int32),
    }


EPS = 1e-06
BASE = 1000000.0
NEGATIVE_FILL = -1e+30

@jax.custom_vjp
def low(v):
    return lax.optimization_barrier(v.astype(jnp.bfloat16)).astype(jnp.float32)

@jax.custom_vjp
def low_back(v):
    return v

def low_keep(v):
    return (low(v), None)

def low_pass(kept, grad):
    return (grad,)

def back_keep(v):
    return (v, None)

def back_low(kept, grad):
    return (low(grad),)
low.defvjp(low_keep, low_pass)
low_back.defvjp(back_keep, back_low)

def row_norm_apply(v, gain):
    return v * lax.rsqrt(lax.optimization_barrier(jnp.mean(v * v, axis=-1, keepdims=True)) + EPS) * gain

def apply_rotary(v, cosine_table, sine_table):
    half = v.shape[-1] // 2
    first = v[..., :half]
    second = v[..., half:]
    return jnp.concatenate([first * cosine_table - second * sine_table, second * cosine_table + first * sine_table], axis=-1)

def matrix_product(left, right):
    return jnp.dot(left, right, precision=lax.Precision.HIGHEST)

def layer(seq_x, positions, attn_gain, w_query, key_projection, value_projection, query_head_gain, key_gain, w_out, mlp_gain, w_gate, w_up, w_down):
    sequence_length = seq_x.shape[0]
    query_group = QUERY_HEADS // KEY_VALUE_HEADS
    first_operand = low(row_norm_apply(seq_x, attn_gain))
    query_unrotated = low_back(matrix_product(first_operand, w_query)).reshape(sequence_length, QUERY_HEADS, HEAD_SIZE)
    key_unrotated = low_back(matrix_product(first_operand, key_projection)).reshape(sequence_length, KEY_VALUE_HEADS, HEAD_SIZE)
    value_rows = low(low_back(matrix_product(first_operand, value_projection))).reshape(sequence_length, KEY_VALUE_HEADS, HEAD_SIZE)
    freqs = BASE ** (-(jnp.arange(HEAD_SIZE // 2, dtype=jnp.int32).astype(jnp.float32) * 2.0) / HEAD_SIZE)
    angles = positions.astype(jnp.float32)[:, None] * freqs[None, :]
    cosine_table = jnp.cos(angles)[:, None, :]
    sine_table = jnp.sin(angles)[:, None, :]
    query_rows = low(apply_rotary(row_norm_apply(query_unrotated, query_head_gain), cosine_table, sine_table)).reshape(sequence_length, KEY_VALUE_HEADS, query_group, HEAD_SIZE)
    keys = low(apply_rotary(row_norm_apply(key_unrotated, key_gain), cosine_table, sine_table))
    rows = min(512, sequence_length)
    scale = HEAD_SIZE ** (-0.5)

    def attend(index):
        start = (index * rows).astype(jnp.int32)
        block_q = lax.dynamic_slice_in_dim(query_rows, start, rows, 0)
        block_pos = lax.dynamic_slice_in_dim(positions, start, rows, 0)
        scores = low_back(jnp.einsum('qgrd,kgd->grqk', block_q, keys, precision=lax.Precision.HIGHEST) * scale)
        visible = positions[None, :] <= block_pos[:, None]
        scores = jnp.where(visible[None, None], scores, NEGATIVE_FILL)
        shifted = scores - lax.optimization_barrier(jnp.max(scores, axis=-1, keepdims=True))
        weights = jnp.exp(shifted)
        probs = low(weights / lax.optimization_barrier(jnp.sum(weights, axis=-1, keepdims=True)))
        return jnp.einsum('grqk,kgd->qgrd', probs, value_rows, precision=lax.Precision.HIGHEST)
    attended = lax.map(jax.checkpoint(attend), jnp.arange(sequence_length // rows, dtype=jnp.int32))
    o_low = low(low_back(attended.reshape(sequence_length, QUERY_HEADS * HEAD_SIZE)))
    hidden = seq_x + low_back(matrix_product(o_low, w_out))
    a_second = low(row_norm_apply(hidden, mlp_gain))
    gate = low_back(matrix_product(a_second, w_gate))
    up_part = low_back(matrix_product(a_second, w_up))
    mixed = low(gate * jax.nn.sigmoid(gate) * up_part)
    return hidden + low_back(matrix_product(mixed, w_down))

def reference(tokens, attn_gain, w_query, key_projection, value_projection, query_head_gain, key_gain, w_out, mlp_gain, w_gate, w_up, w_down, cotangent, span_order):
    params = tuple((w.astype(jnp.float32) for w in (attn_gain, w_query, key_projection, value_projection, query_head_gain, key_gain, w_out, mlp_gain, w_gate, w_up, w_down)))
    places = jnp.arange(SEQ_LEN, dtype=jnp.int32)

    def one_sequence(totals, inputs):
        seq_x, seq_cot, order = inputs
        positions = (order[places // BLK] * BLK + places % BLK).astype(jnp.int32)

        def forward(x_in, *weights):
            return layer(x_in, positions, *weights)
        result, pullback = jax.vjp(forward, seq_x.astype(jnp.float32), *params)
        grads = pullback(seq_cot.astype(jnp.float32))
        totals = tuple((t + g for t, g in zip(totals, grads[1:])))
        return (totals, (result.astype(jnp.bfloat16), grads[0].astype(jnp.bfloat16)))
    start = tuple((jnp.zeros(w.shape, jnp.float32) for w in params))
    totals, outs = lax.scan(one_sequence, start, (tokens, cotangent, span_order))
    return (outs[0], outs[1], totals[0], totals[1], totals[2], totals[3], totals[4], totals[5], totals[6], totals[7], totals[8], totals[9], totals[10])
```

```python
import jax
import jax.numpy as jnp
from jax import lax
from jax.sharding import PartitionSpec as P

from jax.experimental import pallas as pl
from jax.experimental.pallas import tpu as pltpu

QUERY_HEADS = 16
KEY_VALUE_HEADS = 8
HEAD_SIZE = 128
BLK = 64
MB = 2


EPS = 1e-06
BASE = 1000000.0
NEGATIVE_FILL = -1e30


def from_behind(block, axis, distance):
    devices = range(lax.axis_size(axis))
    route = [((i - distance) % len(devices), i) for i in devices]
    return lax.ppermute(block, axis, route)


def row_norm_apply(v, gain):
    return v * lax.rsqrt(jnp.mean(v * v, axis=-1, keepdims=True) + EPS) * gain


def apply_rotary(v, cosine_table, sine_table):
    half = v.shape[-1] // 2
    first = v[..., :half]
    second = v[..., half:]
    return jnp.concatenate(
        [first * cosine_table - second * sine_table, second * cosine_table + first * sine_table],
        axis=-1,
    )


def matrix_multiply(left, right):
    return jnp.dot(left, right, preferred_element_type=jnp.float32)


def row_product(left, right):
    return lax.dot_general(
        left, right, (((0,), (0,)), ((), ())), preferred_element_type=jnp.float32
    )


def product_backward(left, right):
    return lax.dot_general(
        left, right, (((1,), (1,)), ((), ())), preferred_element_type=jnp.float32
    )


def block_positions(order, start, count):
    places = start + lax.iota(jnp.int32, count)
    which = places // BLK
    hits = (which[:, None] == lax.iota(jnp.int32, order.shape[1])[None, :]).astype(jnp.int32)
    spans = jnp.sum(hits[None, :, :] * order[:, None, :], axis=-1)
    return spans * BLK + places % BLK


def pack_shares(members, count):
    return jnp.concatenate([m.reshape(count, -1) for m in members], axis=1).reshape(-1)


def unpack_shares(flat, members, count):
    pieces = []
    offset = 0
    for m in members:
        length = m.size // count
        share_shape = (m.shape[0] // count,) + tuple(m.shape[1:])
        pieces.append(flat[offset : offset + length].reshape(share_shape))
        offset = offset + length
    return pieces


def shards(
    tokens,
    attn_gain,
    w_query,
    key_projection,
    value_projection,
    query_head_gain,
    key_gain,
    w_out,
    mlp_gain,
    w_gate,
    w_up,
    w_down,
    cotangent,
    span_order,
):
    seq_count = lax.axis_size("seq")
    seq_place = lax.axis_index("seq")
    all_count = lax.axis_size(("dp", "seq"))
    local_length = tokens.shape[1]
    width = tokens.shape[2]
    sequence_permutation = tokens.shape[0] // MB
    query_group = QUERY_HEADS // KEY_VALUE_HEADS
    scale = HEAD_SIZE ** (-0.5)
    freqs = BASE ** (-(lax.iota(jnp.float32, HEAD_SIZE // 2) * 2.0) / HEAD_SIZE)
    query_norm_gain = query_head_gain.astype(jnp.float32)
    kgain = key_gain.astype(jnp.float32)
    sums = None
    outputs = []
    input_grads = []
    for batch in range(MB):
        rows_x = tokens[batch * sequence_permutation : (batch + 1) * sequence_permutation]
        rows_cot = cotangent[batch * sequence_permutation : (batch + 1) * sequence_permutation]
        order = span_order[batch * sequence_permutation : (batch + 1) * sequence_permutation]
        gain_a, wq, key_weight, value_weight, output_weight = (
            lax.all_gather(attn_gain, ("dp", "seq"), axis=0, tiled=True),
            lax.all_gather(w_query, ("dp", "seq"), axis=0, tiled=True),
            lax.all_gather(key_projection, ("dp", "seq"), axis=0, tiled=True),
            lax.all_gather(value_projection, ("dp", "seq"), axis=0, tiled=True),
            lax.all_gather(w_out, ("dp", "seq"), axis=0, tiled=True),
        )
        gain_m, wg, wu, wd = (
            lax.all_gather(mlp_gain, ("dp", "seq"), axis=0, tiled=True),
            lax.all_gather(w_gate, ("dp", "seq"), axis=0, tiled=True),
            lax.all_gather(w_up, ("dp", "seq"), axis=0, tiled=True),
            lax.all_gather(w_down, ("dp", "seq"), axis=0, tiled=True),
        )
        own_pos = block_positions(order, seq_place * local_length, local_length)
        angles = own_pos.astype(jnp.float32)[..., None] * freqs
        cosine_table = jnp.cos(angles)[:, :, None, :]
        sine_table = jnp.sin(angles)[:, :, None, :]

        def query_per_head(raw, gain):
            return apply_rotary(row_norm_apply(raw, gain), cosine_table, sine_table)

        flat_x = rows_x.reshape(-1, width).astype(jnp.float32)
        first_operand = row_norm_apply(flat_x, gain_a.astype(jnp.float32)).astype(jnp.bfloat16)
        query_unrotated = matrix_multiply(first_operand, wq).reshape(
            sequence_permutation, local_length, QUERY_HEADS, HEAD_SIZE
        )
        key_unrotated = matrix_multiply(first_operand, key_weight).reshape(
            sequence_permutation, local_length, KEY_VALUE_HEADS, HEAD_SIZE
        )
        value_reduced = (
            matrix_multiply(first_operand, value_weight)
            .astype(jnp.bfloat16)
            .reshape(sequence_permutation, local_length, KEY_VALUE_HEADS, HEAD_SIZE)
        )
        q_low = (
            query_per_head(query_unrotated, query_norm_gain)
            .astype(jnp.bfloat16)
            .reshape(sequence_permutation, local_length, KEY_VALUE_HEADS, query_group, HEAD_SIZE)
        )
        k_low = query_per_head(key_unrotated, kgain).astype(jnp.bfloat16)
        initial_maximum = jnp.full(
            (sequence_permutation, KEY_VALUE_HEADS, query_group, local_length),
            NEGATIVE_FILL,
            jnp.float32,
        )
        top = initial_maximum
        piece_k = lax.all_gather(k_low, "seq", axis=1, tiled=True)
        piece_v = lax.all_gather(value_reduced, "seq", axis=1, tiled=True)
        key_pos = block_positions(order, jnp.int32(0), piece_k.shape[1])
        visible = key_pos[:, None, None, None, :] <= own_pos[:, None, None, :, None]
        scores = (
            jnp.einsum("sqgrd,skgd->sgrqk", q_low, piece_k, preferred_element_type=jnp.float32)
            * scale
        )
        scores = jnp.where(visible, scores, NEGATIVE_FILL)
        new_top = jnp.maximum(top, jnp.max(scores, axis=-1))
        weights = jnp.exp(scores - new_top[..., None])
        new_total = jnp.sum(weights, axis=-1)
        taken = jnp.einsum(
            "sgrqk,skgd->sqgrd",
            weights.astype(jnp.bfloat16),
            piece_v,
            preferred_element_type=jnp.float32,
        )
        top = new_top
        log_total = top + jnp.log(new_total)
        attn = taken / jnp.transpose(new_total, (0, 3, 1, 2))[..., None]
        o_low = attn.astype(jnp.bfloat16).reshape(
            sequence_permutation * local_length, QUERY_HEADS * HEAD_SIZE
        )
        hidden = flat_x + matrix_multiply(o_low, output_weight)
        gain_second = gain_m.astype(jnp.float32)
        a_second = row_norm_apply(hidden, gain_second).astype(jnp.bfloat16)
        gate = matrix_multiply(a_second, wg)
        up_part = matrix_multiply(a_second, wu)
        mixed = (gate * jax.nn.sigmoid(gate) * up_part).astype(jnp.bfloat16)
        result = hidden + matrix_multiply(mixed, wd)
        outputs.append(
            result.astype(jnp.bfloat16).reshape(sequence_permutation, local_length, width)
        )
        gain_a, wq, key_weight, value_weight, output_weight = (
            lax.all_gather(attn_gain, ("dp", "seq"), axis=0, tiled=True),
            lax.all_gather(w_query, ("dp", "seq"), axis=0, tiled=True),
            lax.all_gather(key_projection, ("dp", "seq"), axis=0, tiled=True),
            lax.all_gather(value_projection, ("dp", "seq"), axis=0, tiled=True),
            lax.all_gather(w_out, ("dp", "seq"), axis=0, tiled=True),
        )
        gain_m, wg, wu, wd = (
            lax.all_gather(mlp_gain, ("dp", "seq"), axis=0, tiled=True),
            lax.all_gather(w_gate, ("dp", "seq"), axis=0, tiled=True),
            lax.all_gather(w_up, ("dp", "seq"), axis=0, tiled=True),
            lax.all_gather(w_down, ("dp", "seq"), axis=0, tiled=True),
        )
        flat_cot = rows_cot.reshape(-1, width)
        grad_down = row_product(mixed, flat_cot)
        d_mixed = product_backward(flat_cot, wd)

        def mix(gate_in, up_in):
            return gate_in * jax.nn.sigmoid(gate_in) * up_in

        _, mix_back = jax.vjp(mix, gate, up_part)
        d_gate, d_up = mix_back(d_mixed)
        gate_low = d_gate.astype(jnp.bfloat16)
        up_low = d_up.astype(jnp.bfloat16)
        grad_gate = row_product(a_second, gate_low)
        grad_up = row_product(a_second, up_low)
        d_second = product_backward(gate_low, wg) + product_backward(up_low, wu)
        _, second_back = jax.vjp(row_norm_apply, hidden, gain_second)
        d_hidden_norm, grad_mlp_gain = second_back(d_second)
        d_hidden = flat_cot.astype(jnp.float32) + d_hidden_norm
        grad_output_reduced = d_hidden.astype(jnp.bfloat16)
        grad_out = row_product(o_low, grad_output_reduced)
        do_low = (
            product_backward(grad_output_reduced, output_weight)
            .astype(jnp.bfloat16)
            .reshape(sequence_permutation, local_length, KEY_VALUE_HEADS, query_group, HEAD_SIZE)
        )
        delta = jnp.transpose(jnp.sum(do_low.astype(jnp.float32) * attn, axis=-1), (0, 2, 3, 1))

        def back_terms(held_k, held_v, visible):
            scores = (
                jnp.einsum("sqgrd,skgd->sgrqk", q_low, held_k, preferred_element_type=jnp.float32)
                * scale
            )
            scores = jnp.where(visible, scores, NEGATIVE_FILL)
            probs = jnp.exp(scores - log_total[..., None])
            d_probs = jnp.einsum(
                "sqgrd,skgd->sgrqk", do_low, held_v, preferred_element_type=jnp.float32
            )
            score_low = (probs * (d_probs - delta[..., None])).astype(jnp.bfloat16)
            probs_low = probs.astype(jnp.bfloat16)
            term_q = scale * jnp.einsum(
                "sgrqk,skgd->sqgrd", score_low, held_k, preferred_element_type=jnp.float32
            )
            term_k = scale * jnp.einsum(
                "sgrqk,sqgrd->skgd", score_low, q_low, preferred_element_type=jnp.float32
            )
            term_v = jnp.einsum(
                "sgrqk,sqgrd->skgd", probs_low, do_low, preferred_element_type=jnp.float32
            )
            return (term_k, term_v, term_q)

        def cycle_step(turn, state):
            held_k, held_v, acc_k, acc_v, acc_q = state
            owner = (seq_place - turn) % seq_count
            key_pos = block_positions(order, owner * local_length, local_length)
            visible = key_pos[:, None, None, None, :] <= own_pos[:, None, None, :, None]
            term_k, term_v, term_q = back_terms(held_k, held_v, visible)
            acc_k, acc_v, acc_q = (acc_k + term_k, acc_v + term_v, acc_q + term_q)
            held_k, held_v = from_behind((held_k, held_v), "seq", 1)
            acc_k, acc_v = (
                from_behind(acc_k.astype(jnp.bfloat16), "seq", 1).astype(acc_k.dtype),
                from_behind(acc_v.astype(jnp.bfloat16), "seq", 1).astype(acc_v.dtype),
            )
            return (held_k, held_v, acc_k, acc_v, acc_q)

        def two_steps(pair, state):
            return cycle_step(2 * pair + 1, cycle_step(2 * pair, state))

        blank_key_value = jnp.zeros(
            (sequence_permutation, local_length, KEY_VALUE_HEADS, HEAD_SIZE), jnp.float32
        )
        blank_query = jnp.zeros(
            (sequence_permutation, local_length, KEY_VALUE_HEADS, query_group, HEAD_SIZE),
            jnp.float32,
        )
        state = lax.fori_loop(
            0,
            seq_count // 2,
            two_steps,
            (k_low, value_reduced, blank_key_value, blank_key_value, blank_query),
        )
        _, _, d_keys, grad_value_rows, d_queries = state
        _, query_back = jax.vjp(query_per_head, query_unrotated, query_norm_gain)
        d_q_raw, grad_qgain = query_back(
            d_queries.reshape(sequence_permutation, local_length, QUERY_HEADS, HEAD_SIZE)
        )
        _, key_back = jax.vjp(query_per_head, key_unrotated, kgain)
        grad_key_unrotated, grad_kgain = key_back(d_keys)
        dq_low = d_q_raw.astype(jnp.bfloat16).reshape(
            sequence_permutation * local_length, QUERY_HEADS * HEAD_SIZE
        )
        grad_key_reduced = grad_key_unrotated.astype(jnp.bfloat16).reshape(
            sequence_permutation * local_length, KEY_VALUE_HEADS * HEAD_SIZE
        )
        grad_value_reduced = grad_value_rows.astype(jnp.bfloat16).reshape(
            sequence_permutation * local_length, KEY_VALUE_HEADS * HEAD_SIZE
        )
        grad_query = row_product(first_operand, dq_low)
        grad_key = row_product(first_operand, grad_key_reduced)
        grad_value = row_product(first_operand, grad_value_reduced)
        d_first = (
            product_backward(dq_low, wq)
            + product_backward(grad_key_reduced, key_weight)
            + product_backward(grad_value_reduced, value_weight)
        )
        _, first_back = jax.vjp(row_norm_apply, flat_x, gain_a.astype(jnp.float32))
        d_x_norm, grad_attn_gain = first_back(d_first)
        input_grads.append(
            (d_hidden + d_x_norm)
            .astype(jnp.bfloat16)
            .reshape(sequence_permutation, local_length, width)
        )
        fresh = (
            grad_attn_gain,
            grad_query,
            grad_key,
            grad_value,
            grad_out,
            grad_mlp_gain,
            grad_gate,
            grad_up,
            grad_down,
            grad_qgain,
            grad_kgain,
        )
        if sums is None:
            sums = fresh
        else:
            sums = tuple((a + b for a, b in zip(sums, fresh)))
    attn_members = (sums[0], sums[1], sums[2], sums[3], sums[4])
    mlp_members = (sums[5], sums[6], sums[7], sums[8])
    attn_flat = lax.psum_scatter(
        pack_shares(attn_members, all_count), ("dp", "seq"), scatter_dimension=0, tiled=True
    )
    mlp_flat = lax.psum_scatter(
        pack_shares(mlp_members, all_count), ("dp", "seq"), scatter_dimension=0, tiled=True
    )
    attn_shares = unpack_shares(attn_flat, attn_members, all_count)
    mlp_shares = unpack_shares(mlp_flat, mlp_members, all_count)
    head_sums = lax.psum((sums[9], sums[10]), ("dp", "seq"))
    return (
        jnp.concatenate(outputs, axis=0),
        jnp.concatenate(input_grads, axis=0),
        attn_shares[0],
        attn_shares[1],
        attn_shares[2],
        attn_shares[3],
        head_sums[0],
        head_sums[1],
        attn_shares[4],
        mlp_shares[0],
        mlp_shares[1],
        mlp_shares[2],
        mlp_shares[3],
    )


BF = jnp.bfloat16
F32 = jnp.float32
MESH = pl.DeviceIdType.MESH
TOKENS = 1024
WIDTH = 1024
LOG2E = 1.4426950408889634
VM = pl.BlockSpec(memory_space=pltpu.VMEM)
SM = pl.BlockSpec(memory_space=pltpu.SMEM)
ANY = pl.BlockSpec(memory_space=pl.ANY)
VMEM_BYTES = 60 * 1024 * 1024


def place():
    q = lax.axis_index("dp")
    p = lax.axis_index("seq")
    return q, p, q // 2, lax.rem(q, 2), p // 2, lax.rem(p, 2)


def greet(peers):
    barrier = pltpu.get_barrier_semaphore()
    for peer in peers:
        pl.semaphore_signal(barrier, inc=1, device_id=peer, device_id_type=MESH)
    pl.semaphore_wait(barrier, len(peers))


def remote(src, dst, send, recv, peer):
    return pltpu.make_async_remote_copy(
        src_ref=src, dst_ref=dst, send_sem=send, recv_sem=recv, device_id=peer, device_id_type=MESH
    )


def dims(left, right, lc, rc):
    return lax.dot_general(left, right, (((lc,), (rc,)), ((), ())), preferred_element_type=F32)


def gather_kernel(
    tok, cot, pos, pq, pg, po, pd,
    xf, cf, of, wq, wg, wo, wd,
    loc, ts, tr, fs, fr, ps, pr, as_, ar, zs, zr, ys, yr,
):
    q, p, x, c, z, y = place()
    peers = [(lax.rem(q + k, 4), p) for k in (1, 2, 3)]
    peers += [(q, lax.rem(p + k, 8)) for k in range(1, 8)]
    greet(peers)
    owner_x, owner_c = y, z // 2
    is_owner = jnp.logical_and(x == owner_x, c == owner_c)
    cross = jnp.logical_and(x != owner_x, c == owner_c)
    last = jnp.logical_and(x != owner_x, c != owner_c)
    sends = []
    cols = ((pq, wq), (pg, wg))
    locals_ = []
    for n, (src, dst) in enumerate(cols):
        for k in (1, 2, 3):
            t = lax.rem(q + k, 4)
            cp = remote(src.at[t], dst.at[q, p], as_.at[n, k - 1], ar.at[n, k - 1], (t, p))
            cp.start()
            sends.append(cp)
        cp = pltpu.make_async_copy(src.at[q], dst.at[q, p], loc.at[n])
        cp.start()
        locals_.append(cp)
    for n, (src, dst) in enumerate(((po, wo), (pd, wd))):
        cp = pltpu.make_async_copy(src, dst.at[p], loc.at[2 + n])
        cp.start()
        locals_.append(cp)
    toks = ((tok, xf), (cot, cf))

    def token_copy(a, i):
        src, dst = toks[a]
        goal = 4 * c + 2 * i + x
        return goal, remote(src.at[i], dst.at[p], ts.at[a, i], tr.at[a, p], (q, goal))

    def token_local(a, i):
        src, dst = toks[a]
        return pltpu.make_async_copy(src.at[i], dst.at[p], loc.at[4 + a])

    for a in range(2):
        for i in range(2):
            goal, cp = token_copy(a, i)

            @pl.when(goal != p)
            def _():
                cp.start()

            @pl.when(goal == p)
            def _():
                token_local(a, i).start()

    def share(n):
        return (wq, wg, wo, wd)[n]

    def view(n, chunk):
        ref = share(n)
        return ref.at[:, chunk] if n < 2 else ref.at[chunk]

    def z_send(n):
        for k in (1, 2, 3):
            t = lax.rem(z + k, 4)
            cp = remote(view(n, p), view(n, p), zs.at[n, k - 1], zr.at[n, k - 1], (q, 2 * t + y))
            cp.start()
            sends.append(cp)

    def y_send(n, k):
        chunk = 2 * lax.rem(z + 4 - k, 4) + y
        cp = remote(view(n, chunk), view(n, chunk), ys.at[n, k], yr.at[n, k], (q, 2 * z + 1 - y))
        cp.start()
        sends.append(cp)

    def z_wait(n, k):
        chunk = 2 * lax.rem(z + 4 - k, 4) + y
        remote(view(n, chunk), view(n, chunk), zs.at[n, k - 1], zr.at[n, k - 1], (q, p)).wait_recv()

    def y_wait(n, k):
        chunk = 2 * lax.rem(z + 4 - k, 4) + 1 - y
        remote(view(n, chunk), view(n, chunk), ys.at[n, k], yr.at[n, k], (q, p)).wait_recv()

    def a_wait(n):
        src, dst = cols[n]
        for k in (1, 2, 3):
            f = lax.rem(q + 4 - k, 4)
            remote(src.at[0], dst.at[f, p], as_.at[n, k - 1], ar.at[n, k - 1], (q, p)).wait_recv()

    def t_wait(a, b):
        dst = toks[a][1]
        remote(dst.at[b], dst.at[b], ts.at[a, 0], tr.at[a, b], (q, p)).wait_recv()

    def forwards(a):
        dst = toks[a][1]
        sib = (2 * x + 1 - c, p)
        opp = (2 * (1 - x) + c, p)

        @pl.when(is_owner)
        def _():
            @pl.loop(0, 8)
            def _(b):
                @pl.when(b != p)
                def _():
                    t_wait(a, b)

                @pl.when(b == p)
                def _():
                    token_local(a, 0).wait()

                remote(dst.at[b], dst.at[b], fs.at[a, 0, b], fr.at[a, b], sib).start()
                remote(dst.at[b], dst.at[b], fs.at[a, 1, b], fr.at[a, b], opp).start()

        @pl.when(jnp.logical_not(is_owner))
        def _():
            @pl.loop(0, 8)
            def _(b):
                remote(dst.at[b], dst.at[b], fs.at[a, 0, b], fr.at[a, b], sib).wait_recv()

                @pl.when(cross)
                def _():
                    remote(dst.at[b], dst.at[b], fs.at[a, 0, b], fr.at[a, b], sib).start()

    def forwards_done(a):
        dst = toks[a][1]

        @pl.when(is_owner)
        def _():
            @pl.loop(0, 8)
            def _(b):
                remote(dst.at[b], dst.at[b], fs.at[a, 0, b], fr.at[a, b], (q, p)).wait_send()
                remote(dst.at[b], dst.at[b], fs.at[a, 1, b], fr.at[a, b], (q, p)).wait_send()

        @pl.when(cross)
        def _():
            @pl.loop(0, 8)
            def _(b):
                remote(dst.at[b], dst.at[b], fs.at[a, 0, b], fr.at[a, b], (q, p)).wait_send()

    pos_peers = [(lax.rem(q + k, 4), p) for k in (1, 2, 3)]
    pos_local = pltpu.make_async_copy(pos, of, loc.at[6])

    @pl.when(is_owner)
    def _():
        pos_local.start()
        for k in range(3):
            remote(pos, of, ps.at[k], pr.at[0], pos_peers[k]).start()
        pos_local.wait()

    @pl.when(jnp.logical_not(is_owner))
    def _():
        remote(pos, of, ps.at[0], pr.at[0], (q, p)).wait_recv()

    a_wait(0)
    locals_[0].wait()
    z_send(0)
    y_send(0, 0)
    locals_[2].wait()
    z_send(2)
    y_send(2, 0)
    a_wait(1)
    locals_[1].wait()
    z_send(1)
    y_send(1, 0)
    locals_[3].wait()
    z_send(3)
    y_send(3, 0)
    forwards(0)
    for n in (0, 2):
        for k in (1, 2, 3):
            z_wait(n, k)
            y_send(n, k)
    forwards(1)
    for n in (1, 3):
        for k in (1, 2, 3):
            z_wait(n, k)
            y_send(n, k)
    for n in range(4):
        for k in range(4):
            y_wait(n, k)
    for cp in sends:
        cp.wait_send()
    for a in range(2):
        for i in range(2):
            goal, cp = token_copy(a, i)

            @pl.when(goal != p)
            def _():
                cp.wait_send()
        forwards_done(a)

    @pl.when(is_owner)
    def _():
        for k in range(3):
            remote(pos, of, ps.at[k], pr.at[0], pos_peers[k]).wait_send()


def gather_call(tok, cot, pos, pq, pg, po, pd):
    sem = pltpu.SemaphoreType.DMA
    shape = jax.ShapeDtypeStruct
    return pl.pallas_call(
        gather_kernel,
        out_shape=(
            shape((8, 128, WIDTH), BF),
            shape((8, 128, WIDTH), BF),
            shape((8, 128), jnp.int32),
            shape((4, 8) + pq.shape[1:], BF),
            shape((4, 8) + pg.shape[1:], BF),
            shape((8,) + po.shape, BF),
            shape((8,) + pd.shape, BF),
        ),
        in_specs=[ANY] * 7,
        out_specs=(ANY,) * 7,
        scratch_shapes=[
            sem((7,)), sem((2, 2)), sem((2, 8)), sem((2, 2, 8)), sem((2, 8)), sem((3,)), sem((1,)),
            sem((2, 3)), sem((2, 3)), sem((4, 3)), sem((4, 3)), sem((4, 4)), sem((4, 4)),
        ],
        compiler_params=pltpu.CompilerParams(collective_id=0, has_side_effects=True),
        name="gather_layer",
    )(tok, cot, pos, pq, pg, po, pd)


def allsum_kernel(part, total, own, l1, l2, s1, r1, s2, r2, s3, r3):
    q, p, x, c, z, y = place()
    sib = (2 * x + 1 - c, p)
    opp = (2 * (1 - x) + c, p)
    greet([sib, opp])
    steps = 4
    rows = TOKENS // 2 // steps
    mine = c * (TOKENS // 2)
    other = (1 - c) * (TOKENS // 2)

    def at(base, n):
        return pl.ds(pl.multiple_of(base + n * rows, rows), rows)

    first = [remote(part.at[at(other, n)], l1.at[n], s1.at[n], r1.at[n], sib) for n in range(steps)]
    second = [remote(own.at[n], l2.at[n], s2.at[n], r2.at[n], opp) for n in range(steps)]
    third = [remote(total.at[at(mine, n)], total.at[at(mine, n)], s3.at[n], r3.at[n], sib) for n in range(steps)]
    for cp in first:
        cp.start()
    for n in range(steps):
        first[n].wait_recv()
        own[n] = (part[at(mine, n), :].astype(F32) + l1[n].astype(F32)).astype(BF)
        second[n].start()
    for n in range(steps):
        second[n].wait_recv()
        total[at(mine, n), :] = (own[n].astype(F32) + l2[n].astype(F32)).astype(BF)
        third[n].start()
    for n in range(steps):
        remote(total.at[at(other, n)], total.at[at(other, n)], s3.at[n], r3.at[n], sib).wait_recv()
    for cp in first + second + third:
        cp.wait_send()


def allsum(part, ident):
    sem = pltpu.SemaphoreType.DMA
    return pl.pallas_call(
        allsum_kernel,
        out_shape=jax.ShapeDtypeStruct((TOKENS, WIDTH), BF),
        in_specs=[VM],
        out_specs=VM,
        scratch_shapes=[pltpu.VMEM((4, 128, WIDTH), BF)] * 3 + [sem((4,))] * 6,
        compiler_params=pltpu.CompilerParams(
            collective_id=ident, has_side_effects=True, vmem_limit_bytes=VMEM_BYTES
        ),
        name=f"sum_quarters_{ident}",
    )(part)


def unit(v):
    return lax.rsqrt(jnp.mean(v * v, axis=-1, keepdims=True) + EPS)


def blocks(ref, order, first, count):
    return jnp.concatenate(
        [ref[pl.ds(pl.multiple_of(order[first + t] * BLK, BLK), BLK), :] for t in range(count)], axis=0
    )


def pieces(ref, order, first, count):
    return jnp.concatenate([ref[order[first + t]] for t in range(count)], axis=0)


def rotate(v, cosine, sine):
    return v * cosine + pltpu.roll(v, HEAD_SIZE // 2, 1) * sine


def rotate_back(v, cosine, sine):
    return v * cosine + pltpu.roll(v * sine, HEAD_SIZE // 2, 1)


def lower(s, fill):
    n = s.shape[0]
    i = lax.broadcasted_iota(jnp.int32, (n, n), 0)
    j = lax.broadcasted_iota(jnp.int32, (n, n), 1)
    width = s.shape[1]
    diag = jnp.where(j <= i, s[:, width - n :], fill)
    return diag if width == n else jnp.concatenate([s[:, : width - n], diag], axis=1)


def forward_kernel(inv, x, w, cosf, sinf, qg, kg, wo, xhat, raw_o, qb, kb, vb, ob, lse, part):
    @pl.loop(0, 4)
    def _(n):
        rows = pl.ds(pl.multiple_of(n * 256, 256), 256)
        v = blocks(x, inv, n * 4, 4).astype(F32)
        h = (v * unit(v)).astype(BF)
        xhat[rows, :] = h
        raw = jnp.dot(h, w[...], preferred_element_type=F32)
        raw_o[rows, :] = raw[:, :768]
        cosine = cosf[rows, :]
        sine = sinf[rows, :]
        for t in range(2):
            vb[t, rows, :] = raw[:, 768 + t * 128 : 896 + t * 128].astype(BF)
        for t in range(6):
            u = raw[:, t * 128 : (t + 1) * 128]
            n_ = u * unit(u) * (qg[...] if t < 4 else kg[...])
            r = rotate(n_, cosine, sine).astype(BF)
            if t < 4:
                qb[t, rows, :] = r
            else:
                kb[t - 4, rows, :] = r

    @pl.loop(0, 4)
    def _(h):
        g = h // 2
        for i in range(4):
            length = (i + 1) * 256
            rows = slice(i * 256, length)
            s = dims(qb[h, rows, :], kb[g, :length, :], 1, 1) * (HEAD_SIZE**-0.5 * LOG2E)
            s = lower(s, NEGATIVE_FILL)
            top = jnp.max(s, axis=-1, keepdims=True)
            e = jnp.exp2(s - top)
            total = jnp.sum(e, axis=-1, keepdims=True)
            o = jnp.dot(e.astype(BF), vb[g, :length, :], preferred_element_type=F32) / total
            ob[rows, pl.ds(pl.multiple_of(h * 128, 128), 128)] = o.astype(BF)
            lse[h, rows, :] = top + jnp.log2(total)

    @pl.loop(0, 4)
    def _(n):
        rows = pl.ds(pl.multiple_of(n * 256, 256), 256)
        part[rows, :] = jnp.dot(ob[rows, :], wo[...], preferred_element_type=F32).astype(BF)


def forward_call(inv, x, w, cosf, sinf, qg, kg, wo):
    shape = jax.ShapeDtypeStruct
    return pl.pallas_call(
        forward_kernel,
        out_shape=(
            shape((TOKENS, WIDTH), BF),
            shape((TOKENS, 768), F32),
            shape((4, TOKENS, 128), BF),
            shape((2, TOKENS, 128), BF),
            shape((2, TOKENS, 128), BF),
            shape((TOKENS, 512), BF),
            shape((4, TOKENS, 1), F32),
            shape((TOKENS, WIDTH), BF),
        ),
        in_specs=[SM] + [VM] * 7,
        out_specs=(VM,) * 8,
        compiler_params=pltpu.CompilerParams(vmem_limit_bytes=VMEM_BYTES),
        name="attention_forward",
    )(inv, x, w, cosf, sinf, qg, kg, wo)


def mlp_kernel(inv, order, x, total, cot, wgu, wd, hidden, part, dpart, gd, ggu, a2, cs, mb, dgu):
    @pl.loop(0, 4)
    def _(n):
        rows = pl.ds(pl.multiple_of(n * 256, 256), 256)
        h = blocks(x, inv, n * 4, 4).astype(F32) + total[rows, :].astype(F32)
        hidden[rows, :] = h
        a = (h * unit(h)).astype(BF)
        a2[rows, :] = a
        gu = jnp.dot(a, wgu[...], preferred_element_type=F32)
        gate = gu[:, :768]
        up = gu[:, 768:]
        sig = 1.0 / (1.0 + jnp.exp2(gate * -LOG2E))
        silu = gate * sig
        mb[rows, :] = (silu * up).astype(BF)
        cc = blocks(cot, inv, n * 4, 4)
        cs[rows, :] = cc
        dm = dims(cc, wd[...], 1, 1)
        dg = (dm * up * sig * (1.0 + gate * (1.0 - sig))).astype(BF)
        du = (dm * silu).astype(BF)
        both = jnp.concatenate([dg, du], axis=1)
        dgu[rows, :] = both
        dpart[rows, :] = dims(both, wgu[...], 1, 1).astype(BF)

    @pl.loop(0, 4)
    def _(n):
        rows = pl.ds(pl.multiple_of(n * 256, 256), 256)
        part[rows, :] = jnp.dot(blocks(mb, order, n * 4, 4), wd[...], preferred_element_type=F32).astype(BF)

    @pl.loop(0, 2)
    def _(n):
        g = dims(mb[:, pl.ds(pl.multiple_of(n * 384, 128), 384)], cs[...], 0, 0).astype(BF)
        g = g.reshape(2, 2, 96, WIDTH)
        for t in range(2):
            gd[t, pl.ds(n * 2, 2)] = g[:, t]

    @pl.loop(0, 4)
    def _(n):
        g = dims(a2[:, pl.ds(pl.multiple_of(n * 256, 256), 256)], dgu[...], 0, 0).astype(BF)
        g = g.reshape(4, 2, 32, 1536)
        for t in range(2):
            ggu[t, :, n] = g[:, t]


def mlp_call(inv, order, x, total, cot, wgu, wd):
    shape = jax.ShapeDtypeStruct
    return pl.pallas_call(
        mlp_kernel,
        out_shape=(
            shape((TOKENS, WIDTH), F32),
            shape((TOKENS, WIDTH), BF),
            shape((TOKENS, WIDTH), BF),
            shape((2, 4, 96, WIDTH), BF),
            shape((2, 4, 4, 32, 1536), BF),
        ),
        in_specs=[SM] * 2 + [VM] * 5,
        out_specs=(VM,) * 5,
        scratch_shapes=[
            pltpu.VMEM((TOKENS, WIDTH), BF),
            pltpu.VMEM((TOKENS, WIDTH), BF),
            pltpu.VMEM((TOKENS, 768), BF),
            pltpu.VMEM((TOKENS, 1536), BF),
        ],
        compiler_params=pltpu.CompilerParams(vmem_limit_bytes=VMEM_BYTES),
        name="feed_forward_both",
    )(inv, order, x, total, cot, wgu, wd)


def backward_kernel(
    inv, order, cot, hidden, dtotal, wo, w, xhat, raw_i, qb, kb, vb, ob, lse, cosf, sinf, qg, kg,
    dh, go, gqkv, part, heads, dy, dob, dqkv, dkv,
):
    @pl.loop(0, 4)
    def _(n):
        rows = pl.ds(pl.multiple_of(n * 256, 256), 256)
        h = hidden[rows, :]
        r = unit(h)
        da = dtotal[rows, :].astype(F32)
        back = r * da - h * (r * r * r * jnp.mean(h * da, axis=-1, keepdims=True))
        d = blocks(cot, inv, n * 4, 4).astype(F32) + back
        dh[rows, :] = d
        low = d.astype(BF)
        dy[rows, :] = low
        do = dims(low, wo[...], 1, 1).astype(BF)
        for t in range(4):
            dob[t, rows, :] = do[:, t * 128 : (t + 1) * 128]

    @pl.loop(0, 2)
    def _(n):
        g = dims(ob[:, pl.ds(pl.multiple_of(n * 256, 256), 256)], dy[...], 0, 0).astype(BF)
        g = g.reshape(2, 2, 64, WIDTH)
        for t in range(2):
            go[t, pl.ds(n * 2, 2)] = g[:, t]

    heads[...] = jnp.zeros_like(heads)
    scale = HEAD_SIZE**-0.5

    def norm_back(dn, u, gain, rows):
        dn = rotate_back(dn, cosf[rows, :], sinf[rows, :])
        r = unit(u)
        gd = gain * dn
        du = r * gd - u * (r * r * r * jnp.mean(u * gd, axis=-1, keepdims=True))
        return du.astype(BF), jnp.sum(dn * u * r, axis=0, keepdims=True)

    @pl.loop(0, 2)
    def _(g):
        dkv[...] = jnp.zeros_like(dkv)
        for t in range(2):
            h = g * 2 + t
            lanes = pl.ds(pl.multiple_of(h * 128, 128), 128)
            for i in range(4):
                length = (i + 1) * 256
                rows = slice(i * 256, length)
                qv = qb[h, rows, :]
                kv = kb[g, :length, :]
                dov = dob[h, rows, :]
                s = dims(qv, kv, 1, 1) * (scale * LOG2E)
                pr = lower(jnp.exp2(s - lse[h, rows, :]), 0.0)
                dp = dims(dov, vb[g, :length, :], 1, 1)
                delta = jnp.sum(dov.astype(F32) * ob[rows, lanes].astype(F32), axis=-1, keepdims=True)
                ds_ = lower(pr * (dp - delta), 0.0).astype(BF)
                dq = jnp.dot(ds_, kv, preferred_element_type=F32) * scale
                dkv[0, :length, :] += dims(ds_, qv, 0, 0)
                dkv[1, :length, :] += dims(pr.astype(BF), dov, 0, 0)
                du, dgain = norm_back(dq, raw_i[rows, lanes], qg[...], pl.ds(i * 256, 256))
                dqkv[rows, lanes] = du
                heads[0:1, :] += dgain
        lanes = pl.ds(pl.multiple_of(512 + g * 128, 128), 128)
        for i in range(4):
            rows = slice(i * 256, (i + 1) * 256)
            du, dgain = norm_back(dkv[0, rows, :] * scale, raw_i[rows, lanes], kg[...], pl.ds(i * 256, 256))
            dqkv[rows, lanes] = du
            heads[1:2, :] += dgain
        dqkv[:, pl.ds(pl.multiple_of(768 + g * 128, 128), 128)] = dkv[1].astype(BF)

    @pl.loop(0, 4)
    def _(n):
        rows = pl.ds(pl.multiple_of(n * 256, 256), 256)
        part[rows, :] = dims(blocks(dqkv, order, n * 4, 4), w[...], 1, 1).astype(BF)

    @pl.loop(0, 4)
    def _(n):
        g = dims(xhat[:, pl.ds(pl.multiple_of(n * 256, 256), 256)], dqkv[...], 0, 0).astype(BF)
        g = g.reshape(4, 2, 32, WIDTH)
        for t in range(2):
            gqkv[t, :, n] = g[:, t]


def backward_call(*args):
    shape = jax.ShapeDtypeStruct
    return pl.pallas_call(
        backward_kernel,
        out_shape=(
            shape((TOKENS, WIDTH), F32),
            shape((2, 4, 64, WIDTH), BF),
            shape((2, 4, 4, 32, WIDTH), BF),
            shape((TOKENS, WIDTH), BF),
            shape((8, 128), F32),
        ),
        in_specs=[SM] * 2 + [VM] * 16,
        out_specs=(VM,) * 5,
        scratch_shapes=[
            pltpu.VMEM((TOKENS, WIDTH), BF),
            pltpu.VMEM((4, TOKENS, 128), BF),
            pltpu.VMEM((TOKENS, WIDTH), BF),
            pltpu.VMEM((2, TOKENS, 128), F32),
        ],
        compiler_params=pltpu.CompilerParams(vmem_limit_bytes=VMEM_BYTES),
        name="attention_backward",
    )(*args)


def scatter_kernel(
    gd, ggu, go, gqkv, heads, part, dpart, order, hidden, dh, x,
    out, igrad, od, ogu, oo, oqkv, oheads,
    yd, ygu, yo, yqkv, zd, zgu, zo, zqkv, dgu, dqkv, rgu, rqkv,
    hy, hz, hdp, l1, l2, own, fin,
    ys, yr, zs, zr, ds_, dr, hs, hr, s1, r1, s2, r2, fs, fr, loc,
):
    q, p, x_, c, z, y = place()
    peers = [(2 * x_ + cc, lax.rem(p + k, 8)) for k in range(1, 8) for cc in (0, 1)]
    peers += [(lax.rem(q + k, 4), p) for k in (1, 2, 3)]
    greet(peers)
    ynb = (q, 2 * z + 1 - y)
    sib = (2 * x_ + 1 - c, p)
    opp = (2 * (1 - x_) + c, p)
    owner_x, owner_c = y, z // 2
    half = TOKENS // 2
    sends = []

    def go_(cp):
        cp.start()
        sends.append(cp)

    grads = ((gd, yd, zd), (ggu, ygu, zgu), (go, yo, zo), (gqkv, yqkv, zqkv))
    for n, (g, ly, lz) in enumerate(grads):
        go_(remote(g.at[1 - y], ly, ys.at[n], yr.at[n], ynb))
    go_(remote(heads, hy, hs.at[0], hr.at[0], ynb))
    mine = pl.ds(pl.multiple_of(c * half, half), half)
    other = pl.ds(pl.multiple_of((1 - c) * half, half), half)
    parts = (part, dpart)
    for a in range(2):
        go_(remote(parts[a].at[other], l1.at[a], s1.at[a], r1.at[a], sib))

    for a in range(2):
        remote(parts[a].at[other], l1.at[a], s1.at[a], r1.at[a], sib).wait_recv()
        own[a] = (parts[a][mine, :].astype(F32) + l1[a].astype(F32)).astype(BF)

        @pl.when(x_ != owner_x)
        def _():
            remote(own.at[a], l2.at[a], s2.at[a], r2.at[a], opp).start()

    remote(heads, hy, hs.at[0], hr.at[0], ynb).wait_recv()
    hz[z] = heads[...] + hy[...]
    for k in (1, 2, 3):
        t = lax.rem(z + k, 4)
        go_(remote(hz.at[z], hz.at[z], hs.at[k], hr.at[k], (q, 2 * t + y)))

    def z_step(n):
        g, ly, lz = grads[n]
        remote(g.at[1 - y], ly, ys.at[n], yr.at[n], ynb).wait_recv()

        @pl.loop(0, 4)
        def _(t):
            ly[t] = (ly[t].astype(F32) + g[y, t].astype(F32)).astype(BF)

        for k in (1, 2, 3):
            t = lax.rem(z + k, 4)
            go_(remote(ly.at[t], lz.at[k - 1], zs.at[n, k - 1], zr.at[n, k - 1], (q, 2 * t + y)))

    def z_sum(n):
        g, ly, lz = grads[n]
        for k in (1, 2, 3):
            remote(ly.at[0], lz.at[k - 1], zs.at[n, k - 1], zr.at[n, k - 1], (q, p)).wait_recv()
        return ly[z].astype(F32) + lz[0].astype(F32) + lz[1].astype(F32) + lz[2].astype(F32)

    z_step(0)
    z_step(1)

    @pl.when(x_ == owner_x)
    def _():
        for a in range(2):
            remote(own.at[a], l2.at[a], s2.at[a], r2.at[a], opp).wait_recv()

            @pl.loop(0, 4)
            def _(n):
                rows = pl.ds(pl.multiple_of(n * 128, 128), 128)
                s = own[a, rows, :].astype(F32) + l2[a, rows, :].astype(F32)
                first = c * 8 + n * 2
                if a == 0:
                    s = s + pieces(hidden, order, first, 2)
                else:
                    v = x[pl.ds(pl.multiple_of(c * half + n * 128, 128), 128), :].astype(F32)
                    r = unit(v)
                    s = r * s - v * (r * r * r * jnp.mean(v * s, axis=-1, keepdims=True))
                    s = s + pieces(dh, order, first, 2)
                fin[a, n] = s.astype(BF)

    outs = (out, igrad)
    slot = lax.rem(z, 2)
    goal_q = 2 * owner_x + owner_c

    def home(a, n):
        return remote(fin.at[a, n], outs[a].at[slot], fs.at[a, n], fr.at[a, slot], (goal_q, 4 * c + n))

    def is_self(n):
        return jnp.logical_and(goal_q == q, 4 * c + n == p)

    @pl.when(x_ == owner_x)
    def _():
        for a in range(2):
            for n in range(4):

                @pl.when(jnp.logical_not(is_self(n)))
                def _():
                    home(a, n).start()

                @pl.when(is_self(n))
                def _():
                    cp = pltpu.make_async_copy(fin.at[a, n], outs[a].at[slot], loc.at[a])
                    cp.start()
                    cp.wait()

    z_step(2)
    z_step(3)
    for k in (1, 2, 3):
        f = lax.rem(z + 4 - k, 4)
        remote(hz.at[f], hz.at[f], hs.at[k], hr.at[k], (q, p)).wait_recv()
    hdp[q] = hz[0] + hz[1] + hz[2] + hz[3]
    for k in (1, 2, 3):
        t = lax.rem(q + k, 4)
        go_(remote(hdp.at[q], hdp.at[q], hs.at[3 + k], hr.at[3 + k], (t, p)))
    od[...] = z_sum(0)
    for n, r, land in ((1, rgu, dgu), (3, rqkv, dqkv)):
        if n == 3:
            oo[...] = z_sum(2)
        s = z_sum(n).reshape(r.shape)
        r[...] = s.astype(BF)
        m = n // 2
        for k in (1, 2, 3):
            t = lax.rem(q + k, 4)
            go_(remote(r.at[t], land.at[q], ds_.at[m, k - 1], dr.at[m, k - 1], (t, p)))
        (ogu if n == 1 else oqkv)[q] = r[q].astype(F32)
    for n, r, land, o in ((1, rgu, dgu, ogu), (3, rqkv, dqkv, oqkv)):
        m = n // 2
        for k in (1, 2, 3):
            f = lax.rem(q + 4 - k, 4)
            remote(r.at[0], land.at[f], ds_.at[m, k - 1], dr.at[m, k - 1], (q, p)).wait_recv()
            o[f] = land[f].astype(F32)
    for k in (1, 2, 3):
        f = lax.rem(q + 4 - k, 4)
        remote(hdp.at[f], hdp.at[f], hs.at[3 + k], hr.at[3 + k], (q, p)).wait_recv()
    oheads[...] = hdp[0] + hdp[1] + hdp[2] + hdp[3]
    for a in range(2):
        for i in range(2):
            group = 4 * c + 2 * i + x_
            from_c = p // 4
            here = jnp.logical_and(group == p, from_c == c)

            @pl.when(jnp.logical_not(here))
            def _():
                remote(fin.at[a, 0], outs[a].at[i], fs.at[a, 0], fr.at[a, i], (q, p)).wait_recv()

    for cp in sends:
        cp.wait_send()

    @pl.when(x_ != owner_x)
    def _():
        for a in range(2):
            remote(own.at[a], l2.at[a], s2.at[a], r2.at[a], opp).wait_send()

    @pl.when(x_ == owner_x)
    def _():
        for a in range(2):
            for n in range(4):

                @pl.when(jnp.logical_not(is_self(n)))
                def _():
                    home(a, n).wait_send()


def scatter_call(gd, ggu, go, gqkv, heads, part, dpart, order, hidden, dh, x):
    shape = jax.ShapeDtypeStruct
    sem = pltpu.SemaphoreType.DMA
    vm = pltpu.VMEM
    ggu = ggu.reshape(2, 4, 128, 1536)
    gqkv = gqkv.reshape(2, 4, 128, WIDTH)

    def y_land(g):
        return vm(g.shape[1:], BF)

    def z_land(g):
        return vm((3,) + g.shape[2:], BF)

    return pl.pallas_call(
        scatter_kernel,
        out_shape=(
            shape((2, 128, WIDTH), BF),
            shape((2, 128, WIDTH), BF),
            shape((96, WIDTH), F32),
            shape((4, 32, 1536), F32),
            shape((64, WIDTH), F32),
            shape((4, 32, WIDTH), F32),
            shape((8, 128), F32),
        ),
        in_specs=[VM] * 7 + [SM] + [VM] * 3,
        out_specs=(VM,) * 7,
        scratch_shapes=[
            y_land(gd), y_land(ggu), y_land(go), y_land(gqkv),
            z_land(gd), z_land(ggu), z_land(go), z_land(gqkv),
            vm((4, 32, 1536), BF), vm((4, 32, WIDTH), BF), vm((4, 32, 1536), BF), vm((4, 32, WIDTH), BF),
            vm((8, 128), F32), vm((4, 8, 128), F32), vm((4, 8, 128), F32),
            vm((2, 512, WIDTH), BF), vm((2, 512, WIDTH), BF), vm((2, 512, WIDTH), BF),
            vm((2, 4, 128, WIDTH), BF),
            sem((4,)), sem((4,)), sem((4, 3)), sem((4, 3)), sem((2, 3)), sem((2, 3)), sem((7,)), sem((7,)),
            sem((2,)), sem((2,)), sem((2,)), sem((2,)), sem((2, 4)), sem((2, 2)), sem((2,)),
        ],
        compiler_params=pltpu.CompilerParams(
            collective_id=3, has_side_effects=True, vmem_limit_bytes=VMEM_BYTES
        ),
        name="scatter_layer",
    )(
        gd, ggu, go, gqkv, heads, part, dpart, order,
        hidden.reshape(16, BLK, WIDTH), dh.reshape(16, BLK, WIDTH), x,
    )


def quarter_columns(w, gain):
    rows, cols = w.shape
    v = w if gain is None else (w.astype(F32) * gain).astype(BF)
    return jnp.transpose(v.reshape(rows, 4, cols // 4), (1, 0, 2))


def whole_sequences(
    tokens, attn_gain, w_query, key_projection, value_projection, query_head_gain, key_gain, w_out,
    mlp_gain, w_gate, w_up, w_down, cotangent, span_order,
):
    p = lax.axis_index("seq")
    ga = attn_gain.astype(F32)[:, None]
    gm = mlp_gain.astype(F32)[:, None]
    pq = jnp.concatenate(
        [quarter_columns(w, ga) for w in (w_query, key_projection, value_projection)], axis=2
    )
    pg = jnp.concatenate([quarter_columns(w, gm) for w in (w_gate, w_up)], axis=2)
    row = jnp.where(lax.rem(p // 2, 2) == 0, span_order[0], span_order[1])
    spots = lax.iota(jnp.int32, 16)
    inverse = jnp.sum(jnp.where(row[None, :] == spots[:, None], spots[None, :], 0), axis=1)
    pos = jnp.zeros((8, 128), jnp.int32)
    pos = pos.at[0, :16].set(row).at[1, :16].set(inverse)
    xf, cf, of, wq, wg, wo, wd = gather_call(tokens, cotangent, pos, pq, pg, w_out, w_down)
    order = of[0, :16]
    inv = of[1, :16]
    x = xf.reshape(TOKENS, WIDTH)
    cot = cf.reshape(TOKENS, WIDTH)
    w = wq.reshape(WIDTH, WIDTH)
    wgu = wg.reshape(WIDTH, 1536)
    wo = wo.reshape(512, WIDTH)
    wd = wd.reshape(768, WIDTH)
    freqs = BASE ** (-(lax.iota(F32, HEAD_SIZE // 2) * 2.0) / HEAD_SIZE)
    angles = lax.iota(F32, TOKENS)[:, None] * freqs[None, :]
    cosine = jnp.cos(angles)
    sine = jnp.sin(angles)
    cosf = jnp.concatenate([cosine, cosine], axis=1)
    sinf = jnp.concatenate([-sine, sine], axis=1)
    qg = query_head_gain.astype(F32)[None, :]
    kg = key_gain.astype(F32)[None, :]
    xhat, raw, qb, kb, vb, ob, lse, part1 = forward_call(inv, x, w, cosf, sinf, qg, kg, wo)
    total = allsum(part1, 1)
    hidden, part2, dpart, gd, ggu = mlp_call(inv, order, x, total, cot, wgu, wd)
    dtotal = allsum(dpart, 2)
    dh, go, gqkv, part3, heads = backward_call(
        inv, order, cot, hidden, dtotal, wo, w, xhat, raw, qb, kb, vb, ob, lse, cosf, sinf, qg, kg
    )
    out, igrad, od, ogu, oo, oqkv, oheads = scatter_call(
        gd, ggu, go, gqkv, heads, part2, part3, order, hidden, dh, x
    )
    return finish(
        out, igrad, od, ogu, oo, oqkv, oheads, ga, gm, w_query, key_projection, value_projection, w_gate, w_up
    )


def finish(out, igrad, od, ogu, oo, oqkv, oheads, ga, gm, w_query, key_projection, value_projection, w_gate, w_up):
    def join(part):
        return jnp.transpose(part, (1, 0, 2)).reshape(part.shape[1], -1)

    hq, hk, hv = join(oqkv[:, :, :512]), join(oqkv[:, :, 512:768]), join(oqkv[:, :, 768:])
    hg, hu = join(ogu[:, :, :768]), join(ogu[:, :, 768:])

    def along(w, h):
        return jnp.sum(w.astype(F32) * h, axis=1)

    grad_attn_gain = along(w_query, hq) + along(key_projection, hk) + along(value_projection, hv)
    grad_mlp_gain = along(w_gate, hg) + along(w_up, hu)
    return (
        out,
        igrad,
        grad_attn_gain,
        ga * hq,
        ga * hk,
        ga * hv,
        oheads[0],
        oheads[1],
        oo,
        grad_mlp_gain,
        gm * hg,
        gm * hu,
        od,
    )


def layer(tokens, *rest):
    whole = (
        lax.axis_size("dp") == 4
        and lax.axis_size("seq") == 8
        and tokens.shape == (2, 128, WIDTH)
        and rest[-1].shape == (2, 16)
    )
    return (whole_sequences if whole else shards)(tokens, *rest)


def solution(mesh):
    return jax.shard_map(
        layer,
        mesh=mesh,
        in_specs=(
            P("dp", "seq", None),
            P(("dp", "seq")),
            P(("dp", "seq"), None),
            P(("dp", "seq"), None),
            P(("dp", "seq"), None),
            P(),
            P(),
            P(("dp", "seq"), None),
            P(("dp", "seq")),
            P(("dp", "seq"), None),
            P(("dp", "seq"), None),
            P(("dp", "seq"), None),
            P("dp", "seq", None),
            P("dp", None),
        ),
        out_specs=(
            P("dp", "seq", None),
            P("dp", "seq", None),
            P(("dp", "seq")),
            P(("dp", "seq"), None),
            P(("dp", "seq"), None),
            P(("dp", "seq"), None),
            P(),
            P(),
            P(("dp", "seq"), None),
            P(("dp", "seq")),
            P(("dp", "seq"), None),
            P(("dp", "seq"), None),
            P(("dp", "seq"), None),
        ),
        check_vma=False,
    )
```

```python
import jax
import jax.numpy as jnp
from jax import lax
from jax.sharding import PartitionSpec as P

from jax.experimental import pallas as pl
from jax.experimental.pallas import tpu as pltpu

QUERY_HEADS = 16
KEY_VALUE_HEADS = 8
HEAD_SIZE = 128
BLK = 64
MB = 2


EPS = 1e-06
BASE = 1000000.0
NEGATIVE_FILL = -1e30


def from_behind(block, axis, distance):
    devices = range(lax.axis_size(axis))
    route = [((i - distance) % len(devices), i) for i in devices]
    return lax.ppermute(block, axis, route)


def row_norm_apply(v, gain):
    return v * lax.rsqrt(jnp.mean(v * v, axis=-1, keepdims=True) + EPS) * gain


def apply_rotary(v, cosine_table, sine_table):
    half = v.shape[-1] // 2
    first = v[..., :half]
    second = v[..., half:]
    return jnp.concatenate(
        [first * cosine_table - second * sine_table, second * cosine_table + first * sine_table],
        axis=-1,
    )


def matrix_multiply(left, right):
    return jnp.dot(left, right, preferred_element_type=jnp.float32)


def row_product(left, right):
    return lax.dot_general(
        left, right, (((0,), (0,)), ((), ())), preferred_element_type=jnp.float32
    )


def product_backward(left, right):
    return lax.dot_general(
        left, right, (((1,), (1,)), ((), ())), preferred_element_type=jnp.float32
    )


def block_positions(order, start, count):
    places = start + lax.iota(jnp.int32, count)
    which = places // BLK
    hits = (which[:, None] == lax.iota(jnp.int32, order.shape[1])[None, :]).astype(jnp.int32)
    spans = jnp.sum(hits[None, :, :] * order[:, None, :], axis=-1)
    return spans * BLK + places % BLK


def pack_shares(members, count):
    return jnp.concatenate([m.reshape(count, -1) for m in members], axis=1).reshape(-1)


def unpack_shares(flat, members, count):
    pieces = []
    offset = 0
    for m in members:
        length = m.size // count
        share_shape = (m.shape[0] // count,) + tuple(m.shape[1:])
        pieces.append(flat[offset : offset + length].reshape(share_shape))
        offset = offset + length
    return pieces


def shards(
    tokens,
    attn_gain,
    w_query,
    key_projection,
    value_projection,
    query_head_gain,
    key_gain,
    w_out,
    mlp_gain,
    w_gate,
    w_up,
    w_down,
    cotangent,
    span_order,
):
    seq_count = lax.axis_size("seq")
    seq_place = lax.axis_index("seq")
    all_count = lax.axis_size(("dp", "seq"))
    local_length = tokens.shape[1]
    width = tokens.shape[2]
    sequence_permutation = tokens.shape[0] // MB
    query_group = QUERY_HEADS // KEY_VALUE_HEADS
    scale = HEAD_SIZE ** (-0.5)
    freqs = BASE ** (-(lax.iota(jnp.float32, HEAD_SIZE // 2) * 2.0) / HEAD_SIZE)
    query_norm_gain = query_head_gain.astype(jnp.float32)
    kgain = key_gain.astype(jnp.float32)
    sums = None
    outputs = []
    input_grads = []
    for batch in range(MB):
        rows_x = tokens[batch * sequence_permutation : (batch + 1) * sequence_permutation]
        rows_cot = cotangent[batch * sequence_permutation : (batch + 1) * sequence_permutation]
        order = span_order[batch * sequence_permutation : (batch + 1) * sequence_permutation]
        gain_a, wq, key_weight, value_weight, output_weight = (
            lax.all_gather(attn_gain, ("dp", "seq"), axis=0, tiled=True),
            lax.all_gather(w_query, ("dp", "seq"), axis=0, tiled=True),
            lax.all_gather(key_projection, ("dp", "seq"), axis=0, tiled=True),
            lax.all_gather(value_projection, ("dp", "seq"), axis=0, tiled=True),
            lax.all_gather(w_out, ("dp", "seq"), axis=0, tiled=True),
        )
        gain_m, wg, wu, wd = (
            lax.all_gather(mlp_gain, ("dp", "seq"), axis=0, tiled=True),
            lax.all_gather(w_gate, ("dp", "seq"), axis=0, tiled=True),
            lax.all_gather(w_up, ("dp", "seq"), axis=0, tiled=True),
            lax.all_gather(w_down, ("dp", "seq"), axis=0, tiled=True),
        )
        own_pos = block_positions(order, seq_place * local_length, local_length)
        angles = own_pos.astype(jnp.float32)[..., None] * freqs
        cosine_table = jnp.cos(angles)[:, :, None, :]
        sine_table = jnp.sin(angles)[:, :, None, :]

        def query_per_head(raw, gain):
            return apply_rotary(row_norm_apply(raw, gain), cosine_table, sine_table)

        flat_x = rows_x.reshape(-1, width).astype(jnp.float32)
        first_operand = row_norm_apply(flat_x, gain_a.astype(jnp.float32)).astype(jnp.bfloat16)
        query_unrotated = matrix_multiply(first_operand, wq).reshape(
            sequence_permutation, local_length, QUERY_HEADS, HEAD_SIZE
        )
        key_unrotated = matrix_multiply(first_operand, key_weight).reshape(
            sequence_permutation, local_length, KEY_VALUE_HEADS, HEAD_SIZE
        )
        value_reduced = (
            matrix_multiply(first_operand, value_weight)
            .astype(jnp.bfloat16)
            .reshape(sequence_permutation, local_length, KEY_VALUE_HEADS, HEAD_SIZE)
        )
        q_low = (
            query_per_head(query_unrotated, query_norm_gain)
            .astype(jnp.bfloat16)
            .reshape(sequence_permutation, local_length, KEY_VALUE_HEADS, query_group, HEAD_SIZE)
        )
        k_low = query_per_head(key_unrotated, kgain).astype(jnp.bfloat16)
        initial_maximum = jnp.full(
            (sequence_permutation, KEY_VALUE_HEADS, query_group, local_length),
            NEGATIVE_FILL,
            jnp.float32,
        )
        top = initial_maximum
        piece_k = lax.all_gather(k_low, "seq", axis=1, tiled=True)
        piece_v = lax.all_gather(value_reduced, "seq", axis=1, tiled=True)
        key_pos = block_positions(order, jnp.int32(0), piece_k.shape[1])
        visible = key_pos[:, None, None, None, :] <= own_pos[:, None, None, :, None]
        scores = (
            jnp.einsum("sqgrd,skgd->sgrqk", q_low, piece_k, preferred_element_type=jnp.float32)
            * scale
        )
        scores = jnp.where(visible, scores, NEGATIVE_FILL)
        new_top = jnp.maximum(top, jnp.max(scores, axis=-1))
        weights = jnp.exp(scores - new_top[..., None])
        new_total = jnp.sum(weights, axis=-1)
        taken = jnp.einsum(
            "sgrqk,skgd->sqgrd",
            weights.astype(jnp.bfloat16),
            piece_v,
            preferred_element_type=jnp.float32,
        )
        top = new_top
        log_total = top + jnp.log(new_total)
        attn = taken / jnp.transpose(new_total, (0, 3, 1, 2))[..., None]
        o_low = attn.astype(jnp.bfloat16).reshape(
            sequence_permutation * local_length, QUERY_HEADS * HEAD_SIZE
        )
        hidden = flat_x + matrix_multiply(o_low, output_weight)
        gain_second = gain_m.astype(jnp.float32)
        a_second = row_norm_apply(hidden, gain_second).astype(jnp.bfloat16)
        gate = matrix_multiply(a_second, wg)
        up_part = matrix_multiply(a_second, wu)
        mixed = (gate * jax.nn.sigmoid(gate) * up_part).astype(jnp.bfloat16)
        result = hidden + matrix_multiply(mixed, wd)
        outputs.append(
            result.astype(jnp.bfloat16).reshape(sequence_permutation, local_length, width)
        )
        gain_a, wq, key_weight, value_weight, output_weight = (
            lax.all_gather(attn_gain, ("dp", "seq"), axis=0, tiled=True),
            lax.all_gather(w_query, ("dp", "seq"), axis=0, tiled=True),
            lax.all_gather(key_projection, ("dp", "seq"), axis=0, tiled=True),
            lax.all_gather(value_projection, ("dp", "seq"), axis=0, tiled=True),
            lax.all_gather(w_out, ("dp", "seq"), axis=0, tiled=True),
        )
        gain_m, wg, wu, wd = (
            lax.all_gather(mlp_gain, ("dp", "seq"), axis=0, tiled=True),
            lax.all_gather(w_gate, ("dp", "seq"), axis=0, tiled=True),
            lax.all_gather(w_up, ("dp", "seq"), axis=0, tiled=True),
            lax.all_gather(w_down, ("dp", "seq"), axis=0, tiled=True),
        )
        flat_cot = rows_cot.reshape(-1, width)
        grad_down = row_product(mixed, flat_cot)
        d_mixed = product_backward(flat_cot, wd)

        def mix(gate_in, up_in):
            return gate_in * jax.nn.sigmoid(gate_in) * up_in

        _, mix_back = jax.vjp(mix, gate, up_part)
        d_gate, d_up = mix_back(d_mixed)
        gate_low = d_gate.astype(jnp.bfloat16)
        up_low = d_up.astype(jnp.bfloat16)
        grad_gate = row_product(a_second, gate_low)
        grad_up = row_product(a_second, up_low)
        d_second = product_backward(gate_low, wg) + product_backward(up_low, wu)
        _, second_back = jax.vjp(row_norm_apply, hidden, gain_second)
        d_hidden_norm, grad_mlp_gain = second_back(d_second)
        d_hidden = flat_cot.astype(jnp.float32) + d_hidden_norm
        grad_output_reduced = d_hidden.astype(jnp.bfloat16)
        grad_out = row_product(o_low, grad_output_reduced)
        do_low = (
            product_backward(grad_output_reduced, output_weight)
            .astype(jnp.bfloat16)
            .reshape(sequence_permutation, local_length, KEY_VALUE_HEADS, query_group, HEAD_SIZE)
        )
        delta = jnp.transpose(jnp.sum(do_low.astype(jnp.float32) * attn, axis=-1), (0, 2, 3, 1))

        def back_terms(held_k, held_v, visible):
            scores = (
                jnp.einsum("sqgrd,skgd->sgrqk", q_low, held_k, preferred_element_type=jnp.float32)
                * scale
            )
            scores = jnp.where(visible, scores, NEGATIVE_FILL)
            probs = jnp.exp(scores - log_total[..., None])
            d_probs = jnp.einsum(
                "sqgrd,skgd->sgrqk", do_low, held_v, preferred_element_type=jnp.float32
            )
            score_low = (probs * (d_probs - delta[..., None])).astype(jnp.bfloat16)
            probs_low = probs.astype(jnp.bfloat16)
            term_q = scale * jnp.einsum(
                "sgrqk,skgd->sqgrd", score_low, held_k, preferred_element_type=jnp.float32
            )
            term_k = scale * jnp.einsum(
                "sgrqk,sqgrd->skgd", score_low, q_low, preferred_element_type=jnp.float32
            )
            term_v = jnp.einsum(
                "sgrqk,sqgrd->skgd", probs_low, do_low, preferred_element_type=jnp.float32
            )
            return (term_k, term_v, term_q)

        def cycle_step(turn, state):
            held_k, held_v, acc_k, acc_v, acc_q = state
            owner = (seq_place - turn) % seq_count
            key_pos = block_positions(order, owner * local_length, local_length)
            visible = key_pos[:, None, None, None, :] <= own_pos[:, None, None, :, None]
            term_k, term_v, term_q = back_terms(held_k, held_v, visible)
            acc_k, acc_v, acc_q = (acc_k + term_k, acc_v + term_v, acc_q + term_q)
            held_k, held_v = from_behind((held_k, held_v), "seq", 1)
            acc_k, acc_v = (
                from_behind(acc_k.astype(jnp.bfloat16), "seq", 1).astype(acc_k.dtype),
                from_behind(acc_v.astype(jnp.bfloat16), "seq", 1).astype(acc_v.dtype),
            )
            return (held_k, held_v, acc_k, acc_v, acc_q)

        def two_steps(pair, state):
            return cycle_step(2 * pair + 1, cycle_step(2 * pair, state))

        blank_key_value = jnp.zeros(
            (sequence_permutation, local_length, KEY_VALUE_HEADS, HEAD_SIZE), jnp.float32
        )
        blank_query = jnp.zeros(
            (sequence_permutation, local_length, KEY_VALUE_HEADS, query_group, HEAD_SIZE),
            jnp.float32,
        )
        state = lax.fori_loop(
            0,
            seq_count // 2,
            two_steps,
            (k_low, value_reduced, blank_key_value, blank_key_value, blank_query),
        )
        _, _, d_keys, grad_value_rows, d_queries = state
        _, query_back = jax.vjp(query_per_head, query_unrotated, query_norm_gain)
        d_q_raw, grad_qgain = query_back(
            d_queries.reshape(sequence_permutation, local_length, QUERY_HEADS, HEAD_SIZE)
        )
        _, key_back = jax.vjp(query_per_head, key_unrotated, kgain)
        grad_key_unrotated, grad_kgain = key_back(d_keys)
        dq_low = d_q_raw.astype(jnp.bfloat16).reshape(
            sequence_permutation * local_length, QUERY_HEADS * HEAD_SIZE
        )
        grad_key_reduced = grad_key_unrotated.astype(jnp.bfloat16).reshape(
            sequence_permutation * local_length, KEY_VALUE_HEADS * HEAD_SIZE
        )
        grad_value_reduced = grad_value_rows.astype(jnp.bfloat16).reshape(
            sequence_permutation * local_length, KEY_VALUE_HEADS * HEAD_SIZE
        )
        grad_query = row_product(first_operand, dq_low)
        grad_key = row_product(first_operand, grad_key_reduced)
        grad_value = row_product(first_operand, grad_value_reduced)
        d_first = (
            product_backward(dq_low, wq)
            + product_backward(grad_key_reduced, key_weight)
            + product_backward(grad_value_reduced, value_weight)
        )
        _, first_back = jax.vjp(row_norm_apply, flat_x, gain_a.astype(jnp.float32))
        d_x_norm, grad_attn_gain = first_back(d_first)
        input_grads.append(
            (d_hidden + d_x_norm)
            .astype(jnp.bfloat16)
            .reshape(sequence_permutation, local_length, width)
        )
        fresh = (
            grad_attn_gain,
            grad_query,
            grad_key,
            grad_value,
            grad_out,
            grad_mlp_gain,
            grad_gate,
            grad_up,
            grad_down,
            grad_qgain,
            grad_kgain,
        )
        if sums is None:
            sums = fresh
        else:
            sums = tuple((a + b for a, b in zip(sums, fresh)))
    attn_members = (sums[0], sums[1], sums[2], sums[3], sums[4])
    mlp_members = (sums[5], sums[6], sums[7], sums[8])
    attn_flat = lax.psum_scatter(
        pack_shares(attn_members, all_count), ("dp", "seq"), scatter_dimension=0, tiled=True
    )
    mlp_flat = lax.psum_scatter(
        pack_shares(mlp_members, all_count), ("dp", "seq"), scatter_dimension=0, tiled=True
    )
    attn_shares = unpack_shares(attn_flat, attn_members, all_count)
    mlp_shares = unpack_shares(mlp_flat, mlp_members, all_count)
    head_sums = lax.psum((sums[9], sums[10]), ("dp", "seq"))
    return (
        jnp.concatenate(outputs, axis=0),
        jnp.concatenate(input_grads, axis=0),
        attn_shares[0],
        attn_shares[1],
        attn_shares[2],
        attn_shares[3],
        head_sums[0],
        head_sums[1],
        attn_shares[4],
        mlp_shares[0],
        mlp_shares[1],
        mlp_shares[2],
        mlp_shares[3],
    )


BF = jnp.bfloat16
F32 = jnp.float32
MESH = pl.DeviceIdType.MESH
TOKENS = 1024
WIDTH = 1024
LOG2E = 1.4426950408889634
VM = pl.BlockSpec(memory_space=pltpu.VMEM)
SM = pl.BlockSpec(memory_space=pltpu.SMEM)
ANY = pl.BlockSpec(memory_space=pl.ANY)
VMEM_BYTES = 65100 * 1024


def place():
    q = lax.axis_index("dp")
    p = lax.axis_index("seq")
    return q, p, q // 2, lax.rem(q, 2), p // 2, lax.rem(p, 2)


def greet(peers):
    barrier = pltpu.get_barrier_semaphore()
    for peer in peers:
        pl.semaphore_signal(barrier, inc=1, device_id=peer, device_id_type=MESH)
    pl.semaphore_wait(barrier, len(peers))


def remote(src, dst, send, recv, peer):
    return pltpu.make_async_remote_copy(
        src_ref=src, dst_ref=dst, send_sem=send, recv_sem=recv, device_id=peer, device_id_type=MESH
    )


def dims(left, right, lc, rc):
    return lax.dot_general(left, right, (((lc,), (rc,)), ((), ())), preferred_element_type=F32)


def mod(a, n):
    return a % n


def unit(v):
    return lax.rsqrt(jnp.mean(v * v, axis=-1, keepdims=True) + EPS)


def pieces(ref, spots, which, first, count):
    return jnp.concatenate([ref[spots[which, first + t]] for t in range(count)], axis=0)


def rotate(v, cosine, sine):
    return v * cosine + pltpu.roll(v, HEAD_SIZE // 2, 1) * sine


def rotate_back(v, cosine, sine):
    return v * cosine + pltpu.roll(v * sine, HEAD_SIZE // 2, 1)


def lower(s, fill):
    n = s.shape[0]
    i = lax.broadcasted_iota(jnp.int32, (n, n), 0)
    j = lax.broadcasted_iota(jnp.int32, (n, n), 1)
    width = s.shape[1]
    diag = jnp.where(j <= i, s[:, width - n :], fill)
    return diag if width == n else jnp.concatenate([s[:, : width - n], diag], axis=1)


class Sum:
    def __init__(self, part, total, l1, own, l2, sems, base):
        self.q, self.p, self.x, self.c, _, _ = place()
        self.part, self.total, self.l1, self.own, self.l2 = part, total, l1, own, l2
        self.sems, self.base = sems, base
        self.sib = (2 * self.x + 1 - self.c, self.p)
        self.opp = (2 * (1 - self.x) + self.c, self.p)

    def rows(self, n, c):
        return pl.ds(pl.multiple_of(n * 256 + c * 128, 128), 128)

    def copy(self, step, n):
        s, r = self.sems.at[self.base + 2 * step, n], self.sems.at[self.base + 2 * step + 1, n]
        mine = self.rows(n, self.c)
        if step == 0:
            return remote(self.part.at[self.rows(n, 1 - self.c)], self.l1.at[n], s, r, self.sib)
        if step == 1:
            return remote(self.own.at[n], self.l2.at[n], s, r, self.opp)
        return remote(self.total.at[mine], self.total.at[mine], s, r, self.sib)

    def beside(self, n):
        self.copy(0, n).start()

    def across(self, n):
        self.copy(0, n).wait_recv()
        mine = self.part[self.rows(n, self.c), :].astype(F32)
        self.own[n] = (mine + self.l1[n].astype(F32)).astype(BF)
        self.copy(1, n).start()

    def back(self, n):
        self.copy(1, n).wait_recv()
        self.total[self.rows(n, self.c), :] = (self.own[n].astype(F32) + self.l2[n].astype(F32)).astype(BF)
        self.copy(2, n).start()

    def ready(self, n):
        other = self.rows(n, 1 - self.c)
        s, r = self.sems.at[self.base + 4, n], self.sems.at[self.base + 5, n]
        remote(self.total.at[other], self.total.at[other], s, r, self.sib).wait_recv()

    def close(self):
        @pl.loop(0, 4)
        def _(n):
            for step in range(3):
                self.copy(step, n).wait_send()


def block(ref, b):
    return ref.at[pl.ds(2 * b, 2)]


class Gather:
    def __init__(self, srcs, dsts, sems):
        self.q, self.p, self.x, self.c, self.z, self.y = place()
        self.tok, self.cot, self.pos, self.pq, self.pg, self.po, self.pd = srcs
        self.xf, self.cf, self.of, *self.w = dsts
        (self.loc, self.ts, self.tr, self.fs, self.fr, self.ps, self.pr,
         self.as_, self.ar, self.zs, self.zr, self.ys, self.yr) = sems
        q, p, x, c, z, y = self.q, self.p, self.x, self.c, self.z, self.y
        self.owner_x, self.owner_c = y, z // 2
        self.is_owner = jnp.logical_and(x == self.owner_x, c == self.owner_c)
        self.cross = jnp.logical_and(x != self.owner_x, c == self.owner_c)
        self.sib = (2 * x + 1 - c, p)
        self.opp = (2 * (1 - x) + c, p)

    def peers(self):
        q, p = self.q, self.p
        return [(mod(q + k, 4), p) for k in (1, 2, 3)] + [(q, mod(p + k, 8)) for k in range(1, 8)]

    def col(self, n):
        return (self.pq, self.pg)[n], self.w[n]

    def own_copy(self, n):
        q, p = self.q, self.p
        if n < 2:
            src, dst = self.col(n)
            return pltpu.make_async_copy(src.at[q], dst.at[q, p], self.loc.at[n])
        return pltpu.make_async_copy((self.po, self.pd)[n - 2], self.w[n].at[p], self.loc.at[n])

    def column_copy(self, n, k):
        q, p = self.q, self.p
        src, dst = self.col(n)
        t = mod(q + k, 4)
        return remote(src.at[t], dst.at[q, p], self.as_.at[n, k - 1], self.ar.at[n, k - 1], (t, p))

    def column_start(self, n):
        for k in (1, 2, 3):
            self.column_copy(n, k).start()

    def column_wait(self, n):
        q, p = self.q, self.p
        src, dst = self.col(n)
        for k in (1, 2, 3):
            f = mod(q + 4 - k, 4)
            remote(src.at[0], dst.at[f, p], self.as_.at[n, k - 1], self.ar.at[n, k - 1], (q, p)).wait_recv()

    def view(self, n, chunk):
        return self.w[n].at[:, chunk] if n < 2 else self.w[n].at[chunk]

    def z_copy(self, n, k):
        t = mod(self.z + k, 4)
        v = self.view(n, self.p)
        return remote(v, v, self.zs.at[n, k - 1], self.zr.at[n, k - 1], (self.q, 2 * t + self.y))

    def z_send(self, n):
        for k in (1, 2, 3):
            self.z_copy(n, k).start()

    def y_copy(self, n, k):
        v = self.view(n, 2 * mod(self.z + 4 - k, 4) + self.y)
        return remote(v, v, self.ys.at[n, k], self.yr.at[n, k], (self.q, 2 * self.z + 1 - self.y))

    def y_send(self, n, k):
        self.y_copy(n, k).start()

    def z_wait(self, n, k):
        v = self.view(n, 2 * mod(self.z + 4 - k, 4) + self.y)
        remote(v, v, self.zs.at[n, k - 1], self.zr.at[n, k - 1], (self.q, self.p)).wait_recv()

    def y_wait(self, n):
        for k in range(4):
            v = self.view(n, 2 * mod(self.z + 4 - k, 4) + 1 - self.y)
            remote(v, v, self.ys.at[n, k], self.yr.at[n, k], (self.q, self.p)).wait_recv()

    def pass_on(self, n, k):
        self.z_wait(n, k)
        self.y_send(n, k)

    def tok_dst(self, a):
        return (self.xf, self.cf)[a]

    def token_copy(self, a, i):
        src, dst = (self.tok, self.cot)[a], self.tok_dst(a)
        goal = 4 * self.c + 2 * i + self.x
        return goal, remote(src.at[i], block(dst, self.p), self.ts.at[a, i], self.tr.at[a, self.p], (self.q, goal))

    def token_local(self, a, i):
        return pltpu.make_async_copy((self.tok, self.cot)[a].at[i], block(self.tok_dst(a), self.p), self.loc.at[4 + a])

    def token_start(self, a):
        for i in range(2):
            goal, cp = self.token_copy(a, i)

            @pl.when(goal != self.p)
            def _():
                cp.start()

            @pl.when(goal == self.p)
            def _():
                self.token_local(a, i).start()

    def token_pass(self, a, first=0, end=8):
        dst = self.tok_dst(a)
        q, p = self.q, self.p

        @pl.when(self.is_owner)
        def _():
            @pl.loop(first, end)
            def _(b):
                @pl.when(b != p)
                def _():
                    remote(block(dst, b), block(dst, b), self.ts.at[a, 0], self.tr.at[a, b], (q, p)).wait_recv()

                @pl.when(b == p)
                def _():
                    self.token_local(a, 0).wait()

                remote(block(dst, b), block(dst, b), self.fs.at[a, 0, b], self.fr.at[a, b], self.sib).start()
                remote(block(dst, b), block(dst, b), self.fs.at[a, 1, b], self.fr.at[a, b], self.opp).start()

        @pl.when(jnp.logical_not(self.is_owner))
        def _():
            @pl.loop(first, end)
            def _(b):
                remote(block(dst, b), block(dst, b), self.fs.at[a, 0, b], self.fr.at[a, b], self.sib).wait_recv()

                @pl.when(self.cross)
                def _():
                    remote(block(dst, b), block(dst, b), self.fs.at[a, 0, b], self.fr.at[a, b], self.sib).start()

    def token_close(self, a):
        dst = self.tok_dst(a)
        q, p = self.q, self.p
        for i in range(2):
            goal, cp = self.token_copy(a, i)

            @pl.when(goal != p)
            def _():
                cp.wait_send()

        @pl.when(self.is_owner)
        def _():
            @pl.loop(0, 8)
            def _(b):
                remote(block(dst, b), block(dst, b), self.fs.at[a, 0, b], self.fr.at[a, b], (q, p)).wait_send()
                remote(block(dst, b), block(dst, b), self.fs.at[a, 1, b], self.fr.at[a, b], (q, p)).wait_send()

        @pl.when(self.cross)
        def _():
            @pl.loop(0, 8)
            def _(b):
                remote(block(dst, b), block(dst, b), self.fs.at[a, 0, b], self.fr.at[a, b], (q, p)).wait_send()

    def pos_copy(self, k):
        return remote(self.pos, self.of, self.ps.at[k], self.pr.at[0], (mod(self.q + k + 1, 4), self.p))

    def pos_start(self):
        @pl.when(self.is_owner)
        def _():
            pltpu.make_async_copy(self.pos, self.of, self.loc.at[6]).start()
            for k in range(3):
                self.pos_copy(k).start()

    def pos_finish(self):
        @pl.when(self.is_owner)
        def _():
            pltpu.make_async_copy(self.pos, self.of, self.loc.at[6]).wait()
            for k in range(3):
                self.pos_copy(k).wait_send()

        @pl.when(jnp.logical_not(self.is_owner))
        def _():
            self.pos_copy(0).wait_recv()

    def close(self):
        for n in range(4):
            for k in (1, 2, 3):
                if n < 2:
                    self.column_copy(n, k).wait_send()
                self.z_copy(n, k).wait_send()
            for k in range(4):
                self.y_copy(n, k).wait_send()
        self.token_close(0)
        self.token_close(1)


GATHER_SEMS = ((7,), (2, 2), (2, 8), (2, 2, 8), (2, 8), (3,), (1,), (2, 3), (2, 3), (4, 3), (4, 3), (4, 4), (4, 4))


def first_kernel(
    tok, cot, pos, pq, pg, po, pd, cosf, sinf, qg, kg,
    xf, of, wq, wo, xhat, raw_o, qb, kb, vb, ob, lse, hidden, cs, part2, dtotal, gd, ggu,
    cf, wg, wd, part1, total, dpart, a2, mb, dgu, l1, own, l2, l1b, ownb, l2b, sorts, sorts_sem, sums, *sems,
):
    g = Gather((tok, cot, pos, pq, pg, po, pd), (xf, cf, of, wq, wg, wo, wd), sems)
    greet(g.peers())
    g.pos_start()
    g.column_start(0)
    g.token_start(0)
    for n in range(4):
        g.own_copy(n).start()
    g.column_start(1)
    g.own_copy(0).wait()
    g.column_wait(0)
    g.z_send(0)
    g.y_send(0, 0)
    g.pos_finish()
    sort = pltpu.make_async_copy(of, sorts, sorts_sem.at[0])
    sort.start()
    g.token_pass(0, 0, 4)
    for k in (1, 3, 2):
        g.pass_on(0, k)
    g.own_copy(2).wait()
    g.z_send(2)
    g.y_send(2, 0)
    g.token_pass(0, 4, 8)
    g.own_copy(1).wait()
    g.column_wait(1)
    g.z_send(1)
    g.y_send(1, 0)
    g.own_copy(3).wait()
    g.z_send(3)
    g.y_send(3, 0)
    g.token_start(1)
    sort.wait()
    g.y_wait(0)

    @pl.loop(0, 4)
    def _(n):
        rows = pl.ds(pl.multiple_of(n * 256, 256), 256)
        v = pieces(xf, sorts, 1, n * 4, 4).astype(F32)
        h = (v * unit(v)).astype(BF)
        xhat[rows, :] = h
        raw = jnp.dot(h, wq[...].reshape(WIDTH, WIDTH), preferred_element_type=F32)
        raw_o[rows, :] = raw[:, :768]
        cosine = cosf[rows, :]
        sine = sinf[rows, :]
        for t in range(2):
            vb[t, rows, :] = raw[:, 768 + t * 128 : 896 + t * 128].astype(BF)
        for t in range(6):
            u = raw[:, t * 128 : (t + 1) * 128]
            n_ = u * unit(u) * (qg[...] if t < 4 else kg[...])
            r = rotate(n_, cosine, sine).astype(BF)
            if t < 4:
                qb[t, rows, :] = r
            else:
                kb[t - 4, rows, :] = r

    @pl.loop(0, 4)
    def _(h):
        for turn, todo in enumerate((((2, 1), (2, 3), (2, 2)), ((1, 1),), ((1, 3),), ((1, 2),))):

            @pl.when(h == turn)
            def _():
                for n, k in todo:
                    g.pass_on(n, k)

        kv = h // 2
        for i in range(4):
            length = (i + 1) * 256
            rows = slice(i * 256, length)
            s = dims(qb[h, rows, :], kb[kv, :length, :], 1, 1) * (HEAD_SIZE**-0.5 * LOG2E)
            s = lower(s, NEGATIVE_FILL)
            top = jnp.max(s, axis=-1, keepdims=True)
            e = jnp.exp2(s - top)
            sum_e = jnp.sum(e, axis=-1, keepdims=True)
            o = jnp.dot(e.astype(BF), vb[kv, :length, :], preferred_element_type=F32) / sum_e
            ob[rows, pl.ds(pl.multiple_of(h * 128, 128), 128)] = o.astype(BF)
            lse[h, rows, :] = top + jnp.log2(sum_e)

    g.y_wait(2)
    s1 = Sum(part1, total, l1, own, l2, sums, 0)
    s2 = Sum(dpart, dtotal, l1b, ownb, l2b, sums, 6)

    @pl.loop(0, 4)
    def _(n):
        rows = pl.ds(pl.multiple_of(n * 256, 256), 256)
        out_w = wo[...].reshape(512, WIDTH)
        part1[rows, :] = jnp.dot(ob[rows, :], out_w, preferred_element_type=F32).astype(BF)
        s1.beside(n)

        @pl.when(n > 0)
        def _():
            s1.across(n - 1)

    s1.across(3)
    for k in (1, 3, 2):
        g.pass_on(3, k)
    s1.back(0)
    g.token_pass(1)
    g.y_wait(1)
    g.y_wait(3)

    @pl.loop(0, 4)
    def _(n):
        s1.ready(n)

        @pl.when(n < 3)
        def _():
            s1.back(n + 1)

        rows = pl.ds(pl.multiple_of(n * 256, 256), 256)
        h = pieces(xf, sorts, 1, n * 4, 4).astype(F32) + total[rows, :].astype(F32)
        hidden[rows, :] = h
        a = (h * unit(h)).astype(BF)
        a2[rows, :] = a
        wgu = wg[...].reshape(WIDTH, 1536)
        gu = jnp.dot(a, wgu, preferred_element_type=F32)
        gate = gu[:, :768]
        up = gu[:, 768:]
        sig = 1.0 / (1.0 + jnp.exp2(gate * -LOG2E))
        silu = gate * sig
        mb[pl.ds(n * 4, 4)] = (silu * up).astype(BF).reshape(4, BLK, 768)
        cc = pieces(cf, sorts, 1, n * 4, 4)
        cs[rows, :] = cc
        dm = dims(cc, wd[...].reshape(768, WIDTH), 1, 1)
        dg = (dm * up * sig * (1.0 + gate * (1.0 - sig))).astype(BF)
        du = (dm * silu).astype(BF)
        both = jnp.concatenate([dg, du], axis=1)
        dgu[rows, :] = both
        dpart[rows, :] = dims(both, wgu, 1, 1).astype(BF)
        s2.beside(n)

        @pl.when(n > 0)
        def _():
            s2.across(n - 1)

    s2.across(3)

    @pl.loop(0, 2)
    def _(n):
        m_all = mb[...].reshape(TOKENS, 768)
        for t in range(2):

            @pl.when(n == t)
            def _():
                v = dims(m_all[:, t * 384 : (t + 1) * 384], cs[...], 0, 0).astype(BF)
                v = v.reshape(2, 2, 96, WIDTH)
                for u in range(2):
                    gd[u, 2 * t : 2 * t + 2] = v[:, u]

        s2.back(n)

    @pl.loop(0, 4)
    def _(n):
        v = dims(a2[:, pl.ds(pl.multiple_of(n * 256, 256), 256)], dgu[...], 0, 0).astype(BF)
        v = v.reshape(4, 2, 32, 1536)
        for t in range(2):
            ggu[t, n] = v[:, t]

        @pl.when(n < 2)
        def _():
            s2.back(n + 2)

    @pl.loop(0, 4)
    def _(n):
        rows = pl.ds(pl.multiple_of(n * 256, 256), 256)
        m = pieces(mb, sorts, 0, n * 4, 4)
        part2[rows, :] = jnp.dot(m, wd[...].reshape(768, WIDTH), preferred_element_type=F32).astype(BF)

    for n in range(4):
        s2.ready(n)
    s1.close()
    s2.close()
    g.close()


def first_call(tok, cot, pos, pq, pg, po, pd, cosf, sinf, qg, kg):
    sem = pltpu.SemaphoreType.DMA
    shape = jax.ShapeDtypeStruct
    vm = pltpu.VMEM
    full = (TOKENS, WIDTH)
    return pl.pallas_call(
        first_kernel,
        out_shape=(
            shape((16, BLK, WIDTH), BF),
            shape((8, 128), jnp.int32),
            shape((4, 8) + pq.shape[1:], BF),
            shape((8,) + po.shape, BF),
            shape(full, BF),
            shape((TOKENS, 768), F32),
            shape((4, TOKENS, 128), BF),
            shape((2, TOKENS, 128), BF),
            shape((2, TOKENS, 128), BF),
            shape((TOKENS, 512), BF),
            shape((4, TOKENS, 1), F32),
            shape(full, F32),
            shape(full, BF),
            shape(full, BF),
            shape(full, BF),
            shape((2, 4, 96, WIDTH), BF),
            shape((2, 4, 4, 32, 1536), BF),
        ),
        in_specs=[ANY] * 7 + [VM] * 4,
        out_specs=(VM, ANY) + (VM,) * 15,
        scratch_shapes=[
            vm((16, BLK, WIDTH), BF),
            vm((4, 8) + pg.shape[1:], BF),
            vm((8,) + pd.shape, BF),
            vm(full, BF), vm(full, BF), vm(full, BF), vm(full, BF),
            vm((16, BLK, 768), BF), vm((TOKENS, 1536), BF),
        ]
        + [vm((4, 128, WIDTH), BF)] * 6
        + [pltpu.SMEM((8, 128), jnp.int32), sem((1,)), sem((12, 4))]
        + [sem(n) for n in GATHER_SEMS],
        compiler_params=pltpu.CompilerParams(
            collective_id=0, has_side_effects=True, vmem_limit_bytes=VMEM_BYTES
        ),
        name="forward_and_mlp",
    )(tok, cot, pos, pq, pg, po, pd, cosf, sinf, qg, kg)


class Home:
    def __init__(self, part, out, l1, own, l2, sems, here, base):
        self.q, self.p, self.x, self.c, self.z, self.y = place()
        self.part, self.out, self.l1, self.own, self.l2 = part, out, l1, own, l2
        self.sems, self.here, self.base = sems, here, base
        self.owner_x, self.owner_c = self.y, self.z // 2
        self.keeps = self.x == self.owner_x
        self.sib = (2 * self.x + 1 - self.c, self.p)
        self.opp = (2 * (1 - self.x) + self.c, self.p)
        self.goal_q = 2 * self.owner_x + self.owner_c

    def rows(self, n, c):
        return pl.ds(pl.multiple_of(n * 256 + c * 128, 128), 128)

    def sem(self, k, n):
        return self.sems.at[self.base + k, n]

    def first(self, n):
        return remote(
            self.part.at[self.rows(n, 1 - self.c)], self.l1.at[n], self.sem(0, n), self.sem(1, n), self.sib
        )

    def second(self, n):
        return remote(self.own.at[n], self.l2.at[n], self.sem(2, n), self.sem(3, n), self.opp)

    def third(self, n):
        slot = mod(self.z, 2)
        return remote(
            self.own.at[n], self.out.at[slot], self.sem(4, n), self.sem(5, slot), (self.goal_q, 2 * n + self.c)
        )

    def is_self(self, n):
        return jnp.logical_and(self.goal_q == self.q, 2 * n + self.c == self.p)

    def beside(self, n):
        self.first(n).start()

    def across(self, n):
        self.first(n).wait_recv()
        mine = self.part[self.rows(n, self.c), :].astype(F32)
        self.own[n] = (mine + self.l1[n].astype(F32)).astype(BF)

        @pl.when(jnp.logical_not(self.keeps))
        def _():
            self.second(n).start()

    def finish(self, n, rest):
        @pl.when(self.keeps)
        def _():
            self.second(n).wait_recv()
            s = self.own[n].astype(F32) + self.l2[n].astype(F32)
            self.own[n] = rest(n, s).astype(BF)

            @pl.when(jnp.logical_not(self.is_self(n)))
            def _():
                self.third(n).start()

            @pl.when(self.is_self(n))
            def _():
                cp = pltpu.make_async_copy(self.own.at[n], self.out.at[mod(self.z, 2)], self.here)
                cp.start()
                cp.wait()

    def close(self):
        for i in range(2):
            group = 4 * self.c + 2 * i + self.x
            same = jnp.logical_and(group == self.p, self.y == self.c)

            @pl.when(jnp.logical_not(same))
            def _():
                remote(self.own.at[0], self.out.at[i], self.sem(4, 0), self.sem(5, i), (self.q, self.p)).wait_recv()

        for n in range(4):
            self.first(n).wait_send()

            @pl.when(jnp.logical_not(self.keeps))
            def _():
                self.second(n).wait_send()

            @pl.when(jnp.logical_and(self.keeps, jnp.logical_not(self.is_self(n))))
            def _():
                self.third(n).wait_send()


class Scatter:
    def __init__(self, g, ly, lz, sems, base):
        self.q, self.p, _, _, self.z, self.y = place()
        self.g, self.ly, self.lz, self.sems, self.base = g, ly, lz, sems, base

    def y_copy(self, n):
        s, r = self.sems.at[self.base + n, 0], self.sems.at[self.base + n, 1]
        return remote(self.g.at[1 - self.y, n], self.ly.at[n], s, r, (self.q, 2 * self.z + 1 - self.y))

    def z_copy(self, n, k):
        t = mod(self.z + k, 4)
        s, r = self.sems.at[self.base + n, 2 * k], self.sems.at[self.base + n, 2 * k + 1]
        return remote(self.ly.at[n, t], self.lz.at[n, k - 1], s, r, (self.q, 2 * t + self.y))

    def y_send(self, n):
        self.y_copy(n).start()

    def z_step(self, n):
        self.y_copy(n).wait_recv()

        @pl.loop(0, 4)
        def _(t):
            self.ly[n, t] = (self.ly[n, t].astype(F32) + self.g[self.y, n, t].astype(F32)).astype(BF)

        for k in (1, 2, 3):
            self.z_copy(n, k).start()

    def z_sum(self, n):
        for k in (1, 2, 3):
            self.z_copy(n, k).wait_recv()
        s = self.ly[n, self.z].astype(F32) + self.lz[n, 0].astype(F32)
        return s + self.lz[n, 1].astype(F32) + self.lz[n, 2].astype(F32)

    def close(self, count):
        @pl.loop(0, count)
        def _(n):
            self.y_copy(n).wait_send()
            for k in (1, 2, 3):
                self.z_copy(n, k).wait_send()


class Columns:
    def __init__(self, scatter, r, land, out, sems, base):
        self.scatter, self.r, self.land, self.out = scatter, r, land, out
        self.sems, self.base = sems, base
        self.q, self.p = scatter.q, scatter.p

    def copy(self, t):
        s, r = self.sems.at[self.base, t], self.sems.at[self.base + 1, self.q]
        return remote(self.r.at[t], self.land.at[self.q], s, r, (t, self.p))

    def step(self, t):
        s = self.scatter.z_sum(t)
        self.r[t] = s.astype(BF)

        @pl.when(t != self.q)
        def _():
            self.copy(t).start()

        @pl.when(t == self.q)
        def _():
            self.out[t] = s

    def close(self):
        @pl.loop(0, 4)
        def _(t):
            @pl.when(t != self.q)
            def _():
                r = self.sems.at[self.base + 1, t]
                remote(self.r.at[t], self.land.at[t], self.sems.at[self.base, t], r, (self.q, self.p)).wait_recv()
                self.out[t] = self.land[t].astype(F32)
                self.copy(t).wait_send()


def second_kernel(
    spots, gd, ggu, part2, dtotal, hidden, cs, wo, wq, xhat, raw_i, qb, kb, vb, ob, lse, xf, cosf, sinf, qg, kg,
    out, igrad, od, ogu, oo, oqkv, oheads,
    dh, dy, dob, dqkv, dkv, go, gqkv, heads,
    yd, ygu, yo, yqkv, zd, zgu, zo, zqkv, lgu, lqkv, rgu, rqkv, hy, hz, hdp,
    l1, own, l2, l1b, ownb, l2b,
    gsem, csem, hs, hr, homes, here,
):
    q, p, x_, c, z, y = place()
    peers = [(2 * x_ + cc, mod(p + k, 8)) for k in range(1, 8) for cc in (0, 1)]
    peers += [(mod(q + k, 4), p) for k in (1, 2, 3)]
    greet(peers)
    sd = Scatter(gd, yd, zd, gsem, 0)
    sgu = Scatter(ggu, ygu, zgu, gsem, 1)
    so = Scatter(go, yo, zo, gsem, 5)
    sqkv = Scatter(gqkv, yqkv, zqkv, gsem, 6)
    cgu = Columns(sgu, rgu, lgu, ogu, csem, 0)
    cqkv = Columns(sqkv, rqkv, lqkv, oqkv, csem, 2)
    h_out = Home(part2, out, l1, own, l2, homes, here.at[0], 0)
    h_in = Home(dy, igrad, l1b, ownb, l2b, homes, here.at[1], 6)
    sd.y_send(0)
    for n in range(4):
        h_out.beside(n)
    for n in range(4):
        sgu.y_send(n)

    @pl.loop(0, 4)
    def _(n):
        rows = pl.ds(pl.multiple_of(n * 256, 256), 256)
        h = hidden[pl.ds(n * 4, 4)].reshape(256, WIDTH)
        r = unit(h)
        da = dtotal[rows, :].astype(F32)
        back = r * da - h * (r * r * r * jnp.mean(h * da, axis=-1, keepdims=True))
        d = cs[rows, :].astype(F32) + back
        dh[pl.ds(n * 4, 4)] = d.reshape(4, BLK, WIDTH)
        low = d.astype(BF)
        dy[rows, :] = low
        do = dims(low, wo[...].reshape(512, WIDTH), 1, 1).astype(BF)
        for t in range(4):
            dob[t, rows, :] = do[:, t * 128 : (t + 1) * 128]
        h_out.across(n)

    @pl.loop(0, 2)
    def _(n):
        v = dims(ob[:, pl.ds(pl.multiple_of(n * 256, 256), 256)], dy[...], 0, 0).astype(BF)
        v = v.reshape(2, 2, 64, WIDTH)
        for t in range(2):
            go[t, 0, pl.ds(n * 2, 2)] = v[:, t]

    so.y_send(0)
    heads[...] = jnp.zeros_like(heads)
    scale = HEAD_SIZE**-0.5

    def norm_back(dn, u, gain, rows):
        dn = rotate_back(dn, cosf[rows, :], sinf[rows, :])
        r = unit(u)
        gd_ = gain * dn
        du = r * gd_ - u * (r * r * r * jnp.mean(u * gd_, axis=-1, keepdims=True))
        return du.astype(BF), jnp.sum(dn * u * r, axis=0, keepdims=True)

    def result(n, s):
        return s + pieces(hidden, spots, 0, 4 * n + 2 * c, 2)

    def inward(n, s):
        v = xf[pl.ds(4 * n + 2 * c, 2)].reshape(128, WIDTH).astype(F32)
        r = unit(v)
        s = r * s - v * (r * r * r * jnp.mean(v * s, axis=-1, keepdims=True))
        return s + pieces(dh, spots, 0, 4 * n + 2 * c, 2)

    @pl.loop(0, 2)
    def _(g):
        dkv[...] = jnp.zeros_like(dkv)
        for t in range(2):
            if t == 0:

                @pl.when(g == 0)
                def _():
                    sd.z_step(0)

                @pl.when(g == 1)
                def _():
                    sgu.z_step(2)
                    sgu.z_step(3)
            else:

                @pl.when(g == 0)
                def _():
                    sgu.z_step(0)
                    sgu.z_step(1)

                @pl.when(g == 1)
                def _():
                    @pl.loop(0, 4)
                    def _(n):
                        h_out.finish(n, result)

            h = g * 2 + t
            lanes = pl.ds(pl.multiple_of(h * 128, 128), 128)
            for i in range(4):
                length = (i + 1) * 256
                rows = slice(i * 256, length)
                qv = qb[h, rows, :]
                kv = kb[g, :length, :]
                dov = dob[h, rows, :]
                s = dims(qv, kv, 1, 1) * (scale * LOG2E)
                pr = lower(jnp.exp2(s - lse[h, rows, :]), 0.0)
                dp = dims(dov, vb[g, :length, :], 1, 1)
                delta = jnp.sum(dov.astype(F32) * ob[rows, lanes].astype(F32), axis=-1, keepdims=True)
                ds_ = lower(pr * (dp - delta), 0.0).astype(BF)
                dq = jnp.dot(ds_, kv, preferred_element_type=F32) * scale
                dkv[0, :length, :] += dims(ds_, qv, 0, 0)
                dkv[1, :length, :] += dims(pr.astype(BF), dov, 0, 0)
                du, dgain = norm_back(dq, raw_i[rows, lanes], qg[...], pl.ds(i * 256, 256))
                dqkv[i * 4 : i * 4 + 4, :, lanes] = du.reshape(4, BLK, 128)
                heads[0:1, :] += dgain
        lanes = pl.ds(pl.multiple_of(512 + g * 128, 128), 128)
        for i in range(4):
            rows = slice(i * 256, (i + 1) * 256)
            du, dgain = norm_back(dkv[0, rows, :] * scale, raw_i[rows, lanes], kg[...], pl.ds(i * 256, 256))
            dqkv[i * 4 : i * 4 + 4, :, lanes] = du.reshape(4, BLK, 128)
            heads[1:2, :] += dgain
        dqkv[:, :, pl.ds(pl.multiple_of(768 + g * 128, 128), 128)] = dkv[1].astype(BF).reshape(16, BLK, 128)

    hy_copy = remote(heads, hy, hs.at[0], hr.at[0], (q, 2 * z + 1 - y))
    hy_copy.start()

    @pl.loop(0, 4)
    def _(n):
        rows = pl.ds(pl.multiple_of(n * 256, 256), 256)
        d = pieces(dqkv, spots, 0, n * 4, 4)
        dy[rows, :] = dims(d, wq[...].reshape(WIDTH, WIDTH), 1, 1).astype(BF)
        h_in.beside(n)

        @pl.when(n > 0)
        def _():
            h_in.across(n - 1)

    h_in.across(3)

    @pl.loop(0, 4)
    def _(n):
        v = dims(xhat[:, pl.ds(pl.multiple_of(n * 256, 256), 256)], dqkv[...].reshape(TOKENS, WIDTH), 0, 0).astype(BF)
        v = v.reshape(4, 2, 32, WIDTH)
        for t in range(2):
            gqkv[t, n] = v[:, t]
        sqkv.y_send(n)

    def z_heads(k):
        return remote(hz.at[z], hz.at[z], hs.at[k], hr.at[k], (q, 2 * mod(z + k, 4) + y))

    def dp_heads(k):
        return remote(hdp.at[q], hdp.at[q], hs.at[3 + k], hr.at[3 + k], (mod(q + k, 4), p))

    hy_copy.wait_recv()
    hz[z] = heads[...] + hy[...]
    for k in (1, 2, 3):
        z_heads(k).start()
    so.z_step(0)
    od[...] = sd.z_sum(0)

    @pl.loop(0, 4)
    def _(n):
        cgu.step(n)
        sqkv.z_step(n)
        h_in.finish(n, inward)

    for k in (1, 2, 3):
        f = mod(z + 4 - k, 4)
        remote(hz.at[f], hz.at[f], hs.at[k], hr.at[k], (q, p)).wait_recv()
    hdp[q] = hz[0] + hz[1] + hz[2] + hz[3]
    for k in (1, 2, 3):
        dp_heads(k).start()
    oo[...] = so.z_sum(0)

    @pl.loop(0, 4)
    def _(n):
        cqkv.step(n)

    cgu.close()
    for k in (1, 2, 3):
        f = mod(q + 4 - k, 4)
        remote(hdp.at[f], hdp.at[f], hs.at[3 + k], hr.at[3 + k], (q, p)).wait_recv()
    oheads[...] = hdp[0] + hdp[1] + hdp[2] + hdp[3]
    cqkv.close()
    h_out.close()
    h_in.close()
    sd.close(1)
    sgu.close(4)
    so.close(1)
    sqkv.close(4)
    hy_copy.wait_send()
    for k in (1, 2, 3):
        z_heads(k).wait_send()
        dp_heads(k).wait_send()


def second_call(spots, gd, ggu, part2, dtotal, hidden, cs, wo, wq, xhat, raw, qb, kb, vb, ob, lse, xf, cosf, sinf, qg, kg):
    shape = jax.ShapeDtypeStruct
    sem = pltpu.SemaphoreType.DMA
    vm = pltpu.VMEM
    full = (TOKENS, WIDTH)
    return pl.pallas_call(
        second_kernel,
        out_shape=(
            shape((2, 128, WIDTH), BF),
            shape((2, 128, WIDTH), BF),
            shape((96, WIDTH), F32),
            shape((4, 32, 1536), F32),
            shape((64, WIDTH), F32),
            shape((4, 32, WIDTH), F32),
            shape((8, 128), F32),
        ),
        in_specs=[SM] + [VM] * 20,
        out_specs=(VM,) * 7,
        scratch_shapes=[
            vm((16, BLK, WIDTH), F32), vm(full, BF), vm((4, TOKENS, 128), BF), vm((16, BLK, WIDTH), BF),
            vm((2, TOKENS, 128), F32), vm((2, 1, 4, 64, WIDTH), BF), vm((2, 4, 4, 32, WIDTH), BF),
            vm((8, 128), F32),
            vm((1, 4, 96, WIDTH), BF), vm((4, 4, 32, 1536), BF), vm((1, 4, 64, WIDTH), BF), vm((4, 4, 32, WIDTH), BF),
            vm((1, 3, 96, WIDTH), BF), vm((4, 3, 32, 1536), BF), vm((1, 3, 64, WIDTH), BF), vm((4, 3, 32, WIDTH), BF),
            vm((4, 32, 1536), BF), vm((4, 32, WIDTH), BF), vm((4, 32, 1536), BF), vm((4, 32, WIDTH), BF),
            vm((8, 128), F32), vm((4, 8, 128), F32), vm((4, 8, 128), F32),
        ]
        + [vm((4, 128, WIDTH), BF)] * 6
        + [sem((10, 8)), sem((4, 4)), sem((7,)), sem((7,)), sem((12, 4)), sem((2,))],
        compiler_params=pltpu.CompilerParams(
            collective_id=1, has_side_effects=True, vmem_limit_bytes=VMEM_BYTES
        ),
        name="backward_and_scatter",
    )(
        spots, gd.reshape(2, 1, 4, 96, WIDTH), ggu, part2, dtotal, hidden.reshape(16, BLK, WIDTH), cs, wo, wq, xhat,
        raw, qb, kb, vb, ob, lse, xf, cosf, sinf, qg, kg,
    )


def quarter_columns(w, gain):
    rows, cols = w.shape
    v = w if gain is None else (w.astype(F32) * gain).astype(BF)
    return jnp.transpose(v.reshape(rows, 4, cols // 4), (1, 0, 2))


def whole_sequences(
    tokens, attn_gain, w_query, key_projection, value_projection, query_head_gain, key_gain, w_out,
    mlp_gain, w_gate, w_up, w_down, cotangent, span_order,
):
    p = lax.axis_index("seq")
    ga = attn_gain.astype(F32)[:, None]
    gm = mlp_gain.astype(F32)[:, None]
    pq = jnp.concatenate(
        [quarter_columns(w, ga) for w in (w_query, key_projection, value_projection)], axis=2
    )
    pg = jnp.concatenate([quarter_columns(w, gm) for w in (w_gate, w_up)], axis=2)
    row = jnp.where(lax.rem(p // 2, 2) == 0, span_order[0], span_order[1])
    spots = lax.iota(jnp.int32, 16)
    inverse = jnp.sum(jnp.where(row[None, :] == spots[:, None], spots[None, :], 0), axis=1)
    pos = jnp.zeros((8, 128), jnp.int32)
    pos = pos.at[0, :16].set(row).at[1, :16].set(inverse)
    freqs = BASE ** (-(lax.iota(F32, HEAD_SIZE // 2) * 2.0) / HEAD_SIZE)
    angles = lax.iota(F32, TOKENS)[:, None] * freqs[None, :]
    cosine = jnp.cos(angles)
    sine = jnp.sin(angles)
    cosf = jnp.concatenate([cosine, cosine], axis=1)
    sinf = jnp.concatenate([-sine, sine], axis=1)
    qg = query_head_gain.astype(F32)[None, :]
    kg = key_gain.astype(F32)[None, :]
    xf, of, wq, wo, xhat, raw, qb, kb, vb, ob, lse, hidden, cs, part2, dtotal, gd, ggu = first_call(
        tokens.reshape(2, 2, BLK, WIDTH), cotangent.reshape(2, 2, BLK, WIDTH), pos, pq, pg, w_out, w_down,
        cosf, sinf, qg, kg,
    )
    out, igrad, od, ogu, oo, oqkv, oheads = second_call(
        of, gd, ggu, part2, dtotal, hidden, cs, wo, wq, xhat, raw, qb, kb, vb, ob, lse, xf, cosf, sinf, qg, kg
    )
    return finish(
        out, igrad, od, ogu, oo, oqkv, oheads, ga, gm, w_query, key_projection, value_projection, w_gate, w_up
    )


def finish(out, igrad, od, ogu, oo, oqkv, oheads, ga, gm, w_query, key_projection, value_projection, w_gate, w_up):
    def join(part):
        return jnp.transpose(part, (1, 0, 2)).reshape(part.shape[1], -1)

    hq, hk, hv = join(oqkv[:, :, :512]), join(oqkv[:, :, 512:768]), join(oqkv[:, :, 768:])
    hg, hu = join(ogu[:, :, :768]), join(ogu[:, :, 768:])

    def along(w, h):
        return jnp.sum(w.astype(F32) * h, axis=1)

    grad_attn_gain = along(w_query, hq) + along(key_projection, hk) + along(value_projection, hv)
    grad_mlp_gain = along(w_gate, hg) + along(w_up, hu)
    return (
        out,
        igrad,
        grad_attn_gain,
        ga * hq,
        ga * hk,
        ga * hv,
        oheads[0],
        oheads[1],
        oo,
        grad_mlp_gain,
        gm * hg,
        gm * hu,
        od,
    )


def layer(tokens, *rest):
    whole = (
        lax.axis_size("dp") == 4
        and lax.axis_size("seq") == 8
        and tokens.shape == (2, 128, WIDTH)
        and rest[-1].shape == (2, 16)
    )
    return (whole_sequences if whole else shards)(tokens, *rest)


def solution(mesh):
    return jax.shard_map(
        layer,
        mesh=mesh,
        in_specs=(
            P("dp", "seq", None),
            P(("dp", "seq")),
            P(("dp", "seq"), None),
            P(("dp", "seq"), None),
            P(("dp", "seq"), None),
            P(),
            P(),
            P(("dp", "seq"), None),
            P(("dp", "seq")),
            P(("dp", "seq"), None),
            P(("dp", "seq"), None),
            P(("dp", "seq"), None),
            P("dp", "seq", None),
            P("dp", None),
        ),
        out_specs=(
            P("dp", "seq", None),
            P("dp", "seq", None),
            P(("dp", "seq")),
            P(("dp", "seq"), None),
            P(("dp", "seq"), None),
            P(("dp", "seq"), None),
            P(),
            P(),
            P(("dp", "seq"), None),
            P(("dp", "seq")),
            P(("dp", "seq"), None),
            P(("dp", "seq"), None),
            P(("dp", "seq"), None),
        ),
        check_vma=False,
    )
```

```python
import jax
import jax.numpy as jnp
from jax import lax
from jax.sharding import PartitionSpec as P

import numpy as np
from jax.experimental import pallas as pl
from jax.experimental.pallas import tpu as pltpu

QUERY_HEADS = 16
KEY_VALUE_HEADS = 8
HEAD_SIZE = 128
BLK = 64
MB = 2


EPS = 1e-06
BASE = 1000000.0
NEGATIVE_FILL = -1e30


def from_behind(block, axis, distance):
    devices = range(lax.axis_size(axis))
    route = [((i - distance) % len(devices), i) for i in devices]
    return lax.ppermute(block, axis, route)


def row_norm_apply(v, gain):
    return v * lax.rsqrt(jnp.mean(v * v, axis=-1, keepdims=True) + EPS) * gain


def apply_rotary(v, cosine_table, sine_table):
    half = v.shape[-1] // 2
    first = v[..., :half]
    second = v[..., half:]
    return jnp.concatenate(
        [first * cosine_table - second * sine_table, second * cosine_table + first * sine_table],
        axis=-1,
    )


def matrix_multiply(left, right):
    return jnp.dot(left, right, preferred_element_type=jnp.float32)


def row_product(left, right):
    return lax.dot_general(
        left, right, (((0,), (0,)), ((), ())), preferred_element_type=jnp.float32
    )


def product_backward(left, right):
    return lax.dot_general(
        left, right, (((1,), (1,)), ((), ())), preferred_element_type=jnp.float32
    )


def block_positions(order, start, count):
    places = start + lax.iota(jnp.int32, count)
    which = places // BLK
    hits = (which[:, None] == lax.iota(jnp.int32, order.shape[1])[None, :]).astype(jnp.int32)
    spans = jnp.sum(hits[None, :, :] * order[:, None, :], axis=-1)
    return spans * BLK + places % BLK


def pack_shares(members, count):
    return jnp.concatenate([m.reshape(count, -1) for m in members], axis=1).reshape(-1)


def unpack_shares(flat, members, count):
    pieces = []
    offset = 0
    for m in members:
        length = m.size // count
        share_shape = (m.shape[0] // count,) + tuple(m.shape[1:])
        pieces.append(flat[offset : offset + length].reshape(share_shape))
        offset = offset + length
    return pieces


def shards(
    tokens,
    attn_gain,
    w_query,
    key_projection,
    value_projection,
    query_head_gain,
    key_gain,
    w_out,
    mlp_gain,
    w_gate,
    w_up,
    w_down,
    cotangent,
    span_order,
):
    seq_count = lax.axis_size("seq")
    seq_place = lax.axis_index("seq")
    all_count = lax.axis_size(("dp", "seq"))
    local_length = tokens.shape[1]
    width = tokens.shape[2]
    sequence_permutation = tokens.shape[0] // MB
    query_group = QUERY_HEADS // KEY_VALUE_HEADS
    scale = HEAD_SIZE ** (-0.5)
    freqs = BASE ** (-(lax.iota(jnp.float32, HEAD_SIZE // 2) * 2.0) / HEAD_SIZE)
    query_norm_gain = query_head_gain.astype(jnp.float32)
    kgain = key_gain.astype(jnp.float32)
    sums = None
    outputs = []
    input_grads = []
    for batch in range(MB):
        rows_x = tokens[batch * sequence_permutation : (batch + 1) * sequence_permutation]
        rows_cot = cotangent[batch * sequence_permutation : (batch + 1) * sequence_permutation]
        order = span_order[batch * sequence_permutation : (batch + 1) * sequence_permutation]
        gain_a, wq, key_weight, value_weight, output_weight = (
            lax.all_gather(attn_gain, ("dp", "seq"), axis=0, tiled=True),
            lax.all_gather(w_query, ("dp", "seq"), axis=0, tiled=True),
            lax.all_gather(key_projection, ("dp", "seq"), axis=0, tiled=True),
            lax.all_gather(value_projection, ("dp", "seq"), axis=0, tiled=True),
            lax.all_gather(w_out, ("dp", "seq"), axis=0, tiled=True),
        )
        gain_m, wg, wu, wd = (
            lax.all_gather(mlp_gain, ("dp", "seq"), axis=0, tiled=True),
            lax.all_gather(w_gate, ("dp", "seq"), axis=0, tiled=True),
            lax.all_gather(w_up, ("dp", "seq"), axis=0, tiled=True),
            lax.all_gather(w_down, ("dp", "seq"), axis=0, tiled=True),
        )
        own_pos = block_positions(order, seq_place * local_length, local_length)
        angles = own_pos.astype(jnp.float32)[..., None] * freqs
        cosine_table = jnp.cos(angles)[:, :, None, :]
        sine_table = jnp.sin(angles)[:, :, None, :]

        def query_per_head(raw, gain):
            return apply_rotary(row_norm_apply(raw, gain), cosine_table, sine_table)

        flat_x = rows_x.reshape(-1, width).astype(jnp.float32)
        first_operand = row_norm_apply(flat_x, gain_a.astype(jnp.float32)).astype(jnp.bfloat16)
        query_unrotated = matrix_multiply(first_operand, wq).reshape(
            sequence_permutation, local_length, QUERY_HEADS, HEAD_SIZE
        )
        key_unrotated = matrix_multiply(first_operand, key_weight).reshape(
            sequence_permutation, local_length, KEY_VALUE_HEADS, HEAD_SIZE
        )
        value_reduced = (
            matrix_multiply(first_operand, value_weight)
            .astype(jnp.bfloat16)
            .reshape(sequence_permutation, local_length, KEY_VALUE_HEADS, HEAD_SIZE)
        )
        q_low = (
            query_per_head(query_unrotated, query_norm_gain)
            .astype(jnp.bfloat16)
            .reshape(sequence_permutation, local_length, KEY_VALUE_HEADS, query_group, HEAD_SIZE)
        )
        k_low = query_per_head(key_unrotated, kgain).astype(jnp.bfloat16)
        initial_maximum = jnp.full(
            (sequence_permutation, KEY_VALUE_HEADS, query_group, local_length),
            NEGATIVE_FILL,
            jnp.float32,
        )
        top = initial_maximum
        piece_k = lax.all_gather(k_low, "seq", axis=1, tiled=True)
        piece_v = lax.all_gather(value_reduced, "seq", axis=1, tiled=True)
        key_pos = block_positions(order, jnp.int32(0), piece_k.shape[1])
        visible = key_pos[:, None, None, None, :] <= own_pos[:, None, None, :, None]
        scores = (
            jnp.einsum("sqgrd,skgd->sgrqk", q_low, piece_k, preferred_element_type=jnp.float32)
            * scale
        )
        scores = jnp.where(visible, scores, NEGATIVE_FILL)
        new_top = jnp.maximum(top, jnp.max(scores, axis=-1))
        weights = jnp.exp(scores - new_top[..., None])
        new_total = jnp.sum(weights, axis=-1)
        taken = jnp.einsum(
            "sgrqk,skgd->sqgrd",
            weights.astype(jnp.bfloat16),
            piece_v,
            preferred_element_type=jnp.float32,
        )
        top = new_top
        log_total = top + jnp.log(new_total)
        attn = taken / jnp.transpose(new_total, (0, 3, 1, 2))[..., None]
        o_low = attn.astype(jnp.bfloat16).reshape(
            sequence_permutation * local_length, QUERY_HEADS * HEAD_SIZE
        )
        hidden = flat_x + matrix_multiply(o_low, output_weight)
        gain_second = gain_m.astype(jnp.float32)
        a_second = row_norm_apply(hidden, gain_second).astype(jnp.bfloat16)
        gate = matrix_multiply(a_second, wg)
        up_part = matrix_multiply(a_second, wu)
        mixed = (gate * jax.nn.sigmoid(gate) * up_part).astype(jnp.bfloat16)
        result = hidden + matrix_multiply(mixed, wd)
        outputs.append(
            result.astype(jnp.bfloat16).reshape(sequence_permutation, local_length, width)
        )
        gain_a, wq, key_weight, value_weight, output_weight = (
            lax.all_gather(attn_gain, ("dp", "seq"), axis=0, tiled=True),
            lax.all_gather(w_query, ("dp", "seq"), axis=0, tiled=True),
            lax.all_gather(key_projection, ("dp", "seq"), axis=0, tiled=True),
            lax.all_gather(value_projection, ("dp", "seq"), axis=0, tiled=True),
            lax.all_gather(w_out, ("dp", "seq"), axis=0, tiled=True),
        )
        gain_m, wg, wu, wd = (
            lax.all_gather(mlp_gain, ("dp", "seq"), axis=0, tiled=True),
            lax.all_gather(w_gate, ("dp", "seq"), axis=0, tiled=True),
            lax.all_gather(w_up, ("dp", "seq"), axis=0, tiled=True),
            lax.all_gather(w_down, ("dp", "seq"), axis=0, tiled=True),
        )
        flat_cot = rows_cot.reshape(-1, width)
        grad_down = row_product(mixed, flat_cot)
        d_mixed = product_backward(flat_cot, wd)

        def mix(gate_in, up_in):
            return gate_in * jax.nn.sigmoid(gate_in) * up_in

        _, mix_back = jax.vjp(mix, gate, up_part)
        d_gate, d_up = mix_back(d_mixed)
        gate_low = d_gate.astype(jnp.bfloat16)
        up_low = d_up.astype(jnp.bfloat16)
        grad_gate = row_product(a_second, gate_low)
        grad_up = row_product(a_second, up_low)
        d_second = product_backward(gate_low, wg) + product_backward(up_low, wu)
        _, second_back = jax.vjp(row_norm_apply, hidden, gain_second)
        d_hidden_norm, grad_mlp_gain = second_back(d_second)
        d_hidden = flat_cot.astype(jnp.float32) + d_hidden_norm
        grad_output_reduced = d_hidden.astype(jnp.bfloat16)
        grad_out = row_product(o_low, grad_output_reduced)
        do_low = (
            product_backward(grad_output_reduced, output_weight)
            .astype(jnp.bfloat16)
            .reshape(sequence_permutation, local_length, KEY_VALUE_HEADS, query_group, HEAD_SIZE)
        )
        delta = jnp.transpose(jnp.sum(do_low.astype(jnp.float32) * attn, axis=-1), (0, 2, 3, 1))

        def back_terms(held_k, held_v, visible):
            scores = (
                jnp.einsum("sqgrd,skgd->sgrqk", q_low, held_k, preferred_element_type=jnp.float32)
                * scale
            )
            scores = jnp.where(visible, scores, NEGATIVE_FILL)
            probs = jnp.exp(scores - log_total[..., None])
            d_probs = jnp.einsum(
                "sqgrd,skgd->sgrqk", do_low, held_v, preferred_element_type=jnp.float32
            )
            score_low = (probs * (d_probs - delta[..., None])).astype(jnp.bfloat16)
            probs_low = probs.astype(jnp.bfloat16)
            term_q = scale * jnp.einsum(
                "sgrqk,skgd->sqgrd", score_low, held_k, preferred_element_type=jnp.float32
            )
            term_k = scale * jnp.einsum(
                "sgrqk,sqgrd->skgd", score_low, q_low, preferred_element_type=jnp.float32
            )
            term_v = jnp.einsum(
                "sgrqk,sqgrd->skgd", probs_low, do_low, preferred_element_type=jnp.float32
            )
            return (term_k, term_v, term_q)

        def cycle_step(turn, state):
            held_k, held_v, acc_k, acc_v, acc_q = state
            owner = (seq_place - turn) % seq_count
            key_pos = block_positions(order, owner * local_length, local_length)
            visible = key_pos[:, None, None, None, :] <= own_pos[:, None, None, :, None]
            term_k, term_v, term_q = back_terms(held_k, held_v, visible)
            acc_k, acc_v, acc_q = (acc_k + term_k, acc_v + term_v, acc_q + term_q)
            held_k, held_v = from_behind((held_k, held_v), "seq", 1)
            acc_k, acc_v = (
                from_behind(acc_k.astype(jnp.bfloat16), "seq", 1).astype(acc_k.dtype),
                from_behind(acc_v.astype(jnp.bfloat16), "seq", 1).astype(acc_v.dtype),
            )
            return (held_k, held_v, acc_k, acc_v, acc_q)

        def two_steps(pair, state):
            return cycle_step(2 * pair + 1, cycle_step(2 * pair, state))

        blank_key_value = jnp.zeros(
            (sequence_permutation, local_length, KEY_VALUE_HEADS, HEAD_SIZE), jnp.float32
        )
        blank_query = jnp.zeros(
            (sequence_permutation, local_length, KEY_VALUE_HEADS, query_group, HEAD_SIZE),
            jnp.float32,
        )
        state = lax.fori_loop(
            0,
            seq_count // 2,
            two_steps,
            (k_low, value_reduced, blank_key_value, blank_key_value, blank_query),
        )
        _, _, d_keys, grad_value_rows, d_queries = state
        _, query_back = jax.vjp(query_per_head, query_unrotated, query_norm_gain)
        d_q_raw, grad_qgain = query_back(
            d_queries.reshape(sequence_permutation, local_length, QUERY_HEADS, HEAD_SIZE)
        )
        _, key_back = jax.vjp(query_per_head, key_unrotated, kgain)
        grad_key_unrotated, grad_kgain = key_back(d_keys)
        dq_low = d_q_raw.astype(jnp.bfloat16).reshape(
            sequence_permutation * local_length, QUERY_HEADS * HEAD_SIZE
        )
        grad_key_reduced = grad_key_unrotated.astype(jnp.bfloat16).reshape(
            sequence_permutation * local_length, KEY_VALUE_HEADS * HEAD_SIZE
        )
        grad_value_reduced = grad_value_rows.astype(jnp.bfloat16).reshape(
            sequence_permutation * local_length, KEY_VALUE_HEADS * HEAD_SIZE
        )
        grad_query = row_product(first_operand, dq_low)
        grad_key = row_product(first_operand, grad_key_reduced)
        grad_value = row_product(first_operand, grad_value_reduced)
        d_first = (
            product_backward(dq_low, wq)
            + product_backward(grad_key_reduced, key_weight)
            + product_backward(grad_value_reduced, value_weight)
        )
        _, first_back = jax.vjp(row_norm_apply, flat_x, gain_a.astype(jnp.float32))
        d_x_norm, grad_attn_gain = first_back(d_first)
        input_grads.append(
            (d_hidden + d_x_norm)
            .astype(jnp.bfloat16)
            .reshape(sequence_permutation, local_length, width)
        )
        fresh = (
            grad_attn_gain,
            grad_query,
            grad_key,
            grad_value,
            grad_out,
            grad_mlp_gain,
            grad_gate,
            grad_up,
            grad_down,
            grad_qgain,
            grad_kgain,
        )
        if sums is None:
            sums = fresh
        else:
            sums = tuple((a + b for a, b in zip(sums, fresh)))
    attn_members = (sums[0], sums[1], sums[2], sums[3], sums[4])
    mlp_members = (sums[5], sums[6], sums[7], sums[8])
    attn_flat = lax.psum_scatter(
        pack_shares(attn_members, all_count), ("dp", "seq"), scatter_dimension=0, tiled=True
    )
    mlp_flat = lax.psum_scatter(
        pack_shares(mlp_members, all_count), ("dp", "seq"), scatter_dimension=0, tiled=True
    )
    attn_shares = unpack_shares(attn_flat, attn_members, all_count)
    mlp_shares = unpack_shares(mlp_flat, mlp_members, all_count)
    head_sums = lax.psum((sums[9], sums[10]), ("dp", "seq"))
    return (
        jnp.concatenate(outputs, axis=0),
        jnp.concatenate(input_grads, axis=0),
        attn_shares[0],
        attn_shares[1],
        attn_shares[2],
        attn_shares[3],
        head_sums[0],
        head_sums[1],
        attn_shares[4],
        mlp_shares[0],
        mlp_shares[1],
        mlp_shares[2],
        mlp_shares[3],
    )


BF = jnp.bfloat16
F32 = jnp.float32
MESH = pl.DeviceIdType.MESH
TOKENS = 1024
WIDTH = 1024
LOG2E = 1.4426950408889634
VM = pl.BlockSpec(memory_space=pltpu.VMEM)
SM = pl.BlockSpec(memory_space=pltpu.SMEM)
ANY = pl.BlockSpec(memory_space=pl.ANY)
VMEM_BYTES = 65100 * 1024


def place():
    q = lax.axis_index("dp")
    p = lax.axis_index("seq")
    return q, p, q // 2, lax.rem(q, 2), p // 2, lax.rem(p, 2)


def greet(peers):
    barrier = pltpu.get_barrier_semaphore()
    for peer in peers:
        pl.semaphore_signal(barrier, inc=1, device_id=peer, device_id_type=MESH)
    pl.semaphore_wait(barrier, len(peers))


def remote(src, dst, send, recv, peer):
    return pltpu.make_async_remote_copy(
        src_ref=src, dst_ref=dst, send_sem=send, recv_sem=recv, device_id=peer, device_id_type=MESH
    )


def dims(left, right, lc, rc):
    return lax.dot_general(left, right, (((lc,), (rc,)), ((), ())), preferred_element_type=F32)


def mod(a, n):
    return a % n


def unit(v):
    return lax.rsqrt(jnp.mean(v * v, axis=-1, keepdims=True) + EPS)


def pieces(ref, spots, which, first, count):
    return jnp.concatenate([ref[spots[which, first + t]] for t in range(count)], axis=0)


def turns(table):
    other = pltpu.roll(table, HEAD_SIZE // 2, 1)
    first = lax.broadcasted_iota(jnp.int32, table.shape, 1) < HEAD_SIZE // 2
    return jnp.where(first, table, other), jnp.where(first, -other, table)


def rotate(v, cosine, sine):
    return v * cosine + pltpu.roll(v, HEAD_SIZE // 2, 1) * sine


def rotate_back(v, cosine, sine):
    return v * cosine + pltpu.roll(v * sine, HEAD_SIZE // 2, 1)


def lower(s, fill):
    n = s.shape[0]
    i = lax.broadcasted_iota(jnp.int32, (n, n), 0)
    j = lax.broadcasted_iota(jnp.int32, (n, n), 1)
    width = s.shape[1]
    diag = jnp.where(j <= i, s[:, width - n :], fill)
    return diag if width == n else jnp.concatenate([s[:, : width - n], diag], axis=1)


class Sum:
    def __init__(self, part, total, l1, own, l2, sems, base):
        self.q, self.p, self.x, self.c, _, _ = place()
        self.part, self.total, self.l1, self.own, self.l2 = part, total, l1, own, l2
        self.sems, self.base = sems, base
        self.sib = (2 * self.x + 1 - self.c, self.p)
        self.opp = (2 * (1 - self.x) + self.c, self.p)

    def rows(self, n, c):
        return pl.ds(pl.multiple_of(n * 256 + c * 128, 128), 128)

    def copy(self, step, n):
        s, r = self.sems.at[self.base + 2 * step, n], self.sems.at[self.base + 2 * step + 1, n]
        if step == 0:
            return remote(self.part.at[self.rows(n, 1 - self.c)], self.l1.at[n], s, r, self.sib)
        if step == 1:
            return remote(self.own.at[n], self.l2.at[n], s, r, self.opp)
        mine = self.total_at(n, self.c)
        return remote(mine, mine, s, r, self.sib)

    def total_at(self, n, c):
        if len(self.total.shape) == 2:
            return self.total.at[self.rows(n, c)]
        return self.total.at[(2 * n + c) // 4, (2 * n + c) % 4]

    def beside(self, n):
        self.copy(0, n).start()

    def across(self, n):
        self.copy(0, n).wait_recv()
        mine = self.part[self.rows(n, self.c), :].astype(F32)
        self.own[n] = (mine + self.l1[n].astype(F32)).astype(BF)
        self.copy(1, n).start()

    def back(self, n):
        self.copy(1, n).wait_recv()
        total = self.total_at(n, self.c)
        total[...] = (self.own[n].astype(F32) + self.l2[n].astype(F32)).astype(BF).reshape(total.shape)
        self.copy(2, n).start()

    def ready(self, n):
        other = self.total_at(n, 1 - self.c)
        s, r = self.sems.at[self.base + 4, n], self.sems.at[self.base + 5, n]
        remote(other, other, s, r, self.sib).wait_recv()

    def close(self, *steps):
        @pl.loop(0, 4)
        def _(n):
            for step in steps:
                self.copy(step, n).wait_send()


PIECES = ((0, None), (2, None), (1, 0), (1, 1), (1, 2), (1, 3), (3, None))


def block(ref, b):
    return ref.at[pl.ds(2 * b, 2)]


class Gather:
    def __init__(self, srcs, dsts, sems):
        self.q, self.p, self.x, self.c, self.z, self.y = place()
        self.tok, self.cot, self.pos, self.pq, self.pg, self.po, self.pd = srcs
        self.xf, self.cf, self.of, *self.w = dsts
        (self.loc, self.ts, self.tr, self.fs, self.fr, self.ps, self.pr,
         self.as_, self.ar, self.zs, self.zr, self.ys, self.yr) = sems
        q, p, x, c, z, y = self.q, self.p, self.x, self.c, self.z, self.y
        self.owner_x, self.owner_c = y, z // 2
        self.is_owner = jnp.logical_and(x == self.owner_x, c == self.owner_c)
        self.cross = jnp.logical_and(x != self.owner_x, c == self.owner_c)
        self.sib = (2 * x + 1 - c, p)
        self.opp = (2 * (1 - x) + c, p)

    def peers(self):
        q, p = self.q, self.p
        return [(mod(q + k, 4), p) for k in (1, 2, 3)] + [(q, mod(p + k, 8)) for k in range(1, 8)]

    def col(self, n):
        return (self.pq, self.pg)[n], self.w[n]

    def own_copy(self, n):
        q, p = self.q, self.p
        if n < 2:
            src, dst = self.col(n)
            return pltpu.make_async_copy(src.at[q], dst.at[q, p], self.loc.at[n])
        return pltpu.make_async_copy((self.po, self.pd)[n - 2], self.w[n].at[p], self.loc.at[n])

    def column_copy(self, n, k):
        q, p = self.q, self.p
        src, dst = self.col(n)
        t = mod(q + k, 4)
        return remote(src.at[t], dst.at[q, p], self.as_.at[n, k - 1], self.ar.at[n, k - 1], (t, p))

    def column_start(self, n):
        for k in (1, 2, 3):
            self.column_copy(n, k).start()

    def column_wait(self, n):
        q, p = self.q, self.p
        src, dst = self.col(n)
        for k in (1, 2, 3):
            f = mod(q + 4 - k, 4)
            remote(src.at[0], dst.at[f, p], self.as_.at[n, k - 1], self.ar.at[n, k - 1], (q, p)).wait_recv()

    def view(self, piece, chunk):
        n, part = PIECES[piece]
        if n >= 2:
            return self.w[n].at[chunk]
        return self.w[n].at[:, chunk] if part is None else self.w[n].at[part, chunk]

    def z_copy(self, piece, src, way):
        v = self.view(piece, 2 * src + self.y)
        s = self.zs.at[piece, src + (4 if way < 0 else 0)]
        return remote(v, v, s, self.zr.at[piece, src], (self.q, 2 * (self.z + way) + self.y))

    def y_copy(self, piece, src):
        v = self.view(piece, 2 * src + self.y)
        return remote(v, v, self.ys.at[piece, src], self.yr.at[piece, src], (self.q, 2 * self.z + 1 - self.y))

    def spread(self, piece, src, up, down):
        if up:

            @pl.when(self.z < 3)
            def _():
                self.z_copy(piece, src, 1).start()

        if down:

            @pl.when(self.z > 0)
            def _():
                self.z_copy(piece, src, -1).start()

        self.y_copy(piece, src).start()

    def begin(self, *pieces_):
        for piece in pieces_:
            self.spread(piece, self.z, True, True)

    def step(self, piece, dist):
        low, high = self.z - dist, self.z + dist

        @pl.when(low >= 0)
        def _():
            v = self.view(piece, 2 * low + self.y)
            remote(v, v, self.zs.at[piece, 0], self.zr.at[piece, low], (self.q, self.p)).wait_recv()
            self.spread(piece, low, True, False)

        @pl.when(high < 4)
        def _():
            v = self.view(piece, 2 * high + self.y)
            remote(v, v, self.zs.at[piece, 0], self.zr.at[piece, high], (self.q, self.p)).wait_recv()
            self.spread(piece, high, False, True)

    def steps(self, *pieces_):
        for piece in pieces_:
            for dist in (1, 2, 3):
                self.step(piece, dist)

    def y_wait(self, *pieces_):
        for piece in pieces_:
            for src in range(4):
                v = self.view(piece, 2 * src + 1 - self.y)
                remote(v, v, self.ys.at[piece, src], self.yr.at[piece, src], (self.q, self.p)).wait_recv()

    def tok_dst(self, a):
        return (self.xf, self.cf)[a]

    def token_copy(self, a, i):
        src, dst = (self.tok, self.cot)[a], self.tok_dst(a)
        goal = 4 * self.c + 2 * i + self.x
        return goal, remote(src.at[i], block(dst, self.p), self.ts.at[a, i], self.tr.at[a, self.p], (self.q, goal))

    def token_local(self, a, i):
        return pltpu.make_async_copy((self.tok, self.cot)[a].at[i], block(self.tok_dst(a), self.p), self.loc.at[4 + a])

    def token_start(self, a):
        for i in range(2):
            goal, cp = self.token_copy(a, i)

            @pl.when(goal != self.p)
            def _():
                cp.start()

            @pl.when(goal == self.p)
            def _():
                self.token_local(a, i).start()

    def token_pass(self, a, first=0, end=8):
        dst = self.tok_dst(a)
        q, p = self.q, self.p

        @pl.when(self.is_owner)
        def _():
            @pl.loop(first, end)
            def _(b):
                @pl.when(b != p)
                def _():
                    remote(block(dst, b), block(dst, b), self.ts.at[a, 0], self.tr.at[a, b], (q, p)).wait_recv()

                @pl.when(b == p)
                def _():
                    self.token_local(a, 0).wait()

                remote(block(dst, b), block(dst, b), self.fs.at[a, 0, b], self.fr.at[a, b], self.sib).start()
                remote(block(dst, b), block(dst, b), self.fs.at[a, 1, b], self.fr.at[a, b], self.opp).start()

        @pl.when(jnp.logical_not(self.is_owner))
        def _():
            @pl.loop(first, end)
            def _(b):
                remote(block(dst, b), block(dst, b), self.fs.at[a, 0, b], self.fr.at[a, b], self.sib).wait_recv()

                @pl.when(self.cross)
                def _():
                    remote(block(dst, b), block(dst, b), self.fs.at[a, 0, b], self.fr.at[a, b], self.sib).start()

    def token_close(self, a):
        dst = self.tok_dst(a)
        q, p = self.q, self.p
        for i in range(2):
            goal, cp = self.token_copy(a, i)

            @pl.when(goal != p)
            def _():
                cp.wait_send()

        @pl.when(self.is_owner)
        def _():
            @pl.loop(0, 8)
            def _(b):
                remote(block(dst, b), block(dst, b), self.fs.at[a, 0, b], self.fr.at[a, b], (q, p)).wait_send()
                remote(block(dst, b), block(dst, b), self.fs.at[a, 1, b], self.fr.at[a, b], (q, p)).wait_send()

        @pl.when(self.cross)
        def _():
            @pl.loop(0, 8)
            def _(b):
                remote(block(dst, b), block(dst, b), self.fs.at[a, 0, b], self.fr.at[a, b], (q, p)).wait_send()

    def pos_copy(self, k):
        return remote(self.pos, self.of, self.ps.at[k], self.pr.at[0], (mod(self.q + k + 1, 4), self.p))

    def pos_start(self):
        @pl.when(self.is_owner)
        def _():
            pltpu.make_async_copy(self.pos, self.of, self.loc.at[6]).start()
            for k in range(3):
                self.pos_copy(k).start()

    def pos_finish(self):
        @pl.when(self.is_owner)
        def _():
            pltpu.make_async_copy(self.pos, self.of, self.loc.at[6]).wait()
            for k in range(3):
                self.pos_copy(k).wait_send()

        @pl.when(jnp.logical_not(self.is_owner))
        def _():
            self.pos_copy(0).wait_recv()

    def close(self):
        for n in range(2):
            for k in (1, 2, 3):
                self.column_copy(n, k).wait_send()
        for piece in range(len(PIECES)):
            for src in range(4):
                self.y_copy(piece, src).wait_send()

                @pl.when(jnp.logical_and(self.z < 3, src <= self.z))
                def _():
                    self.z_copy(piece, src, 1).wait_send()

                @pl.when(jnp.logical_and(self.z > 0, src >= self.z))
                def _():
                    self.z_copy(piece, src, -1).wait_send()

        self.token_close(0)
        self.token_close(1)


GATHER_SEMS = ((7,), (2, 2), (2, 8), (2, 2, 8), (2, 8), (3,), (1,), (2, 3), (2, 3), (7, 8), (7, 4), (7, 4), (7, 4))


class Home:
    def __init__(self, part, out, l1, own, l2, sems, here, base):
        self.q, self.p, self.x, self.c, self.z, self.y = place()
        self.part, self.out, self.l1, self.own, self.l2 = part, out, l1, own, l2
        self.sems, self.here, self.base = sems, here, base
        self.owner_x, self.owner_c = self.y, self.z // 2
        self.keeps = self.x == self.owner_x
        self.sib = (2 * self.x + 1 - self.c, self.p)
        self.opp = (2 * (1 - self.x) + self.c, self.p)
        self.goal_q = 2 * self.owner_x + self.owner_c

    def rows(self, n, c):
        return pl.ds(pl.multiple_of(n * 256 + c * 128, 128), 128)

    def sem(self, k, n):
        return self.sems.at[self.base + k, n]

    def first(self, n):
        return remote(
            self.part.at[self.rows(n, 1 - self.c)], self.l1.at[n], self.sem(0, n), self.sem(1, n), self.sib
        )

    def second(self, n):
        return remote(self.own.at[n], self.l2.at[n], self.sem(2, n), self.sem(3, n), self.opp)

    def third(self, n):
        slot = mod(self.z, 2)
        return remote(
            self.own.at[n], self.out.at[slot], self.sem(4, n), self.sem(5, slot), (self.goal_q, 2 * n + self.c)
        )

    def is_self(self, n):
        return jnp.logical_and(self.goal_q == self.q, 2 * n + self.c == self.p)

    def beside(self, n):
        self.first(n).start()

    def across(self, n):
        self.first(n).wait_recv()
        mine = self.part[self.rows(n, self.c), :].astype(F32)
        self.own[n] = (mine + self.l1[n].astype(F32)).astype(BF)

        @pl.when(jnp.logical_not(self.keeps))
        def _():
            self.second(n).start()

    def finish(self, n, rest):
        @pl.when(self.keeps)
        def _():
            self.second(n).wait_recv()
            s = self.own[n].astype(F32) + self.l2[n].astype(F32)
            self.own[n] = rest(n, s).astype(BF)

            @pl.when(jnp.logical_not(self.is_self(n)))
            def _():
                self.third(n).start()

            @pl.when(self.is_self(n))
            def _():
                cp = pltpu.make_async_copy(self.own.at[n], self.out.at[mod(self.z, 2)], self.here)
                cp.start()
                cp.wait()

    def close(self):
        for i in range(2):
            group = 4 * self.c + 2 * i + self.x
            same = jnp.logical_and(group == self.p, self.y == self.c)

            @pl.when(jnp.logical_not(same))
            def _():
                remote(self.own.at[0], self.out.at[i], self.sem(4, 0), self.sem(5, i), (self.q, self.p)).wait_recv()

        for n in range(4):
            self.first(n).wait_send()

            @pl.when(jnp.logical_not(self.keeps))
            def _():
                self.second(n).wait_send()

            @pl.when(jnp.logical_and(self.keeps, jnp.logical_not(self.is_self(n))))
            def _():
                self.third(n).wait_send()


class Scatter:
    def __init__(self, g, ly, lz, sems, base):
        self.q, self.p, _, _, self.z, self.y = place()
        self.g, self.ly, self.lz, self.sems, self.base = g, ly, lz, sems, base

    def y_copy(self, n):
        s, r = self.sems.at[self.base + n, 0], self.sems.at[self.base + n, 1]
        return remote(self.g.at[1 - self.y, n], self.ly(n), s, r, (self.q, 2 * self.z + 1 - self.y))

    def z_copy(self, n, k):
        t = mod(self.z + k, 4)
        s, r = self.sems.at[self.base + n, 2 * k], self.sems.at[self.base + n, 2 * k + 1]
        return remote(self.ly(n).at[t], self.lz(n).at[k - 1], s, r, (self.q, 2 * t + self.y))

    def y_send(self, n):
        self.y_copy(n).start()

    def z_step(self, n):
        self.y_copy(n).wait_recv()
        ly = self.ly(n)

        @pl.loop(0, 4)
        def _(t):
            ly[t] = (ly[t].astype(F32) + self.g[self.y, n, t].astype(F32)).astype(BF)

        for k in (1, 2, 3):
            self.z_copy(n, k).start()

    def z_sum(self, n):
        for k in (1, 2, 3):
            self.z_copy(n, k).wait_recv()
        ly, lz = self.ly(n), self.lz(n)
        return ly[self.z].astype(F32) + lz[0].astype(F32) + lz[1].astype(F32) + lz[2].astype(F32)

    def close(self, count):
        @pl.loop(0, count)
        def _(n):
            self.y_copy(n).wait_send()
            for k in (1, 2, 3):
                self.z_copy(n, k).wait_send()


class Columns:
    def __init__(self, scatter, land, sems, base):
        self.scatter, self.land = scatter, land
        self.sems, self.base = sems, base
        self.q, self.p = scatter.q, scatter.p

    def copy(self, t):
        s, r = self.sems.at[self.base, t], self.sems.at[self.base + 1, self.q]
        return remote(self.scatter.ly(t).at[self.scatter.z], self.land.at[self.q], s, r, (t, self.p))

    def step(self, t):
        s = self.scatter.z_sum(t).astype(BF)

        @pl.when(t != self.q)
        def _():
            ly = self.scatter.ly(t)
            ly[self.scatter.z] = s
            self.copy(t).start()

        @pl.when(t == self.q)
        def _():
            self.land[t] = s

    def close(self):
        for t in range(4):

            @pl.when(t != self.q)
            def _():
                r = self.sems.at[self.base + 1, t]
                remote(self.land.at[t], self.land.at[t], self.sems.at[self.base, t], r, (self.q, self.p)).wait_recv()
                self.copy(t).wait_send()


def column(table, h):
    lane = lax.broadcasted_iota(jnp.int32, table.shape, 1)
    return jnp.sum(jnp.where(lane == h, table, 0.0), axis=1, keepdims=True)


def layer_kernel(
    tok, cot, pos, pq, pg, po, pd, table, qg, kg,
    out, igrad, od, ogu, oo, oqkv, oheads, of,
    xf, cf, wq, wg, wo, wd, raw_o, qb, kb, vb, ob, lse, hidden, rest, cs, pa, pb, pc, mb, dgu, gd, ggu,
    dkv, go, gqkv, yo, yqkv, zo, zqkv, heads, hy, hz, hdp,
    l1, own, l2, l1b, ownb, l2b, l2c, sorts, sorts_sem, free, sums, gsem, csem, hs, hr, homes, here, *sems,
):
    q, p, x_, c, z, y = place()
    sd = Scatter(gd, lambda n: wd.at[pl.ds(0, 4)], lambda n: wd.at[pl.ds(4, 3)], gsem, 0)
    sgu = Scatter(ggu, lambda n: wg.at[n, pl.ds(0, 4)], lambda n: wg.at[n, pl.ds(4, 3)], gsem, 1)
    so = Scatter(go, lambda n: yo.at[n], lambda n: zo.at[n], gsem, 5)
    sqkv = Scatter(gqkv, lambda n: yqkv.at[n], lambda n: zqkv.at[n], gsem, 6)
    cgu = Columns(sgu, ogu, csem, 0)
    cqkv = Columns(sqkv, oqkv, csem, 2)
    h_out = Home(pb, out, l1, own, l2, homes, here.at[0], 0)
    h_in = Home(pc, igrad, l1b, ownb, l2c, homes, here.at[1], 6)
    order = [(sd, 0)] + [(sgu, n) for n in range(4)] + [(so, 0)] + [(sqkv, n) for n in range(4)]

    def y_send(j):
        which, n = order[j]
        which.y_send(n)

    def step(j):
        which, n = order[j]
        which.z_step(n)
        if j + 2 < len(order):
            y_send(j + 2)

    g = Gather((tok, cot, pos, pq, pg, po, pd), (xf, cf, of, wq, wg, wo, wd), sems)
    peers = [(2 * x_ + cc, mod(p + k, 8)) for k in range(1, 8) for cc in (0, 1)]
    peers += [(mod(q + k, 4), p) for k in (1, 2, 3)]
    greet(peers)
    g.pos_start()
    g.token_start(0)
    g.column_start(0)
    for n in range(4):
        g.own_copy(n).start()
    g.column_start(1)
    g.own_copy(0).wait()
    g.column_wait(0)
    g.begin(0)
    g.pos_finish()
    sort = pltpu.make_async_copy(of, sorts, sorts_sem.at[0])
    sort.start()
    lse[...] = jnp.zeros_like(lse)
    g.step(0, 1)
    g.token_pass(0, 0, 4)
    g.step(0, 2)
    g.own_copy(2).wait()
    g.begin(1)
    g.step(0, 3)
    g.own_copy(1).wait()
    g.column_wait(1)
    g.begin(2)
    g.token_pass(0, 4, 8)
    g.own_copy(3).wait()
    g.begin(3)
    sort.wait()
    g.y_wait(0)

    @pl.loop(0, 4)
    def _(n):
        rows = pl.ds(pl.multiple_of(n * 256, 256), 256)
        v = pieces(xf, sorts, 1, n * 4, 4).astype(F32)
        h = (v * unit(v)).astype(BF)

        @pl.when(n == 1)
        def _():
            g.step(1, 1)
            g.begin(4)

        @pl.when(n == 3)
        def _():
            g.step(1, 2)
            g.step(2, 1)

        raw = jnp.dot(h, wq[...].reshape(WIDTH, WIDTH), preferred_element_type=F32)
        raw_o[rows, :] = raw[:, :768]
        cosine, sine = turns(table[rows, :])
        for t in range(2):
            vb[t, rows, :] = raw[:, 768 + t * 128 : 896 + t * 128].astype(BF)
        for t in range(6):
            u = raw[:, t * 128 : (t + 1) * 128]
            n_ = u * unit(u) * (qg[...] if t < 4 else kg[...])
            r = rotate(n_, cosine, sine).astype(BF)
            if t < 4:
                qb[t, rows, :] = r
            else:
                kb[t - 4, rows, :] = r

    @pl.loop(0, 4)
    def _(h):
        for turn, (piece, dist) in enumerate(((1, 3), (2, 2), (2, 3), (3, 1))):

            @pl.when(h == turn)
            def _():
                g.step(piece, dist)
                if turn == 0:
                    g.begin(5)
                if turn == 2:
                    g.begin(6)
                    g.token_start(1)

        kv = h // 2
        for i in range(4):
            length = (i + 1) * 256
            rows = slice(i * 256, length)
            s = dims(qb[h, rows, :], kb[kv, :length, :], 1, 1) * (HEAD_SIZE**-0.5 * LOG2E)
            s = lower(s, NEGATIVE_FILL)
            top = jnp.max(s, axis=-1, keepdims=True)
            e = jnp.exp2(s - top)
            sum_e = jnp.sum(e, axis=-1, keepdims=True)
            o = jnp.dot(e.astype(BF), vb[kv, :length, :], preferred_element_type=F32) / sum_e
            ob[rows, pl.ds(pl.multiple_of(h * 128, 128), 128)] = o.astype(BF)
            lane = lax.broadcasted_iota(jnp.int32, (256, 128), 1)
            lse[rows, :] = jnp.where(lane == h, top + jnp.log2(sum_e), lse[rows, :])

    g.y_wait(1)
    s1 = Sum(pa, pb, l1, own, l2, sums, 0)
    s2 = Sum(pc, gqkv, l1b, ownb, l2b, sums, 6)

    @pl.loop(0, 4)
    def _(n):
        rows = pl.ds(pl.multiple_of(n * 256, 256), 256)
        out_w = wo[...].reshape(512, WIDTH)
        pa[rows, :] = jnp.dot(ob[rows, :], out_w, preferred_element_type=F32).astype(BF)
        s1.beside(n)

        @pl.when(n > 0)
        def _():
            s1.across(n - 1)

    s1.across(3)
    g.step(3, 2)
    g.step(4, 1)
    s1.back(0)
    g.step(3, 3)
    g.step(4, 2)
    s1.back(1)
    g.step(4, 3)
    g.step(5, 1)
    s1.back(2)
    g.step(5, 2)
    g.token_pass(1, 0, 3)
    s1.back(3)
    g.step(5, 3)
    g.token_pass(1, 3, 6)
    g.step(6, 1)
    g.step(6, 2)
    g.step(6, 3)
    g.token_pass(1, 6, 8)
    g.y_wait(2, 3, 4, 5, 6)
    s1.close(0)

    @pl.loop(0, 4)
    def _(n):
        s1.ready(n)
        rows = pl.ds(pl.multiple_of(n * 256, 256), 256)
        h = pieces(xf, sorts, 1, n * 4, 4).astype(F32) + pb[rows, :].astype(F32)
        hidden[pl.ds(n * 4, 4)] = h.reshape(4, BLK, WIDTH)
        a = (h * unit(h)).astype(BF)
        pa[rows, :] = a
        wgu = wg[...].reshape(WIDTH, 1536)
        gu = jnp.dot(a, wgu, preferred_element_type=F32)
        gate = gu[:, :768]
        up = gu[:, 768:]
        sig = 1.0 / (1.0 + jnp.exp2(gate * -LOG2E))
        silu = gate * sig
        mb[pl.ds(n * 4, 4)] = (silu * up).astype(BF).reshape(4, BLK, 768)
        cc = pieces(cf, sorts, 1, n * 4, 4)
        cs[rows, :] = cc
        dm = dims(cc, wd[...].reshape(768, WIDTH), 1, 1)
        dg = (dm * up * sig * (1.0 + gate * (1.0 - sig))).astype(BF)
        du = (dm * silu).astype(BF)
        both = jnp.concatenate([dg, du], axis=1)
        dgu[rows, :] = both
        pc[rows, :] = dims(both, wgu, 1, 1).astype(BF)
        s2.beside(n)

        @pl.when(n > 0)
        def _():
            s2.across(n - 1)

    s2.across(3)
    s1.close(1, 2)

    @pl.loop(0, 4)
    def _(n):
        rows = pl.ds(pl.multiple_of(n * 256, 256), 256)
        m = pieces(mb, sorts, 0, n * 4, 4)
        pb[rows, :] = jnp.dot(m, wd[...].reshape(768, WIDTH), preferred_element_type=F32).astype(BF)
        rest[n] = pieces(hidden, sorts, 0, 4 * n + 2 * g.c, 2)

    g.close()
    near = [(q, 2 * z + 1 - y), (2 * x_ + 1 - c, p), (2 * (1 - x_) + c, p)]
    near += [(q, 2 * mod(z + k, 4) + y) for k in (1, 2, 3)]
    for peer in near:
        pl.semaphore_signal(free, inc=1, device_id=peer, device_id_type=MESH)
    s2.back(0)

    @pl.loop(0, 2)
    def _(n):
        m_all = mb[...].reshape(TOKENS, 768)
        for t in range(2):

            @pl.when(n == t)
            def _():
                v = dims(m_all[:, t * 384 : (t + 1) * 384], cs[...], 0, 0).astype(BF)
                v = v.reshape(2, 2, 96, WIDTH)
                for u in range(2):
                    gd[u, 0, 2 * t : 2 * t + 2] = v[:, u]

    s2.back(1)
    pl.semaphore_wait(free, len(near))
    y_send(0)
    for n in range(4):
        h_out.beside(n)

    @pl.loop(0, 4)
    def _(n):
        v = dims(pa[:, pl.ds(pl.multiple_of(n * 256, 256), 256)], dgu[...], 0, 0).astype(BF)
        v = v.reshape(4, 2, 32, 1536)
        for t in range(2):
            ggu[t, n] = v[:, t]

        @pl.when(n == 0)
        def _():
            y_send(1)

        @pl.when(n < 2)
        def _():
            s2.back(n + 2)

    @pl.loop(0, 4)
    def _(n):
        rows = pl.ds(pl.multiple_of(n * 256, 256), 256)
        h = hidden[pl.ds(n * 4, 4)].reshape(256, WIDTH)
        r = unit(h)
        s2.ready(n)
        da = gqkv[n // 2, pl.ds(2 * (n % 2), 2)].reshape(256, WIDTH).astype(F32)
        back = r * da - h * (r * r * r * jnp.mean(h * da, axis=-1, keepdims=True))
        d = cs[rows, :].astype(F32) + back
        hidden[pl.ds(n * 4, 4)] = d.reshape(4, BLK, WIDTH)
        low = d.astype(BF)
        pa[rows, :] = low
        do = dims(low, wo[...].reshape(512, WIDTH), 1, 1).astype(BF)
        cs[rows, :512] = do
        h_out.across(n)

    @pl.loop(0, 2)
    def _(n):
        v = dims(ob[:, pl.ds(pl.multiple_of(n * 256, 256), 256)], pa[...], 0, 0).astype(BF)
        v = v.reshape(2, 2, 64, WIDTH)
        for t in range(2):
            go[t, 0, pl.ds(n * 2, 2)] = v[:, t]

    s2.close(0, 1, 2)
    heads[...] = jnp.zeros_like(heads)
    scale = HEAD_SIZE**-0.5

    def norm_back(dn, u, gain, rows):
        dn = rotate_back(dn, *turns(table[rows, :]))
        r = unit(u)
        gd_ = gain * dn
        du = r * gd_ - u * (r * r * r * jnp.mean(u * gd_, axis=-1, keepdims=True))
        return du.astype(BF), jnp.sum(dn * u * r, axis=0, keepdims=True)

    def result(n, s):
        return s + rest[n]

    def inward(n, s):
        v = xf[pl.ds(4 * n + 2 * c, 2)].reshape(128, WIDTH).astype(F32)
        r = unit(v)
        s = r * s - v * (r * r * r * jnp.mean(v * s, axis=-1, keepdims=True))
        return s + pieces(hidden, sorts, 0, 4 * n + 2 * c, 2)

    @pl.loop(0, 2)
    def _(g):
        dkv[...] = jnp.zeros_like(dkv)
        for t in range(2):
            for turn in range(2):

                @pl.when(g == turn)
                def _():
                    step(2 * turn + t)
                    if turn == 1:
                        h_out.finish(2 * t, result)
                        h_out.finish(2 * t + 1, result)

            h = g * 2 + t
            lanes = pl.ds(pl.multiple_of(h * 128, 128), 128)
            for i in range(4):
                length = (i + 1) * 256
                rows = slice(i * 256, length)
                qv = qb[h, rows, :]
                kv = kb[g, :length, :]
                dov = cs[rows, lanes]
                s = dims(qv, kv, 1, 1) * (scale * LOG2E)
                pr = lower(jnp.exp2(s - column(lse[rows, :], h)), 0.0)
                dp = dims(dov, vb[g, :length, :], 1, 1)
                delta = jnp.sum(dov.astype(F32) * ob[rows, lanes].astype(F32), axis=-1, keepdims=True)
                ds_ = lower(pr * (dp - delta), 0.0).astype(BF)
                dq = jnp.dot(ds_, kv, preferred_element_type=F32) * scale
                dkv[0, :length, :] += dims(ds_, qv, 0, 0)
                dkv[1, :length, :] += dims(pr.astype(BF), dov, 0, 0)
                du, dgain = norm_back(dq, raw_o[rows, lanes], qg[...], pl.ds(i * 256, 256))
                cf[i * 4 : i * 4 + 4, :, lanes] = du.reshape(4, BLK, 128)
                heads[0:1, :] += dgain
        lanes = pl.ds(pl.multiple_of(512 + g * 128, 128), 128)
        for i in range(4):
            rows = slice(i * 256, (i + 1) * 256)
            du, dgain = norm_back(dkv[0, rows, :] * scale, raw_o[rows, lanes], kg[...], pl.ds(i * 256, 256))
            cf[i * 4 : i * 4 + 4, :, lanes] = du.reshape(4, BLK, 128)
            heads[1:2, :] += dgain
        cf[:, :, pl.ds(pl.multiple_of(768 + g * 128, 128), 128)] = dkv[1].astype(BF).reshape(16, BLK, 128)

    hy_copy = remote(heads, hy, hs.at[0], hr.at[0], (q, 2 * z + 1 - y))
    hy_copy.start()

    @pl.loop(0, 4)
    def _(n):
        rows = pl.ds(pl.multiple_of(n * 256, 256), 256)
        d = pieces(cf, sorts, 0, n * 4, 4)
        pc[rows, :] = dims(d, wq[...].reshape(WIDTH, WIDTH), 1, 1).astype(BF)
        h_in.beside(n)

        @pl.when(n > 0)
        def _():
            h_in.across(n - 1)

    h_in.across(3)

    @pl.loop(0, 4)
    def _(n):
        rows = pl.ds(pl.multiple_of(n * 256, 256), 256)
        v = pieces(xf, sorts, 1, n * 4, 4).astype(F32)
        pa[rows, :] = (v * unit(v)).astype(BF)

    @pl.loop(0, 4)
    def _(n):
        v = dims(pa[:, pl.ds(pl.multiple_of(n * 256, 256), 256)], cf[...].reshape(TOKENS, WIDTH), 0, 0).astype(BF)
        v = v.reshape(4, 2, 32, WIDTH)
        for t in range(2):
            gqkv[t, n] = v[:, t]

    step(4)

    def z_heads(k):
        return remote(hz.at[z], hz.at[z], hs.at[k], hr.at[k], (q, 2 * mod(z + k, 4) + y))

    def dp_heads(k):
        return remote(hdp.at[q], hdp.at[q], hs.at[3 + k], hr.at[3 + k], (mod(q + k, 4), p))

    hy_copy.wait_recv()
    hz[z] = heads[...] + hy[...]
    for k in (1, 2, 3):
        z_heads(k).start()
    h_in.finish(0, inward)
    od[...] = sd.z_sum(0)
    for n in range(4):
        step(5 + n)
        cgu.step(n)
        if n < 3:
            h_in.finish(n + 1, inward)
    step(9)
    for k in (1, 2, 3):
        f = mod(z + 4 - k, 4)
        remote(hz.at[f], hz.at[f], hs.at[k], hr.at[k], (q, p)).wait_recv()
    hdp[q] = hz[0] + hz[1] + hz[2] + hz[3]
    for k in (1, 2, 3):
        dp_heads(k).start()
    oo[...] = so.z_sum(0)

    @pl.loop(0, 4)
    def _(n):
        cqkv.step(n)

    cgu.close()
    for k in (1, 2, 3):
        f = mod(q + 4 - k, 4)
        remote(hdp.at[f], hdp.at[f], hs.at[3 + k], hr.at[3 + k], (q, p)).wait_recv()
    oheads[...] = hdp[0] + hdp[1] + hdp[2] + hdp[3]
    cqkv.close()
    h_out.close()
    h_in.close()
    sd.close(1)
    sgu.close(4)
    so.close(1)
    sqkv.close(4)
    hy_copy.wait_send()
    for k in (1, 2, 3):
        z_heads(k).wait_send()
        dp_heads(k).wait_send()


def layer_call(tok, cot, pos, pq, pg, po, pd, table, qg, kg):
    sem = pltpu.SemaphoreType.DMA
    shape = jax.ShapeDtypeStruct
    vm = pltpu.VMEM
    full = (TOKENS, WIDTH)
    return pl.pallas_call(
        layer_kernel,
        out_shape=(
            shape((2, 128, WIDTH), BF),
            shape((2, 128, WIDTH), BF),
            shape((96, WIDTH), F32),
            shape((4, 32, 1536), BF),
            shape((64, WIDTH), F32),
            shape((4, 32, WIDTH), BF),
            shape((8, 128), F32),
            shape((8, 128), jnp.int32),
        ),
        in_specs=[ANY] * 7 + [VM] * 3,
        out_specs=(ANY, ANY) + (VM,) * 5 + (ANY,),
        scratch_shapes=[
            vm((16, BLK, WIDTH), BF), vm((16, BLK, WIDTH), BF),
            vm((4, 8) + pq.shape[1:], BF), vm((4, 8) + pg.shape[1:], BF),
            vm((8,) + po.shape, BF), vm((8,) + pd.shape, BF),
            vm((TOKENS, 768), F32),
            vm((4, TOKENS, 128), BF), vm((2, TOKENS, 128), BF), vm((2, TOKENS, 128), BF), vm((TOKENS, 512), BF),
            vm((TOKENS, 128), F32), vm((16, BLK, WIDTH), F32), vm((4, 128, WIDTH), F32),
            vm(full, BF), vm(full, BF), vm(full, BF), vm(full, BF),
            vm((16, BLK, 768), BF), vm((TOKENS, 1536), BF),
            vm((2, 1, 4, 96, WIDTH), BF), vm((2, 4, 4, 32, 1536), BF),
            vm((2, TOKENS, 128), F32),
            vm((2, 1, 4, 64, WIDTH), BF), vm((2, 4, 4, 32, WIDTH), BF),
            vm((1, 4, 64, WIDTH), BF), vm((4, 4, 32, WIDTH), BF),
            vm((1, 3, 64, WIDTH), BF), vm((4, 3, 32, WIDTH), BF),
            vm((8, 128), F32), vm((8, 128), F32), vm((4, 8, 128), F32), vm((4, 8, 128), F32),
        ]
        + [vm((4, 128, WIDTH), BF)] * 7
        + [
            pltpu.SMEM((8, 128), jnp.int32), sem((1,)), pltpu.SemaphoreType.REGULAR, sem((12, 4)),
            sem((10, 8)), sem((4, 4)), sem((7,)), sem((7,)), sem((12, 4)), sem((2,)),
        ]
        + [sem(n) for n in GATHER_SEMS],
        compiler_params=pltpu.CompilerParams(
            collective_id=0, has_side_effects=True, vmem_limit_bytes=VMEM_BYTES
        ),
        name="layer_both_ways",
    )(tok, cot, pos, pq, pg, po, pd, table, qg, kg)


def quarter_columns(w, gain):
    rows, cols = w.shape
    v = w if gain is None else (w.astype(F32) * gain).astype(BF)
    return jnp.transpose(v.reshape(rows, 4, cols // 4), (1, 0, 2))


def whole_sequences(
    tokens, attn_gain, w_query, key_projection, value_projection, query_head_gain, key_gain, w_out,
    mlp_gain, w_gate, w_up, w_down, cotangent, span_order,
):
    p = lax.axis_index("seq")
    ga = attn_gain.astype(F32)[:, None]
    gm = mlp_gain.astype(F32)[:, None]
    pq = jnp.concatenate(
        [quarter_columns(w, ga) for w in (w_query, key_projection, value_projection)], axis=2
    )
    pg = jnp.concatenate([quarter_columns(w, gm) for w in (w_gate, w_up)], axis=2)
    row = jnp.where(lax.rem(p // 2, 2) == 0, span_order[0], span_order[1])
    spots = lax.iota(jnp.int32, 16)
    inverse = jnp.sum(jnp.where(row[None, :] == spots[:, None], spots[None, :], 0), axis=1)
    pos = jnp.zeros((8, 128), jnp.int32)
    pos = pos.at[0, :16].set(row).at[1, :16].set(inverse)
    freqs = BASE ** (-np.arange(HEAD_SIZE // 2) * 2.0 / HEAD_SIZE)
    angles = np.arange(TOKENS)[:, None] * freqs.astype(np.float32)[None, :].astype(np.float64)
    table = np.concatenate([np.cos(angles), np.sin(angles)], axis=1).astype(np.float32)
    qg = query_head_gain.astype(F32)[None, :]
    kg = key_gain.astype(F32)[None, :]
    out, igrad, od, ogu, oo, oqkv, oheads, _ = layer_call(
        tokens.reshape(2, 2, BLK, WIDTH), cotangent.reshape(2, 2, BLK, WIDTH), pos, pq, pg, w_out, w_down,
        table, qg, kg,
    )
    ogu, oqkv = ogu.astype(F32), oqkv.astype(F32)
    return finish(
        out, igrad, od, ogu, oo, oqkv, oheads, ga, gm, w_query, key_projection, value_projection, w_gate, w_up
    )


def finish(out, igrad, od, ogu, oo, oqkv, oheads, ga, gm, w_query, key_projection, value_projection, w_gate, w_up):
    def join(part):
        return jnp.transpose(part, (1, 0, 2)).reshape(part.shape[1], -1)

    hq, hk, hv = join(oqkv[:, :, :512]), join(oqkv[:, :, 512:768]), join(oqkv[:, :, 768:])
    hg, hu = join(ogu[:, :, :768]), join(ogu[:, :, 768:])

    def along(w, h):
        return jnp.sum(w.astype(F32) * h, axis=1)

    grad_attn_gain = along(w_query, hq) + along(key_projection, hk) + along(value_projection, hv)
    grad_mlp_gain = along(w_gate, hg) + along(w_up, hu)
    return (
        out,
        igrad,
        grad_attn_gain,
        ga * hq,
        ga * hk,
        ga * hv,
        oheads[0],
        oheads[1],
        oo,
        grad_mlp_gain,
        gm * hg,
        gm * hu,
        od,
    )


def layer(tokens, *rest):
    whole = (
        lax.axis_size("dp") == 4
        and lax.axis_size("seq") == 8
        and tokens.shape == (2, 128, WIDTH)
        and rest[-1].shape == (2, 16)
    )
    return (whole_sequences if whole else shards)(tokens, *rest)


def solution(mesh):
    return jax.shard_map(
        layer,
        mesh=mesh,
        in_specs=(
            P("dp", "seq", None),
            P(("dp", "seq")),
            P(("dp", "seq"), None),
            P(("dp", "seq"), None),
            P(("dp", "seq"), None),
            P(),
            P(),
            P(("dp", "seq"), None),
            P(("dp", "seq")),
            P(("dp", "seq"), None),
            P(("dp", "seq"), None),
            P(("dp", "seq"), None),
            P("dp", "seq", None),
            P("dp", None),
        ),
        out_specs=(
            P("dp", "seq", None),
            P("dp", "seq", None),
            P(("dp", "seq")),
            P(("dp", "seq"), None),
            P(("dp", "seq"), None),
            P(("dp", "seq"), None),
            P(),
            P(),
            P(("dp", "seq"), None),
            P(("dp", "seq")),
            P(("dp", "seq"), None),
            P(("dp", "seq"), None),
            P(("dp", "seq"), None),
        ),
        check_vma=False,
    )
```

```python
import jax
import jax.numpy as jnp
from jax import lax
from jax.sharding import PartitionSpec as P

import numpy as np
from jax.experimental import pallas as pl
from jax.experimental.pallas import tpu as pltpu

QUERY_HEADS = 16
KEY_VALUE_HEADS = 8
HEAD_SIZE = 128
BLK = 64
MB = 2


EPS = 1e-06
BASE = 1000000.0
NEGATIVE_FILL = -1e30


def from_behind(block, axis, distance):
    devices = range(lax.axis_size(axis))
    route = [((i - distance) % len(devices), i) for i in devices]
    return lax.ppermute(block, axis, route)


def row_norm_apply(v, gain):
    return v * lax.rsqrt(jnp.mean(v * v, axis=-1, keepdims=True) + EPS) * gain


def apply_rotary(v, cosine_table, sine_table):
    half = v.shape[-1] // 2
    first = v[..., :half]
    second = v[..., half:]
    return jnp.concatenate(
        [first * cosine_table - second * sine_table, second * cosine_table + first * sine_table],
        axis=-1,
    )


def matrix_multiply(left, right):
    return jnp.dot(left, right, preferred_element_type=jnp.float32)


def row_product(left, right):
    return lax.dot_general(
        left, right, (((0,), (0,)), ((), ())), preferred_element_type=jnp.float32
    )


def product_backward(left, right):
    return lax.dot_general(
        left, right, (((1,), (1,)), ((), ())), preferred_element_type=jnp.float32
    )


def block_positions(order, start, count):
    places = start + lax.iota(jnp.int32, count)
    which = places // BLK
    hits = (which[:, None] == lax.iota(jnp.int32, order.shape[1])[None, :]).astype(jnp.int32)
    spans = jnp.sum(hits[None, :, :] * order[:, None, :], axis=-1)
    return spans * BLK + places % BLK


def pack_shares(members, count):
    return jnp.concatenate([m.reshape(count, -1) for m in members], axis=1).reshape(-1)


def unpack_shares(flat, members, count):
    pieces = []
    offset = 0
    for m in members:
        length = m.size // count
        share_shape = (m.shape[0] // count,) + tuple(m.shape[1:])
        pieces.append(flat[offset : offset + length].reshape(share_shape))
        offset = offset + length
    return pieces


def shards(
    tokens,
    attn_gain,
    w_query,
    key_projection,
    value_projection,
    query_head_gain,
    key_gain,
    w_out,
    mlp_gain,
    w_gate,
    w_up,
    w_down,
    cotangent,
    span_order,
):
    seq_count = lax.axis_size("seq")
    seq_place = lax.axis_index("seq")
    all_count = lax.axis_size(("dp", "seq"))
    local_length = tokens.shape[1]
    width = tokens.shape[2]
    sequence_permutation = tokens.shape[0] // MB
    query_group = QUERY_HEADS // KEY_VALUE_HEADS
    scale = HEAD_SIZE ** (-0.5)
    freqs = BASE ** (-(lax.iota(jnp.float32, HEAD_SIZE // 2) * 2.0) / HEAD_SIZE)
    query_norm_gain = query_head_gain.astype(jnp.float32)
    kgain = key_gain.astype(jnp.float32)
    sums = None
    outputs = []
    input_grads = []
    for batch in range(MB):
        rows_x = tokens[batch * sequence_permutation : (batch + 1) * sequence_permutation]
        rows_cot = cotangent[batch * sequence_permutation : (batch + 1) * sequence_permutation]
        order = span_order[batch * sequence_permutation : (batch + 1) * sequence_permutation]
        gain_a, wq, key_weight, value_weight, output_weight = (
            lax.all_gather(attn_gain, ("dp", "seq"), axis=0, tiled=True),
            lax.all_gather(w_query, ("dp", "seq"), axis=0, tiled=True),
            lax.all_gather(key_projection, ("dp", "seq"), axis=0, tiled=True),
            lax.all_gather(value_projection, ("dp", "seq"), axis=0, tiled=True),
            lax.all_gather(w_out, ("dp", "seq"), axis=0, tiled=True),
        )
        gain_m, wg, wu, wd = (
            lax.all_gather(mlp_gain, ("dp", "seq"), axis=0, tiled=True),
            lax.all_gather(w_gate, ("dp", "seq"), axis=0, tiled=True),
            lax.all_gather(w_up, ("dp", "seq"), axis=0, tiled=True),
            lax.all_gather(w_down, ("dp", "seq"), axis=0, tiled=True),
        )
        own_pos = block_positions(order, seq_place * local_length, local_length)
        angles = own_pos.astype(jnp.float32)[..., None] * freqs
        cosine_table = jnp.cos(angles)[:, :, None, :]
        sine_table = jnp.sin(angles)[:, :, None, :]

        def query_per_head(raw, gain):
            return apply_rotary(row_norm_apply(raw, gain), cosine_table, sine_table)

        flat_x = rows_x.reshape(-1, width).astype(jnp.float32)
        first_operand = row_norm_apply(flat_x, gain_a.astype(jnp.float32)).astype(jnp.bfloat16)
        query_unrotated = matrix_multiply(first_operand, wq).reshape(
            sequence_permutation, local_length, QUERY_HEADS, HEAD_SIZE
        )
        key_unrotated = matrix_multiply(first_operand, key_weight).reshape(
            sequence_permutation, local_length, KEY_VALUE_HEADS, HEAD_SIZE
        )
        value_reduced = (
            matrix_multiply(first_operand, value_weight)
            .astype(jnp.bfloat16)
            .reshape(sequence_permutation, local_length, KEY_VALUE_HEADS, HEAD_SIZE)
        )
        q_low = (
            query_per_head(query_unrotated, query_norm_gain)
            .astype(jnp.bfloat16)
            .reshape(sequence_permutation, local_length, KEY_VALUE_HEADS, query_group, HEAD_SIZE)
        )
        k_low = query_per_head(key_unrotated, kgain).astype(jnp.bfloat16)
        initial_maximum = jnp.full(
            (sequence_permutation, KEY_VALUE_HEADS, query_group, local_length),
            NEGATIVE_FILL,
            jnp.float32,
        )
        top = initial_maximum
        piece_k = lax.all_gather(k_low, "seq", axis=1, tiled=True)
        piece_v = lax.all_gather(value_reduced, "seq", axis=1, tiled=True)
        key_pos = block_positions(order, jnp.int32(0), piece_k.shape[1])
        visible = key_pos[:, None, None, None, :] <= own_pos[:, None, None, :, None]
        scores = (
            jnp.einsum("sqgrd,skgd->sgrqk", q_low, piece_k, preferred_element_type=jnp.float32)
            * scale
        )
        scores = jnp.where(visible, scores, NEGATIVE_FILL)
        new_top = jnp.maximum(top, jnp.max(scores, axis=-1))
        weights = jnp.exp(scores - new_top[..., None])
        new_total = jnp.sum(weights, axis=-1)
        taken = jnp.einsum(
            "sgrqk,skgd->sqgrd",
            weights.astype(jnp.bfloat16),
            piece_v,
            preferred_element_type=jnp.float32,
        )
        top = new_top
        log_total = top + jnp.log(new_total)
        attn = taken / jnp.transpose(new_total, (0, 3, 1, 2))[..., None]
        o_low = attn.astype(jnp.bfloat16).reshape(
            sequence_permutation * local_length, QUERY_HEADS * HEAD_SIZE
        )
        hidden = flat_x + matrix_multiply(o_low, output_weight)
        gain_second = gain_m.astype(jnp.float32)
        a_second = row_norm_apply(hidden, gain_second).astype(jnp.bfloat16)
        gate = matrix_multiply(a_second, wg)
        up_part = matrix_multiply(a_second, wu)
        mixed = (gate * jax.nn.sigmoid(gate) * up_part).astype(jnp.bfloat16)
        result = hidden + matrix_multiply(mixed, wd)
        outputs.append(
            result.astype(jnp.bfloat16).reshape(sequence_permutation, local_length, width)
        )
        gain_a, wq, key_weight, value_weight, output_weight = (
            lax.all_gather(attn_gain, ("dp", "seq"), axis=0, tiled=True),
            lax.all_gather(w_query, ("dp", "seq"), axis=0, tiled=True),
            lax.all_gather(key_projection, ("dp", "seq"), axis=0, tiled=True),
            lax.all_gather(value_projection, ("dp", "seq"), axis=0, tiled=True),
            lax.all_gather(w_out, ("dp", "seq"), axis=0, tiled=True),
        )
        gain_m, wg, wu, wd = (
            lax.all_gather(mlp_gain, ("dp", "seq"), axis=0, tiled=True),
            lax.all_gather(w_gate, ("dp", "seq"), axis=0, tiled=True),
            lax.all_gather(w_up, ("dp", "seq"), axis=0, tiled=True),
            lax.all_gather(w_down, ("dp", "seq"), axis=0, tiled=True),
        )
        flat_cot = rows_cot.reshape(-1, width)
        grad_down = row_product(mixed, flat_cot)
        d_mixed = product_backward(flat_cot, wd)

        def mix(gate_in, up_in):
            return gate_in * jax.nn.sigmoid(gate_in) * up_in

        _, mix_back = jax.vjp(mix, gate, up_part)
        d_gate, d_up = mix_back(d_mixed)
        gate_low = d_gate.astype(jnp.bfloat16)
        up_low = d_up.astype(jnp.bfloat16)
        grad_gate = row_product(a_second, gate_low)
        grad_up = row_product(a_second, up_low)
        d_second = product_backward(gate_low, wg) + product_backward(up_low, wu)
        _, second_back = jax.vjp(row_norm_apply, hidden, gain_second)
        d_hidden_norm, grad_mlp_gain = second_back(d_second)
        d_hidden = flat_cot.astype(jnp.float32) + d_hidden_norm
        grad_output_reduced = d_hidden.astype(jnp.bfloat16)
        grad_out = row_product(o_low, grad_output_reduced)
        do_low = (
            product_backward(grad_output_reduced, output_weight)
            .astype(jnp.bfloat16)
            .reshape(sequence_permutation, local_length, KEY_VALUE_HEADS, query_group, HEAD_SIZE)
        )
        delta = jnp.transpose(jnp.sum(do_low.astype(jnp.float32) * attn, axis=-1), (0, 2, 3, 1))

        def back_terms(held_k, held_v, visible):
            scores = (
                jnp.einsum("sqgrd,skgd->sgrqk", q_low, held_k, preferred_element_type=jnp.float32)
                * scale
            )
            scores = jnp.where(visible, scores, NEGATIVE_FILL)
            probs = jnp.exp(scores - log_total[..., None])
            d_probs = jnp.einsum(
                "sqgrd,skgd->sgrqk", do_low, held_v, preferred_element_type=jnp.float32
            )
            score_low = (probs * (d_probs - delta[..., None])).astype(jnp.bfloat16)
            probs_low = probs.astype(jnp.bfloat16)
            term_q = scale * jnp.einsum(
                "sgrqk,skgd->sqgrd", score_low, held_k, preferred_element_type=jnp.float32
            )
            term_k = scale * jnp.einsum(
                "sgrqk,sqgrd->skgd", score_low, q_low, preferred_element_type=jnp.float32
            )
            term_v = jnp.einsum(
                "sgrqk,sqgrd->skgd", probs_low, do_low, preferred_element_type=jnp.float32
            )
            return (term_k, term_v, term_q)

        def cycle_step(turn, state):
            held_k, held_v, acc_k, acc_v, acc_q = state
            owner = (seq_place - turn) % seq_count
            key_pos = block_positions(order, owner * local_length, local_length)
            visible = key_pos[:, None, None, None, :] <= own_pos[:, None, None, :, None]
            term_k, term_v, term_q = back_terms(held_k, held_v, visible)
            acc_k, acc_v, acc_q = (acc_k + term_k, acc_v + term_v, acc_q + term_q)
            held_k, held_v = from_behind((held_k, held_v), "seq", 1)
            acc_k, acc_v = (
                from_behind(acc_k.astype(jnp.bfloat16), "seq", 1).astype(acc_k.dtype),
                from_behind(acc_v.astype(jnp.bfloat16), "seq", 1).astype(acc_v.dtype),
            )
            return (held_k, held_v, acc_k, acc_v, acc_q)

        def two_steps(pair, state):
            return cycle_step(2 * pair + 1, cycle_step(2 * pair, state))

        blank_key_value = jnp.zeros(
            (sequence_permutation, local_length, KEY_VALUE_HEADS, HEAD_SIZE), jnp.float32
        )
        blank_query = jnp.zeros(
            (sequence_permutation, local_length, KEY_VALUE_HEADS, query_group, HEAD_SIZE),
            jnp.float32,
        )
        state = lax.fori_loop(
            0,
            seq_count // 2,
            two_steps,
            (k_low, value_reduced, blank_key_value, blank_key_value, blank_query),
        )
        _, _, d_keys, grad_value_rows, d_queries = state
        _, query_back = jax.vjp(query_per_head, query_unrotated, query_norm_gain)
        d_q_raw, grad_qgain = query_back(
            d_queries.reshape(sequence_permutation, local_length, QUERY_HEADS, HEAD_SIZE)
        )
        _, key_back = jax.vjp(query_per_head, key_unrotated, kgain)
        grad_key_unrotated, grad_kgain = key_back(d_keys)
        dq_low = d_q_raw.astype(jnp.bfloat16).reshape(
            sequence_permutation * local_length, QUERY_HEADS * HEAD_SIZE
        )
        grad_key_reduced = grad_key_unrotated.astype(jnp.bfloat16).reshape(
            sequence_permutation * local_length, KEY_VALUE_HEADS * HEAD_SIZE
        )
        grad_value_reduced = grad_value_rows.astype(jnp.bfloat16).reshape(
            sequence_permutation * local_length, KEY_VALUE_HEADS * HEAD_SIZE
        )
        grad_query = row_product(first_operand, dq_low)
        grad_key = row_product(first_operand, grad_key_reduced)
        grad_value = row_product(first_operand, grad_value_reduced)
        d_first = (
            product_backward(dq_low, wq)
            + product_backward(grad_key_reduced, key_weight)
            + product_backward(grad_value_reduced, value_weight)
        )
        _, first_back = jax.vjp(row_norm_apply, flat_x, gain_a.astype(jnp.float32))
        d_x_norm, grad_attn_gain = first_back(d_first)
        input_grads.append(
            (d_hidden + d_x_norm)
            .astype(jnp.bfloat16)
            .reshape(sequence_permutation, local_length, width)
        )
        fresh = (
            grad_attn_gain,
            grad_query,
            grad_key,
            grad_value,
            grad_out,
            grad_mlp_gain,
            grad_gate,
            grad_up,
            grad_down,
            grad_qgain,
            grad_kgain,
        )
        if sums is None:
            sums = fresh
        else:
            sums = tuple((a + b for a, b in zip(sums, fresh)))
    attn_members = (sums[0], sums[1], sums[2], sums[3], sums[4])
    mlp_members = (sums[5], sums[6], sums[7], sums[8])
    attn_flat = lax.psum_scatter(
        pack_shares(attn_members, all_count), ("dp", "seq"), scatter_dimension=0, tiled=True
    )
    mlp_flat = lax.psum_scatter(
        pack_shares(mlp_members, all_count), ("dp", "seq"), scatter_dimension=0, tiled=True
    )
    attn_shares = unpack_shares(attn_flat, attn_members, all_count)
    mlp_shares = unpack_shares(mlp_flat, mlp_members, all_count)
    head_sums = lax.psum((sums[9], sums[10]), ("dp", "seq"))
    return (
        jnp.concatenate(outputs, axis=0),
        jnp.concatenate(input_grads, axis=0),
        attn_shares[0],
        attn_shares[1],
        attn_shares[2],
        attn_shares[3],
        head_sums[0],
        head_sums[1],
        attn_shares[4],
        mlp_shares[0],
        mlp_shares[1],
        mlp_shares[2],
        mlp_shares[3],
    )


BF = jnp.bfloat16
F32 = jnp.float32
MESH = pl.DeviceIdType.MESH
TOKENS = 1024
WIDTH = 1024
LOG2E = 1.4426950408889634
VM = pl.BlockSpec(memory_space=pltpu.VMEM)
SM = pl.BlockSpec(memory_space=pltpu.SMEM)
ANY = pl.BlockSpec(memory_space=pl.ANY)
VMEM_BYTES = 65100 * 1024


def place():
    q = lax.axis_index("dp")
    p = lax.axis_index("seq")
    return q, p, q // 2, lax.rem(q, 2), p // 2, lax.rem(p, 2)


def home_group(x, c, i):
    return 4 * c + 2 * i + (x if i == 0 else 1 - x)


def greet(peers):
    barrier = pltpu.get_barrier_semaphore()
    for peer in peers:
        pl.semaphore_signal(barrier, inc=1, device_id=peer, device_id_type=MESH)
    pl.semaphore_wait(barrier, len(peers))


def remote(src, dst, send, recv, peer):
    return pltpu.make_async_remote_copy(
        src_ref=src, dst_ref=dst, send_sem=send, recv_sem=recv, device_id=peer, device_id_type=MESH
    )


def dims(left, right, lc, rc):
    return lax.dot_general(left, right, (((lc,), (rc,)), ((), ())), preferred_element_type=F32)


def mod(a, n):
    return a % n


def unit(v):
    return lax.rsqrt(jnp.mean(v * v, axis=-1, keepdims=True) + EPS)


def pieces(ref, spots, which, first, count):
    return jnp.concatenate([ref[spots[which, first + t]] for t in range(count)], axis=0)


def turns(table):
    other = pltpu.roll(table, HEAD_SIZE // 2, 1)
    first = lax.broadcasted_iota(jnp.int32, table.shape, 1) < HEAD_SIZE // 2
    return jnp.where(first, table, other), jnp.where(first, -other, table)


def rotate(v, cosine, sine):
    return v * cosine + pltpu.roll(v, HEAD_SIZE // 2, 1) * sine


def rotate_back(v, cosine, sine):
    return v * cosine + pltpu.roll(v * sine, HEAD_SIZE // 2, 1)


def lower(s, fill):
    n = s.shape[0]
    i = lax.broadcasted_iota(jnp.int32, (n, n), 0)
    j = lax.broadcasted_iota(jnp.int32, (n, n), 1)
    width = s.shape[1]
    diag = jnp.where(j <= i, s[:, width - n :], fill)
    return diag if width == n else jnp.concatenate([s[:, : width - n], diag], axis=1)


class Sum:
    def __init__(self, part, total, l1, own, l2, sems, base):
        self.q, self.p, self.x, self.c, _, _ = place()
        self.part, self.total, self.l1, self.own, self.l2 = part, total, l1, own, l2
        self.sems, self.base = sems, base
        self.sib = (2 * self.x + 1 - self.c, self.p)
        self.opp = (2 * (1 - self.x) + self.c, self.p)

    def rows(self, n, c):
        return pl.ds(pl.multiple_of(n * 256 + c * 128, 128), 128)

    def copy(self, step, n):
        s, r = self.sems.at[self.base + 2 * step, n], self.sems.at[self.base + 2 * step + 1, n]
        if step == 0:
            return remote(self.part.at[self.rows(n, 1 - self.c)], self.l1.at[n], s, r, self.sib)
        if step == 1:
            return remote(self.own.at[n], self.l2.at[n], s, r, self.opp)
        mine = self.total_at(n, self.c)
        return remote(mine, mine, s, r, self.sib)

    def total_at(self, n, c):
        if len(self.total.shape) == 2:
            return self.total.at[self.rows(n, c)]
        return self.total.at[(2 * n + c) // 4, (2 * n + c) % 4]

    def beside(self, n):
        self.copy(0, n).start()

    def across(self, n):
        self.copy(0, n).wait_recv()
        mine = self.part[self.rows(n, self.c), :].astype(F32)
        self.own[n] = (mine + self.l1[n].astype(F32)).astype(BF)
        self.copy(1, n).start()

    def back(self, n):
        self.copy(1, n).wait_recv()
        total = self.total_at(n, self.c)
        total[...] = (self.own[n].astype(F32) + self.l2[n].astype(F32)).astype(BF).reshape(total.shape)
        self.copy(2, n).start()

    def ready(self, n):
        other = self.total_at(n, 1 - self.c)
        s, r = self.sems.at[self.base + 4, n], self.sems.at[self.base + 5, n]
        remote(other, other, s, r, self.sib).wait_recv()

    def close(self, *steps):
        @pl.loop(0, 4)
        def _(n):
            for step in steps:
                self.copy(step, n).wait_send()


LINES = 6
PIECES = ((0, None), (2, None), (1, 0), (1, 1), (1, 2), (1, 3), (3, None))


def block(ref, b):
    return ref.at[pl.ds(2 * b, 2)]


class Gather:
    def __init__(self, srcs, dsts, sems):
        self.q, self.p, self.x, self.c, self.z, self.y = place()
        self.tok, self.cot, self.pos, self.pq, self.pg, self.po, self.pd = srcs
        self.xf, self.cf, self.of, *self.w = dsts
        (self.loc, self.ts, self.tr, self.fs, self.fr, self.ps, self.pr,
         self.as_, self.ar, self.zs, self.zr, self.ys, self.yr, self.ls, self.lr) = sems
        q, p, x, c, z, y = self.q, self.p, self.x, self.c, self.z, self.y
        self.owner_x, self.owner_c = mod(y + z, 2), z // 2
        self.is_owner = jnp.logical_and(x == self.owner_x, c == self.owner_c)
        self.cross = jnp.logical_and(x != self.owner_x, c == self.owner_c)
        self.sib = (2 * x + 1 - c, p)
        self.opp = (2 * (1 - x) + c, p)

    def peers(self):
        q, p = self.q, self.p
        return [(mod(q + k, 4), p) for k in (1, 2, 3)] + [(q, mod(p + k, 8)) for k in range(1, 8)]

    def col(self, n):
        return (self.pq, self.pg)[n], self.w[n]

    def own_copy(self, n):
        q, p = self.q, self.p
        if n < 2:
            src, dst = self.col(n)
            return pltpu.make_async_copy(src.at[q], dst.at[q, p], self.loc.at[n])
        return pltpu.make_async_copy((self.po, self.pd)[n - 2], self.w[n].at[p], self.loc.at[n])

    def column_copy(self, n, k):
        q, p = self.q, self.p
        src, dst = self.col(n)
        t = mod(q + k, 4)
        return remote(src.at[t], dst.at[q, p], self.as_.at[n, k - 1], self.ar.at[n, k - 1], (t, p))

    def column_start(self, n):
        for k in (1, 2, 3):
            self.column_copy(n, k).start()

    def column_wait(self, n):
        q, p = self.q, self.p
        src, dst = self.col(n)
        for k in (1, 2, 3):
            f = mod(q + 4 - k, 4)
            remote(src.at[0], dst.at[f, p], self.as_.at[n, k - 1], self.ar.at[n, k - 1], (q, p)).wait_recv()

    def view(self, piece, chunk):
        n, part = PIECES[piece]
        if n >= 2:
            return self.w[n].at[chunk]
        return self.w[n].at[:, chunk] if part is None else self.w[n].at[part, chunk]

    def z_copy(self, piece, src, way):
        v = self.view(piece, 2 * src + self.y)
        s = self.zs.at[piece, src + (4 if way < 0 else 0)]
        return remote(v, v, s, self.zr.at[piece, src], (self.q, 2 * (self.z + way) + self.y))

    def y_copy(self, piece, src):
        v = self.view(piece, 2 * src + self.y)
        return remote(v, v, self.ys.at[piece, src], self.yr.at[piece, src], (self.q, 2 * self.z + 1 - self.y))

    def spread(self, piece, src, up, down):
        if up:

            @pl.when(self.z < 3)
            def _():
                self.z_copy(piece, src, 1).start()

        if down:

            @pl.when(self.z > 0)
            def _():
                self.z_copy(piece, src, -1).start()

        self.y_copy(piece, src).start()

    def begin(self, *pieces_):
        for piece in pieces_:
            self.spread(piece, self.z, True, True)

    def line_copy(self, line, src, way):
        v = self.view(LINES, 2 * src + line)
        s = self.ls.at[line, src + (4 if way < 0 else 0)]
        return remote(v, v, s, self.lr.at[line, src], (self.q, 2 * (self.z + way) + self.y))

    def line_spread(self, line, src, up, down):
        if up:

            @pl.when(self.z < 3)
            def _():
                self.line_copy(line, src, 1).start()

        if down:

            @pl.when(self.z > 0)
            def _():
                self.line_copy(line, src, -1).start()

    def lines_begin(self):
        self.y_copy(LINES, self.z).start()
        self.line_spread(self.y, self.z, True, True)

    def lines_turn(self):
        v = self.view(LINES, 2 * self.z + 1 - self.y)
        remote(v, v, self.ys.at[LINES, self.z], self.yr.at[LINES, self.z], (self.q, self.p)).wait_recv()
        self.line_spread(1 - self.y, self.z, True, True)

    def line_step(self, other, dist):
        line = 1 - self.y if other else self.y
        low, high = self.z - dist, self.z + dist

        @pl.when(low >= 0)
        def _():
            v = self.view(LINES, 2 * low + line)
            remote(v, v, self.ls.at[line, 0], self.lr.at[line, low], (self.q, self.p)).wait_recv()
            self.line_spread(line, low, True, False)

        @pl.when(high < 4)
        def _():
            v = self.view(LINES, 2 * high + line)
            remote(v, v, self.ls.at[line, 0], self.lr.at[line, high], (self.q, self.p)).wait_recv()
            self.line_spread(line, high, False, True)

    def step(self, piece, dist):
        low, high = self.z - dist, self.z + dist

        @pl.when(low >= 0)
        def _():
            v = self.view(piece, 2 * low + self.y)
            remote(v, v, self.zs.at[piece, 0], self.zr.at[piece, low], (self.q, self.p)).wait_recv()
            self.spread(piece, low, True, False)

        @pl.when(high < 4)
        def _():
            v = self.view(piece, 2 * high + self.y)
            remote(v, v, self.zs.at[piece, 0], self.zr.at[piece, high], (self.q, self.p)).wait_recv()
            self.spread(piece, high, False, True)

    def steps(self, *pieces_):
        for piece in pieces_:
            for dist in (1, 2, 3):
                self.step(piece, dist)

    def y_wait(self, *pieces_):
        for piece in pieces_:
            for src in range(4):
                v = self.view(piece, 2 * src + 1 - self.y)
                remote(v, v, self.ys.at[piece, src], self.yr.at[piece, src], (self.q, self.p)).wait_recv()

    def tok_dst(self, a):
        return (self.xf, self.cf)[a]

    def token_copy(self, a, i):
        src, dst = (self.tok, self.cot)[a], self.tok_dst(a)
        goal = home_group(self.x, self.c, i)
        return goal, remote(src.at[i], block(dst, self.p), self.ts.at[a, i], self.tr.at[a, self.p], (self.q, goal))

    def token_local(self, a, i):
        return pltpu.make_async_copy((self.tok, self.cot)[a].at[i], block(self.tok_dst(a), self.p), self.loc.at[4 + a])

    def token_start(self, a):
        for i in range(2):
            goal, cp = self.token_copy(a, i)

            @pl.when(goal != self.p)
            def _():
                cp.start()

            @pl.when(goal == self.p)
            def _():
                self.token_local(a, i).start()

    def token_pass(self, a, first=0, end=8):
        dst = self.tok_dst(a)
        q, p = self.q, self.p

        @pl.when(self.is_owner)
        def _():
            @pl.loop(first, end)
            def _(b):
                @pl.when(b != p)
                def _():
                    remote(block(dst, b), block(dst, b), self.ts.at[a, 0], self.tr.at[a, b], (q, p)).wait_recv()

                @pl.when(b == p)
                def _():
                    self.token_local(a, 0).wait()

                remote(block(dst, b), block(dst, b), self.fs.at[a, 0, b], self.fr.at[a, b], self.sib).start()
                remote(block(dst, b), block(dst, b), self.fs.at[a, 1, b], self.fr.at[a, b], self.opp).start()

        @pl.when(jnp.logical_not(self.is_owner))
        def _():
            @pl.loop(first, end)
            def _(b):
                remote(block(dst, b), block(dst, b), self.fs.at[a, 0, b], self.fr.at[a, b], self.sib).wait_recv()

                @pl.when(self.cross)
                def _():
                    remote(block(dst, b), block(dst, b), self.fs.at[a, 0, b], self.fr.at[a, b], self.sib).start()

    def token_close(self, a):
        dst = self.tok_dst(a)
        q, p = self.q, self.p
        for i in range(2):
            goal, cp = self.token_copy(a, i)

            @pl.when(goal != p)
            def _():
                cp.wait_send()

        @pl.when(self.is_owner)
        def _():
            @pl.loop(0, 8)
            def _(b):
                remote(block(dst, b), block(dst, b), self.fs.at[a, 0, b], self.fr.at[a, b], (q, p)).wait_send()
                remote(block(dst, b), block(dst, b), self.fs.at[a, 1, b], self.fr.at[a, b], (q, p)).wait_send()

        @pl.when(self.cross)
        def _():
            @pl.loop(0, 8)
            def _(b):
                remote(block(dst, b), block(dst, b), self.fs.at[a, 0, b], self.fr.at[a, b], (q, p)).wait_send()

    def pos_copy(self, k):
        return remote(self.pos, self.of, self.ps.at[k], self.pr.at[0], (mod(self.q + k + 1, 4), self.p))

    def pos_start(self):
        @pl.when(self.is_owner)
        def _():
            pltpu.make_async_copy(self.pos, self.of, self.loc.at[6]).start()
            for k in range(3):
                self.pos_copy(k).start()

    def pos_finish(self):
        @pl.when(self.is_owner)
        def _():
            pltpu.make_async_copy(self.pos, self.of, self.loc.at[6]).wait()
            for k in range(3):
                self.pos_copy(k).wait_send()

        @pl.when(jnp.logical_not(self.is_owner))
        def _():
            self.pos_copy(0).wait_recv()

    def close(self):
        for n in range(2):
            for k in (1, 2, 3):
                self.column_copy(n, k).wait_send()
        self.y_copy(LINES, self.z).wait_send()
        for line in range(2):
            for src in range(4):

                @pl.when(jnp.logical_and(self.z < 3, src <= self.z))
                def _():
                    self.line_copy(line, src, 1).wait_send()

                @pl.when(jnp.logical_and(self.z > 0, src >= self.z))
                def _():
                    self.line_copy(line, src, -1).wait_send()

        for piece in range(LINES):
            for src in range(4):
                self.y_copy(piece, src).wait_send()

                @pl.when(jnp.logical_and(self.z < 3, src <= self.z))
                def _():
                    self.z_copy(piece, src, 1).wait_send()

                @pl.when(jnp.logical_and(self.z > 0, src >= self.z))
                def _():
                    self.z_copy(piece, src, -1).wait_send()

        self.token_close(0)
        self.token_close(1)


GATHER_SEMS = ((7,), (2, 2), (2, 8), (2, 2, 8), (2, 8), (3,), (1,), (2, 3), (2, 3), (7, 8), (7, 4), (7, 4), (7, 4), (2, 8), (2, 4))


class Home:
    def __init__(self, part, out, l1, own, l2, sems, here, base):
        self.q, self.p, self.x, self.c, self.z, self.y = place()
        self.part, self.out, self.l1, self.own, self.l2 = part, out, l1, own, l2
        self.sems, self.here, self.base = sems, here, base
        self.owner_x, self.owner_c = mod(self.y + self.z, 2), self.z // 2
        self.keeps = self.x == self.owner_x
        self.sib = (2 * self.x + 1 - self.c, self.p)
        self.opp = (2 * (1 - self.x) + self.c, self.p)
        self.goal_q = 2 * self.owner_x + self.owner_c

    def rows(self, n, c):
        return pl.ds(pl.multiple_of(n * 256 + c * 128, 128), 128)

    def sem(self, k, n):
        return self.sems.at[self.base + k, n]

    def first(self, n):
        return remote(
            self.part.at[self.rows(n, 1 - self.c)], self.l1.at[n], self.sem(0, n), self.sem(1, n), self.sib
        )

    def second(self, n):
        return remote(self.own.at[n], self.l2.at[n], self.sem(2, n), self.sem(3, n), self.opp)

    def third(self, n):
        slot = mod(self.z, 2)
        return remote(
            self.own.at[n], self.out.at[slot], self.sem(4, n), self.sem(5, slot), (self.goal_q, 2 * n + self.c)
        )

    def is_self(self, n):
        return jnp.logical_and(self.goal_q == self.q, 2 * n + self.c == self.p)

    def beside(self, n):
        self.first(n).start()

    def across(self, n):
        self.first(n).wait_recv()
        mine = self.part[self.rows(n, self.c), :].astype(F32)
        self.own[n] = (mine + self.l1[n].astype(F32)).astype(BF)

        @pl.when(jnp.logical_not(self.keeps))
        def _():
            self.second(n).start()

    def finish(self, n, rest):
        @pl.when(self.keeps)
        def _():
            self.second(n).wait_recv()
            s = self.own[n].astype(F32) + self.l2[n].astype(F32)
            self.own[n] = rest(n, s).astype(BF)

            @pl.when(jnp.logical_not(self.is_self(n)))
            def _():
                self.third(n).start()

            @pl.when(self.is_self(n))
            def _():
                cp = pltpu.make_async_copy(self.own.at[n], self.out.at[mod(self.z, 2)], self.here)
                cp.start()
                cp.wait()

    def close(self):
        for i in range(2):
            group = home_group(self.x, self.c, i)
            same = jnp.logical_and(group == self.p, self.y == self.c)

            @pl.when(jnp.logical_not(same))
            def _():
                remote(self.own.at[0], self.out.at[i], self.sem(4, 0), self.sem(5, i), (self.q, self.p)).wait_recv()

        for n in range(4):
            self.first(n).wait_send()

            @pl.when(jnp.logical_not(self.keeps))
            def _():
                self.second(n).wait_send()

            @pl.when(jnp.logical_and(self.keeps, jnp.logical_not(self.is_self(n))))
            def _():
                self.third(n).wait_send()


class Scatter:
    def __init__(self, g, ly, lz, sems, base):
        self.q, self.p, _, _, self.z, self.y = place()
        self.g, self.ly, self.lz, self.sems, self.base = g, ly, lz, sems, base

    def y_copy(self, n):
        s, r = self.sems.at[self.base + n, 0], self.sems.at[self.base + n, 1]
        return remote(self.g.at[1 - self.y, n], self.ly(n), s, r, (self.q, 2 * self.z + 1 - self.y))

    def z_copy(self, n, k):
        t = mod(self.z + k, 4)
        s, r = self.sems.at[self.base + n, 2 * k], self.sems.at[self.base + n, 2 * k + 1]
        return remote(self.ly(n).at[t], self.lz(n).at[k - 1], s, r, (self.q, 2 * t + self.y))

    def y_send(self, n):
        self.y_copy(n).start()

    def z_step(self, n):
        self.y_copy(n).wait_recv()
        ly = self.ly(n)

        @pl.loop(0, 4)
        def _(t):
            ly[t] = (ly[t].astype(F32) + self.g[self.y, n, t].astype(F32)).astype(BF)

        for k in (1, 2, 3):
            self.z_copy(n, k).start()

    def z_sum(self, n):
        for k in (1, 2, 3):
            self.z_copy(n, k).wait_recv()
        ly, lz = self.ly(n), self.lz(n)
        return ly[self.z].astype(F32) + lz[0].astype(F32) + lz[1].astype(F32) + lz[2].astype(F32)

    def close(self, count):
        @pl.loop(0, count)
        def _(n):
            self.y_copy(n).wait_send()
            for k in (1, 2, 3):
                self.z_copy(n, k).wait_send()


class Columns:
    def __init__(self, scatter, land, sems, base):
        self.scatter, self.land = scatter, land
        self.sems, self.base = sems, base
        self.q, self.p = scatter.q, scatter.p

    def copy(self, t):
        s, r = self.sems.at[self.base, t], self.sems.at[self.base + 1, self.q]
        return remote(self.scatter.ly(t).at[self.scatter.z], self.land.at[self.q], s, r, (t, self.p))

    def step(self, t):
        s = self.scatter.z_sum(t).astype(BF)

        @pl.when(t != self.q)
        def _():
            ly = self.scatter.ly(t)
            ly[self.scatter.z] = s
            self.copy(t).start()

        @pl.when(t == self.q)
        def _():
            self.land[t] = s

    def close(self):
        for t in range(4):

            @pl.when(t != self.q)
            def _():
                r = self.sems.at[self.base + 1, t]
                remote(self.land.at[t], self.land.at[t], self.sems.at[self.base, t], r, (self.q, self.p)).wait_recv()
                self.copy(t).wait_send()


def column(table, h):
    lane = lax.broadcasted_iota(jnp.int32, table.shape, 1)
    return jnp.sum(jnp.where(lane == h, table, 0.0), axis=1, keepdims=True)


def layer_kernel(
    tok, cot, pos, pq, pg, po, pd, table, qg, kg,
    out, igrad, od, ogu, oo, oqkv, oheads, of,
    xf, cf, wq, wg, wo, wd, raw_o, qb, kb, vb, ob, lse, hidden, rest, cs, pa, pb, pc, mb, dgu, gd, ggu,
    dkv, go, gqkv, yo, yqkv, zo, zqkv, heads, hy, hz, hdp,
    l1, own, l2, l1b, ownb, l2b, l2c, sorts, sorts_sem, free, sums, gsem, csem, hs, hr, homes, here, *sems,
):
    q, p, x_, c, z, y = place()
    sd = Scatter(gd, lambda n: wd.at[pl.ds(0, 4)], lambda n: wd.at[pl.ds(4, 3)], gsem, 0)
    sgu = Scatter(ggu, lambda n: wg.at[n, pl.ds(0, 4)], lambda n: wg.at[n, pl.ds(4, 3)], gsem, 1)
    so = Scatter(go, lambda n: yo.at[n], lambda n: zo.at[n], gsem, 5)
    sqkv = Scatter(gqkv, lambda n: yqkv.at[n], lambda n: zqkv.at[n], gsem, 6)
    cgu = Columns(sgu, ogu, csem, 0)
    cqkv = Columns(sqkv, oqkv, csem, 2)
    h_out = Home(pb, out, l1, own, l2, homes, here.at[0], 0)
    h_in = Home(pc, igrad, l1b, ownb, l2c, homes, here.at[1], 6)
    order = [(sd, 0)] + [(sgu, n) for n in range(4)] + [(so, 0)] + [(sqkv, n) for n in range(4)]

    def y_send(j):
        which, n = order[j]
        which.y_send(n)

    def step(j):
        which, n = order[j]
        which.z_step(n)
        if j + 2 < len(order):
            y_send(j + 2)

    g = Gather((tok, cot, pos, pq, pg, po, pd), (xf, cf, of, wq, wg, wo, wd), sems)
    peers = [(2 * x_ + cc, mod(p + k, 8)) for k in range(1, 8) for cc in (0, 1)]
    peers += [(mod(q + k, 4), p) for k in (1, 2, 3)]
    greet(peers)
    g.pos_start()
    g.token_start(0)
    g.column_start(0)
    for n in range(4):
        g.own_copy(n).start()
    g.column_start(1)
    g.own_copy(0).wait()
    g.column_wait(0)
    g.begin(0)
    g.pos_finish()
    sort = pltpu.make_async_copy(of, sorts, sorts_sem.at[0])
    sort.start()
    lse[...] = jnp.zeros_like(lse)
    g.step(0, 1)
    g.token_pass(0, 0, 2)
    g.step(0, 2)
    g.token_pass(0, 2, 4)
    g.token_start(1)
    g.step(0, 3)
    g.token_pass(0, 4, 8)
    g.own_copy(2).wait()
    g.begin(1)
    g.own_copy(1).wait()
    g.column_wait(1)
    g.begin(2)
    g.own_copy(3).wait()
    sort.wait()
    g.y_wait(0)

    @pl.loop(0, 4)
    def _(n):
        rows = pl.ds(pl.multiple_of(n * 256, 256), 256)
        v = pieces(xf, sorts, 1, n * 4, 4).astype(F32)
        h = (v * unit(v)).astype(BF)

        @pl.when(n == 2)
        def _():
            g.token_pass(1, 0, 3)
            g.begin(3)

        raw = jnp.dot(h, wq[...].reshape(WIDTH, WIDTH), preferred_element_type=F32)
        raw_o[rows, :] = raw[:, :768]
        cosine, sine = turns(table[rows, :])
        for t in range(2):
            vb[t, rows, :] = raw[:, 768 + t * 128 : 896 + t * 128].astype(BF)
        for t in range(6):
            u = raw[:, t * 128 : (t + 1) * 128]
            n_ = u * unit(u) * (qg[...] if t < 4 else kg[...])
            r = rotate(n_, cosine, sine).astype(BF)
            if t < 4:
                qb[t, rows, :] = r
            else:
                kb[t - 4, rows, :] = r

    @pl.loop(0, 4)
    def _(h):
        @pl.when(h == 0)
        def _():
            g.step(1, 1)
            g.token_pass(1, 3, 6)

        @pl.when(h == 1)
        def _():
            g.step(1, 2)
            g.token_pass(1, 6, 8)
            g.begin(4)

        @pl.when(h == 2)
        def _():
            g.step(1, 3)
            g.step(2, 1)
            g.begin(5)

        @pl.when(h == 3)
        def _():
            g.step(2, 2)
            g.step(2, 3)
            g.lines_begin()

        kv = h // 2
        for i in range(4):
            length = (i + 1) * 256
            rows = slice(i * 256, length)
            s = dims(qb[h, rows, :], kb[kv, :length, :], 1, 1) * (HEAD_SIZE**-0.5 * LOG2E)
            s = lower(s, NEGATIVE_FILL)
            top = jnp.max(s, axis=-1, keepdims=True)
            e = jnp.exp2(s - top)
            sum_e = jnp.sum(e, axis=-1, keepdims=True)
            o = jnp.dot(e.astype(BF), vb[kv, :length, :], preferred_element_type=F32) / sum_e
            ob[rows, pl.ds(pl.multiple_of(h * 128, 128), 128)] = o.astype(BF)
            lane = lax.broadcasted_iota(jnp.int32, (256, 128), 1)
            lse[rows, :] = jnp.where(lane == h, top + jnp.log2(sum_e), lse[rows, :])

    g.y_wait(1)
    s1 = Sum(pa, pb, l1, own, l2, sums, 0)
    s2 = Sum(pc, gqkv, l1b, ownb, l2b, sums, 6)

    @pl.loop(0, 4)
    def _(n):
        rows = pl.ds(pl.multiple_of(n * 256, 256), 256)
        out_w = wo[...].reshape(512, WIDTH)
        pa[rows, :] = jnp.dot(ob[rows, :], out_w, preferred_element_type=F32).astype(BF)
        s1.beside(n)

        @pl.when(n > 0)
        def _():
            s1.across(n - 1)

    s1.across(3)
    g.step(3, 1)
    g.step(3, 2)
    s1.back(0)
    g.step(3, 3)
    g.step(4, 1)
    s1.back(1)
    g.lines_turn()
    g.step(4, 2)
    g.step(4, 3)
    s1.back(2)
    g.step(5, 1)
    g.line_step(False, 1)
    g.step(5, 2)
    g.line_step(True, 1)
    s1.back(3)
    g.step(5, 3)
    g.line_step(False, 2)
    g.line_step(True, 2)
    g.line_step(False, 3)
    g.line_step(True, 3)
    g.y_wait(2, 3, 4, 5)
    s1.close(0)

    @pl.loop(0, 4)
    def _(n):
        s1.ready(n)
        rows = pl.ds(pl.multiple_of(n * 256, 256), 256)
        h = pieces(xf, sorts, 1, n * 4, 4).astype(F32) + pb[rows, :].astype(F32)
        hidden[pl.ds(n * 4, 4)] = h.reshape(4, BLK, WIDTH)
        a = (h * unit(h)).astype(BF)
        pa[rows, :] = a
        wgu = wg[...].reshape(WIDTH, 1536)
        gu = jnp.dot(a, wgu, preferred_element_type=F32)
        gate = gu[:, :768]
        up = gu[:, 768:]
        sig = 1.0 / (1.0 + jnp.exp2(gate * -LOG2E))
        silu = gate * sig
        mb[pl.ds(n * 4, 4)] = (silu * up).astype(BF).reshape(4, BLK, 768)
        cc = pieces(cf, sorts, 1, n * 4, 4)
        cs[rows, :] = cc
        dm = dims(cc, wd[...].reshape(768, WIDTH), 1, 1)
        dg = (dm * up * sig * (1.0 + gate * (1.0 - sig))).astype(BF)
        du = (dm * silu).astype(BF)
        both = jnp.concatenate([dg, du], axis=1)
        dgu[rows, :] = both
        pc[rows, :] = dims(both, wgu, 1, 1).astype(BF)
        s2.beside(n)

        @pl.when(n > 0)
        def _():
            s2.across(n - 1)

    s2.across(3)
    s1.close(1, 2)

    @pl.loop(0, 2)
    def _(n):
        m_all = mb[...].reshape(TOKENS, 768)
        for t in range(2):

            @pl.when(n == t)
            def _():
                v = dims(m_all[:, t * 384 : (t + 1) * 384], cs[...], 0, 0).astype(BF)
                v = v.reshape(2, 2, 96, WIDTH)
                for u in range(2):
                    gd[u, 0, 2 * t : 2 * t + 2] = v[:, u]

    @pl.loop(0, 4)
    def _(n):
        rows = pl.ds(pl.multiple_of(n * 256, 256), 256)
        m = pieces(mb, sorts, 0, n * 4, 4)
        pb[rows, :] = jnp.dot(m, wd[...].reshape(768, WIDTH), preferred_element_type=F32).astype(BF)
        rest[n] = pieces(hidden, sorts, 0, 4 * n + 2 * g.c, 2)

    g.close()
    near = [(q, 2 * z + 1 - y), (2 * x_ + 1 - c, p), (2 * (1 - x_) + c, p)]
    near += [(q, 2 * mod(z + k, 4) + y) for k in (1, 2, 3)]
    for peer in near:
        pl.semaphore_signal(free, inc=1, device_id=peer, device_id_type=MESH)
    s2.back(0)

    s2.back(1)
    pl.semaphore_wait(free, len(near))
    y_send(0)
    for n in range(4):
        h_out.beside(n)

    @pl.loop(0, 4)
    def _(n):
        v = dims(pa[:, pl.ds(pl.multiple_of(n * 256, 256), 256)], dgu[...], 0, 0).astype(BF)
        v = v.reshape(4, 2, 32, 1536)
        for t in range(2):
            ggu[t, n] = v[:, t]

        @pl.when(n == 0)
        def _():
            y_send(1)

        @pl.when(n < 2)
        def _():
            s2.back(n + 2)

    @pl.loop(0, 4)
    def _(n):
        rows = pl.ds(pl.multiple_of(n * 256, 256), 256)
        h = hidden[pl.ds(n * 4, 4)].reshape(256, WIDTH)
        r = unit(h)
        s2.ready(n)
        da = gqkv[n // 2, pl.ds(2 * (n % 2), 2)].reshape(256, WIDTH).astype(F32)
        back = r * da - h * (r * r * r * jnp.mean(h * da, axis=-1, keepdims=True))
        d = cs[rows, :].astype(F32) + back
        hidden[pl.ds(n * 4, 4)] = d.reshape(4, BLK, WIDTH)
        low = d.astype(BF)
        pa[rows, :] = low
        do = dims(low, wo[...].reshape(512, WIDTH), 1, 1).astype(BF)
        cs[rows, :512] = do
        h_out.across(n)

    @pl.loop(0, 2)
    def _(n):
        v = dims(ob[:, pl.ds(pl.multiple_of(n * 256, 256), 256)], pa[...], 0, 0).astype(BF)
        v = v.reshape(2, 2, 64, WIDTH)
        for t in range(2):
            go[t, 0, pl.ds(n * 2, 2)] = v[:, t]

    s2.close(0, 1, 2)
    heads[...] = jnp.zeros_like(heads)
    scale = HEAD_SIZE**-0.5

    def norm_back(dn, u, gain, rows):
        dn = rotate_back(dn, *turns(table[rows, :]))
        r = unit(u)
        gd_ = gain * dn
        du = r * gd_ - u * (r * r * r * jnp.mean(u * gd_, axis=-1, keepdims=True))
        return du.astype(BF), jnp.sum(dn * u * r, axis=0, keepdims=True)

    def result(n, s):
        return s + rest[n]

    def inward(n, s):
        v = xf[pl.ds(4 * n + 2 * c, 2)].reshape(128, WIDTH).astype(F32)
        r = unit(v)
        s = r * s - v * (r * r * r * jnp.mean(v * s, axis=-1, keepdims=True))
        return s + pieces(hidden, sorts, 0, 4 * n + 2 * c, 2)

    @pl.loop(0, 2)
    def _(g):
        dkv[...] = jnp.zeros_like(dkv)
        for t in range(2):
            if t == 0:

                @pl.when(g == 1)
                def _():
                    step(1)
            else:
                for turn in range(2):

                    @pl.when(g == turn)
                    def _():
                        step(2 * turn)
                        if turn == 1:
                            h_out.finish(0, result)
                            h_out.finish(1, result)

            h = g * 2 + t
            lanes = pl.ds(pl.multiple_of(h * 128, 128), 128)
            for i in range(4):
                length = (i + 1) * 256
                rows = slice(i * 256, length)
                qv = qb[h, rows, :]
                kv = kb[g, :length, :]
                dov = cs[rows, lanes]
                s = dims(qv, kv, 1, 1) * (scale * LOG2E)
                pr = lower(jnp.exp2(s - column(lse[rows, :], h)), 0.0)
                dp = dims(dov, vb[g, :length, :], 1, 1)
                delta = jnp.sum(dov.astype(F32) * ob[rows, lanes].astype(F32), axis=-1, keepdims=True)
                ds_ = lower(pr * (dp - delta), 0.0).astype(BF)
                dq = jnp.dot(ds_, kv, preferred_element_type=F32) * scale
                dkv[0, :length, :] += dims(ds_, qv, 0, 0)
                dkv[1, :length, :] += dims(pr.astype(BF), dov, 0, 0)
                du, dgain = norm_back(dq, raw_o[rows, lanes], qg[...], pl.ds(i * 256, 256))
                cf[i * 4 : i * 4 + 4, :, lanes] = du.reshape(4, BLK, 128)
                heads[0:1, :] += dgain
        lanes = pl.ds(pl.multiple_of(512 + g * 128, 128), 128)
        for i in range(4):
            rows = slice(i * 256, (i + 1) * 256)
            du, dgain = norm_back(dkv[0, rows, :] * scale, raw_o[rows, lanes], kg[...], pl.ds(i * 256, 256))
            cf[i * 4 : i * 4 + 4, :, lanes] = du.reshape(4, BLK, 128)
            heads[1:2, :] += dgain
        cf[:, :, pl.ds(pl.multiple_of(768 + g * 128, 128), 128)] = dkv[1].astype(BF).reshape(16, BLK, 128)

    step(3)
    h_out.finish(2, result)
    h_out.finish(3, result)
    hy_copy = remote(heads, hy, hs.at[0], hr.at[0], (q, 2 * z + 1 - y))
    hy_copy.start()

    @pl.loop(0, 4)
    def _(n):
        rows = pl.ds(pl.multiple_of(n * 256, 256), 256)
        d = pieces(cf, sorts, 0, n * 4, 4)
        pc[rows, :] = dims(d, wq[...].reshape(WIDTH, WIDTH), 1, 1).astype(BF)
        h_in.beside(n)

        @pl.when(n > 0)
        def _():
            h_in.across(n - 1)

    h_in.across(3)

    @pl.loop(0, 4)
    def _(n):
        rows = pl.ds(pl.multiple_of(n * 256, 256), 256)
        v = pieces(xf, sorts, 1, n * 4, 4).astype(F32)
        pa[rows, :] = (v * unit(v)).astype(BF)

    @pl.loop(0, 4)
    def _(n):
        v = dims(pa[:, pl.ds(pl.multiple_of(n * 256, 256), 256)], cf[...].reshape(TOKENS, WIDTH), 0, 0).astype(BF)
        v = v.reshape(4, 2, 32, WIDTH)
        for t in range(2):
            gqkv[t, n] = v[:, t]

    step(4)

    def z_heads(k):
        return remote(hz.at[z], hz.at[z], hs.at[k], hr.at[k], (q, 2 * mod(z + k, 4) + y))

    def dp_heads(k):
        return remote(hdp.at[q], hdp.at[q], hs.at[3 + k], hr.at[3 + k], (mod(q + k, 4), p))

    hy_copy.wait_recv()
    hz[z] = heads[...] + hy[...]
    for k in (1, 2, 3):
        z_heads(k).start()
    h_in.finish(0, inward)
    od[...] = sd.z_sum(0)
    for n in range(4):
        step(5 + n)
        cgu.step(n)
        if n < 3:
            h_in.finish(n + 1, inward)
    step(9)
    for k in (1, 2, 3):
        f = mod(z + 4 - k, 4)
        remote(hz.at[f], hz.at[f], hs.at[k], hr.at[k], (q, p)).wait_recv()
    hdp[q] = hz[0] + hz[1] + hz[2] + hz[3]
    for k in (1, 2, 3):
        dp_heads(k).start()
    oo[...] = so.z_sum(0)

    @pl.loop(0, 4)
    def _(n):
        cqkv.step(n)

    cgu.close()
    for k in (1, 2, 3):
        f = mod(q + 4 - k, 4)
        remote(hdp.at[f], hdp.at[f], hs.at[3 + k], hr.at[3 + k], (q, p)).wait_recv()
    oheads[...] = hdp[0] + hdp[1] + hdp[2] + hdp[3]
    cqkv.close()
    h_out.close()
    h_in.close()
    sd.close(1)
    sgu.close(4)
    so.close(1)
    sqkv.close(4)
    hy_copy.wait_send()
    for k in (1, 2, 3):
        z_heads(k).wait_send()
        dp_heads(k).wait_send()


def layer_call(tok, cot, pos, pq, pg, po, pd, table, qg, kg):
    sem = pltpu.SemaphoreType.DMA
    shape = jax.ShapeDtypeStruct
    vm = pltpu.VMEM
    full = (TOKENS, WIDTH)
    return pl.pallas_call(
        layer_kernel,
        out_shape=(
            shape((2, 128, WIDTH), BF),
            shape((2, 128, WIDTH), BF),
            shape((96, WIDTH), F32),
            shape((4, 32, 1536), BF),
            shape((64, WIDTH), F32),
            shape((4, 32, WIDTH), BF),
            shape((8, 128), F32),
            shape((8, 128), jnp.int32),
        ),
        in_specs=[ANY] * 7 + [VM] * 3,
        out_specs=(ANY, ANY) + (VM,) * 5 + (ANY,),
        scratch_shapes=[
            vm((16, BLK, WIDTH), BF), vm((16, BLK, WIDTH), BF),
            vm((4, 8) + pq.shape[1:], BF), vm((4, 8) + pg.shape[1:], BF),
            vm((8,) + po.shape, BF), vm((8,) + pd.shape, BF),
            vm((TOKENS, 768), F32),
            vm((4, TOKENS, 128), BF), vm((2, TOKENS, 128), BF), vm((2, TOKENS, 128), BF), vm((TOKENS, 512), BF),
            vm((TOKENS, 128), F32), vm((16, BLK, WIDTH), F32), vm((4, 128, WIDTH), F32),
            vm(full, BF), vm(full, BF), vm(full, BF), vm(full, BF),
            vm((16, BLK, 768), BF), vm((TOKENS, 1536), BF),
            vm((2, 1, 4, 96, WIDTH), BF), vm((2, 4, 4, 32, 1536), BF),
            vm((2, TOKENS, 128), F32),
            vm((2, 1, 4, 64, WIDTH), BF), vm((2, 4, 4, 32, WIDTH), BF),
            vm((1, 4, 64, WIDTH), BF), vm((4, 4, 32, WIDTH), BF),
            vm((1, 3, 64, WIDTH), BF), vm((4, 3, 32, WIDTH), BF),
            vm((8, 128), F32), vm((8, 128), F32), vm((4, 8, 128), F32), vm((4, 8, 128), F32),
        ]
        + [vm((4, 128, WIDTH), BF)] * 7
        + [
            pltpu.SMEM((8, 128), jnp.int32), sem((1,)), pltpu.SemaphoreType.REGULAR, sem((12, 4)),
            sem((10, 8)), sem((4, 4)), sem((7,)), sem((7,)), sem((12, 4)), sem((2,)),
        ]
        + [sem(n) for n in GATHER_SEMS],
        compiler_params=pltpu.CompilerParams(
            collective_id=0, has_side_effects=True, vmem_limit_bytes=VMEM_BYTES
        ),
        name="layer_both_ways",
    )(tok, cot, pos, pq, pg, po, pd, table, qg, kg)


def quarter_columns(w, gain):
    rows, cols = w.shape
    v = w if gain is None else (w.astype(F32) * gain).astype(BF)
    return jnp.transpose(v.reshape(rows, 4, cols // 4), (1, 0, 2))


def whole_sequences(
    tokens, attn_gain, w_query, key_projection, value_projection, query_head_gain, key_gain, w_out,
    mlp_gain, w_gate, w_up, w_down, cotangent, span_order,
):
    p = lax.axis_index("seq")
    ga = attn_gain.astype(F32)[:, None]
    gm = mlp_gain.astype(F32)[:, None]
    pq = jnp.concatenate(
        [quarter_columns(w, ga) for w in (w_query, key_projection, value_projection)], axis=2
    )
    pg = jnp.concatenate([quarter_columns(w, gm) for w in (w_gate, w_up)], axis=2)
    row = jnp.where(lax.rem(p // 2, 2) == 0, span_order[0], span_order[1])
    spots = lax.iota(jnp.int32, 16)
    inverse = jnp.sum(jnp.where(row[None, :] == spots[:, None], spots[None, :], 0), axis=1)
    pos = jnp.zeros((8, 128), jnp.int32)
    pos = pos.at[0, :16].set(row).at[1, :16].set(inverse)
    freqs = BASE ** (-np.arange(HEAD_SIZE // 2) * 2.0 / HEAD_SIZE)
    angles = np.arange(TOKENS)[:, None] * freqs.astype(np.float32)[None, :].astype(np.float64)
    table = np.concatenate([np.cos(angles), np.sin(angles)], axis=1).astype(np.float32)
    qg = query_head_gain.astype(F32)[None, :]
    kg = key_gain.astype(F32)[None, :]
    out, igrad, od, ogu, oo, oqkv, oheads, _ = layer_call(
        tokens.reshape(2, 2, BLK, WIDTH), cotangent.reshape(2, 2, BLK, WIDTH), pos, pq, pg, w_out, w_down,
        table, qg, kg,
    )
    return finish(
        out, igrad, od, ogu, oo, oqkv, oheads, attn_gain[None, :], mlp_gain[None, :], w_query, key_projection, value_projection, w_gate, w_up
    )


def finish_kernel(
    out_i, igrad_i, od_i, ogu, oo_i, oqkv, oheads, ga, gm, w_query, key_projection, value_projection, w_gate, w_up,
    out, igrad, attn, query, key, value, qgain, kgain, oo, mlp, gate, up, od,
):
    out[...] = out_i[...]
    igrad[...] = igrad_i[...]
    od[...] = od_i[...]
    oo[...] = oo_i[...]
    qgain[...] = oheads[0:1, :]
    kgain[...] = oheads[1:2, :]
    eye = lax.broadcasted_iota(jnp.int32, (32, 32), 0) == lax.broadcasted_iota(jnp.int32, (32, 32), 1)

    def upright(row):
        return jnp.sum(jnp.where(eye, jnp.broadcast_to(row, (32, 32)), 0.0), axis=1, keepdims=True)

    def flat(col):
        return jnp.sum(jnp.where(eye, jnp.broadcast_to(col, (32, 32)), 0.0), axis=0, keepdims=True)

    for gain, grads, total, todo in (
        (ga, oqkv, attn, ((w_query, query, 0, 512), (key_projection, key, 512, 256), (value_projection, value, 768, 256))),
        (gm, ogu, mlp, ((w_gate, gate, 0, 768), (w_up, up, 768, 768))),
    ):
        g = upright(gain[...].astype(F32))
        dot = jnp.zeros((32, 1), F32)
        for w, o, first, width in todo:
            for t in range(4):
                h = grads[t, :, first : first + width].astype(F32)
                lanes = slice(t * width, (t + 1) * width)
                o[:, lanes] = g * h
                dot = dot + jnp.sum(w[:, lanes].astype(F32) * h, axis=1, keepdims=True)
        total[...] = flat(dot)


def finish(*args):
    shape = jax.ShapeDtypeStruct
    ws = args[9:]
    res = pl.pallas_call(
        finish_kernel,
        out_shape=(
            shape(args[0].shape, BF),
            shape(args[1].shape, BF),
            shape((1, 32), F32),
            *[shape(w.shape, F32) for w in ws[:3]],
            shape((1, 128), F32),
            shape((1, 128), F32),
            shape(args[4].shape, F32),
            shape((1, 32), F32),
            *[shape(w.shape, F32) for w in ws[3:]],
            shape(args[2].shape, F32),
        ),
        in_specs=[VM] * 14,
        out_specs=(VM,) * 13,
        name="gains_and_layout",
    )(*args)
    res = list(res)
    for i in (2, 6, 7, 9):
        res[i] = res[i].reshape(-1)
    return tuple(res)


def layer(tokens, *rest):
    whole = (
        lax.axis_size("dp") == 4
        and lax.axis_size("seq") == 8
        and tokens.shape == (2, 128, WIDTH)
        and rest[-1].shape == (2, 16)
    )
    return (whole_sequences if whole else shards)(tokens, *rest)


def solution(mesh):
    return jax.shard_map(
        layer,
        mesh=mesh,
        in_specs=(
            P("dp", "seq", None),
            P(("dp", "seq")),
            P(("dp", "seq"), None),
            P(("dp", "seq"), None),
            P(("dp", "seq"), None),
            P(),
            P(),
            P(("dp", "seq"), None),
            P(("dp", "seq")),
            P(("dp", "seq"), None),
            P(("dp", "seq"), None),
            P(("dp", "seq"), None),
            P("dp", "seq", None),
            P("dp", None),
        ),
        out_specs=(
            P("dp", "seq", None),
            P("dp", "seq", None),
            P(("dp", "seq")),
            P(("dp", "seq"), None),
            P(("dp", "seq"), None),
            P(("dp", "seq"), None),
            P(),
            P(),
            P(("dp", "seq"), None),
            P(("dp", "seq")),
            P(("dp", "seq"), None),
            P(("dp", "seq"), None),
            P(("dp", "seq"), None),
        ),
        check_vma=False,
    )
```

```python
import jax
import jax.numpy as jnp
from jax import lax
from jax.sharding import PartitionSpec as P

import numpy as np
from jax.experimental import pallas as pl
from jax.experimental.pallas import tpu as pltpu

QUERY_HEADS = 16
KEY_VALUE_HEADS = 8
HEAD_SIZE = 128
BLK = 64
MB = 2


EPS = 1e-06
BASE = 1000000.0
NEGATIVE_FILL = -1e30


def from_behind(block, axis, distance):
    devices = range(lax.axis_size(axis))
    route = [((i - distance) % len(devices), i) for i in devices]
    return lax.ppermute(block, axis, route)


def row_norm_apply(v, gain):
    return v * lax.rsqrt(jnp.mean(v * v, axis=-1, keepdims=True) + EPS) * gain


def apply_rotary(v, cosine_table, sine_table):
    half = v.shape[-1] // 2
    first = v[..., :half]
    second = v[..., half:]
    return jnp.concatenate(
        [first * cosine_table - second * sine_table, second * cosine_table + first * sine_table],
        axis=-1,
    )


def matrix_multiply(left, right):
    return jnp.dot(left, right, preferred_element_type=jnp.float32)


def row_product(left, right):
    return lax.dot_general(
        left, right, (((0,), (0,)), ((), ())), preferred_element_type=jnp.float32
    )


def product_backward(left, right):
    return lax.dot_general(
        left, right, (((1,), (1,)), ((), ())), preferred_element_type=jnp.float32
    )


def block_positions(order, start, count):
    places = start + lax.iota(jnp.int32, count)
    which = places // BLK
    hits = (which[:, None] == lax.iota(jnp.int32, order.shape[1])[None, :]).astype(jnp.int32)
    spans = jnp.sum(hits[None, :, :] * order[:, None, :], axis=-1)
    return spans * BLK + places % BLK


def pack_shares(members, count):
    return jnp.concatenate([m.reshape(count, -1) for m in members], axis=1).reshape(-1)


def unpack_shares(flat, members, count):
    pieces = []
    offset = 0
    for m in members:
        length = m.size // count
        share_shape = (m.shape[0] // count,) + tuple(m.shape[1:])
        pieces.append(flat[offset : offset + length].reshape(share_shape))
        offset = offset + length
    return pieces


def shards(
    tokens,
    attn_gain,
    w_query,
    key_projection,
    value_projection,
    query_head_gain,
    key_gain,
    w_out,
    mlp_gain,
    w_gate,
    w_up,
    w_down,
    cotangent,
    span_order,
):
    seq_count = lax.axis_size("seq")
    seq_place = lax.axis_index("seq")
    all_count = lax.axis_size(("dp", "seq"))
    local_length = tokens.shape[1]
    width = tokens.shape[2]
    sequence_permutation = tokens.shape[0] // MB
    query_group = QUERY_HEADS // KEY_VALUE_HEADS
    scale = HEAD_SIZE ** (-0.5)
    freqs = BASE ** (-(lax.iota(jnp.float32, HEAD_SIZE // 2) * 2.0) / HEAD_SIZE)
    query_norm_gain = query_head_gain.astype(jnp.float32)
    kgain = key_gain.astype(jnp.float32)
    sums = None
    outputs = []
    input_grads = []
    for batch in range(MB):
        rows_x = tokens[batch * sequence_permutation : (batch + 1) * sequence_permutation]
        rows_cot = cotangent[batch * sequence_permutation : (batch + 1) * sequence_permutation]
        order = span_order[batch * sequence_permutation : (batch + 1) * sequence_permutation]
        gain_a, wq, key_weight, value_weight, output_weight = (
            lax.all_gather(attn_gain, ("dp", "seq"), axis=0, tiled=True),
            lax.all_gather(w_query, ("dp", "seq"), axis=0, tiled=True),
            lax.all_gather(key_projection, ("dp", "seq"), axis=0, tiled=True),
            lax.all_gather(value_projection, ("dp", "seq"), axis=0, tiled=True),
            lax.all_gather(w_out, ("dp", "seq"), axis=0, tiled=True),
        )
        gain_m, wg, wu, wd = (
            lax.all_gather(mlp_gain, ("dp", "seq"), axis=0, tiled=True),
            lax.all_gather(w_gate, ("dp", "seq"), axis=0, tiled=True),
            lax.all_gather(w_up, ("dp", "seq"), axis=0, tiled=True),
            lax.all_gather(w_down, ("dp", "seq"), axis=0, tiled=True),
        )
        own_pos = block_positions(order, seq_place * local_length, local_length)
        angles = own_pos.astype(jnp.float32)[..., None] * freqs
        cosine_table = jnp.cos(angles)[:, :, None, :]
        sine_table = jnp.sin(angles)[:, :, None, :]

        def query_per_head(raw, gain):
            return apply_rotary(row_norm_apply(raw, gain), cosine_table, sine_table)

        flat_x = rows_x.reshape(-1, width).astype(jnp.float32)
        first_operand = row_norm_apply(flat_x, gain_a.astype(jnp.float32)).astype(jnp.bfloat16)
        query_unrotated = matrix_multiply(first_operand, wq).reshape(
            sequence_permutation, local_length, QUERY_HEADS, HEAD_SIZE
        )
        key_unrotated = matrix_multiply(first_operand, key_weight).reshape(
            sequence_permutation, local_length, KEY_VALUE_HEADS, HEAD_SIZE
        )
        value_reduced = (
            matrix_multiply(first_operand, value_weight)
            .astype(jnp.bfloat16)
            .reshape(sequence_permutation, local_length, KEY_VALUE_HEADS, HEAD_SIZE)
        )
        q_low = (
            query_per_head(query_unrotated, query_norm_gain)
            .astype(jnp.bfloat16)
            .reshape(sequence_permutation, local_length, KEY_VALUE_HEADS, query_group, HEAD_SIZE)
        )
        k_low = query_per_head(key_unrotated, kgain).astype(jnp.bfloat16)
        initial_maximum = jnp.full(
            (sequence_permutation, KEY_VALUE_HEADS, query_group, local_length),
            NEGATIVE_FILL,
            jnp.float32,
        )
        top = initial_maximum
        piece_k = lax.all_gather(k_low, "seq", axis=1, tiled=True)
        piece_v = lax.all_gather(value_reduced, "seq", axis=1, tiled=True)
        key_pos = block_positions(order, jnp.int32(0), piece_k.shape[1])
        visible = key_pos[:, None, None, None, :] <= own_pos[:, None, None, :, None]
        scores = (
            jnp.einsum("sqgrd,skgd->sgrqk", q_low, piece_k, preferred_element_type=jnp.float32)
            * scale
        )
        scores = jnp.where(visible, scores, NEGATIVE_FILL)
        new_top = jnp.maximum(top, jnp.max(scores, axis=-1))
        weights = jnp.exp(scores - new_top[..., None])
        new_total = jnp.sum(weights, axis=-1)
        taken = jnp.einsum(
            "sgrqk,skgd->sqgrd",
            weights.astype(jnp.bfloat16),
            piece_v,
            preferred_element_type=jnp.float32,
        )
        top = new_top
        log_total = top + jnp.log(new_total)
        attn = taken / jnp.transpose(new_total, (0, 3, 1, 2))[..., None]
        o_low = attn.astype(jnp.bfloat16).reshape(
            sequence_permutation * local_length, QUERY_HEADS * HEAD_SIZE
        )
        hidden = flat_x + matrix_multiply(o_low, output_weight)
        gain_second = gain_m.astype(jnp.float32)
        a_second = row_norm_apply(hidden, gain_second).astype(jnp.bfloat16)
        gate = matrix_multiply(a_second, wg)
        up_part = matrix_multiply(a_second, wu)
        mixed = (gate * jax.nn.sigmoid(gate) * up_part).astype(jnp.bfloat16)
        result = hidden + matrix_multiply(mixed, wd)
        outputs.append(
            result.astype(jnp.bfloat16).reshape(sequence_permutation, local_length, width)
        )
        gain_a, wq, key_weight, value_weight, output_weight = (
            lax.all_gather(attn_gain, ("dp", "seq"), axis=0, tiled=True),
            lax.all_gather(w_query, ("dp", "seq"), axis=0, tiled=True),
            lax.all_gather(key_projection, ("dp", "seq"), axis=0, tiled=True),
            lax.all_gather(value_projection, ("dp", "seq"), axis=0, tiled=True),
            lax.all_gather(w_out, ("dp", "seq"), axis=0, tiled=True),
        )
        gain_m, wg, wu, wd = (
            lax.all_gather(mlp_gain, ("dp", "seq"), axis=0, tiled=True),
            lax.all_gather(w_gate, ("dp", "seq"), axis=0, tiled=True),
            lax.all_gather(w_up, ("dp", "seq"), axis=0, tiled=True),
            lax.all_gather(w_down, ("dp", "seq"), axis=0, tiled=True),
        )
        flat_cot = rows_cot.reshape(-1, width)
        grad_down = row_product(mixed, flat_cot)
        d_mixed = product_backward(flat_cot, wd)

        def mix(gate_in, up_in):
            return gate_in * jax.nn.sigmoid(gate_in) * up_in

        _, mix_back = jax.vjp(mix, gate, up_part)
        d_gate, d_up = mix_back(d_mixed)
        gate_low = d_gate.astype(jnp.bfloat16)
        up_low = d_up.astype(jnp.bfloat16)
        grad_gate = row_product(a_second, gate_low)
        grad_up = row_product(a_second, up_low)
        d_second = product_backward(gate_low, wg) + product_backward(up_low, wu)
        _, second_back = jax.vjp(row_norm_apply, hidden, gain_second)
        d_hidden_norm, grad_mlp_gain = second_back(d_second)
        d_hidden = flat_cot.astype(jnp.float32) + d_hidden_norm
        grad_output_reduced = d_hidden.astype(jnp.bfloat16)
        grad_out = row_product(o_low, grad_output_reduced)
        do_low = (
            product_backward(grad_output_reduced, output_weight)
            .astype(jnp.bfloat16)
            .reshape(sequence_permutation, local_length, KEY_VALUE_HEADS, query_group, HEAD_SIZE)
        )
        delta = jnp.transpose(jnp.sum(do_low.astype(jnp.float32) * attn, axis=-1), (0, 2, 3, 1))

        def back_terms(held_k, held_v, visible):
            scores = (
                jnp.einsum("sqgrd,skgd->sgrqk", q_low, held_k, preferred_element_type=jnp.float32)
                * scale
            )
            scores = jnp.where(visible, scores, NEGATIVE_FILL)
            probs = jnp.exp(scores - log_total[..., None])
            d_probs = jnp.einsum(
                "sqgrd,skgd->sgrqk", do_low, held_v, preferred_element_type=jnp.float32
            )
            score_low = (probs * (d_probs - delta[..., None])).astype(jnp.bfloat16)
            probs_low = probs.astype(jnp.bfloat16)
            term_q = scale * jnp.einsum(
                "sgrqk,skgd->sqgrd", score_low, held_k, preferred_element_type=jnp.float32
            )
            term_k = scale * jnp.einsum(
                "sgrqk,sqgrd->skgd", score_low, q_low, preferred_element_type=jnp.float32
            )
            term_v = jnp.einsum(
                "sgrqk,sqgrd->skgd", probs_low, do_low, preferred_element_type=jnp.float32
            )
            return (term_k, term_v, term_q)

        def cycle_step(turn, state):
            held_k, held_v, acc_k, acc_v, acc_q = state
            owner = (seq_place - turn) % seq_count
            key_pos = block_positions(order, owner * local_length, local_length)
            visible = key_pos[:, None, None, None, :] <= own_pos[:, None, None, :, None]
            term_k, term_v, term_q = back_terms(held_k, held_v, visible)
            acc_k, acc_v, acc_q = (acc_k + term_k, acc_v + term_v, acc_q + term_q)
            held_k, held_v = from_behind((held_k, held_v), "seq", 1)
            acc_k, acc_v = (
                from_behind(acc_k.astype(jnp.bfloat16), "seq", 1).astype(acc_k.dtype),
                from_behind(acc_v.astype(jnp.bfloat16), "seq", 1).astype(acc_v.dtype),
            )
            return (held_k, held_v, acc_k, acc_v, acc_q)

        def two_steps(pair, state):
            return cycle_step(2 * pair + 1, cycle_step(2 * pair, state))

        blank_key_value = jnp.zeros(
            (sequence_permutation, local_length, KEY_VALUE_HEADS, HEAD_SIZE), jnp.float32
        )
        blank_query = jnp.zeros(
            (sequence_permutation, local_length, KEY_VALUE_HEADS, query_group, HEAD_SIZE),
            jnp.float32,
        )
        state = lax.fori_loop(
            0,
            seq_count // 2,
            two_steps,
            (k_low, value_reduced, blank_key_value, blank_key_value, blank_query),
        )
        _, _, d_keys, grad_value_rows, d_queries = state
        _, query_back = jax.vjp(query_per_head, query_unrotated, query_norm_gain)
        d_q_raw, grad_qgain = query_back(
            d_queries.reshape(sequence_permutation, local_length, QUERY_HEADS, HEAD_SIZE)
        )
        _, key_back = jax.vjp(query_per_head, key_unrotated, kgain)
        grad_key_unrotated, grad_kgain = key_back(d_keys)
        dq_low = d_q_raw.astype(jnp.bfloat16).reshape(
            sequence_permutation * local_length, QUERY_HEADS * HEAD_SIZE
        )
        grad_key_reduced = grad_key_unrotated.astype(jnp.bfloat16).reshape(
            sequence_permutation * local_length, KEY_VALUE_HEADS * HEAD_SIZE
        )
        grad_value_reduced = grad_value_rows.astype(jnp.bfloat16).reshape(
            sequence_permutation * local_length, KEY_VALUE_HEADS * HEAD_SIZE
        )
        grad_query = row_product(first_operand, dq_low)
        grad_key = row_product(first_operand, grad_key_reduced)
        grad_value = row_product(first_operand, grad_value_reduced)
        d_first = (
            product_backward(dq_low, wq)
            + product_backward(grad_key_reduced, key_weight)
            + product_backward(grad_value_reduced, value_weight)
        )
        _, first_back = jax.vjp(row_norm_apply, flat_x, gain_a.astype(jnp.float32))
        d_x_norm, grad_attn_gain = first_back(d_first)
        input_grads.append(
            (d_hidden + d_x_norm)
            .astype(jnp.bfloat16)
            .reshape(sequence_permutation, local_length, width)
        )
        fresh = (
            grad_attn_gain,
            grad_query,
            grad_key,
            grad_value,
            grad_out,
            grad_mlp_gain,
            grad_gate,
            grad_up,
            grad_down,
            grad_qgain,
            grad_kgain,
        )
        if sums is None:
            sums = fresh
        else:
            sums = tuple((a + b for a, b in zip(sums, fresh)))
    attn_members = (sums[0], sums[1], sums[2], sums[3], sums[4])
    mlp_members = (sums[5], sums[6], sums[7], sums[8])
    attn_flat = lax.psum_scatter(
        pack_shares(attn_members, all_count), ("dp", "seq"), scatter_dimension=0, tiled=True
    )
    mlp_flat = lax.psum_scatter(
        pack_shares(mlp_members, all_count), ("dp", "seq"), scatter_dimension=0, tiled=True
    )
    attn_shares = unpack_shares(attn_flat, attn_members, all_count)
    mlp_shares = unpack_shares(mlp_flat, mlp_members, all_count)
    head_sums = lax.psum((sums[9], sums[10]), ("dp", "seq"))
    return (
        jnp.concatenate(outputs, axis=0),
        jnp.concatenate(input_grads, axis=0),
        attn_shares[0],
        attn_shares[1],
        attn_shares[2],
        attn_shares[3],
        head_sums[0],
        head_sums[1],
        attn_shares[4],
        mlp_shares[0],
        mlp_shares[1],
        mlp_shares[2],
        mlp_shares[3],
    )


BF = jnp.bfloat16
F32 = jnp.float32
MESH = pl.DeviceIdType.MESH
TOKENS = 1024
WIDTH = 1024
LOG2E = 1.4426950408889634
VM = pl.BlockSpec(memory_space=pltpu.VMEM)
SM = pl.BlockSpec(memory_space=pltpu.SMEM)
ANY = pl.BlockSpec(memory_space=pl.ANY)
VMEM_BYTES = 65100 * 1024


def place():
    q = lax.axis_index("dp")
    p = lax.axis_index("seq")
    return q, p, q // 2, lax.rem(q, 2), p // 2, lax.rem(p, 2)


def home_group(x, c, i):
    return 4 * c + 2 * i + (x if i == 0 else 1 - x)


def greet(peers):
    barrier = pltpu.get_barrier_semaphore()
    for peer in peers:
        pl.semaphore_signal(barrier, inc=1, device_id=peer, device_id_type=MESH)
    pl.semaphore_wait(barrier, len(peers))


def remote(src, dst, send, recv, peer):
    return pltpu.make_async_remote_copy(
        src_ref=src, dst_ref=dst, send_sem=send, recv_sem=recv, device_id=peer, device_id_type=MESH
    )


def dims(left, right, lc, rc):
    return lax.dot_general(left, right, (((lc,), (rc,)), ((), ())), preferred_element_type=F32)


def mod(a, n):
    return a % n


def unit(v):
    return lax.rsqrt(jnp.mean(v * v, axis=-1, keepdims=True) + EPS)


def pieces(ref, spots, which, first, count):
    return jnp.concatenate([ref[spots[which, first + t]] for t in range(count)], axis=0)


def turns(table):
    other = pltpu.roll(table, HEAD_SIZE // 2, 1)
    first = lax.broadcasted_iota(jnp.int32, table.shape, 1) < HEAD_SIZE // 2
    return jnp.where(first, table, other), jnp.where(first, -other, table)


def rotate(v, cosine, sine):
    return v * cosine + pltpu.roll(v, HEAD_SIZE // 2, 1) * sine


def rotate_back(v, cosine, sine):
    return v * cosine + pltpu.roll(v * sine, HEAD_SIZE // 2, 1)


def lower(s, fill):
    n = s.shape[0]
    i = lax.broadcasted_iota(jnp.int32, (n, n), 0)
    j = lax.broadcasted_iota(jnp.int32, (n, n), 1)
    width = s.shape[1]
    diag = jnp.where(j <= i, s[:, width - n :], fill)
    return diag if width == n else jnp.concatenate([s[:, : width - n], diag], axis=1)


class Sum:
    def __init__(self, part, total, l1, own, l2, sems, base):
        self.q, self.p, self.x, self.c, _, _ = place()
        self.part, self.total, self.l1, self.own, self.l2 = part, total, l1, own, l2
        self.sems, self.base = sems, base
        self.sib = (2 * self.x + 1 - self.c, self.p)
        self.opp = (2 * (1 - self.x) + self.c, self.p)

    def rows(self, n, c):
        return pl.ds(pl.multiple_of(n * 256 + c * 128, 128), 128)

    def copy(self, step, n):
        s, r = self.sems.at[self.base + 2 * step, n], self.sems.at[self.base + 2 * step + 1, n]
        if step == 0:
            return remote(self.part.at[self.rows(n, 1 - self.c)], self.l1.at[n], s, r, self.sib)
        if step == 1:
            return remote(self.own.at[n], self.l2.at[n], s, r, self.opp)
        mine = self.total_at(n, self.c)
        return remote(mine, mine, s, r, self.sib)

    def total_at(self, n, c):
        if len(self.total.shape) == 2:
            return self.total.at[self.rows(n, c)]
        return self.total.at[(2 * n + c) // 4, (2 * n + c) % 4]

    def beside(self, n):
        self.copy(0, n).start()

    def across(self, n):
        self.copy(0, n).wait_recv()
        mine = self.part[self.rows(n, self.c), :].astype(F32)
        self.own[n] = (mine + self.l1[n].astype(F32)).astype(BF)
        self.copy(1, n).start()

    def back(self, n):
        self.copy(1, n).wait_recv()
        total = self.total_at(n, self.c)
        total[...] = (self.own[n].astype(F32) + self.l2[n].astype(F32)).astype(BF).reshape(total.shape)
        self.copy(2, n).start()

    def ready(self, n):
        other = self.total_at(n, 1 - self.c)
        s, r = self.sems.at[self.base + 4, n], self.sems.at[self.base + 5, n]
        remote(other, other, s, r, self.sib).wait_recv()

    def close(self, *steps):
        @pl.loop(0, 4)
        def _(n):
            for step in steps:
                self.copy(step, n).wait_send()


LINES = 6
PIECES = ((0, None), (2, None), (1, 0), (1, 1), (1, 2), (1, 3), (3, None))


def block(ref, b):
    return ref.at[pl.ds(2 * b, 2)]


class Gather:
    def __init__(self, srcs, dsts, sems):
        self.q, self.p, self.x, self.c, self.z, self.y = place()
        self.tok, self.cot, self.pos, self.pq, self.pg, self.po, self.pd = srcs
        self.xf, self.cf, self.of, *self.w = dsts
        (self.loc, self.ts, self.tr, self.fs, self.fr, self.ps, self.pr,
         self.as_, self.ar, self.zs, self.zr, self.ys, self.yr, self.ls, self.lr) = sems
        q, p, x, c, z, y = self.q, self.p, self.x, self.c, self.z, self.y
        self.owner_x, self.owner_c = mod(y + z, 2), z // 2
        self.is_owner = jnp.logical_and(x == self.owner_x, c == self.owner_c)
        self.cross = jnp.logical_and(x != self.owner_x, c == self.owner_c)
        self.sib = (2 * x + 1 - c, p)
        self.opp = (2 * (1 - x) + c, p)

    def peers(self):
        q, p = self.q, self.p
        return [(mod(q + k, 4), p) for k in (1, 2, 3)] + [(q, mod(p + k, 8)) for k in range(1, 8)]

    def col(self, n):
        return (self.pq, self.pg)[n], self.w[n]

    def own_copy(self, n):
        q, p = self.q, self.p
        if n < 2:
            src, dst = self.col(n)
            return pltpu.make_async_copy(src.at[q], dst.at[q, p], self.loc.at[n])
        return pltpu.make_async_copy((self.po, self.pd)[n - 2], self.w[n].at[p], self.loc.at[n])

    def column_copy(self, n, k):
        q, p = self.q, self.p
        src, dst = self.col(n)
        t = mod(q + k, 4)
        return remote(src.at[t], dst.at[q, p], self.as_.at[n, k - 1], self.ar.at[n, k - 1], (t, p))

    def column_start(self, n):
        for k in (1, 2, 3):
            self.column_copy(n, k).start()

    def column_wait(self, n):
        q, p = self.q, self.p
        src, dst = self.col(n)
        for k in (1, 2, 3):
            f = mod(q + 4 - k, 4)
            remote(src.at[0], dst.at[f, p], self.as_.at[n, k - 1], self.ar.at[n, k - 1], (q, p)).wait_recv()

    def view(self, piece, chunk):
        n, part = PIECES[piece]
        if n >= 2:
            return self.w[n].at[chunk]
        return self.w[n].at[:, chunk] if part is None else self.w[n].at[part, chunk]

    def z_copy(self, piece, src, way):
        v = self.view(piece, 2 * src + self.y)
        s = self.zs.at[piece, src + (4 if way < 0 else 0)]
        return remote(v, v, s, self.zr.at[piece, src], (self.q, 2 * (self.z + way) + self.y))

    def y_copy(self, piece, src):
        v = self.view(piece, 2 * src + self.y)
        return remote(v, v, self.ys.at[piece, src], self.yr.at[piece, src], (self.q, 2 * self.z + 1 - self.y))

    def spread(self, piece, src, up, down):
        if up:

            @pl.when(self.z < 3)
            def _():
                self.z_copy(piece, src, 1).start()

        if down:

            @pl.when(self.z > 0)
            def _():
                self.z_copy(piece, src, -1).start()

        self.y_copy(piece, src).start()

    def begin(self, *pieces_):
        for piece in pieces_:
            self.spread(piece, self.z, True, True)

    def line_copy(self, line, src, way):
        v = self.view(LINES, 2 * src + line)
        s = self.ls.at[line, src + (4 if way < 0 else 0)]
        return remote(v, v, s, self.lr.at[line, src], (self.q, 2 * (self.z + way) + self.y))

    def line_spread(self, line, src, up, down):
        if up:

            @pl.when(self.z < 3)
            def _():
                self.line_copy(line, src, 1).start()

        if down:

            @pl.when(self.z > 0)
            def _():
                self.line_copy(line, src, -1).start()

    def lines_begin(self):
        self.y_copy(LINES, self.z).start()
        self.line_spread(self.y, self.z, True, True)

    def lines_turn(self):
        v = self.view(LINES, 2 * self.z + 1 - self.y)
        remote(v, v, self.ys.at[LINES, self.z], self.yr.at[LINES, self.z], (self.q, self.p)).wait_recv()
        self.line_spread(1 - self.y, self.z, True, True)

    def line_step(self, other, dist):
        line = 1 - self.y if other else self.y
        low, high = self.z - dist, self.z + dist

        @pl.when(low >= 0)
        def _():
            v = self.view(LINES, 2 * low + line)
            remote(v, v, self.ls.at[line, 0], self.lr.at[line, low], (self.q, self.p)).wait_recv()
            self.line_spread(line, low, True, False)

        @pl.when(high < 4)
        def _():
            v = self.view(LINES, 2 * high + line)
            remote(v, v, self.ls.at[line, 0], self.lr.at[line, high], (self.q, self.p)).wait_recv()
            self.line_spread(line, high, False, True)

    def step(self, piece, dist):
        low, high = self.z - dist, self.z + dist

        @pl.when(low >= 0)
        def _():
            v = self.view(piece, 2 * low + self.y)
            remote(v, v, self.zs.at[piece, 0], self.zr.at[piece, low], (self.q, self.p)).wait_recv()
            self.spread(piece, low, True, False)

        @pl.when(high < 4)
        def _():
            v = self.view(piece, 2 * high + self.y)
            remote(v, v, self.zs.at[piece, 0], self.zr.at[piece, high], (self.q, self.p)).wait_recv()
            self.spread(piece, high, False, True)

    def steps(self, *pieces_):
        for piece in pieces_:
            for dist in (1, 2, 3):
                self.step(piece, dist)

    def y_wait(self, *pieces_):
        for piece in pieces_:
            for src in range(4):
                v = self.view(piece, 2 * src + 1 - self.y)
                remote(v, v, self.ys.at[piece, src], self.yr.at[piece, src], (self.q, self.p)).wait_recv()

    def tok_dst(self, a):
        return (self.xf, self.cf)[a]

    def token_copy(self, a, i):
        src, dst = (self.tok, self.cot)[a], self.tok_dst(a)
        goal = home_group(self.x, self.c, i)
        return goal, remote(src.at[i], block(dst, self.p), self.ts.at[a, i], self.tr.at[a, self.p], (self.q, goal))

    def token_local(self, a, i):
        return pltpu.make_async_copy((self.tok, self.cot)[a].at[i], block(self.tok_dst(a), self.p), self.loc.at[4 + a])

    def token_start(self, a):
        for i in range(2):
            goal, cp = self.token_copy(a, i)

            @pl.when(goal != self.p)
            def _():
                cp.start()

            @pl.when(goal == self.p)
            def _():
                self.token_local(a, i).start()

    def token_pass(self, a, first=0, end=8):
        dst = self.tok_dst(a)
        q, p = self.q, self.p

        @pl.when(self.is_owner)
        def _():
            @pl.loop(first, end)
            def _(b):
                @pl.when(b != p)
                def _():
                    remote(block(dst, b), block(dst, b), self.ts.at[a, 0], self.tr.at[a, b], (q, p)).wait_recv()

                @pl.when(b == p)
                def _():
                    self.token_local(a, 0).wait()

                remote(block(dst, b), block(dst, b), self.fs.at[a, 0, b], self.fr.at[a, b], self.sib).start()
                remote(block(dst, b), block(dst, b), self.fs.at[a, 1, b], self.fr.at[a, b], self.opp).start()

        @pl.when(jnp.logical_not(self.is_owner))
        def _():
            @pl.loop(first, end)
            def _(b):
                remote(block(dst, b), block(dst, b), self.fs.at[a, 0, b], self.fr.at[a, b], self.sib).wait_recv()

                @pl.when(self.cross)
                def _():
                    remote(block(dst, b), block(dst, b), self.fs.at[a, 0, b], self.fr.at[a, b], self.sib).start()

    def token_close(self, a):
        dst = self.tok_dst(a)
        q, p = self.q, self.p
        for i in range(2):
            goal, cp = self.token_copy(a, i)

            @pl.when(goal != p)
            def _():
                cp.wait_send()

        @pl.when(self.is_owner)
        def _():
            @pl.loop(0, 8)
            def _(b):
                remote(block(dst, b), block(dst, b), self.fs.at[a, 0, b], self.fr.at[a, b], (q, p)).wait_send()
                remote(block(dst, b), block(dst, b), self.fs.at[a, 1, b], self.fr.at[a, b], (q, p)).wait_send()

        @pl.when(self.cross)
        def _():
            @pl.loop(0, 8)
            def _(b):
                remote(block(dst, b), block(dst, b), self.fs.at[a, 0, b], self.fr.at[a, b], (q, p)).wait_send()

    def pos_copy(self, k):
        return remote(self.pos, self.of, self.ps.at[k], self.pr.at[0], (mod(self.q + k + 1, 4), self.p))

    def pos_start(self):
        @pl.when(self.is_owner)
        def _():
            pltpu.make_async_copy(self.pos, self.of, self.loc.at[6]).start()
            for k in range(3):
                self.pos_copy(k).start()

    def pos_finish(self):
        @pl.when(self.is_owner)
        def _():
            pltpu.make_async_copy(self.pos, self.of, self.loc.at[6]).wait()
            for k in range(3):
                self.pos_copy(k).wait_send()

        @pl.when(jnp.logical_not(self.is_owner))
        def _():
            self.pos_copy(0).wait_recv()

    def close(self):
        for n in range(2):
            for k in (1, 2, 3):
                self.column_copy(n, k).wait_send()
        self.y_copy(LINES, self.z).wait_send()
        for line in range(2):
            for src in range(4):

                @pl.when(jnp.logical_and(self.z < 3, src <= self.z))
                def _():
                    self.line_copy(line, src, 1).wait_send()

                @pl.when(jnp.logical_and(self.z > 0, src >= self.z))
                def _():
                    self.line_copy(line, src, -1).wait_send()

        for piece in range(LINES):
            for src in range(4):
                self.y_copy(piece, src).wait_send()

                @pl.when(jnp.logical_and(self.z < 3, src <= self.z))
                def _():
                    self.z_copy(piece, src, 1).wait_send()

                @pl.when(jnp.logical_and(self.z > 0, src >= self.z))
                def _():
                    self.z_copy(piece, src, -1).wait_send()

        self.token_close(0)
        self.token_close(1)


GATHER_SEMS = ((7,), (2, 2), (2, 8), (2, 2, 8), (2, 8), (3,), (1,), (2, 3), (2, 3), (7, 8), (7, 4), (7, 4), (7, 4), (2, 8), (2, 4))


class Home:
    def __init__(self, part, out, l1, own, l2, sems, here, base):
        self.q, self.p, self.x, self.c, self.z, self.y = place()
        self.part, self.out, self.l1, self.own, self.l2 = part, out, l1, own, l2
        self.sems, self.here, self.base = sems, here, base
        self.owner_x, self.owner_c = mod(self.y + self.z, 2), self.z // 2
        self.keeps = self.x == self.owner_x
        self.sib = (2 * self.x + 1 - self.c, self.p)
        self.opp = (2 * (1 - self.x) + self.c, self.p)
        self.goal_q = 2 * self.owner_x + self.owner_c

    def rows(self, n, c):
        return pl.ds(pl.multiple_of(n * 256 + c * 128, 128), 128)

    def sem(self, k, n):
        return self.sems.at[self.base + k, n]

    def first(self, n):
        return remote(
            self.part.at[self.rows(n, 1 - self.c)], self.l1.at[n], self.sem(0, n), self.sem(1, n), self.sib
        )

    def second(self, n):
        return remote(self.own.at[n], self.l2.at[n], self.sem(2, n), self.sem(3, n), self.opp)

    def third(self, n):
        slot = mod(self.z, 2)
        return remote(
            self.own.at[n], self.out.at[slot], self.sem(4, n), self.sem(5, slot), (self.goal_q, 2 * n + self.c)
        )

    def is_self(self, n):
        return jnp.logical_and(self.goal_q == self.q, 2 * n + self.c == self.p)

    def beside(self, n):
        self.first(n).start()

    def across(self, n):
        self.first(n).wait_recv()
        mine = self.part[self.rows(n, self.c), :].astype(F32)
        self.own[n] = (mine + self.l1[n].astype(F32)).astype(BF)

        @pl.when(jnp.logical_not(self.keeps))
        def _():
            self.second(n).start()

    def finish(self, n, rest):
        @pl.when(self.keeps)
        def _():
            self.second(n).wait_recv()
            s = self.own[n].astype(F32) + self.l2[n].astype(F32)
            self.own[n] = rest(n, s).astype(BF)

            @pl.when(jnp.logical_not(self.is_self(n)))
            def _():
                self.third(n).start()

            @pl.when(self.is_self(n))
            def _():
                cp = pltpu.make_async_copy(self.own.at[n], self.out.at[mod(self.z, 2)], self.here)
                cp.start()
                cp.wait()

    def close(self):
        for i in range(2):
            group = home_group(self.x, self.c, i)
            same = jnp.logical_and(group == self.p, self.y == self.c)

            @pl.when(jnp.logical_not(same))
            def _():
                remote(self.own.at[0], self.out.at[i], self.sem(4, 0), self.sem(5, i), (self.q, self.p)).wait_recv()

        for n in range(4):
            self.first(n).wait_send()

            @pl.when(jnp.logical_not(self.keeps))
            def _():
                self.second(n).wait_send()

            @pl.when(jnp.logical_and(self.keeps, jnp.logical_not(self.is_self(n))))
            def _():
                self.third(n).wait_send()


class Scatter:
    def __init__(self, g, ly, lz, sems, base):
        self.q, self.p, _, _, self.z, self.y = place()
        self.g, self.ly, self.lz, self.sems, self.base = g, ly, lz, sems, base

    def y_copy(self, n):
        s, r = self.sems.at[self.base + n, 0], self.sems.at[self.base + n, 1]
        return remote(self.g.at[1 - self.y, n], self.ly(n), s, r, (self.q, 2 * self.z + 1 - self.y))

    def z_copy(self, n, k):
        t = mod(self.z + k, 4)
        s, r = self.sems.at[self.base + n, 2 * k], self.sems.at[self.base + n, 2 * k + 1]
        return remote(self.ly(n).at[t], self.lz(n).at[k - 1], s, r, (self.q, 2 * t + self.y))

    def y_send(self, n):
        self.y_copy(n).start()

    def z_step(self, n):
        self.y_copy(n).wait_recv()
        ly = self.ly(n)

        @pl.loop(0, 4)
        def _(t):
            ly[t] = (ly[t].astype(F32) + self.g[self.y, n, t].astype(F32)).astype(BF)

        lz = self.lz(n)
        z = self.z

        @pl.when(z != 3)
        def _():
            self.z_copy(n, 1).start()

        @pl.when(z != 0)
        def _():
            self.z_copy(n, 3).start()

        for end, unused in ((0, 0), (3, 2)):

            @pl.when(z == end)
            def _():
                self.z_copy(n, 2).start()
                self.relay_copy(n).start()
                lz[unused] = jnp.zeros(lz.shape[1:], BF)

    def relay_copy(self, n):
        s, r = self.sems.at[self.base + n, 8], self.sems.at[self.base + n, 9]
        near = 1 + self.z // 3
        return remote(self.ly(n).at[3 - self.z], self.lz(n).at[3], s, r, (self.q, 2 * near + self.y))

    def relay(self, n):
        @pl.when(jnp.logical_and(self.z > 0, self.z < 3))
        def _():
            ly, lz = self.ly(n), self.lz(n)
            t = mod(self.z + 2, 4)
            s, r = self.sems.at[self.base + n, 8], self.sems.at[self.base + n, 9]
            remote(ly.at[t], lz.at[3], s, r, (self.q, self.p)).wait_recv()
            ly[t] = (ly[t].astype(F32) + lz[3].astype(F32)).astype(BF)
            self.z_copy(n, 2).start()

    def z_sum(self, n):
        @pl.when(self.z != 0)
        def _():
            self.z_copy(n, 1).wait_recv()

        self.z_copy(n, 2).wait_recv()

        @pl.when(self.z != 3)
        def _():
            self.z_copy(n, 3).wait_recv()

        ly, lz = self.ly(n), self.lz(n)
        return ly[self.z].astype(F32) + lz[0].astype(F32) + lz[1].astype(F32) + lz[2].astype(F32)

    def close(self, count):
        @pl.loop(0, count)
        def _(n):
            self.y_copy(n).wait_send()
            self.z_copy(n, 2).wait_send()

            @pl.when(self.z != 3)
            def _():
                self.z_copy(n, 1).wait_send()

            @pl.when(self.z != 0)
            def _():
                self.z_copy(n, 3).wait_send()

            @pl.when(jnp.logical_or(self.z == 0, self.z == 3))
            def _():
                self.relay_copy(n).wait_send()


class Columns:
    def __init__(self, scatter, land, sems, base):
        self.scatter, self.land = scatter, land
        self.sems, self.base = sems, base
        self.q, self.p = scatter.q, scatter.p

    def copy(self, t):
        s, r = self.sems.at[self.base, t], self.sems.at[self.base + 1, self.q]
        return remote(self.scatter.ly(t).at[self.scatter.z], self.land.at[self.q], s, r, (t, self.p))

    def step(self, t):
        s = self.scatter.z_sum(t).astype(BF)

        @pl.when(t != self.q)
        def _():
            ly = self.scatter.ly(t)
            ly[self.scatter.z] = s
            self.copy(t).start()

        @pl.when(t == self.q)
        def _():
            self.land[t] = s

    def close(self):
        for t in range(4):

            @pl.when(t != self.q)
            def _():
                r = self.sems.at[self.base + 1, t]
                remote(self.land.at[t], self.land.at[t], self.sems.at[self.base, t], r, (self.q, self.p)).wait_recv()
                self.copy(t).wait_send()


def column(table, h):
    lane = lax.broadcasted_iota(jnp.int32, table.shape, 1)
    return jnp.sum(jnp.where(lane == h, table, 0.0), axis=1, keepdims=True)


def layer_kernel(
    tok, cot, pos, po, pd, table, qg, kg, ga, gm, w_query, key_projection, value_projection, w_gate, w_up,
    out, igrad, od, ogu, oo, oqkv, oheads, of,
    xf, cf, wq, wg, wo, wd, raw_o, qb, kb, vb, ob, lse, hidden, rest, cs, pa, pb, pc, mb, dgu, gd, ggu,
    dkv, go, gqkv, yo, yqkv, zo, zqkv, heads, hy, hz, hdp,
    l1, own, l2, l1b, ownb, l2b, l2c, rows_of_two, sorts, sorts_sem, free, sums, gsem, csem, hs, hr, homes, here, *sems,
):
    q, p, x_, c, z, y = place()
    sd = Scatter(gd, lambda n: wd.at[pl.ds(0, 4)], lambda n: wd.at[pl.ds(4, 4)], gsem, 0)
    sgu = Scatter(ggu, lambda n: wg.at[n, pl.ds(0, 4)], lambda n: wg.at[n, pl.ds(4, 4)], gsem, 1)
    so = Scatter(go, lambda n: yo.at[n], lambda n: zo.at[n], gsem, 5)
    sqkv = Scatter(gqkv, lambda n: yqkv.at[n], lambda n: zqkv.at[n], gsem, 6)
    cgu = Columns(sgu, ogu, csem, 0)
    cqkv = Columns(sqkv, oqkv, csem, 2)
    h_out = Home(pb, out, l1, own, l2, homes, here.at[0], 0)
    h_in = Home(pc, igrad, l1b, ownb, l2c, homes, here.at[1], 6)
    order = [(sd, 0)] + [(sgu, n) for n in range(4)] + [(so, 0)] + [(sqkv, n) for n in range(4)]

    def y_send(j):
        which, n = order[j]
        which.y_send(n)

    def relay(j):
        which, n = order[j]
        which.relay(n)

    def step(j):
        which, n = order[j]
        which.z_step(n)
        if j + 2 < len(order):
            y_send(j + 2)
        if j > 0:
            relay(j - 1)

    pq, pg = yqkv.at[0], ggu.at[0, 0]
    for gain, dst, todo in (
        (ga, pq, ((w_query, 0, 512), (key_projection, 512, 256), (value_projection, 768, 256))),
        (gm, pg, ((w_gate, 0, 768), (w_up, 768, 768))),
    ):
        up = upright(gain[...].astype(F32))
        for w, first, width in todo:
            for t in range(4):
                v = w[:, t * width : (t + 1) * width].astype(F32) * up
                dst[t, :, first : first + width] = v.astype(BF)
    g = Gather((tok, cot, pos, pq, pg, po, pd), (xf, cf, of, wq, wg, wo, wd), sems)
    peers = [(2 * x_ + cc, mod(p + k, 8)) for k in range(1, 8) for cc in (0, 1)]
    peers += [(mod(q + k, 4), p) for k in (1, 2, 3)]
    greet(peers)
    g.pos_start()
    g.token_start(0)
    g.column_start(0)
    for n in range(4):
        g.own_copy(n).start()
    g.column_start(1)
    g.own_copy(0).wait()
    g.column_wait(0)
    g.begin(0)
    g.pos_finish()
    sort = pltpu.make_async_copy(of, rows_of_two, sorts_sem.at[0])
    sort.start()
    lse[...] = jnp.zeros_like(lse)
    g.step(0, 1)
    g.token_pass(0, 0, 2)
    g.step(0, 2)
    g.token_pass(0, 2, 4)
    g.token_start(1)
    g.step(0, 3)
    g.token_pass(0, 4, 8)
    g.own_copy(2).wait()
    g.begin(1)
    g.own_copy(1).wait()
    g.column_wait(1)
    g.begin(2, 3)
    g.own_copy(3).wait()
    sort.wait()
    slot = mod(z, 2)
    for j in range(16):
        sorts[0, j] = rows_of_two[slot, j]
        where = jnp.int32(0)
        for b in range(16):
            where = jnp.where(rows_of_two[slot, b] == j, b, where)
        sorts[1, j] = where
    g.y_wait(0)

    @pl.loop(0, 4)
    def _(n):
        rows = pl.ds(pl.multiple_of(n * 256, 256), 256)
        v = pieces(xf, sorts, 1, n * 4, 4).astype(F32)
        h = (v * unit(v)).astype(BF)

        @pl.when(n == 2)
        def _():
            g.token_pass(1, 0, 3)
            g.begin(4)

        raw = jnp.dot(h, wq[...].reshape(WIDTH, WIDTH), preferred_element_type=F32)
        raw_o[rows, :] = raw[:, :768]
        cosine, sine = turns(table[rows, :])
        for t in range(2):
            vb[t, rows, :] = raw[:, 768 + t * 128 : 896 + t * 128].astype(BF)
        for t in range(6):
            u = raw[:, t * 128 : (t + 1) * 128]
            n_ = u * unit(u) * (qg[...] if t < 4 else kg[...])
            r = rotate(n_, cosine, sine).astype(BF)
            if t < 4:
                qb[t, rows, :] = r
            else:
                kb[t - 4, rows, :] = r

    @pl.loop(0, 4)
    def _(h):
        @pl.when(h == 0)
        def _():
            g.step(1, 1)
            g.token_pass(1, 3, 6)

        @pl.when(h == 1)
        def _():
            g.step(1, 2)
            g.token_pass(1, 6, 8)
            g.begin(5)

        @pl.when(h == 2)
        def _():
            g.step(1, 3)
            g.step(2, 1)
            g.lines_begin()

        @pl.when(h == 3)
        def _():
            g.step(2, 2)
            g.step(2, 3)

        kv = h // 2
        for i in range(4):
            length = (i + 1) * 256
            rows = slice(i * 256, length)
            s = dims(qb[h, rows, :], kb[kv, :length, :], 1, 1) * (HEAD_SIZE**-0.5 * LOG2E)
            s = lower(s, NEGATIVE_FILL)
            top = jnp.max(s, axis=-1, keepdims=True)
            e = jnp.exp2(s - top)
            sum_e = jnp.sum(e, axis=-1, keepdims=True)
            o = jnp.dot(e.astype(BF), vb[kv, :length, :], preferred_element_type=F32) / sum_e
            ob[rows, pl.ds(pl.multiple_of(h * 128, 128), 128)] = o.astype(BF)
            lane = lax.broadcasted_iota(jnp.int32, (256, 128), 1)
            lse[rows, :] = jnp.where(lane == h, top + jnp.log2(sum_e), lse[rows, :])

    g.y_wait(1)
    s1 = Sum(pa, pb, l1, own, l2, sums, 0)
    s2 = Sum(pc, gqkv, l1b, ownb, l2b, sums, 6)

    @pl.loop(0, 4)
    def _(n):
        rows = pl.ds(pl.multiple_of(n * 256, 256), 256)
        out_w = wo[...].reshape(512, WIDTH)
        pa[rows, :] = jnp.dot(ob[rows, :], out_w, preferred_element_type=F32).astype(BF)
        s1.beside(n)

        @pl.when(n > 0)
        def _():
            s1.across(n - 1)

    s1.across(3)
    g.step(3, 1)
    g.step(3, 2)
    s1.back(0)
    g.step(3, 3)
    g.step(4, 1)
    s1.back(1)
    g.lines_turn()
    g.step(4, 2)
    g.step(4, 3)
    s1.back(2)
    g.step(5, 1)
    g.line_step(False, 1)
    g.step(5, 2)
    g.line_step(True, 1)
    s1.back(3)
    g.step(5, 3)
    g.line_step(False, 2)
    g.line_step(True, 2)
    g.line_step(False, 3)
    g.line_step(True, 3)
    g.y_wait(2, 3, 4, 5)
    s1.close(0)

    @pl.loop(0, 4)
    def _(n):
        s1.ready(n)
        rows = pl.ds(pl.multiple_of(n * 256, 256), 256)
        h = pieces(xf, sorts, 1, n * 4, 4).astype(F32) + pb[rows, :].astype(F32)
        hidden[pl.ds(n * 4, 4)] = h.reshape(4, BLK, WIDTH)
        a = (h * unit(h)).astype(BF)
        pa[rows, :] = a
        wgu = wg[...].reshape(WIDTH, 1536)
        gu = jnp.dot(a, wgu, preferred_element_type=F32)
        gate = gu[:, :768]
        up = gu[:, 768:]
        sig = 1.0 / (1.0 + jnp.exp2(gate * -LOG2E))
        silu = gate * sig
        mb[pl.ds(n * 4, 4)] = (silu * up).astype(BF).reshape(4, BLK, 768)
        cc = pieces(cf, sorts, 1, n * 4, 4)
        cs[rows, :] = cc
        dm = dims(cc, wd[...].reshape(768, WIDTH), 1, 1)
        dg = (dm * up * sig * (1.0 + gate * (1.0 - sig))).astype(BF)
        du = (dm * silu).astype(BF)
        both = jnp.concatenate([dg, du], axis=1)
        dgu[rows, :] = both
        pc[rows, :] = dims(both, wgu, 1, 1).astype(BF)
        s2.beside(n)

        @pl.when(n > 0)
        def _():
            s2.across(n - 1)

    s2.across(3)
    s1.close(1, 2)

    @pl.loop(0, 2)
    def _(n):
        m_all = mb[...].reshape(TOKENS, 768)
        for t in range(2):

            @pl.when(n == t)
            def _():
                v = dims(m_all[:, t * 384 : (t + 1) * 384], cs[...], 0, 0).astype(BF)
                v = v.reshape(2, 2, 96, WIDTH)
                for u in range(2):
                    gd[u, 0, 2 * t : 2 * t + 2] = v[:, u]

    @pl.loop(0, 4)
    def _(n):
        rows = pl.ds(pl.multiple_of(n * 256, 256), 256)
        m = pieces(mb, sorts, 0, n * 4, 4)
        pb[rows, :] = jnp.dot(m, wd[...].reshape(768, WIDTH), preferred_element_type=F32).astype(BF)
        rest[n] = pieces(hidden, sorts, 0, 4 * n + 2 * g.c, 2)

    g.close()
    near = [(q, 2 * z + 1 - y), (2 * x_ + 1 - c, p), (2 * (1 - x_) + c, p)]
    near += [(q, 2 * mod(z + k, 4) + y) for k in (1, 2, 3)]
    for peer in near:
        pl.semaphore_signal(free, inc=1, device_id=peer, device_id_type=MESH)
    s2.back(0)

    s2.back(1)
    pl.semaphore_wait(free, len(near))
    y_send(0)
    for n in range(4):
        h_out.beside(n)

    @pl.loop(0, 4)
    def _(n):
        v = dims(pa[:, pl.ds(pl.multiple_of(n * 256, 256), 256)], dgu[...], 0, 0).astype(BF)
        v = v.reshape(4, 2, 32, 1536)
        for t in range(2):
            ggu[t, n] = v[:, t]

        @pl.when(n == 0)
        def _():
            y_send(1)

        @pl.when(n < 2)
        def _():
            s2.back(n + 2)

    @pl.loop(0, 4)
    def _(n):
        rows = pl.ds(pl.multiple_of(n * 256, 256), 256)
        h = hidden[pl.ds(n * 4, 4)].reshape(256, WIDTH)
        r = unit(h)
        s2.ready(n)
        da = gqkv[n // 2, pl.ds(2 * (n % 2), 2)].reshape(256, WIDTH).astype(F32)
        back = r * da - h * (r * r * r * jnp.mean(h * da, axis=-1, keepdims=True))
        d = cs[rows, :].astype(F32) + back
        hidden[pl.ds(n * 4, 4)] = d.reshape(4, BLK, WIDTH)
        low = d.astype(BF)
        pa[rows, :] = low
        do = dims(low, wo[...].reshape(512, WIDTH), 1, 1).astype(BF)
        cs[rows, :512] = do
        h_out.across(n)

    @pl.loop(0, 2)
    def _(n):
        v = dims(ob[:, pl.ds(pl.multiple_of(n * 256, 256), 256)], pa[...], 0, 0).astype(BF)
        v = v.reshape(2, 2, 64, WIDTH)
        for t in range(2):
            go[t, 0, pl.ds(n * 2, 2)] = v[:, t]

    s2.close(0, 1, 2)
    heads[...] = jnp.zeros_like(heads)
    scale = HEAD_SIZE**-0.5

    def norm_back(dn, u, gain, rows):
        dn = rotate_back(dn, *turns(table[rows, :]))
        r = unit(u)
        gd_ = gain * dn
        du = r * gd_ - u * (r * r * r * jnp.mean(u * gd_, axis=-1, keepdims=True))
        return du.astype(BF), jnp.sum(dn * u * r, axis=0, keepdims=True)

    def result(n, s):
        return s + rest[n]

    def inward(n, s):
        v = xf[pl.ds(4 * n + 2 * c, 2)].reshape(128, WIDTH).astype(F32)
        r = unit(v)
        s = r * s - v * (r * r * r * jnp.mean(v * s, axis=-1, keepdims=True))
        return s + pieces(hidden, sorts, 0, 4 * n + 2 * c, 2)

    @pl.loop(0, 2)
    def _(g):
        dkv[...] = jnp.zeros_like(dkv)
        for t in range(2):
            if t == 0:

                @pl.when(g == 1)
                def _():
                    step(1)
            else:
                for turn in range(2):

                    @pl.when(g == turn)
                    def _():
                        step(2 * turn)
                        if turn == 1:
                            h_out.finish(0, result)
                            h_out.finish(1, result)

            h = g * 2 + t
            lanes = pl.ds(pl.multiple_of(h * 128, 128), 128)
            for i in range(4):
                length = (i + 1) * 256
                rows = slice(i * 256, length)
                qv = qb[h, rows, :]
                kv = kb[g, :length, :]
                dov = cs[rows, lanes]
                s = dims(qv, kv, 1, 1) * (scale * LOG2E)
                pr = lower(jnp.exp2(s - column(lse[rows, :], h)), 0.0)
                dp = dims(dov, vb[g, :length, :], 1, 1)
                delta = jnp.sum(dov.astype(F32) * ob[rows, lanes].astype(F32), axis=-1, keepdims=True)
                ds_ = lower(pr * (dp - delta), 0.0).astype(BF)
                dq = jnp.dot(ds_, kv, preferred_element_type=F32) * scale
                dkv[0, :length, :] += dims(ds_, qv, 0, 0)
                dkv[1, :length, :] += dims(pr.astype(BF), dov, 0, 0)
                du, dgain = norm_back(dq, raw_o[rows, lanes], qg[...], pl.ds(i * 256, 256))
                cf[i * 4 : i * 4 + 4, :, lanes] = du.reshape(4, BLK, 128)
                heads[0:1, :] += dgain
        lanes = pl.ds(pl.multiple_of(512 + g * 128, 128), 128)
        for i in range(4):
            rows = slice(i * 256, (i + 1) * 256)
            du, dgain = norm_back(dkv[0, rows, :] * scale, raw_o[rows, lanes], kg[...], pl.ds(i * 256, 256))
            cf[i * 4 : i * 4 + 4, :, lanes] = du.reshape(4, BLK, 128)
            heads[1:2, :] += dgain
        cf[:, :, pl.ds(pl.multiple_of(768 + g * 128, 128), 128)] = dkv[1].astype(BF).reshape(16, BLK, 128)

    step(3)
    h_out.finish(2, result)
    h_out.finish(3, result)
    hy_copy = remote(heads, hy, hs.at[0], hr.at[0], (q, 2 * z + 1 - y))
    hy_copy.start()

    @pl.loop(0, 4)
    def _(n):
        rows = pl.ds(pl.multiple_of(n * 256, 256), 256)
        d = pieces(cf, sorts, 0, n * 4, 4)
        pc[rows, :] = dims(d, wq[...].reshape(WIDTH, WIDTH), 1, 1).astype(BF)
        h_in.beside(n)

        @pl.when(n > 0)
        def _():
            h_in.across(n - 1)

    h_in.across(3)

    @pl.loop(0, 4)
    def _(n):
        rows = pl.ds(pl.multiple_of(n * 256, 256), 256)
        v = pieces(xf, sorts, 1, n * 4, 4).astype(F32)
        pa[rows, :] = (v * unit(v)).astype(BF)

    @pl.loop(0, 4)
    def _(n):
        v = dims(pa[:, pl.ds(pl.multiple_of(n * 256, 256), 256)], cf[...].reshape(TOKENS, WIDTH), 0, 0).astype(BF)
        v = v.reshape(4, 2, 32, WIDTH)
        for t in range(2):
            gqkv[t, n] = v[:, t]

    step(4)

    def z_heads(k):
        return remote(hz.at[z], hz.at[z], hs.at[k], hr.at[k], (q, 2 * mod(z + k, 4) + y))

    def dp_heads(k):
        return remote(hdp.at[q], hdp.at[q], hs.at[3 + k], hr.at[3 + k], (mod(q + k, 4), p))

    hy_copy.wait_recv()
    hz[z] = heads[...] + hy[...]
    for k in (1, 2, 3):
        z_heads(k).start()
    h_in.finish(0, inward)
    od[...] = sd.z_sum(0)
    for n in range(4):
        step(5 + n)
        cgu.step(n)
        if n < 3:
            h_in.finish(n + 1, inward)
    step(9)
    relay(9)
    for k in (1, 2, 3):
        f = mod(z + 4 - k, 4)
        remote(hz.at[f], hz.at[f], hs.at[k], hr.at[k], (q, p)).wait_recv()
    hdp[q] = hz[0] + hz[1] + hz[2] + hz[3]
    for k in (1, 2, 3):
        dp_heads(k).start()
    oo[...] = so.z_sum(0)

    @pl.loop(0, 4)
    def _(n):
        cqkv.step(n)

    cgu.close()
    for k in (1, 2, 3):
        f = mod(q + 4 - k, 4)
        remote(hdp.at[f], hdp.at[f], hs.at[3 + k], hr.at[3 + k], (q, p)).wait_recv()
    oheads[...] = hdp[0] + hdp[1] + hdp[2] + hdp[3]
    cqkv.close()
    h_out.close()
    h_in.close()
    sd.close(1)
    sgu.close(4)
    so.close(1)
    sqkv.close(4)
    hy_copy.wait_send()
    for k in (1, 2, 3):
        z_heads(k).wait_send()
        dp_heads(k).wait_send()


def layer_call(tok, cot, pos, po, pd, table, qg, kg, *rest):
    sem = pltpu.SemaphoreType.DMA
    shape = jax.ShapeDtypeStruct
    vm = pltpu.VMEM
    full = (TOKENS, WIDTH)
    return pl.pallas_call(
        layer_kernel,
        out_shape=(
            shape((2, 128, WIDTH), BF),
            shape((2, 128, WIDTH), BF),
            shape((96, WIDTH), F32),
            shape((4, 32, 1536), BF),
            shape((64, WIDTH), F32),
            shape((4, 32, WIDTH), BF),
            shape((8, 128), F32),
            shape((8, 128), jnp.int32),
        ),
        in_specs=[ANY] * 5 + [VM] * 10,
        out_specs=(ANY, ANY) + (VM,) * 5 + (ANY,),
        scratch_shapes=[
            vm((16, BLK, WIDTH), BF), vm((16, BLK, WIDTH), BF),
            vm((4, 8, 32, WIDTH), BF), vm((4, 8, 32, 1536), BF),
            vm((8,) + po.shape, BF), vm((8,) + pd.shape, BF),
            vm((TOKENS, 768), F32),
            vm((4, TOKENS, 128), BF), vm((2, TOKENS, 128), BF), vm((2, TOKENS, 128), BF), vm((TOKENS, 512), BF),
            vm((TOKENS, 128), F32), vm((16, BLK, WIDTH), F32), vm((4, 128, WIDTH), F32),
            vm(full, BF), vm(full, BF), vm(full, BF), vm(full, BF),
            vm((16, BLK, 768), BF), vm((TOKENS, 1536), BF),
            vm((2, 1, 4, 96, WIDTH), BF), vm((2, 4, 4, 32, 1536), BF),
            vm((2, TOKENS, 128), F32),
            vm((2, 1, 4, 64, WIDTH), BF), vm((2, 4, 4, 32, WIDTH), BF),
            vm((1, 4, 64, WIDTH), BF), vm((4, 4, 32, WIDTH), BF),
            vm((1, 4, 64, WIDTH), BF), vm((4, 4, 32, WIDTH), BF),
            vm((8, 128), F32), vm((8, 128), F32), vm((4, 8, 128), F32), vm((4, 8, 128), F32),
        ]
        + [vm((4, 128, WIDTH), BF)] * 7
        + [
            pltpu.SMEM((8, 128), jnp.int32), pltpu.SMEM((2, 16), jnp.int32), sem((1,)), pltpu.SemaphoreType.REGULAR, sem((12, 4)),
            sem((10, 10)), sem((4, 4)), sem((7,)), sem((7,)), sem((12, 4)), sem((2,)),
        ]
        + [sem(n) for n in GATHER_SEMS],
        compiler_params=pltpu.CompilerParams(
            collective_id=0, has_side_effects=True, vmem_limit_bytes=VMEM_BYTES
        ),
        name="layer_both_ways",
    )(tok, cot, pos, po, pd, table, qg, kg, *rest)


def whole_sequences(
    tokens, attn_gain, w_query, key_projection, value_projection, query_head_gain, key_gain, w_out,
    mlp_gain, w_gate, w_up, w_down, cotangent, span_order,
):
    pos = jnp.pad(span_order, ((0, 6), (0, 112)))
    gains = attn_gain[None, :], mlp_gain[None, :]
    weights = w_query, key_projection, value_projection, w_gate, w_up
    freqs = BASE ** (-np.arange(HEAD_SIZE // 2) * 2.0 / HEAD_SIZE)
    angles = np.arange(TOKENS)[:, None] * freqs.astype(np.float32)[None, :].astype(np.float64)
    table = np.concatenate([np.cos(angles), np.sin(angles)], axis=1).astype(np.float32)
    qg = query_head_gain.astype(F32)[None, :]
    kg = key_gain.astype(F32)[None, :]
    out, igrad, od, ogu, oo, oqkv, oheads, _ = layer_call(
        tokens.reshape(2, 2, BLK, WIDTH), cotangent.reshape(2, 2, BLK, WIDTH), pos, w_out, w_down,
        table, qg, kg, *gains, *weights,
    )
    return finish(out, igrad, od, ogu, oo, oqkv, oheads, *gains, *weights)


def diagonal(v):
    i = lax.broadcasted_iota(jnp.int32, (32, 32), 0)
    j = lax.broadcasted_iota(jnp.int32, (32, 32), 1)
    return jnp.where(i == j, jnp.broadcast_to(v, (32, 32)), 0.0)


def upright(row):
    return jnp.sum(diagonal(row), axis=1, keepdims=True)


def flat_row(col):
    return jnp.sum(diagonal(col), axis=0, keepdims=True)


def finish_kernel(
    out_i, igrad_i, od_i, ogu, oo_i, oqkv, oheads, ga, gm, w_query, key_projection, value_projection, w_gate, w_up,
    out, igrad, attn, query, key, value, qgain, kgain, oo, mlp, gate, up, od,
):
    out[...] = out_i[...]
    igrad[...] = igrad_i[...]
    od[...] = od_i[...]
    oo[...] = oo_i[...]
    qgain[...] = oheads[0:1, :]
    kgain[...] = oheads[1:2, :]
    for gain, grads, total, todo in (
        (ga, oqkv, attn, ((w_query, query, 0, 512), (key_projection, key, 512, 256), (value_projection, value, 768, 256))),
        (gm, ogu, mlp, ((w_gate, gate, 0, 768), (w_up, up, 768, 768))),
    ):
        g = upright(gain[...].astype(F32))
        dot = jnp.zeros((32, 1), F32)
        for w, o, first, width in todo:
            for t in range(4):
                h = grads[t, :, first : first + width].astype(F32)
                lanes = slice(t * width, (t + 1) * width)
                o[:, lanes] = g * h
                dot = dot + jnp.sum(w[:, lanes].astype(F32) * h, axis=1, keepdims=True)
        total[...] = flat_row(dot)


def finish(*args):
    shape = jax.ShapeDtypeStruct
    ws = args[9:]
    res = pl.pallas_call(
        finish_kernel,
        out_shape=(
            shape(args[0].shape, BF),
            shape(args[1].shape, BF),
            shape((1, 32), F32),
            *[shape(w.shape, F32) for w in ws[:3]],
            shape((1, 128), F32),
            shape((1, 128), F32),
            shape(args[4].shape, F32),
            shape((1, 32), F32),
            *[shape(w.shape, F32) for w in ws[3:]],
            shape(args[2].shape, F32),
        ),
        in_specs=[VM] * 14,
        out_specs=(VM,) * 13,
        name="gains_and_layout",
    )(*args)
    res = list(res)
    for i in (2, 6, 7, 9):
        res[i] = res[i].reshape(-1)
    return tuple(res)


def layer(tokens, *rest):
    whole = (
        lax.axis_size("dp") == 4
        and lax.axis_size("seq") == 8
        and tokens.shape == (2, 128, WIDTH)
        and rest[-1].shape == (2, 16)
    )
    return (whole_sequences if whole else shards)(tokens, *rest)


def solution(mesh):
    return jax.shard_map(
        layer,
        mesh=mesh,
        in_specs=(
            P("dp", "seq", None),
            P(("dp", "seq")),
            P(("dp", "seq"), None),
            P(("dp", "seq"), None),
            P(("dp", "seq"), None),
            P(),
            P(),
            P(("dp", "seq"), None),
            P(("dp", "seq")),
            P(("dp", "seq"), None),
            P(("dp", "seq"), None),
            P(("dp", "seq"), None),
            P("dp", "seq", None),
            P("dp", None),
        ),
        out_specs=(
            P("dp", "seq", None),
            P("dp", "seq", None),
            P(("dp", "seq")),
            P(("dp", "seq"), None),
            P(("dp", "seq"), None),
            P(("dp", "seq"), None),
            P(),
            P(),
            P(("dp", "seq"), None),
            P(("dp", "seq")),
            P(("dp", "seq"), None),
            P(("dp", "seq"), None),
            P(("dp", "seq"), None),
        ),
        check_vma=False,
    )
```

```python
import jax
import jax.numpy as jnp
from jax import lax
from jax.sharding import PartitionSpec as P

import numpy as np
from jax.experimental import pallas as pl
from jax.experimental.pallas import tpu as pltpu

QUERY_HEADS = 16
KEY_VALUE_HEADS = 8
HEAD_SIZE = 128
BLK = 64
MB = 2


EPS = 1e-06
BASE = 1000000.0
NEGATIVE_FILL = -1e30


def from_behind(block, axis, distance):
    devices = range(lax.axis_size(axis))
    route = [((i - distance) % len(devices), i) for i in devices]
    return lax.ppermute(block, axis, route)


def row_norm_apply(v, gain):
    return v * lax.rsqrt(jnp.mean(v * v, axis=-1, keepdims=True) + EPS) * gain


def apply_rotary(v, cosine_table, sine_table):
    half = v.shape[-1] // 2
    first = v[..., :half]
    second = v[..., half:]
    return jnp.concatenate(
        [first * cosine_table - second * sine_table, second * cosine_table + first * sine_table],
        axis=-1,
    )


def matrix_multiply(left, right):
    return jnp.dot(left, right, preferred_element_type=jnp.float32)


def row_product(left, right):
    return lax.dot_general(
        left, right, (((0,), (0,)), ((), ())), preferred_element_type=jnp.float32
    )


def product_backward(left, right):
    return lax.dot_general(
        left, right, (((1,), (1,)), ((), ())), preferred_element_type=jnp.float32
    )


def block_positions(order, start, count):
    places = start + lax.iota(jnp.int32, count)
    which = places // BLK
    hits = (which[:, None] == lax.iota(jnp.int32, order.shape[1])[None, :]).astype(jnp.int32)
    spans = jnp.sum(hits[None, :, :] * order[:, None, :], axis=-1)
    return spans * BLK + places % BLK


def pack_shares(members, count):
    return jnp.concatenate([m.reshape(count, -1) for m in members], axis=1).reshape(-1)


def unpack_shares(flat, members, count):
    pieces = []
    offset = 0
    for m in members:
        length = m.size // count
        share_shape = (m.shape[0] // count,) + tuple(m.shape[1:])
        pieces.append(flat[offset : offset + length].reshape(share_shape))
        offset = offset + length
    return pieces


def shards(
    tokens,
    attn_gain,
    w_query,
    key_projection,
    value_projection,
    query_head_gain,
    key_gain,
    w_out,
    mlp_gain,
    w_gate,
    w_up,
    w_down,
    cotangent,
    span_order,
):
    seq_count = lax.axis_size("seq")
    seq_place = lax.axis_index("seq")
    all_count = lax.axis_size(("dp", "seq"))
    local_length = tokens.shape[1]
    width = tokens.shape[2]
    sequence_permutation = tokens.shape[0] // MB
    query_group = QUERY_HEADS // KEY_VALUE_HEADS
    scale = HEAD_SIZE ** (-0.5)
    freqs = BASE ** (-(lax.iota(jnp.float32, HEAD_SIZE // 2) * 2.0) / HEAD_SIZE)
    query_norm_gain = query_head_gain.astype(jnp.float32)
    kgain = key_gain.astype(jnp.float32)
    sums = None
    outputs = []
    input_grads = []
    for batch in range(MB):
        rows_x = tokens[batch * sequence_permutation : (batch + 1) * sequence_permutation]
        rows_cot = cotangent[batch * sequence_permutation : (batch + 1) * sequence_permutation]
        order = span_order[batch * sequence_permutation : (batch + 1) * sequence_permutation]
        gain_a, wq, key_weight, value_weight, output_weight = (
            lax.all_gather(attn_gain, ("dp", "seq"), axis=0, tiled=True),
            lax.all_gather(w_query, ("dp", "seq"), axis=0, tiled=True),
            lax.all_gather(key_projection, ("dp", "seq"), axis=0, tiled=True),
            lax.all_gather(value_projection, ("dp", "seq"), axis=0, tiled=True),
            lax.all_gather(w_out, ("dp", "seq"), axis=0, tiled=True),
        )
        gain_m, wg, wu, wd = (
            lax.all_gather(mlp_gain, ("dp", "seq"), axis=0, tiled=True),
            lax.all_gather(w_gate, ("dp", "seq"), axis=0, tiled=True),
            lax.all_gather(w_up, ("dp", "seq"), axis=0, tiled=True),
            lax.all_gather(w_down, ("dp", "seq"), axis=0, tiled=True),
        )
        own_pos = block_positions(order, seq_place * local_length, local_length)
        angles = own_pos.astype(jnp.float32)[..., None] * freqs
        cosine_table = jnp.cos(angles)[:, :, None, :]
        sine_table = jnp.sin(angles)[:, :, None, :]

        def query_per_head(raw, gain):
            return apply_rotary(row_norm_apply(raw, gain), cosine_table, sine_table)

        flat_x = rows_x.reshape(-1, width).astype(jnp.float32)
        first_operand = row_norm_apply(flat_x, gain_a.astype(jnp.float32)).astype(jnp.bfloat16)
        query_unrotated = matrix_multiply(first_operand, wq).reshape(
            sequence_permutation, local_length, QUERY_HEADS, HEAD_SIZE
        )
        key_unrotated = matrix_multiply(first_operand, key_weight).reshape(
            sequence_permutation, local_length, KEY_VALUE_HEADS, HEAD_SIZE
        )
        value_reduced = (
            matrix_multiply(first_operand, value_weight)
            .astype(jnp.bfloat16)
            .reshape(sequence_permutation, local_length, KEY_VALUE_HEADS, HEAD_SIZE)
        )
        q_low = (
            query_per_head(query_unrotated, query_norm_gain)
            .astype(jnp.bfloat16)
            .reshape(sequence_permutation, local_length, KEY_VALUE_HEADS, query_group, HEAD_SIZE)
        )
        k_low = query_per_head(key_unrotated, kgain).astype(jnp.bfloat16)
        initial_maximum = jnp.full(
            (sequence_permutation, KEY_VALUE_HEADS, query_group, local_length),
            NEGATIVE_FILL,
            jnp.float32,
        )
        top = initial_maximum
        piece_k = lax.all_gather(k_low, "seq", axis=1, tiled=True)
        piece_v = lax.all_gather(value_reduced, "seq", axis=1, tiled=True)
        key_pos = block_positions(order, jnp.int32(0), piece_k.shape[1])
        visible = key_pos[:, None, None, None, :] <= own_pos[:, None, None, :, None]
        scores = (
            jnp.einsum("sqgrd,skgd->sgrqk", q_low, piece_k, preferred_element_type=jnp.float32)
            * scale
        )
        scores = jnp.where(visible, scores, NEGATIVE_FILL)
        new_top = jnp.maximum(top, jnp.max(scores, axis=-1))
        weights = jnp.exp(scores - new_top[..., None])
        new_total = jnp.sum(weights, axis=-1)
        taken = jnp.einsum(
            "sgrqk,skgd->sqgrd",
            weights.astype(jnp.bfloat16),
            piece_v,
            preferred_element_type=jnp.float32,
        )
        top = new_top
        log_total = top + jnp.log(new_total)
        attn = taken / jnp.transpose(new_total, (0, 3, 1, 2))[..., None]
        o_low = attn.astype(jnp.bfloat16).reshape(
            sequence_permutation * local_length, QUERY_HEADS * HEAD_SIZE
        )
        hidden = flat_x + matrix_multiply(o_low, output_weight)
        gain_second = gain_m.astype(jnp.float32)
        a_second = row_norm_apply(hidden, gain_second).astype(jnp.bfloat16)
        gate = matrix_multiply(a_second, wg)
        up_part = matrix_multiply(a_second, wu)
        mixed = (gate * jax.nn.sigmoid(gate) * up_part).astype(jnp.bfloat16)
        result = hidden + matrix_multiply(mixed, wd)
        outputs.append(
            result.astype(jnp.bfloat16).reshape(sequence_permutation, local_length, width)
        )
        gain_a, wq, key_weight, value_weight, output_weight = (
            lax.all_gather(attn_gain, ("dp", "seq"), axis=0, tiled=True),
            lax.all_gather(w_query, ("dp", "seq"), axis=0, tiled=True),
            lax.all_gather(key_projection, ("dp", "seq"), axis=0, tiled=True),
            lax.all_gather(value_projection, ("dp", "seq"), axis=0, tiled=True),
            lax.all_gather(w_out, ("dp", "seq"), axis=0, tiled=True),
        )
        gain_m, wg, wu, wd = (
            lax.all_gather(mlp_gain, ("dp", "seq"), axis=0, tiled=True),
            lax.all_gather(w_gate, ("dp", "seq"), axis=0, tiled=True),
            lax.all_gather(w_up, ("dp", "seq"), axis=0, tiled=True),
            lax.all_gather(w_down, ("dp", "seq"), axis=0, tiled=True),
        )
        flat_cot = rows_cot.reshape(-1, width)
        grad_down = row_product(mixed, flat_cot)
        d_mixed = product_backward(flat_cot, wd)

        def mix(gate_in, up_in):
            return gate_in * jax.nn.sigmoid(gate_in) * up_in

        _, mix_back = jax.vjp(mix, gate, up_part)
        d_gate, d_up = mix_back(d_mixed)
        gate_low = d_gate.astype(jnp.bfloat16)
        up_low = d_up.astype(jnp.bfloat16)
        grad_gate = row_product(a_second, gate_low)
        grad_up = row_product(a_second, up_low)
        d_second = product_backward(gate_low, wg) + product_backward(up_low, wu)
        _, second_back = jax.vjp(row_norm_apply, hidden, gain_second)
        d_hidden_norm, grad_mlp_gain = second_back(d_second)
        d_hidden = flat_cot.astype(jnp.float32) + d_hidden_norm
        grad_output_reduced = d_hidden.astype(jnp.bfloat16)
        grad_out = row_product(o_low, grad_output_reduced)
        do_low = (
            product_backward(grad_output_reduced, output_weight)
            .astype(jnp.bfloat16)
            .reshape(sequence_permutation, local_length, KEY_VALUE_HEADS, query_group, HEAD_SIZE)
        )
        delta = jnp.transpose(jnp.sum(do_low.astype(jnp.float32) * attn, axis=-1), (0, 2, 3, 1))

        def back_terms(held_k, held_v, visible):
            scores = (
                jnp.einsum("sqgrd,skgd->sgrqk", q_low, held_k, preferred_element_type=jnp.float32)
                * scale
            )
            scores = jnp.where(visible, scores, NEGATIVE_FILL)
            probs = jnp.exp(scores - log_total[..., None])
            d_probs = jnp.einsum(
                "sqgrd,skgd->sgrqk", do_low, held_v, preferred_element_type=jnp.float32
            )
            score_low = (probs * (d_probs - delta[..., None])).astype(jnp.bfloat16)
            probs_low = probs.astype(jnp.bfloat16)
            term_q = scale * jnp.einsum(
                "sgrqk,skgd->sqgrd", score_low, held_k, preferred_element_type=jnp.float32
            )
            term_k = scale * jnp.einsum(
                "sgrqk,sqgrd->skgd", score_low, q_low, preferred_element_type=jnp.float32
            )
            term_v = jnp.einsum(
                "sgrqk,sqgrd->skgd", probs_low, do_low, preferred_element_type=jnp.float32
            )
            return (term_k, term_v, term_q)

        def cycle_step(turn, state):
            held_k, held_v, acc_k, acc_v, acc_q = state
            owner = (seq_place - turn) % seq_count
            key_pos = block_positions(order, owner * local_length, local_length)
            visible = key_pos[:, None, None, None, :] <= own_pos[:, None, None, :, None]
            term_k, term_v, term_q = back_terms(held_k, held_v, visible)
            acc_k, acc_v, acc_q = (acc_k + term_k, acc_v + term_v, acc_q + term_q)
            held_k, held_v = from_behind((held_k, held_v), "seq", 1)
            acc_k, acc_v = (
                from_behind(acc_k.astype(jnp.bfloat16), "seq", 1).astype(acc_k.dtype),
                from_behind(acc_v.astype(jnp.bfloat16), "seq", 1).astype(acc_v.dtype),
            )
            return (held_k, held_v, acc_k, acc_v, acc_q)

        def two_steps(pair, state):
            return cycle_step(2 * pair + 1, cycle_step(2 * pair, state))

        blank_key_value = jnp.zeros(
            (sequence_permutation, local_length, KEY_VALUE_HEADS, HEAD_SIZE), jnp.float32
        )
        blank_query = jnp.zeros(
            (sequence_permutation, local_length, KEY_VALUE_HEADS, query_group, HEAD_SIZE),
            jnp.float32,
        )
        state = lax.fori_loop(
            0,
            seq_count // 2,
            two_steps,
            (k_low, value_reduced, blank_key_value, blank_key_value, blank_query),
        )
        _, _, d_keys, grad_value_rows, d_queries = state
        _, query_back = jax.vjp(query_per_head, query_unrotated, query_norm_gain)
        d_q_raw, grad_qgain = query_back(
            d_queries.reshape(sequence_permutation, local_length, QUERY_HEADS, HEAD_SIZE)
        )
        _, key_back = jax.vjp(query_per_head, key_unrotated, kgain)
        grad_key_unrotated, grad_kgain = key_back(d_keys)
        dq_low = d_q_raw.astype(jnp.bfloat16).reshape(
            sequence_permutation * local_length, QUERY_HEADS * HEAD_SIZE
        )
        grad_key_reduced = grad_key_unrotated.astype(jnp.bfloat16).reshape(
            sequence_permutation * local_length, KEY_VALUE_HEADS * HEAD_SIZE
        )
        grad_value_reduced = grad_value_rows.astype(jnp.bfloat16).reshape(
            sequence_permutation * local_length, KEY_VALUE_HEADS * HEAD_SIZE
        )
        grad_query = row_product(first_operand, dq_low)
        grad_key = row_product(first_operand, grad_key_reduced)
        grad_value = row_product(first_operand, grad_value_reduced)
        d_first = (
            product_backward(dq_low, wq)
            + product_backward(grad_key_reduced, key_weight)
            + product_backward(grad_value_reduced, value_weight)
        )
        _, first_back = jax.vjp(row_norm_apply, flat_x, gain_a.astype(jnp.float32))
        d_x_norm, grad_attn_gain = first_back(d_first)
        input_grads.append(
            (d_hidden + d_x_norm)
            .astype(jnp.bfloat16)
            .reshape(sequence_permutation, local_length, width)
        )
        fresh = (
            grad_attn_gain,
            grad_query,
            grad_key,
            grad_value,
            grad_out,
            grad_mlp_gain,
            grad_gate,
            grad_up,
            grad_down,
            grad_qgain,
            grad_kgain,
        )
        if sums is None:
            sums = fresh
        else:
            sums = tuple((a + b for a, b in zip(sums, fresh)))
    attn_members = (sums[0], sums[1], sums[2], sums[3], sums[4])
    mlp_members = (sums[5], sums[6], sums[7], sums[8])
    attn_flat = lax.psum_scatter(
        pack_shares(attn_members, all_count), ("dp", "seq"), scatter_dimension=0, tiled=True
    )
    mlp_flat = lax.psum_scatter(
        pack_shares(mlp_members, all_count), ("dp", "seq"), scatter_dimension=0, tiled=True
    )
    attn_shares = unpack_shares(attn_flat, attn_members, all_count)
    mlp_shares = unpack_shares(mlp_flat, mlp_members, all_count)
    head_sums = lax.psum((sums[9], sums[10]), ("dp", "seq"))
    return (
        jnp.concatenate(outputs, axis=0),
        jnp.concatenate(input_grads, axis=0),
        attn_shares[0],
        attn_shares[1],
        attn_shares[2],
        attn_shares[3],
        head_sums[0],
        head_sums[1],
        attn_shares[4],
        mlp_shares[0],
        mlp_shares[1],
        mlp_shares[2],
        mlp_shares[3],
    )


BF = jnp.bfloat16
F32 = jnp.float32
MESH = pl.DeviceIdType.MESH
TOKENS = 1024
WIDTH = 1024
LOG2E = 1.4426950408889634
VM = pl.BlockSpec(memory_space=pltpu.VMEM)
SM = pl.BlockSpec(memory_space=pltpu.SMEM)
ANY = pl.BlockSpec(memory_space=pl.ANY)
VMEM_BYTES = 65100 * 1024


def place():
    q = lax.axis_index("dp")
    p = lax.axis_index("seq")
    return q, p, q // 2, lax.rem(q, 2), p // 2, lax.rem(p, 2)


def home_group(x, c, i):
    return 4 * c + 2 * i + (x if i == 0 else 1 - x)


def greet(peers):
    barrier = pltpu.get_barrier_semaphore()
    for peer in peers:
        pl.semaphore_signal(barrier, inc=1, device_id=peer, device_id_type=MESH)
    pl.semaphore_wait(barrier, len(peers))


def remote(src, dst, send, recv, peer):
    return pltpu.make_async_remote_copy(
        src_ref=src, dst_ref=dst, send_sem=send, recv_sem=recv, device_id=peer, device_id_type=MESH
    )


def dims(left, right, lc, rc):
    return lax.dot_general(left, right, (((lc,), (rc,)), ((), ())), preferred_element_type=F32)


def mod(a, n):
    return a % n


def unit(v):
    return lax.rsqrt(jnp.mean(v * v, axis=-1, keepdims=True) + EPS)


def pieces(ref, spots, which, first, count):
    return jnp.concatenate([ref[spots[which, first + t]] for t in range(count)], axis=0)


def turns(table):
    other = pltpu.roll(table, HEAD_SIZE // 2, 1)
    first = lax.broadcasted_iota(jnp.int32, table.shape, 1) < HEAD_SIZE // 2
    return jnp.where(first, table, other), jnp.where(first, -other, table)


def rotate(v, cosine, sine):
    return v * cosine + pltpu.roll(v, HEAD_SIZE // 2, 1) * sine


def rotate_back(v, cosine, sine):
    return v * cosine + pltpu.roll(v * sine, HEAD_SIZE // 2, 1)


def lower(s, fill):
    n = s.shape[0]
    i = lax.broadcasted_iota(jnp.int32, (n, n), 0)
    j = lax.broadcasted_iota(jnp.int32, (n, n), 1)
    width = s.shape[1]
    diag = jnp.where(j <= i, s[:, width - n :], fill)
    return diag if width == n else jnp.concatenate([s[:, : width - n], diag], axis=1)


class Sum:
    def __init__(self, part, total, l1, own, l2, sems, base):
        self.q, self.p, self.x, self.c, _, _ = place()
        self.part, self.total, self.l1, self.own, self.l2 = part, total, l1, own, l2
        self.sems, self.base = sems, base
        self.sib = (2 * self.x + 1 - self.c, self.p)
        self.opp = (2 * (1 - self.x) + self.c, self.p)

    def rows(self, n, c):
        return pl.ds(pl.multiple_of(n * 256 + c * 128, 128), 128)

    def copy(self, step, n):
        s, r = self.sems.at[self.base + 2 * step, n], self.sems.at[self.base + 2 * step + 1, n]
        if step == 0:
            return remote(self.part.at[self.rows(n, 1 - self.c)], self.l1.at[n], s, r, self.sib)
        if step == 1:
            return remote(self.own.at[n], self.l2.at[n], s, r, self.opp)
        mine = self.total_at(n, self.c)
        return remote(mine, mine, s, r, self.sib)

    def total_at(self, n, c):
        if len(self.total.shape) == 2:
            return self.total.at[self.rows(n, c)]
        return self.total.at[(2 * n + c) // 4, (2 * n + c) % 4]

    def beside(self, n):
        self.copy(0, n).start()

    def across(self, n):
        self.copy(0, n).wait_recv()
        mine = self.part[self.rows(n, self.c), :].astype(F32)
        self.own[n] = (mine + self.l1[n].astype(F32)).astype(BF)
        self.copy(1, n).start()

    def back(self, n):
        self.copy(1, n).wait_recv()
        total = self.total_at(n, self.c)
        total[...] = (self.own[n].astype(F32) + self.l2[n].astype(F32)).astype(BF).reshape(total.shape)
        self.copy(2, n).start()

    def ready(self, n):
        other = self.total_at(n, 1 - self.c)
        s, r = self.sems.at[self.base + 4, n], self.sems.at[self.base + 5, n]
        remote(other, other, s, r, self.sib).wait_recv()

    def close(self, *steps):
        @pl.loop(0, 4)
        def _(n):
            for step in steps:
                self.copy(step, n).wait_send()


LINES = 6
PIECES = ((0, None), (2, None), (1, 0), (1, 1), (1, 2), (1, 3), (3, None))


def block(ref, b):
    return ref.at[pl.ds(2 * b, 2)]


class Gather:
    def __init__(self, srcs, dsts, sems):
        self.q, self.p, self.x, self.c, self.z, self.y = place()
        self.tok, self.cot, self.pos, self.pq, self.pg, self.po, self.pd = srcs
        self.xf, self.cf, self.of, *self.w = dsts
        (self.loc, self.ts, self.tr, self.fs, self.fr, self.ps, self.pr,
         self.as_, self.ar, self.zs, self.zr, self.ys, self.yr, self.ls, self.lr) = sems
        q, p, x, c, z, y = self.q, self.p, self.x, self.c, self.z, self.y
        self.owner_x, self.owner_c = mod(y + z, 2), z // 2
        self.is_owner = jnp.logical_and(x == self.owner_x, c == self.owner_c)
        self.cross = jnp.logical_and(x != self.owner_x, c == self.owner_c)
        self.sib = (2 * x + 1 - c, p)
        self.opp = (2 * (1 - x) + c, p)

    def peers(self):
        q, p = self.q, self.p
        return [(mod(q + k, 4), p) for k in (1, 2, 3)] + [(q, mod(p + k, 8)) for k in range(1, 8)]

    def col(self, n):
        return (self.pq, self.pg)[n], self.w[n]

    def own_copy(self, n):
        q, p = self.q, self.p
        if n < 2:
            src, dst = self.col(n)
            return pltpu.make_async_copy(src.at[q], dst.at[q, p], self.loc.at[n])
        return pltpu.make_async_copy((self.po, self.pd)[n - 2], self.w[n].at[p], self.loc.at[n])

    def column_copy(self, n, k):
        q, p = self.q, self.p
        src, dst = self.col(n)
        t = mod(q + k, 4)
        return remote(src.at[t], dst.at[q, p], self.as_.at[n, k - 1], self.ar.at[n, k - 1], (t, p))

    def column_start(self, n):
        for k in (1, 2, 3):
            self.column_copy(n, k).start()

    def column_wait(self, n):
        q, p = self.q, self.p
        src, dst = self.col(n)
        for k in (1, 2, 3):
            f = mod(q + 4 - k, 4)
            remote(src.at[0], dst.at[f, p], self.as_.at[n, k - 1], self.ar.at[n, k - 1], (q, p)).wait_recv()

    def view(self, piece, chunk):
        n, part = PIECES[piece]
        if n >= 2:
            return self.w[n].at[chunk]
        return self.w[n].at[:, chunk] if part is None else self.w[n].at[part, chunk]

    def z_copy(self, piece, src, way):
        v = self.view(piece, 2 * src + self.y)
        s = self.zs.at[piece, src + (4 if way < 0 else 0)]
        return remote(v, v, s, self.zr.at[piece, src], (self.q, 2 * (self.z + way) + self.y))

    def y_copy(self, piece, src):
        v = self.view(piece, 2 * src + self.y)
        return remote(v, v, self.ys.at[piece, src], self.yr.at[piece, src], (self.q, 2 * self.z + 1 - self.y))

    def spread(self, piece, src, up, down):
        if up:

            @pl.when(self.z < 3)
            def _():
                self.z_copy(piece, src, 1).start()

        if down:

            @pl.when(self.z > 0)
            def _():
                self.z_copy(piece, src, -1).start()

        self.y_copy(piece, src).start()

    def begin(self, *pieces_):
        for piece in pieces_:
            self.spread(piece, self.z, True, True)

    def line_copy(self, line, src, way):
        v = self.view(LINES, 2 * src + line)
        s = self.ls.at[line, src + (4 if way < 0 else 0)]
        return remote(v, v, s, self.lr.at[line, src], (self.q, 2 * (self.z + way) + self.y))

    def line_spread(self, line, src, up, down):
        if up:

            @pl.when(self.z < 3)
            def _():
                self.line_copy(line, src, 1).start()

        if down:

            @pl.when(self.z > 0)
            def _():
                self.line_copy(line, src, -1).start()

    def lines_begin(self):
        self.y_copy(LINES, self.z).start()
        self.line_spread(self.y, self.z, True, True)

    def lines_turn(self):
        v = self.view(LINES, 2 * self.z + 1 - self.y)
        remote(v, v, self.ys.at[LINES, self.z], self.yr.at[LINES, self.z], (self.q, self.p)).wait_recv()
        self.line_spread(1 - self.y, self.z, True, True)

    def line_step(self, other, dist):
        line = 1 - self.y if other else self.y
        low, high = self.z - dist, self.z + dist

        @pl.when(low >= 0)
        def _():
            v = self.view(LINES, 2 * low + line)
            remote(v, v, self.ls.at[line, 0], self.lr.at[line, low], (self.q, self.p)).wait_recv()
            self.line_spread(line, low, True, False)

        @pl.when(high < 4)
        def _():
            v = self.view(LINES, 2 * high + line)
            remote(v, v, self.ls.at[line, 0], self.lr.at[line, high], (self.q, self.p)).wait_recv()
            self.line_spread(line, high, False, True)

    def step(self, piece, dist):
        low, high = self.z - dist, self.z + dist

        @pl.when(low >= 0)
        def _():
            v = self.view(piece, 2 * low + self.y)
            remote(v, v, self.zs.at[piece, 0], self.zr.at[piece, low], (self.q, self.p)).wait_recv()
            self.spread(piece, low, True, False)

        @pl.when(high < 4)
        def _():
            v = self.view(piece, 2 * high + self.y)
            remote(v, v, self.zs.at[piece, 0], self.zr.at[piece, high], (self.q, self.p)).wait_recv()
            self.spread(piece, high, False, True)

    def steps(self, *pieces_):
        for piece in pieces_:
            for dist in (1, 2, 3):
                self.step(piece, dist)

    def y_wait(self, *pieces_):
        for piece in pieces_:
            for src in range(4):
                v = self.view(piece, 2 * src + 1 - self.y)
                remote(v, v, self.ys.at[piece, src], self.yr.at[piece, src], (self.q, self.p)).wait_recv()

    def tok_dst(self, a):
        return (self.xf, self.cf)[a]

    def token_copy(self, a, i):
        src, dst = (self.tok, self.cot)[a], self.tok_dst(a)
        goal = home_group(self.x, self.c, i)
        return goal, remote(src.at[i], block(dst, self.p), self.ts.at[a, i], self.tr.at[a, self.p], (self.q, goal))

    def token_local(self, a, i):
        return pltpu.make_async_copy((self.tok, self.cot)[a].at[i], block(self.tok_dst(a), self.p), self.loc.at[4 + a])

    def token_start(self, a):
        for i in range(2):
            goal, cp = self.token_copy(a, i)

            @pl.when(goal != self.p)
            def _():
                cp.start()

            @pl.when(goal == self.p)
            def _():
                self.token_local(a, i).start()

    def token_pass(self, a, first=0, end=8):
        dst = self.tok_dst(a)
        q, p = self.q, self.p

        @pl.when(self.is_owner)
        def _():
            @pl.loop(first, end)
            def _(b):
                @pl.when(b != p)
                def _():
                    remote(block(dst, b), block(dst, b), self.ts.at[a, 0], self.tr.at[a, b], (q, p)).wait_recv()

                @pl.when(b == p)
                def _():
                    self.token_local(a, 0).wait()

                remote(block(dst, b), block(dst, b), self.fs.at[a, 0, b], self.fr.at[a, b], self.sib).start()
                remote(block(dst, b), block(dst, b), self.fs.at[a, 1, b], self.fr.at[a, b], self.opp).start()

        @pl.when(jnp.logical_not(self.is_owner))
        def _():
            @pl.loop(first, end)
            def _(b):
                remote(block(dst, b), block(dst, b), self.fs.at[a, 0, b], self.fr.at[a, b], self.sib).wait_recv()

                @pl.when(self.cross)
                def _():
                    remote(block(dst, b), block(dst, b), self.fs.at[a, 0, b], self.fr.at[a, b], self.sib).start()

    def token_close(self, a):
        dst = self.tok_dst(a)
        q, p = self.q, self.p
        for i in range(2):
            goal, cp = self.token_copy(a, i)

            @pl.when(goal != p)
            def _():
                cp.wait_send()

        @pl.when(self.is_owner)
        def _():
            @pl.loop(0, 8)
            def _(b):
                remote(block(dst, b), block(dst, b), self.fs.at[a, 0, b], self.fr.at[a, b], (q, p)).wait_send()
                remote(block(dst, b), block(dst, b), self.fs.at[a, 1, b], self.fr.at[a, b], (q, p)).wait_send()

        @pl.when(self.cross)
        def _():
            @pl.loop(0, 8)
            def _(b):
                remote(block(dst, b), block(dst, b), self.fs.at[a, 0, b], self.fr.at[a, b], (q, p)).wait_send()

    def pos_copy(self, k):
        return remote(self.pos, self.of, self.ps.at[k], self.pr.at[0], (mod(self.q + k + 1, 4), self.p))

    def pos_start(self):
        @pl.when(self.is_owner)
        def _():
            pltpu.make_async_copy(self.pos, self.of, self.loc.at[6]).start()
            for k in range(3):
                self.pos_copy(k).start()

    def pos_finish(self):
        @pl.when(self.is_owner)
        def _():
            pltpu.make_async_copy(self.pos, self.of, self.loc.at[6]).wait()
            for k in range(3):
                self.pos_copy(k).wait_send()

        @pl.when(jnp.logical_not(self.is_owner))
        def _():
            self.pos_copy(0).wait_recv()

    def close(self):
        for n in range(2):
            for k in (1, 2, 3):
                self.column_copy(n, k).wait_send()
        self.y_copy(LINES, self.z).wait_send()
        for line in range(2):
            for src in range(4):

                @pl.when(jnp.logical_and(self.z < 3, src <= self.z))
                def _():
                    self.line_copy(line, src, 1).wait_send()

                @pl.when(jnp.logical_and(self.z > 0, src >= self.z))
                def _():
                    self.line_copy(line, src, -1).wait_send()

        for piece in range(LINES):
            for src in range(4):
                self.y_copy(piece, src).wait_send()

                @pl.when(jnp.logical_and(self.z < 3, src <= self.z))
                def _():
                    self.z_copy(piece, src, 1).wait_send()

                @pl.when(jnp.logical_and(self.z > 0, src >= self.z))
                def _():
                    self.z_copy(piece, src, -1).wait_send()

        self.token_close(0)
        self.token_close(1)


GATHER_SEMS = ((7,), (2, 2), (2, 8), (2, 2, 8), (2, 8), (3,), (1,), (2, 3), (2, 3), (7, 8), (7, 4), (7, 4), (7, 4), (2, 8), (2, 4))


class Home:
    def __init__(self, part, out, l1, own, l2, sems, here, base):
        self.q, self.p, self.x, self.c, self.z, self.y = place()
        self.part, self.out, self.l1, self.own, self.l2 = part, out, l1, own, l2
        self.sems, self.here, self.base = sems, here, base
        self.owner_x, self.owner_c = mod(self.y + self.z, 2), self.z // 2
        self.keeps = self.x == self.owner_x
        self.sib = (2 * self.x + 1 - self.c, self.p)
        self.opp = (2 * (1 - self.x) + self.c, self.p)
        self.goal_q = 2 * self.owner_x + self.owner_c

    def rows(self, n, c):
        return pl.ds(pl.multiple_of(n * 256 + c * 128, 128), 128)

    def sem(self, k, n):
        return self.sems.at[self.base + k, n]

    def first(self, n):
        return remote(
            self.part.at[self.rows(n, 1 - self.c)], self.l1.at[n], self.sem(0, n), self.sem(1, n), self.sib
        )

    def second(self, n):
        return remote(self.own.at[n], self.l2.at[n], self.sem(2, n), self.sem(3, n), self.opp)

    def third(self, n):
        slot = mod(self.z, 2)
        return remote(
            self.own.at[n], self.out.at[slot], self.sem(4, n), self.sem(5, slot), (self.goal_q, 2 * n + self.c)
        )

    def is_self(self, n):
        return jnp.logical_and(self.goal_q == self.q, 2 * n + self.c == self.p)

    def beside(self, n):
        self.first(n).start()

    def across(self, n):
        self.first(n).wait_recv()
        mine = self.part[self.rows(n, self.c), :].astype(F32)
        self.own[n] = (mine + self.l1[n].astype(F32)).astype(BF)

        @pl.when(jnp.logical_not(self.keeps))
        def _():
            self.second(n).start()

    def finish(self, n, rest):
        @pl.when(self.keeps)
        def _():
            self.second(n).wait_recv()
            s = self.own[n].astype(F32) + self.l2[n].astype(F32)
            self.own[n] = rest(n, s).astype(BF)

            @pl.when(jnp.logical_not(self.is_self(n)))
            def _():
                self.third(n).start()

            @pl.when(self.is_self(n))
            def _():
                cp = pltpu.make_async_copy(self.own.at[n], self.out.at[mod(self.z, 2)], self.here)
                cp.start()
                cp.wait()

    def close(self):
        for i in range(2):
            group = home_group(self.x, self.c, i)
            same = jnp.logical_and(group == self.p, self.y == self.c)

            @pl.when(jnp.logical_not(same))
            def _():
                remote(self.own.at[0], self.out.at[i], self.sem(4, 0), self.sem(5, i), (self.q, self.p)).wait_recv()

        for n in range(4):
            self.first(n).wait_send()

            @pl.when(jnp.logical_not(self.keeps))
            def _():
                self.second(n).wait_send()

            @pl.when(jnp.logical_and(self.keeps, jnp.logical_not(self.is_self(n))))
            def _():
                self.third(n).wait_send()


class Scatter:
    def __init__(self, g, ly, lz, sems, base):
        self.q, self.p, _, _, self.z, self.y = place()
        self.g, self.ly, self.lz, self.sems, self.base = g, ly, lz, sems, base

    def y_copy(self, n):
        s, r = self.sems.at[self.base + n, 0], self.sems.at[self.base + n, 1]
        return remote(self.g.at[1 - self.y, n], self.ly(n), s, r, (self.q, 2 * self.z + 1 - self.y))

    def z_copy(self, n, k):
        t = mod(self.z + k, 4)
        s, r = self.sems.at[self.base + n, 2 * k], self.sems.at[self.base + n, 2 * k + 1]
        return remote(self.ly(n).at[t], self.lz(n).at[k - 1], s, r, (self.q, 2 * t + self.y))

    def y_send(self, n):
        self.y_copy(n).start()

    def z_step(self, n):
        self.y_copy(n).wait_recv()
        ly = self.ly(n)

        @pl.loop(0, 4)
        def _(t):
            ly[t] = (ly[t].astype(F32) + self.g[self.y, n, t].astype(F32)).astype(BF)

        lz = self.lz(n)
        z = self.z

        @pl.when(z != 3)
        def _():
            self.z_copy(n, 1).start()

        @pl.when(z != 0)
        def _():
            self.z_copy(n, 3).start()

        for end, unused in ((0, 0), (3, 2)):

            @pl.when(z == end)
            def _():
                self.z_copy(n, 2).start()
                self.relay_copy(n).start()
                lz[unused] = jnp.zeros(lz.shape[1:], BF)

    def relay_copy(self, n):
        s, r = self.sems.at[self.base + n, 8], self.sems.at[self.base + n, 9]
        near = 1 + self.z // 3
        return remote(self.ly(n).at[3 - self.z], self.lz(n).at[3], s, r, (self.q, 2 * near + self.y))

    def relay(self, n):
        @pl.when(jnp.logical_and(self.z > 0, self.z < 3))
        def _():
            ly, lz = self.ly(n), self.lz(n)
            t = mod(self.z + 2, 4)
            s, r = self.sems.at[self.base + n, 8], self.sems.at[self.base + n, 9]
            remote(ly.at[t], lz.at[3], s, r, (self.q, self.p)).wait_recv()
            ly[t] = (ly[t].astype(F32) + lz[3].astype(F32)).astype(BF)
            self.z_copy(n, 2).start()

    def z_sum(self, n):
        @pl.when(self.z != 0)
        def _():
            self.z_copy(n, 1).wait_recv()

        self.z_copy(n, 2).wait_recv()

        @pl.when(self.z != 3)
        def _():
            self.z_copy(n, 3).wait_recv()

        ly, lz = self.ly(n), self.lz(n)
        return ly[self.z].astype(F32) + lz[0].astype(F32) + lz[1].astype(F32) + lz[2].astype(F32)

    def close(self, count):
        @pl.loop(0, count)
        def _(n):
            self.y_copy(n).wait_send()
            self.z_copy(n, 2).wait_send()

            @pl.when(self.z != 3)
            def _():
                self.z_copy(n, 1).wait_send()

            @pl.when(self.z != 0)
            def _():
                self.z_copy(n, 3).wait_send()

            @pl.when(jnp.logical_or(self.z == 0, self.z == 3))
            def _():
                self.relay_copy(n).wait_send()


class Columns:
    def __init__(self, scatter, out, sems, base, here):
        self.scatter, self.out, self.here = scatter, out, here
        self.sems, self.base = sems, base
        self.q, self.p = scatter.q, scatter.p

    def copy(self, t):
        s, r = self.sems.at[self.base, t], self.sems.at[self.base + 1, self.q]
        return remote(self.scatter.ly(t).at[self.scatter.z], self.out.at[self.q], s, r, (t, self.p))

    def own(self, t):
        return pltpu.make_async_copy(self.scatter.ly(t).at[self.scatter.z], self.out.at[t], self.here)

    def step(self, t):
        s = self.scatter.z_sum(t).astype(BF)
        ly = self.scatter.ly(t)
        ly[self.scatter.z] = s

        @pl.when(t != self.q)
        def _():
            self.copy(t).start()

        @pl.when(t == self.q)
        def _():
            self.own(t).start()

    def close(self):
        for t in range(4):

            @pl.when(t != self.q)
            def _():
                r = self.sems.at[self.base + 1, t]
                remote(self.out.at[t], self.out.at[t], self.sems.at[self.base, t], r, (self.q, self.p)).wait_recv()
                self.copy(t).wait_send()

            @pl.when(t == self.q)
            def _():
                self.own(t).wait()


def column(table, h):
    lane = lax.broadcasted_iota(jnp.int32, table.shape, 1)
    return jnp.sum(jnp.where(lane == h, table, 0.0), axis=1, keepdims=True)


def layer_kernel(
    tok, cot, pos, po, pd, table, qg, kg, ga, gm, w_query, key_projection, value_projection, w_gate, w_up,
    out, igrad, od, ogu, oo, oqkv, oheads, of,
    xf, cf, wq, wg, wo, wd, raw_o, qb, kb, vb, ob, lse, hidden, rest, cs, pa, pb, pc, mb, dgu, gd, ggu,
    dkv, go, gqkv, yo, yqkv, zo, zqkv, sums_d, sums_o, heads, hy, hz, hdp,
    l1, own, l2, l1b, ownb, l2b, l2c, rows_of_two, sorts, sorts_sem, free, sums, gsem, csem, hs, hr, homes, here, kept, *sems,
):
    q, p, x_, c, z, y = place()
    sd = Scatter(gd, lambda n: wd.at[pl.ds(0, 4)], lambda n: wd.at[pl.ds(4, 4)], gsem, 0)
    sgu = Scatter(ggu, lambda n: wg.at[n, pl.ds(0, 4)], lambda n: wg.at[n, pl.ds(4, 4)], gsem, 1)
    so = Scatter(go, lambda n: yo.at[n], lambda n: zo.at[n], gsem, 5)
    sqkv = Scatter(gqkv, lambda n: yqkv.at[n], lambda n: zqkv.at[n], gsem, 6)
    cgu = Columns(sgu, ogu, csem, 0, kept.at[0])
    cqkv = Columns(sqkv, oqkv, csem, 2, kept.at[1])
    h_out = Home(pb, out, l1, own, l2, homes, here.at[0], 0)
    h_in = Home(pc, igrad, l1b, ownb, l2c, homes, here.at[1], 6)
    order = [(sd, 0)] + [(sgu, n) for n in range(4)] + [(so, 0)] + [(sqkv, n) for n in range(4)]

    def y_send(j):
        which, n = order[j]
        which.y_send(n)

    def relay(j):
        which, n = order[j]
        which.relay(n)

    def step(j):
        which, n = order[j]
        which.z_step(n)
        if j + 2 < len(order):
            y_send(j + 2)
        if j > 0:
            relay(j - 1)

    pq, pg = yqkv.at[0], ggu.at[0, 0]
    for gain, dst, todo in (
        (ga, pq, ((w_query, 0, 512), (key_projection, 512, 256), (value_projection, 768, 256))),
        (gm, pg, ((w_gate, 0, 768), (w_up, 768, 768))),
    ):
        up = upright(gain[...].astype(F32))
        for w, first, width in todo:
            for t in range(4):
                v = w[:, t * width : (t + 1) * width].astype(F32) * up
                dst[t, :, first : first + width] = v.astype(BF)
    g = Gather((tok, cot, pos, pq, pg, po, pd), (xf, cf, of, wq, wg, wo, wd), sems)
    peers = [(2 * x_ + cc, mod(p + k, 8)) for k in range(1, 8) for cc in (0, 1)]
    peers += [(mod(q + k, 4), p) for k in (1, 2, 3)]
    greet(peers)
    g.pos_start()
    g.token_start(0)
    g.column_start(0)
    for n in range(4):
        g.own_copy(n).start()
    g.column_start(1)
    g.own_copy(0).wait()
    g.column_wait(0)
    g.begin(0)
    g.pos_finish()
    sort = pltpu.make_async_copy(of, rows_of_two, sorts_sem.at[0])
    sort.start()
    lse[...] = jnp.zeros_like(lse)
    g.step(0, 1)
    g.token_pass(0, 0, 2)
    g.step(0, 2)
    g.token_pass(0, 2, 4)
    g.token_start(1)
    g.step(0, 3)
    g.token_pass(0, 4, 8)
    g.own_copy(2).wait()
    g.begin(1)
    g.own_copy(1).wait()
    g.column_wait(1)
    g.begin(2, 3)
    g.own_copy(3).wait()
    sort.wait()
    slot = mod(z, 2)
    for j in range(16):
        sorts[0, j] = rows_of_two[slot, j]
        where = jnp.int32(0)
        for b in range(16):
            where = jnp.where(rows_of_two[slot, b] == j, b, where)
        sorts[1, j] = where
    g.y_wait(0)

    @pl.loop(0, 4)
    def _(n):
        rows = pl.ds(pl.multiple_of(n * 256, 256), 256)
        v = pieces(xf, sorts, 1, n * 4, 4).astype(F32)
        h = (v * unit(v)).astype(BF)

        @pl.when(n == 2)
        def _():
            g.token_pass(1, 0, 3)
            g.begin(4)

        raw = jnp.dot(h, wq[...].reshape(WIDTH, WIDTH), preferred_element_type=F32)
        raw_o[rows, :] = raw[:, :768]
        cosine, sine = turns(table[rows, :])
        for t in range(2):
            vb[t, rows, :] = raw[:, 768 + t * 128 : 896 + t * 128].astype(BF)
        for t in range(6):
            u = raw[:, t * 128 : (t + 1) * 128]
            n_ = u * unit(u) * (qg[...] if t < 4 else kg[...])
            r = rotate(n_, cosine, sine).astype(BF)
            if t < 4:
                qb[t, rows, :] = r
            else:
                kb[t - 4, rows, :] = r

    @pl.loop(0, 4)
    def _(h):
        @pl.when(h == 0)
        def _():
            g.step(1, 1)
            g.token_pass(1, 3, 6)

        @pl.when(h == 1)
        def _():
            g.step(1, 2)
            g.token_pass(1, 6, 8)
            g.begin(5)

        @pl.when(h == 2)
        def _():
            g.step(1, 3)
            g.step(2, 1)
            g.lines_begin()

        @pl.when(h == 3)
        def _():
            g.step(2, 2)
            g.step(2, 3)

        kv = h // 2
        for i in range(4):
            length = (i + 1) * 256
            rows = slice(i * 256, length)
            s = dims(qb[h, rows, :], kb[kv, :length, :], 1, 1) * (HEAD_SIZE**-0.5 * LOG2E)
            s = lower(s, NEGATIVE_FILL)
            top = jnp.max(s, axis=-1, keepdims=True)
            e = jnp.exp2(s - top)
            sum_e = jnp.sum(e, axis=-1, keepdims=True)
            o = jnp.dot(e.astype(BF), vb[kv, :length, :], preferred_element_type=F32) / sum_e
            ob[rows, pl.ds(pl.multiple_of(h * 128, 128), 128)] = o.astype(BF)
            lane = lax.broadcasted_iota(jnp.int32, (256, 128), 1)
            lse[rows, :] = jnp.where(lane == h, top + jnp.log2(sum_e), lse[rows, :])

    g.y_wait(1)
    s1 = Sum(pa, pb, l1, own, l2, sums, 0)
    s2 = Sum(pc, gqkv, l1b, ownb, l2b, sums, 6)

    @pl.loop(0, 4)
    def _(n):
        rows = pl.ds(pl.multiple_of(n * 256, 256), 256)
        out_w = wo[...].reshape(512, WIDTH)
        pa[rows, :] = jnp.dot(ob[rows, :], out_w, preferred_element_type=F32).astype(BF)
        s1.beside(n)

        @pl.when(n > 0)
        def _():
            s1.across(n - 1)

    s1.across(3)
    g.step(3, 1)
    g.step(3, 2)
    s1.back(0)
    g.step(3, 3)
    g.step(4, 1)
    s1.back(1)
    g.lines_turn()
    g.step(4, 2)
    g.step(4, 3)
    s1.back(2)
    g.step(5, 1)
    g.line_step(False, 1)
    g.step(5, 2)
    g.line_step(True, 1)
    s1.back(3)
    g.step(5, 3)
    g.line_step(False, 2)
    g.line_step(True, 2)
    g.line_step(False, 3)
    g.line_step(True, 3)
    g.y_wait(2, 3, 4, 5)
    s1.close(0)

    @pl.loop(0, 4)
    def _(n):
        s1.ready(n)
        rows = pl.ds(pl.multiple_of(n * 256, 256), 256)
        h = pieces(xf, sorts, 1, n * 4, 4).astype(F32) + pb[rows, :].astype(F32)
        hidden[pl.ds(n * 4, 4)] = h.reshape(4, BLK, WIDTH)
        a = (h * unit(h)).astype(BF)
        pa[rows, :] = a
        wgu = wg[...].reshape(WIDTH, 1536)
        gu = jnp.dot(a, wgu, preferred_element_type=F32)
        gate = gu[:, :768]
        up = gu[:, 768:]
        sig = 1.0 / (1.0 + jnp.exp2(gate * -LOG2E))
        silu = gate * sig
        mb[pl.ds(n * 4, 4)] = (silu * up).astype(BF).reshape(4, BLK, 768)
        cc = pieces(cf, sorts, 1, n * 4, 4)
        cs[rows, :] = cc
        dm = dims(cc, wd[...].reshape(768, WIDTH), 1, 1)
        dg = (dm * up * sig * (1.0 + gate * (1.0 - sig))).astype(BF)
        du = (dm * silu).astype(BF)
        both = jnp.concatenate([dg, du], axis=1)
        dgu[rows, :] = both
        pc[rows, :] = dims(both, wgu, 1, 1).astype(BF)
        s2.beside(n)

        @pl.when(n > 0)
        def _():
            s2.across(n - 1)

    s2.across(3)
    s1.close(1, 2)

    @pl.loop(0, 2)
    def _(n):
        m_all = mb[...].reshape(TOKENS, 768)
        for t in range(2):

            @pl.when(n == t)
            def _():
                v = dims(m_all[:, t * 384 : (t + 1) * 384], cs[...], 0, 0).astype(BF)
                v = v.reshape(2, 2, 96, WIDTH)
                for u in range(2):
                    gd[u, 0, 2 * t : 2 * t + 2] = v[:, u]

    @pl.loop(0, 4)
    def _(n):
        rows = pl.ds(pl.multiple_of(n * 256, 256), 256)
        m = pieces(mb, sorts, 0, n * 4, 4)
        pb[rows, :] = jnp.dot(m, wd[...].reshape(768, WIDTH), preferred_element_type=F32).astype(BF)
        rest[n] = pieces(hidden, sorts, 0, 4 * n + 2 * g.c, 2)

    g.close()
    near = [(q, 2 * z + 1 - y), (2 * x_ + 1 - c, p), (2 * (1 - x_) + c, p)]
    near += [(q, 2 * mod(z + k, 4) + y) for k in (1, 2, 3)]
    for peer in near:
        pl.semaphore_signal(free, inc=1, device_id=peer, device_id_type=MESH)
    s2.back(0)

    s2.back(1)
    pl.semaphore_wait(free, len(near))
    y_send(0)
    for n in range(4):
        h_out.beside(n)

    @pl.loop(0, 4)
    def _(n):
        v = dims(pa[:, pl.ds(pl.multiple_of(n * 256, 256), 256)], dgu[...], 0, 0).astype(BF)
        v = v.reshape(4, 2, 32, 1536)
        for t in range(2):
            ggu[t, n] = v[:, t]

        @pl.when(n == 0)
        def _():
            y_send(1)

        @pl.when(n < 2)
        def _():
            s2.back(n + 2)

    @pl.loop(0, 4)
    def _(n):
        rows = pl.ds(pl.multiple_of(n * 256, 256), 256)
        h = hidden[pl.ds(n * 4, 4)].reshape(256, WIDTH)
        r = unit(h)
        s2.ready(n)
        da = gqkv[n // 2, pl.ds(2 * (n % 2), 2)].reshape(256, WIDTH).astype(F32)
        back = r * da - h * (r * r * r * jnp.mean(h * da, axis=-1, keepdims=True))
        d = cs[rows, :].astype(F32) + back
        hidden[pl.ds(n * 4, 4)] = d.reshape(4, BLK, WIDTH)
        low = d.astype(BF)
        pa[rows, :] = low
        do = dims(low, wo[...].reshape(512, WIDTH), 1, 1).astype(BF)
        cs[rows, :512] = do
        h_out.across(n)

    @pl.loop(0, 2)
    def _(n):
        v = dims(ob[:, pl.ds(pl.multiple_of(n * 256, 256), 256)], pa[...], 0, 0).astype(BF)
        v = v.reshape(2, 2, 64, WIDTH)
        for t in range(2):
            go[t, 0, pl.ds(n * 2, 2)] = v[:, t]

    s2.close(0, 1, 2)
    heads[...] = jnp.zeros_like(heads)
    scale = HEAD_SIZE**-0.5

    def norm_back(dn, u, gain, rows):
        dn = rotate_back(dn, *turns(table[rows, :]))
        r = unit(u)
        gd_ = gain * dn
        du = r * gd_ - u * (r * r * r * jnp.mean(u * gd_, axis=-1, keepdims=True))
        return du.astype(BF), jnp.sum(dn * u * r, axis=0, keepdims=True)

    def result(n, s):
        return s + rest[n]

    def inward(n, s):
        v = xf[pl.ds(4 * n + 2 * c, 2)].reshape(128, WIDTH).astype(F32)
        r = unit(v)
        s = r * s - v * (r * r * r * jnp.mean(v * s, axis=-1, keepdims=True))
        return s + pieces(hidden, sorts, 0, 4 * n + 2 * c, 2)

    @pl.loop(0, 2)
    def _(g):
        dkv[...] = jnp.zeros_like(dkv)
        for t in range(2):
            if t == 0:

                @pl.when(g == 1)
                def _():
                    step(1)
            else:
                for turn in range(2):

                    @pl.when(g == turn)
                    def _():
                        step(2 * turn)
                        if turn == 1:
                            h_out.finish(0, result)
                            h_out.finish(1, result)

            h = g * 2 + t
            lanes = pl.ds(pl.multiple_of(h * 128, 128), 128)
            for i in range(4):
                length = (i + 1) * 256
                rows = slice(i * 256, length)
                qv = qb[h, rows, :]
                kv = kb[g, :length, :]
                dov = cs[rows, lanes]
                s = dims(qv, kv, 1, 1) * (scale * LOG2E)
                pr = lower(jnp.exp2(s - column(lse[rows, :], h)), 0.0)
                dp = dims(dov, vb[g, :length, :], 1, 1)
                delta = jnp.sum(dov.astype(F32) * ob[rows, lanes].astype(F32), axis=-1, keepdims=True)
                ds_ = lower(pr * (dp - delta), 0.0).astype(BF)
                dq = jnp.dot(ds_, kv, preferred_element_type=F32) * scale
                dkv[0, :length, :] += dims(ds_, qv, 0, 0)
                dkv[1, :length, :] += dims(pr.astype(BF), dov, 0, 0)
                du, dgain = norm_back(dq, raw_o[rows, lanes], qg[...], pl.ds(i * 256, 256))
                cf[i * 4 : i * 4 + 4, :, lanes] = du.reshape(4, BLK, 128)
                heads[0:1, :] += dgain
        lanes = pl.ds(pl.multiple_of(512 + g * 128, 128), 128)
        for i in range(4):
            rows = slice(i * 256, (i + 1) * 256)
            du, dgain = norm_back(dkv[0, rows, :] * scale, raw_o[rows, lanes], kg[...], pl.ds(i * 256, 256))
            cf[i * 4 : i * 4 + 4, :, lanes] = du.reshape(4, BLK, 128)
            heads[1:2, :] += dgain
        cf[:, :, pl.ds(pl.multiple_of(768 + g * 128, 128), 128)] = dkv[1].astype(BF).reshape(16, BLK, 128)

    step(3)
    h_out.finish(2, result)
    h_out.finish(3, result)
    hy_copy = remote(heads, hy, hs.at[0], hr.at[0], (q, 2 * z + 1 - y))
    hy_copy.start()

    @pl.loop(0, 4)
    def _(n):
        rows = pl.ds(pl.multiple_of(n * 256, 256), 256)
        d = pieces(cf, sorts, 0, n * 4, 4)
        pc[rows, :] = dims(d, wq[...].reshape(WIDTH, WIDTH), 1, 1).astype(BF)
        h_in.beside(n)

        @pl.when(n > 0)
        def _():
            h_in.across(n - 1)

    h_in.across(3)

    @pl.loop(0, 4)
    def _(n):
        rows = pl.ds(pl.multiple_of(n * 256, 256), 256)
        v = pieces(xf, sorts, 1, n * 4, 4).astype(F32)
        pa[rows, :] = (v * unit(v)).astype(BF)

    @pl.loop(0, 4)
    def _(n):
        v = dims(pa[:, pl.ds(pl.multiple_of(n * 256, 256), 256)], cf[...].reshape(TOKENS, WIDTH), 0, 0).astype(BF)
        v = v.reshape(4, 2, 32, WIDTH)
        for t in range(2):
            gqkv[t, n] = v[:, t]

    step(4)

    def z_heads(k):
        return remote(hz.at[z], hz.at[z], hs.at[k], hr.at[k], (q, 2 * mod(z + k, 4) + y))

    def dp_heads(k):
        return remote(hdp.at[q], hdp.at[q], hs.at[3 + k], hr.at[3 + k], (mod(q + k, 4), p))

    hy_copy.wait()
    hz[z] = heads[...] + hy[...]
    for k in (1, 2, 3):
        z_heads(k).start()
    sums_d[...] = sd.z_sum(0)
    to_d = pltpu.make_async_copy(sums_d, od, kept.at[2])
    to_d.start()
    for n in range(4):
        step(5 + n)
        cgu.step(n)
        if n == 3:
            h_in.finish(0, inward)
    step(9)
    relay(9)
    for n in (1, 2, 3):
        h_in.finish(n, inward)
    for k in (1, 2, 3):
        f = mod(z + 4 - k, 4)
        remote(hz.at[f], hz.at[f], hs.at[k], hr.at[k], (q, p)).wait_recv()
    hdp[q] = hz[0] + hz[1] + hz[2] + hz[3]
    for k in (1, 2, 3):
        dp_heads(k).start()
    sums_o[...] = so.z_sum(0)
    to_o = pltpu.make_async_copy(sums_o, oo, kept.at[3])
    to_o.start()

    @pl.loop(0, 4)
    def _(n):
        cqkv.step(n)

    cgu.close()
    for k in (1, 2, 3):
        f = mod(q + 4 - k, 4)
        remote(hdp.at[f], hdp.at[f], hs.at[3 + k], hr.at[3 + k], (q, p)).wait_recv()
    heads[...] = hdp[0] + hdp[1] + hdp[2] + hdp[3]
    to_h = pltpu.make_async_copy(heads, oheads, kept.at[4])
    to_h.start()
    cqkv.close()
    h_out.close()
    h_in.close()
    sd.close(1)
    sgu.close(4)
    so.close(1)
    sqkv.close(4)
    for cp in (to_d, to_o, to_h):
        cp.wait()
    for k in (1, 2, 3):
        z_heads(k).wait_send()
        dp_heads(k).wait_send()


def layer_call(tok, cot, pos, po, pd, table, qg, kg, *rest):
    sem = pltpu.SemaphoreType.DMA
    shape = jax.ShapeDtypeStruct
    vm = pltpu.VMEM
    full = (TOKENS, WIDTH)
    return pl.pallas_call(
        layer_kernel,
        out_shape=(
            shape((2, 128, WIDTH), BF),
            shape((2, 128, WIDTH), BF),
            shape((96, WIDTH), F32),
            shape((4, 32, 1536), BF),
            shape((64, WIDTH), F32),
            shape((4, 32, WIDTH), BF),
            shape((8, 128), F32),
            shape((8, 128), jnp.int32),
        ),
        in_specs=[ANY] * 5 + [VM] * 10,
        out_specs=(ANY,) * 8,
        scratch_shapes=[
            vm((16, BLK, WIDTH), BF), vm((16, BLK, WIDTH), BF),
            vm((4, 8, 32, WIDTH), BF), vm((4, 8, 32, 1536), BF),
            vm((8,) + po.shape, BF), vm((8,) + pd.shape, BF),
            vm((TOKENS, 768), F32),
            vm((4, TOKENS, 128), BF), vm((2, TOKENS, 128), BF), vm((2, TOKENS, 128), BF), vm((TOKENS, 512), BF),
            vm((TOKENS, 128), F32), vm((16, BLK, WIDTH), F32), vm((4, 128, WIDTH), F32),
            vm(full, BF), vm(full, BF), vm(full, BF), vm(full, BF),
            vm((16, BLK, 768), BF), vm((TOKENS, 1536), BF),
            vm((2, 1, 4, 96, WIDTH), BF), vm((2, 4, 4, 32, 1536), BF),
            vm((2, TOKENS, 128), F32),
            vm((2, 1, 4, 64, WIDTH), BF), vm((2, 4, 4, 32, WIDTH), BF),
            vm((1, 4, 64, WIDTH), BF), vm((4, 4, 32, WIDTH), BF),
            vm((1, 4, 64, WIDTH), BF), vm((4, 4, 32, WIDTH), BF),
            vm((96, WIDTH), F32), vm((64, WIDTH), F32), vm((8, 128), F32), vm((8, 128), F32), vm((4, 8, 128), F32), vm((4, 8, 128), F32),
        ]
        + [vm((4, 128, WIDTH), BF)] * 7
        + [
            pltpu.SMEM((8, 128), jnp.int32), pltpu.SMEM((2, 16), jnp.int32), sem((1,)), pltpu.SemaphoreType.REGULAR, sem((12, 4)),
            sem((10, 10)), sem((4, 4)), sem((7,)), sem((7,)), sem((12, 4)), sem((2,)), sem((5,)),
        ]
        + [sem(n) for n in GATHER_SEMS],
        compiler_params=pltpu.CompilerParams(
            collective_id=0, has_side_effects=True, vmem_limit_bytes=VMEM_BYTES
        ),
        name="layer_both_ways",
    )(tok, cot, pos, po, pd, table, qg, kg, *rest)


def whole_sequences(
    tokens, attn_gain, w_query, key_projection, value_projection, query_head_gain, key_gain, w_out,
    mlp_gain, w_gate, w_up, w_down, cotangent, span_order,
):
    pos = jnp.pad(span_order, ((0, 6), (0, 112)))
    gains = attn_gain[None, :], mlp_gain[None, :]
    weights = w_query, key_projection, value_projection, w_gate, w_up
    freqs = BASE ** (-np.arange(HEAD_SIZE // 2) * 2.0 / HEAD_SIZE)
    angles = np.arange(TOKENS)[:, None] * freqs.astype(np.float32)[None, :].astype(np.float64)
    table = np.concatenate([np.cos(angles), np.sin(angles)], axis=1).astype(np.float32)
    qg = query_head_gain.astype(F32)[None, :]
    kg = key_gain.astype(F32)[None, :]
    out, igrad, od, ogu, oo, oqkv, oheads, _ = layer_call(
        tokens.reshape(2, 2, BLK, WIDTH), cotangent.reshape(2, 2, BLK, WIDTH), pos, w_out, w_down,
        table, qg, kg, *gains, *weights,
    )
    return finish(out, igrad, od, ogu, oo, oqkv, oheads, *gains, *weights)


def diagonal(v):
    i = lax.broadcasted_iota(jnp.int32, (32, 32), 0)
    j = lax.broadcasted_iota(jnp.int32, (32, 32), 1)
    return jnp.where(i == j, jnp.broadcast_to(v, (32, 32)), 0.0)


def upright(row):
    return jnp.sum(diagonal(row), axis=1, keepdims=True)


def flat_row(col):
    return jnp.sum(diagonal(col), axis=0, keepdims=True)


def finish_kernel(
    out_i, igrad_i, od_i, ogu, oo_i, oqkv, oheads, ga, gm, w_query, key_projection, value_projection, w_gate, w_up,
    out, igrad, attn, query, key, value, qgain, kgain, oo, mlp, gate, up, od,
):
    out[...] = out_i[...]
    igrad[...] = igrad_i[...]
    od[...] = od_i[...]
    oo[...] = oo_i[...]
    qgain[...] = oheads[0:1, :]
    kgain[...] = oheads[1:2, :]
    for gain, grads, total, todo in (
        (ga, oqkv, attn, ((w_query, query, 0, 512), (key_projection, key, 512, 256), (value_projection, value, 768, 256))),
        (gm, ogu, mlp, ((w_gate, gate, 0, 768), (w_up, up, 768, 768))),
    ):
        g = upright(gain[...].astype(F32))
        dot = jnp.zeros((32, 1), F32)
        for w, o, first, width in todo:
            for t in range(4):
                h = grads[t, :, first : first + width].astype(F32)
                lanes = slice(t * width, (t + 1) * width)
                o[:, lanes] = g * h
                dot = dot + jnp.sum(w[:, lanes].astype(F32) * h, axis=1, keepdims=True)
        total[...] = flat_row(dot)


def finish(*args):
    shape = jax.ShapeDtypeStruct
    ws = args[9:]
    res = pl.pallas_call(
        finish_kernel,
        out_shape=(
            shape(args[0].shape, BF),
            shape(args[1].shape, BF),
            shape((1, 32), F32),
            *[shape(w.shape, F32) for w in ws[:3]],
            shape((1, 128), F32),
            shape((1, 128), F32),
            shape(args[4].shape, F32),
            shape((1, 32), F32),
            *[shape(w.shape, F32) for w in ws[3:]],
            shape(args[2].shape, F32),
        ),
        in_specs=[VM] * 14,
        out_specs=(VM,) * 13,
        name="gains_and_layout",
    )(*args)
    res = list(res)
    for i in (2, 6, 7, 9):
        res[i] = res[i].reshape(-1)
    return tuple(res)


def layer(tokens, *rest):
    whole = (
        lax.axis_size("dp") == 4
        and lax.axis_size("seq") == 8
        and tokens.shape == (2, 128, WIDTH)
        and rest[-1].shape == (2, 16)
    )
    return (whole_sequences if whole else shards)(tokens, *rest)


def solution(mesh):
    return jax.shard_map(
        layer,
        mesh=mesh,
        in_specs=(
            P("dp", "seq", None),
            P(("dp", "seq")),
            P(("dp", "seq"), None),
            P(("dp", "seq"), None),
            P(("dp", "seq"), None),
            P(),
            P(),
            P(("dp", "seq"), None),
            P(("dp", "seq")),
            P(("dp", "seq"), None),
            P(("dp", "seq"), None),
            P(("dp", "seq"), None),
            P("dp", "seq", None),
            P("dp", None),
        ),
        out_specs=(
            P("dp", "seq", None),
            P("dp", "seq", None),
            P(("dp", "seq")),
            P(("dp", "seq"), None),
            P(("dp", "seq"), None),
            P(("dp", "seq"), None),
            P(),
            P(),
            P(("dp", "seq"), None),
            P(("dp", "seq")),
            P(("dp", "seq"), None),
            P(("dp", "seq"), None),
            P(("dp", "seq"), None),
        ),
        check_vma=False,
    )
```

```python
import jax
import jax.numpy as jnp
from jax import lax
from jax.sharding import PartitionSpec as P

import numpy as np
from jax.experimental import pallas as pl
from jax.experimental.pallas import tpu as pltpu

QUERY_HEADS = 16
KEY_VALUE_HEADS = 8
HEAD_SIZE = 128
BLK = 64
MB = 2


EPS = 1e-06
BASE = 1000000.0
NEGATIVE_FILL = -1e30


def from_behind(block, axis, distance):
    devices = range(lax.axis_size(axis))
    route = [((i - distance) % len(devices), i) for i in devices]
    return lax.ppermute(block, axis, route)


def row_norm_apply(v, gain):
    return v * lax.rsqrt(jnp.mean(v * v, axis=-1, keepdims=True) + EPS) * gain


def apply_rotary(v, cosine_table, sine_table):
    half = v.shape[-1] // 2
    first = v[..., :half]
    second = v[..., half:]
    return jnp.concatenate(
        [first * cosine_table - second * sine_table, second * cosine_table + first * sine_table],
        axis=-1,
    )


def matrix_multiply(left, right):
    return jnp.dot(left, right, preferred_element_type=jnp.float32)


def row_product(left, right):
    return lax.dot_general(
        left, right, (((0,), (0,)), ((), ())), preferred_element_type=jnp.float32
    )


def product_backward(left, right):
    return lax.dot_general(
        left, right, (((1,), (1,)), ((), ())), preferred_element_type=jnp.float32
    )


def block_positions(order, start, count):
    places = start + lax.iota(jnp.int32, count)
    which = places // BLK
    hits = (which[:, None] == lax.iota(jnp.int32, order.shape[1])[None, :]).astype(jnp.int32)
    spans = jnp.sum(hits[None, :, :] * order[:, None, :], axis=-1)
    return spans * BLK + places % BLK


def pack_shares(members, count):
    return jnp.concatenate([m.reshape(count, -1) for m in members], axis=1).reshape(-1)


def unpack_shares(flat, members, count):
    pieces = []
    offset = 0
    for m in members:
        length = m.size // count
        share_shape = (m.shape[0] // count,) + tuple(m.shape[1:])
        pieces.append(flat[offset : offset + length].reshape(share_shape))
        offset = offset + length
    return pieces


def shards(
    tokens,
    attn_gain,
    w_query,
    key_projection,
    value_projection,
    query_head_gain,
    key_gain,
    w_out,
    mlp_gain,
    w_gate,
    w_up,
    w_down,
    cotangent,
    span_order,
):
    seq_count = lax.axis_size("seq")
    seq_place = lax.axis_index("seq")
    all_count = lax.axis_size(("dp", "seq"))
    local_length = tokens.shape[1]
    width = tokens.shape[2]
    sequence_permutation = tokens.shape[0] // MB
    query_group = QUERY_HEADS // KEY_VALUE_HEADS
    scale = HEAD_SIZE ** (-0.5)
    freqs = BASE ** (-(lax.iota(jnp.float32, HEAD_SIZE // 2) * 2.0) / HEAD_SIZE)
    query_norm_gain = query_head_gain.astype(jnp.float32)
    kgain = key_gain.astype(jnp.float32)
    sums = None
    outputs = []
    input_grads = []
    for batch in range(MB):
        rows_x = tokens[batch * sequence_permutation : (batch + 1) * sequence_permutation]
        rows_cot = cotangent[batch * sequence_permutation : (batch + 1) * sequence_permutation]
        order = span_order[batch * sequence_permutation : (batch + 1) * sequence_permutation]
        gain_a, wq, key_weight, value_weight, output_weight = (
            lax.all_gather(attn_gain, ("dp", "seq"), axis=0, tiled=True),
            lax.all_gather(w_query, ("dp", "seq"), axis=0, tiled=True),
            lax.all_gather(key_projection, ("dp", "seq"), axis=0, tiled=True),
            lax.all_gather(value_projection, ("dp", "seq"), axis=0, tiled=True),
            lax.all_gather(w_out, ("dp", "seq"), axis=0, tiled=True),
        )
        gain_m, wg, wu, wd = (
            lax.all_gather(mlp_gain, ("dp", "seq"), axis=0, tiled=True),
            lax.all_gather(w_gate, ("dp", "seq"), axis=0, tiled=True),
            lax.all_gather(w_up, ("dp", "seq"), axis=0, tiled=True),
            lax.all_gather(w_down, ("dp", "seq"), axis=0, tiled=True),
        )
        own_pos = block_positions(order, seq_place * local_length, local_length)
        angles = own_pos.astype(jnp.float32)[..., None] * freqs
        cosine_table = jnp.cos(angles)[:, :, None, :]
        sine_table = jnp.sin(angles)[:, :, None, :]

        def query_per_head(raw, gain):
            return apply_rotary(row_norm_apply(raw, gain), cosine_table, sine_table)

        flat_x = rows_x.reshape(-1, width).astype(jnp.float32)
        first_operand = row_norm_apply(flat_x, gain_a.astype(jnp.float32)).astype(jnp.bfloat16)
        query_unrotated = matrix_multiply(first_operand, wq).reshape(
            sequence_permutation, local_length, QUERY_HEADS, HEAD_SIZE
        )
        key_unrotated = matrix_multiply(first_operand, key_weight).reshape(
            sequence_permutation, local_length, KEY_VALUE_HEADS, HEAD_SIZE
        )
        value_reduced = (
            matrix_multiply(first_operand, value_weight)
            .astype(jnp.bfloat16)
            .reshape(sequence_permutation, local_length, KEY_VALUE_HEADS, HEAD_SIZE)
        )
        q_low = (
            query_per_head(query_unrotated, query_norm_gain)
            .astype(jnp.bfloat16)
            .reshape(sequence_permutation, local_length, KEY_VALUE_HEADS, query_group, HEAD_SIZE)
        )
        k_low = query_per_head(key_unrotated, kgain).astype(jnp.bfloat16)
        initial_maximum = jnp.full(
            (sequence_permutation, KEY_VALUE_HEADS, query_group, local_length),
            NEGATIVE_FILL,
            jnp.float32,
        )
        top = initial_maximum
        piece_k = lax.all_gather(k_low, "seq", axis=1, tiled=True)
        piece_v = lax.all_gather(value_reduced, "seq", axis=1, tiled=True)
        key_pos = block_positions(order, jnp.int32(0), piece_k.shape[1])
        visible = key_pos[:, None, None, None, :] <= own_pos[:, None, None, :, None]
        scores = (
            jnp.einsum("sqgrd,skgd->sgrqk", q_low, piece_k, preferred_element_type=jnp.float32)
            * scale
        )
        scores = jnp.where(visible, scores, NEGATIVE_FILL)
        new_top = jnp.maximum(top, jnp.max(scores, axis=-1))
        weights = jnp.exp(scores - new_top[..., None])
        new_total = jnp.sum(weights, axis=-1)
        taken = jnp.einsum(
            "sgrqk,skgd->sqgrd",
            weights.astype(jnp.bfloat16),
            piece_v,
            preferred_element_type=jnp.float32,
        )
        top = new_top
        log_total = top + jnp.log(new_total)
        attn = taken / jnp.transpose(new_total, (0, 3, 1, 2))[..., None]
        o_low = attn.astype(jnp.bfloat16).reshape(
            sequence_permutation * local_length, QUERY_HEADS * HEAD_SIZE
        )
        hidden = flat_x + matrix_multiply(o_low, output_weight)
        gain_second = gain_m.astype(jnp.float32)
        a_second = row_norm_apply(hidden, gain_second).astype(jnp.bfloat16)
        gate = matrix_multiply(a_second, wg)
        up_part = matrix_multiply(a_second, wu)
        mixed = (gate * jax.nn.sigmoid(gate) * up_part).astype(jnp.bfloat16)
        result = hidden + matrix_multiply(mixed, wd)
        outputs.append(
            result.astype(jnp.bfloat16).reshape(sequence_permutation, local_length, width)
        )
        gain_a, wq, key_weight, value_weight, output_weight = (
            lax.all_gather(attn_gain, ("dp", "seq"), axis=0, tiled=True),
            lax.all_gather(w_query, ("dp", "seq"), axis=0, tiled=True),
            lax.all_gather(key_projection, ("dp", "seq"), axis=0, tiled=True),
            lax.all_gather(value_projection, ("dp", "seq"), axis=0, tiled=True),
            lax.all_gather(w_out, ("dp", "seq"), axis=0, tiled=True),
        )
        gain_m, wg, wu, wd = (
            lax.all_gather(mlp_gain, ("dp", "seq"), axis=0, tiled=True),
            lax.all_gather(w_gate, ("dp", "seq"), axis=0, tiled=True),
            lax.all_gather(w_up, ("dp", "seq"), axis=0, tiled=True),
            lax.all_gather(w_down, ("dp", "seq"), axis=0, tiled=True),
        )
        flat_cot = rows_cot.reshape(-1, width)
        grad_down = row_product(mixed, flat_cot)
        d_mixed = product_backward(flat_cot, wd)

        def mix(gate_in, up_in):
            return gate_in * jax.nn.sigmoid(gate_in) * up_in

        _, mix_back = jax.vjp(mix, gate, up_part)
        d_gate, d_up = mix_back(d_mixed)
        gate_low = d_gate.astype(jnp.bfloat16)
        up_low = d_up.astype(jnp.bfloat16)
        grad_gate = row_product(a_second, gate_low)
        grad_up = row_product(a_second, up_low)
        d_second = product_backward(gate_low, wg) + product_backward(up_low, wu)
        _, second_back = jax.vjp(row_norm_apply, hidden, gain_second)
        d_hidden_norm, grad_mlp_gain = second_back(d_second)
        d_hidden = flat_cot.astype(jnp.float32) + d_hidden_norm
        grad_output_reduced = d_hidden.astype(jnp.bfloat16)
        grad_out = row_product(o_low, grad_output_reduced)
        do_low = (
            product_backward(grad_output_reduced, output_weight)
            .astype(jnp.bfloat16)
            .reshape(sequence_permutation, local_length, KEY_VALUE_HEADS, query_group, HEAD_SIZE)
        )
        delta = jnp.transpose(jnp.sum(do_low.astype(jnp.float32) * attn, axis=-1), (0, 2, 3, 1))

        def back_terms(held_k, held_v, visible):
            scores = (
                jnp.einsum("sqgrd,skgd->sgrqk", q_low, held_k, preferred_element_type=jnp.float32)
                * scale
            )
            scores = jnp.where(visible, scores, NEGATIVE_FILL)
            probs = jnp.exp(scores - log_total[..., None])
            d_probs = jnp.einsum(
                "sqgrd,skgd->sgrqk", do_low, held_v, preferred_element_type=jnp.float32
            )
            score_low = (probs * (d_probs - delta[..., None])).astype(jnp.bfloat16)
            probs_low = probs.astype(jnp.bfloat16)
            term_q = scale * jnp.einsum(
                "sgrqk,skgd->sqgrd", score_low, held_k, preferred_element_type=jnp.float32
            )
            term_k = scale * jnp.einsum(
                "sgrqk,sqgrd->skgd", score_low, q_low, preferred_element_type=jnp.float32
            )
            term_v = jnp.einsum(
                "sgrqk,sqgrd->skgd", probs_low, do_low, preferred_element_type=jnp.float32
            )
            return (term_k, term_v, term_q)

        def cycle_step(turn, state):
            held_k, held_v, acc_k, acc_v, acc_q = state
            owner = (seq_place - turn) % seq_count
            key_pos = block_positions(order, owner * local_length, local_length)
            visible = key_pos[:, None, None, None, :] <= own_pos[:, None, None, :, None]
            term_k, term_v, term_q = back_terms(held_k, held_v, visible)
            acc_k, acc_v, acc_q = (acc_k + term_k, acc_v + term_v, acc_q + term_q)
            held_k, held_v = from_behind((held_k, held_v), "seq", 1)
            acc_k, acc_v = (
                from_behind(acc_k.astype(jnp.bfloat16), "seq", 1).astype(acc_k.dtype),
                from_behind(acc_v.astype(jnp.bfloat16), "seq", 1).astype(acc_v.dtype),
            )
            return (held_k, held_v, acc_k, acc_v, acc_q)

        def two_steps(pair, state):
            return cycle_step(2 * pair + 1, cycle_step(2 * pair, state))

        blank_key_value = jnp.zeros(
            (sequence_permutation, local_length, KEY_VALUE_HEADS, HEAD_SIZE), jnp.float32
        )
        blank_query = jnp.zeros(
            (sequence_permutation, local_length, KEY_VALUE_HEADS, query_group, HEAD_SIZE),
            jnp.float32,
        )
        state = lax.fori_loop(
            0,
            seq_count // 2,
            two_steps,
            (k_low, value_reduced, blank_key_value, blank_key_value, blank_query),
        )
        _, _, d_keys, grad_value_rows, d_queries = state
        _, query_back = jax.vjp(query_per_head, query_unrotated, query_norm_gain)
        d_q_raw, grad_qgain = query_back(
            d_queries.reshape(sequence_permutation, local_length, QUERY_HEADS, HEAD_SIZE)
        )
        _, key_back = jax.vjp(query_per_head, key_unrotated, kgain)
        grad_key_unrotated, grad_kgain = key_back(d_keys)
        dq_low = d_q_raw.astype(jnp.bfloat16).reshape(
            sequence_permutation * local_length, QUERY_HEADS * HEAD_SIZE
        )
        grad_key_reduced = grad_key_unrotated.astype(jnp.bfloat16).reshape(
            sequence_permutation * local_length, KEY_VALUE_HEADS * HEAD_SIZE
        )
        grad_value_reduced = grad_value_rows.astype(jnp.bfloat16).reshape(
            sequence_permutation * local_length, KEY_VALUE_HEADS * HEAD_SIZE
        )
        grad_query = row_product(first_operand, dq_low)
        grad_key = row_product(first_operand, grad_key_reduced)
        grad_value = row_product(first_operand, grad_value_reduced)
        d_first = (
            product_backward(dq_low, wq)
            + product_backward(grad_key_reduced, key_weight)
            + product_backward(grad_value_reduced, value_weight)
        )
        _, first_back = jax.vjp(row_norm_apply, flat_x, gain_a.astype(jnp.float32))
        d_x_norm, grad_attn_gain = first_back(d_first)
        input_grads.append(
            (d_hidden + d_x_norm)
            .astype(jnp.bfloat16)
            .reshape(sequence_permutation, local_length, width)
        )
        fresh = (
            grad_attn_gain,
            grad_query,
            grad_key,
            grad_value,
            grad_out,
            grad_mlp_gain,
            grad_gate,
            grad_up,
            grad_down,
            grad_qgain,
            grad_kgain,
        )
        if sums is None:
            sums = fresh
        else:
            sums = tuple((a + b for a, b in zip(sums, fresh)))
    attn_members = (sums[0], sums[1], sums[2], sums[3], sums[4])
    mlp_members = (sums[5], sums[6], sums[7], sums[8])
    attn_flat = lax.psum_scatter(
        pack_shares(attn_members, all_count), ("dp", "seq"), scatter_dimension=0, tiled=True
    )
    mlp_flat = lax.psum_scatter(
        pack_shares(mlp_members, all_count), ("dp", "seq"), scatter_dimension=0, tiled=True
    )
    attn_shares = unpack_shares(attn_flat, attn_members, all_count)
    mlp_shares = unpack_shares(mlp_flat, mlp_members, all_count)
    head_sums = lax.psum((sums[9], sums[10]), ("dp", "seq"))
    return (
        jnp.concatenate(outputs, axis=0),
        jnp.concatenate(input_grads, axis=0),
        attn_shares[0],
        attn_shares[1],
        attn_shares[2],
        attn_shares[3],
        head_sums[0],
        head_sums[1],
        attn_shares[4],
        mlp_shares[0],
        mlp_shares[1],
        mlp_shares[2],
        mlp_shares[3],
    )


BF = jnp.bfloat16
F32 = jnp.float32
MESH = pl.DeviceIdType.MESH
TOKENS = 1024
WIDTH = 1024
LOG2E = 1.4426950408889634
VM = pl.BlockSpec(memory_space=pltpu.VMEM)
SM = pl.BlockSpec(memory_space=pltpu.SMEM)
ANY = pl.BlockSpec(memory_space=pl.ANY)
VMEM_BYTES = 65100 * 1024


def place():
    q = lax.axis_index("dp")
    p = lax.axis_index("seq")
    return q, p, q // 2, lax.rem(q, 2), p // 2, lax.rem(p, 2)


def home_group(x, c, i):
    return 4 * c + 2 * i + (x if i == 0 else 1 - x)


def greet(peers):
    barrier = pltpu.get_barrier_semaphore()
    for peer in peers:
        pl.semaphore_signal(barrier, inc=1, device_id=peer, device_id_type=MESH)
    pl.semaphore_wait(barrier, len(peers))


def remote(src, dst, send, recv, peer):
    return pltpu.make_async_remote_copy(
        src_ref=src, dst_ref=dst, send_sem=send, recv_sem=recv, device_id=peer, device_id_type=MESH
    )


def dims(left, right, lc, rc):
    return lax.dot_general(left, right, (((lc,), (rc,)), ((), ())), preferred_element_type=F32)


def mod(a, n):
    return a % n


def unit(v):
    return lax.rsqrt(jnp.mean(v * v, axis=-1, keepdims=True) + EPS)


def pieces(ref, spots, which, first, count):
    return jnp.concatenate([ref[spots[which, first + t]] for t in range(count)], axis=0)


def turns(table):
    other = pltpu.roll(table, HEAD_SIZE // 2, 1)
    first = lax.broadcasted_iota(jnp.int32, table.shape, 1) < HEAD_SIZE // 2
    return jnp.where(first, table, other), jnp.where(first, -other, table)


def rotate(v, cosine, sine):
    return v * cosine + pltpu.roll(v, HEAD_SIZE // 2, 1) * sine


def rotate_back(v, cosine, sine):
    return v * cosine + pltpu.roll(v * sine, HEAD_SIZE // 2, 1)


def lower(s, fill):
    n = s.shape[0]
    i = lax.broadcasted_iota(jnp.int32, (n, n), 0)
    j = lax.broadcasted_iota(jnp.int32, (n, n), 1)
    width = s.shape[1]
    diag = jnp.where(j <= i, s[:, width - n :], fill)
    return diag if width == n else jnp.concatenate([s[:, : width - n], diag], axis=1)


class Sum:
    def __init__(self, part, total, l1, own, l2, sems, base):
        self.q, self.p, self.x, self.c, _, _ = place()
        self.part, self.total, self.l1, self.own, self.l2 = part, total, l1, own, l2
        self.sems, self.base = sems, base
        self.sib = (2 * self.x + 1 - self.c, self.p)
        self.opp = (2 * (1 - self.x) + self.c, self.p)

    def rows(self, n, c):
        return pl.ds(pl.multiple_of(n * 256 + c * 128, 128), 128)

    def copy(self, step, n):
        s, r = self.sems.at[self.base + 2 * step, n], self.sems.at[self.base + 2 * step + 1, n]
        if step == 0:
            return remote(self.part.at[self.rows(n, 1 - self.c)], self.l1.at[n], s, r, self.sib)
        if step == 1:
            return remote(self.own.at[n], self.l2.at[n], s, r, self.opp)
        mine = self.total_at(n, self.c)
        return remote(mine, mine, s, r, self.sib)

    def total_at(self, n, c):
        if len(self.total.shape) == 2:
            return self.total.at[self.rows(n, c)]
        return self.total.at[(2 * n + c) // 4, (2 * n + c) % 4]

    def beside(self, n):
        self.copy(0, n).start()

    def across(self, n):
        self.copy(0, n).wait_recv()
        mine = self.part[self.rows(n, self.c), :].astype(F32)
        self.own[n] = (mine + self.l1[n].astype(F32)).astype(BF)
        self.copy(1, n).start()

    def back(self, n):
        self.copy(1, n).wait_recv()
        total = self.total_at(n, self.c)
        total[...] = (self.own[n].astype(F32) + self.l2[n].astype(F32)).astype(BF).reshape(total.shape)
        self.copy(2, n).start()

    def ready(self, n):
        other = self.total_at(n, 1 - self.c)
        s, r = self.sems.at[self.base + 4, n], self.sems.at[self.base + 5, n]
        remote(other, other, s, r, self.sib).wait_recv()

    def close(self, *steps):
        @pl.loop(0, 4)
        def _(n):
            for step in steps:
                self.copy(step, n).wait_send()


LINES = 6
PIECES = ((0, None), (2, None), (1, 0), (1, 1), (1, 2), (1, 3), (3, None))


def block(ref, b):
    return ref.at[pl.ds(2 * b, 2)]


class Gather:
    def __init__(self, srcs, dsts, sems):
        self.q, self.p, self.x, self.c, self.z, self.y = place()
        self.tok, self.cot, self.pos, self.pq, self.pg, self.po, self.pd = srcs
        self.xf, self.cf, self.of, *self.w = dsts
        (self.loc, self.ts, self.tr, self.fs, self.fr, self.ps, self.pr,
         self.as_, self.ar, self.zs, self.zr, self.ys, self.yr, self.ls, self.lr) = sems
        q, p, x, c, z, y = self.q, self.p, self.x, self.c, self.z, self.y
        self.owner_x, self.owner_c = mod(y + z, 2), z // 2
        self.is_owner = jnp.logical_and(x == self.owner_x, c == self.owner_c)
        self.cross = jnp.logical_and(x != self.owner_x, c == self.owner_c)
        self.sib = (2 * x + 1 - c, p)
        self.opp = (2 * (1 - x) + c, p)

    def peers(self):
        q, p = self.q, self.p
        return [(mod(q + k, 4), p) for k in (1, 2, 3)] + [(q, mod(p + k, 8)) for k in range(1, 8)]

    def col(self, n):
        return (self.pq, self.pg)[n], self.w[n]

    def own_copy(self, n):
        q, p = self.q, self.p
        if n < 2:
            src, dst = self.col(n)
            return pltpu.make_async_copy(src.at[q], dst.at[q, p], self.loc.at[n])
        return pltpu.make_async_copy((self.po, self.pd)[n - 2], self.w[n].at[p], self.loc.at[n])

    def column_copy(self, n, k):
        q, p = self.q, self.p
        src, dst = self.col(n)
        t = mod(q + k, 4)
        return remote(src.at[t], dst.at[q, p], self.as_.at[n, k - 1], self.ar.at[n, k - 1], (t, p))

    def column_start(self, n):
        for k in (1, 2, 3):
            self.column_copy(n, k).start()

    def column_wait(self, n):
        q, p = self.q, self.p
        src, dst = self.col(n)
        for k in (1, 2, 3):
            f = mod(q + 4 - k, 4)
            remote(src.at[0], dst.at[f, p], self.as_.at[n, k - 1], self.ar.at[n, k - 1], (q, p)).wait_recv()

    def view(self, piece, chunk):
        n, part = PIECES[piece]
        if n >= 2:
            return self.w[n].at[chunk]
        return self.w[n].at[:, chunk] if part is None else self.w[n].at[part, chunk]

    def z_copy(self, piece, src, way):
        v = self.view(piece, 2 * src + self.y)
        s = self.zs.at[piece, src + (1 if way < 0 else 0)]
        return remote(v, v, s, self.zr.at[piece, src], (self.q, 2 * (self.z + way) + self.y))

    def y_copy(self, piece, src):
        v = self.view(piece, 2 * src + self.y)
        return remote(v, v, self.ys.at[piece, src], self.yr.at[piece, src], (self.q, 2 * self.z + 1 - self.y))

    def spread(self, piece, src, up, down):
        if up:

            @pl.when(self.z < 3)
            def _():
                self.z_copy(piece, src, 1).start()

        if down:

            @pl.when(self.z > 0)
            def _():
                self.z_copy(piece, src, -1).start()

        self.y_copy(piece, src).start()

    def begin(self, *pieces_):
        for piece in pieces_:
            self.spread(piece, self.z, True, True)

    def line_copy(self, line, src, way):
        v = self.view(LINES, 2 * src + line)
        s = self.ls.at[line, src + (1 if way < 0 else 0)]
        return remote(v, v, s, self.lr.at[line, src], (self.q, 2 * (self.z + way) + self.y))

    def line_spread(self, line, src, up, down):
        if up:

            @pl.when(self.z < 3)
            def _():
                self.line_copy(line, src, 1).start()

        if down:

            @pl.when(self.z > 0)
            def _():
                self.line_copy(line, src, -1).start()

    def lines_begin(self):
        self.y_copy(LINES, self.z).start()
        self.line_spread(self.y, self.z, True, True)

    def lines_turn(self):
        v = self.view(LINES, 2 * self.z + 1 - self.y)
        remote(v, v, self.ys.at[LINES, self.z], self.yr.at[LINES, self.z], (self.q, self.p)).wait_recv()
        self.line_spread(1 - self.y, self.z, True, True)

    def line_step(self, other, dist):
        line = 1 - self.y if other else self.y
        low, high = self.z - dist, self.z + dist

        @pl.when(low >= 0)
        def _():
            v = self.view(LINES, 2 * low + line)
            remote(v, v, self.ls.at[line, 0], self.lr.at[line, low], (self.q, self.p)).wait_recv()
            self.line_spread(line, low, True, False)

        @pl.when(high < 4)
        def _():
            v = self.view(LINES, 2 * high + line)
            remote(v, v, self.ls.at[line, 0], self.lr.at[line, high], (self.q, self.p)).wait_recv()
            self.line_spread(line, high, False, True)

    def step(self, piece, dist):
        low, high = self.z - dist, self.z + dist

        @pl.when(low >= 0)
        def _():
            v = self.view(piece, 2 * low + self.y)
            remote(v, v, self.zs.at[piece, 0], self.zr.at[piece, low], (self.q, self.p)).wait_recv()
            self.spread(piece, low, True, False)

        @pl.when(high < 4)
        def _():
            v = self.view(piece, 2 * high + self.y)
            remote(v, v, self.zs.at[piece, 0], self.zr.at[piece, high], (self.q, self.p)).wait_recv()
            self.spread(piece, high, False, True)

    def steps(self, *pieces_):
        for piece in pieces_:
            for dist in (1, 2, 3):
                self.step(piece, dist)

    def y_wait(self, *pieces_):
        for piece in pieces_:
            for src in range(4):
                v = self.view(piece, 2 * src + 1 - self.y)
                remote(v, v, self.ys.at[piece, src], self.yr.at[piece, src], (self.q, self.p)).wait_recv()

    def tok_dst(self, a):
        return (self.xf, self.cf)[a]

    def token_copy(self, a, i):
        src, dst = (self.tok, self.cot)[a], self.tok_dst(a)
        goal = home_group(self.x, self.c, i)
        return goal, remote(src.at[i], block(dst, self.p), self.ts.at[a, i], self.tr.at[a, self.p], (self.q, goal))

    def token_local(self, a, i):
        return pltpu.make_async_copy((self.tok, self.cot)[a].at[i], block(self.tok_dst(a), self.p), self.loc.at[4 + a])

    def token_start(self, a):
        for i in range(2):
            goal, cp = self.token_copy(a, i)

            @pl.when(goal != self.p)
            def _():
                cp.start()

            @pl.when(goal == self.p)
            def _():
                self.token_local(a, i).start()

    def token_pass(self, a, first=0, end=8):
        dst = self.tok_dst(a)
        q, p = self.q, self.p

        @pl.when(self.is_owner)
        def _():
            @pl.loop(first, end)
            def _(b):
                @pl.when(b != p)
                def _():
                    remote(block(dst, b), block(dst, b), self.ts.at[a, 0], self.tr.at[a, b], (q, p)).wait_recv()

                @pl.when(b == p)
                def _():
                    self.token_local(a, 0).wait()

                remote(block(dst, b), block(dst, b), self.fs.at[a, 0, b], self.fr.at[a, b], self.sib).start()
                remote(block(dst, b), block(dst, b), self.fs.at[a, 1, b], self.fr.at[a, b], self.opp).start()

        @pl.when(jnp.logical_not(self.is_owner))
        def _():
            @pl.loop(first, end)
            def _(b):
                remote(block(dst, b), block(dst, b), self.fs.at[a, 0, b], self.fr.at[a, b], self.sib).wait_recv()

                @pl.when(self.cross)
                def _():
                    remote(block(dst, b), block(dst, b), self.fs.at[a, 0, b], self.fr.at[a, b], self.sib).start()

    def token_close(self, a):
        dst = self.tok_dst(a)
        q, p = self.q, self.p
        for i in range(2):
            goal, cp = self.token_copy(a, i)

            @pl.when(goal != p)
            def _():
                cp.wait_send()

        @pl.when(self.is_owner)
        def _():
            @pl.loop(0, 8)
            def _(b):
                remote(block(dst, b), block(dst, b), self.fs.at[a, 0, b], self.fr.at[a, b], (q, p)).wait_send()
                remote(block(dst, b), block(dst, b), self.fs.at[a, 1, b], self.fr.at[a, b], (q, p)).wait_send()

        @pl.when(self.cross)
        def _():
            @pl.loop(0, 8)
            def _(b):
                remote(block(dst, b), block(dst, b), self.fs.at[a, 0, b], self.fr.at[a, b], (q, p)).wait_send()

    def pos_copy(self, k):
        return remote(self.pos, self.of, self.ps.at[k], self.pr.at[0], (mod(self.q + k + 1, 4), self.p))

    def pos_start(self):
        @pl.when(self.is_owner)
        def _():
            pltpu.make_async_copy(self.pos, self.of, self.loc.at[6]).start()
            for k in range(3):
                self.pos_copy(k).start()

    def pos_finish(self):
        @pl.when(self.is_owner)
        def _():
            pltpu.make_async_copy(self.pos, self.of, self.loc.at[6]).wait()
            for k in range(3):
                self.pos_copy(k).wait_send()

        @pl.when(jnp.logical_not(self.is_owner))
        def _():
            self.pos_copy(0).wait_recv()

    def close(self):
        for n in range(2):
            for k in (1, 2, 3):
                self.column_copy(n, k).wait_send()
        self.y_copy(LINES, self.z).wait_send()
        for line in range(2):
            for src in range(4):

                @pl.when(jnp.logical_and(self.z < 3, src <= self.z))
                def _():
                    self.line_copy(line, src, 1).wait_send()

                @pl.when(jnp.logical_and(self.z > 0, src >= self.z))
                def _():
                    self.line_copy(line, src, -1).wait_send()

        for piece in range(LINES):
            for src in range(4):
                self.y_copy(piece, src).wait_send()

                @pl.when(jnp.logical_and(self.z < 3, src <= self.z))
                def _():
                    self.z_copy(piece, src, 1).wait_send()

                @pl.when(jnp.logical_and(self.z > 0, src >= self.z))
                def _():
                    self.z_copy(piece, src, -1).wait_send()

        self.token_close(0)
        self.token_close(1)


GATHER_SEMS = ((7,), (2, 2), (2, 8), (2, 2, 8), (2, 8), (3,), (1,), (2, 3), (2, 3), (6, 5), (6, 4), (7, 4), (7, 4), (2, 5), (2, 4))


class Home:
    def __init__(self, part, out, l1, own, l2, sems, here, base):
        self.q, self.p, self.x, self.c, self.z, self.y = place()
        self.part, self.out, self.l1, self.own, self.l2 = part, out, l1, own, l2
        self.sems, self.here, self.base = sems, here, base
        self.owner_x, self.owner_c = mod(self.y + self.z, 2), self.z // 2
        self.keeps = self.x == self.owner_x
        self.sib = (2 * self.x + 1 - self.c, self.p)
        self.opp = (2 * (1 - self.x) + self.c, self.p)
        self.goal_q = 2 * self.owner_x + self.owner_c

    def rows(self, n, c):
        return pl.ds(pl.multiple_of(n * 256 + c * 128, 128), 128)

    def sem(self, k, n):
        return self.sems.at[self.base + k, n]

    def first(self, n):
        return remote(
            self.part.at[self.rows(n, 1 - self.c)], self.l1.at[n], self.sem(0, n), self.sem(1, n), self.sib
        )

    def second(self, n):
        return remote(self.own.at[n], self.l2.at[n], self.sem(2, n), self.sem(3, n), self.opp)

    def third(self, n):
        slot = mod(self.z, 2)
        return remote(
            self.own.at[n], self.out.at[slot], self.sem(4, n), self.sem(5, slot), (self.goal_q, 2 * n + self.c)
        )

    def is_self(self, n):
        return jnp.logical_and(self.goal_q == self.q, 2 * n + self.c == self.p)

    def beside(self, n):
        self.first(n).start()

    def across(self, n):
        self.first(n).wait_recv()
        mine = self.part[self.rows(n, self.c), :].astype(F32)
        self.own[n] = (mine + self.l1[n].astype(F32)).astype(BF)

        @pl.when(jnp.logical_not(self.keeps))
        def _():
            self.second(n).start()

    def finish(self, n, rest):
        @pl.when(self.keeps)
        def _():
            self.second(n).wait_recv()
            s = self.own[n].astype(F32) + self.l2[n].astype(F32)
            self.own[n] = rest(n, s).astype(BF)

            @pl.when(jnp.logical_not(self.is_self(n)))
            def _():
                self.third(n).start()

            @pl.when(self.is_self(n))
            def _():
                cp = pltpu.make_async_copy(self.own.at[n], self.out.at[mod(self.z, 2)], self.here)
                cp.start()
                cp.wait()

    def close(self):
        for i in range(2):
            group = home_group(self.x, self.c, i)
            same = jnp.logical_and(group == self.p, self.y == self.c)

            @pl.when(jnp.logical_not(same))
            def _():
                remote(self.own.at[0], self.out.at[i], self.sem(4, 0), self.sem(5, i), (self.q, self.p)).wait_recv()

        for n in range(4):
            self.first(n).wait_send()

            @pl.when(jnp.logical_not(self.keeps))
            def _():
                self.second(n).wait_send()

            @pl.when(jnp.logical_and(self.keeps, jnp.logical_not(self.is_self(n))))
            def _():
                self.third(n).wait_send()


class Scatter:
    def __init__(self, g, ly, lz, sems, base):
        self.q, self.p, _, _, self.z, self.y = place()
        self.g, self.ly, self.lz, self.sems, self.base = g, ly, lz, sems, base

    def y_copy(self, n):
        s, r = self.sems.at[self.base + n, 0], self.sems.at[self.base + n, 1]
        return remote(self.g.at[1 - self.y, n], self.ly(n), s, r, (self.q, 2 * self.z + 1 - self.y))

    def z_copy(self, n, k):
        t = mod(self.z + k, 4)
        s, r = self.sems.at[self.base + n, 2 * k], self.sems.at[self.base + n, 2 * k + 1]
        return remote(self.ly(n).at[t], self.lz(n).at[k - 1], s, r, (self.q, 2 * t + self.y))

    def y_send(self, n):
        self.y_copy(n).start()

    def z_step(self, n):
        self.y_copy(n).wait_recv()
        ly = self.ly(n)

        @pl.loop(0, 4)
        def _(t):
            ly[t] = (ly[t].astype(F32) + self.g[self.y, n, t].astype(F32)).astype(BF)

        lz = self.lz(n)
        z = self.z

        @pl.when(z != 3)
        def _():
            self.z_copy(n, 1).start()

        @pl.when(z != 0)
        def _():
            self.z_copy(n, 3).start()

        for end, unused in ((0, 0), (3, 2)):

            @pl.when(z == end)
            def _():
                self.z_copy(n, 2).start()
                self.relay_copy(n).start()
                lz[unused] = jnp.zeros(lz.shape[1:], BF)

    def relay_copy(self, n):
        s, r = self.sems.at[self.base + n, 8], self.sems.at[self.base + n, 9]
        near = 1 + self.z // 3
        return remote(self.ly(n).at[3 - self.z], self.lz(n).at[3], s, r, (self.q, 2 * near + self.y))

    def relay(self, n):
        @pl.when(jnp.logical_and(self.z > 0, self.z < 3))
        def _():
            ly, lz = self.ly(n), self.lz(n)
            t = mod(self.z + 2, 4)
            s, r = self.sems.at[self.base + n, 8], self.sems.at[self.base + n, 9]
            remote(ly.at[t], lz.at[3], s, r, (self.q, self.p)).wait_recv()
            ly[t] = (ly[t].astype(F32) + lz[3].astype(F32)).astype(BF)
            self.z_copy(n, 2).start()

    def z_sum(self, n):
        @pl.when(self.z != 0)
        def _():
            self.z_copy(n, 1).wait_recv()

        self.z_copy(n, 2).wait_recv()

        @pl.when(self.z != 3)
        def _():
            self.z_copy(n, 3).wait_recv()

        ly, lz = self.ly(n), self.lz(n)
        return ly[self.z].astype(F32) + lz[0].astype(F32) + lz[1].astype(F32) + lz[2].astype(F32)

    def close(self, count):
        @pl.loop(0, count)
        def _(n):
            self.y_copy(n).wait_send()
            self.z_copy(n, 2).wait_send()

            @pl.when(self.z != 3)
            def _():
                self.z_copy(n, 1).wait_send()

            @pl.when(self.z != 0)
            def _():
                self.z_copy(n, 3).wait_send()

            @pl.when(jnp.logical_or(self.z == 0, self.z == 3))
            def _():
                self.relay_copy(n).wait_send()


class Columns:
    def __init__(self, scatter, out, sems, base, here):
        self.scatter, self.out, self.here = scatter, out, here
        self.sems, self.base = sems, base
        self.q, self.p = scatter.q, scatter.p

    def copy(self, t):
        s, r = self.sems.at[self.base, t], self.sems.at[self.base + 1, self.q]
        return remote(self.scatter.ly(t).at[self.scatter.z], self.out.at[self.q], s, r, (t, self.p))

    def own(self, t):
        return pltpu.make_async_copy(self.scatter.ly(t).at[self.scatter.z], self.out.at[t], self.here)

    def step(self, t):
        s = self.scatter.z_sum(t).astype(BF)
        ly = self.scatter.ly(t)
        ly[self.scatter.z] = s

        @pl.when(t != self.q)
        def _():
            self.copy(t).start()

        @pl.when(t == self.q)
        def _():
            self.own(t).start()

    def close(self):
        for t in range(4):

            @pl.when(t != self.q)
            def _():
                r = self.sems.at[self.base + 1, t]
                remote(self.out.at[t], self.out.at[t], self.sems.at[self.base, t], r, (self.q, self.p)).wait_recv()
                self.copy(t).wait_send()

            @pl.when(t == self.q)
            def _():
                self.own(t).wait()


def column(table, h):
    lane = lax.broadcasted_iota(jnp.int32, table.shape, 1)
    return jnp.sum(jnp.where(lane == h, table, 0.0), axis=1, keepdims=True)


def layer_kernel(
    tok, cot, pos, po, pd, table, qg, kg, ga, gm, w_query, key_projection, value_projection, w_gate, w_up,
    out, igrad, od, ogu, oo, oqkv, oheads, of,
    xf, cf, wq, wg, wo, wd, raw_o, qb, kb, vb, ob, lse, hidden, rest, cs, pa, pb, pc, mb, dgu, gd, ggu,
    dkv, go, gqkv, yo, yqkv, zo, zqkv, sums_d, sums_o, heads, hy, hz, hdp,
    l1, own, l2, l1b, ownb, l2b, l2c, rows_of_two, sorts, sorts_sem, free, sums, gsem, csem, hs, hr, homes, here, kept, *sems,
):
    q, p, x_, c, z, y = place()
    sd = Scatter(gd, lambda n: wd.at[pl.ds(0, 4)], lambda n: wd.at[pl.ds(4, 4)], gsem, 0)
    sgu = Scatter(ggu, lambda n: wg.at[n, pl.ds(0, 4)], lambda n: wg.at[n, pl.ds(4, 4)], gsem, 1)
    so = Scatter(go, lambda n: yo.at[n], lambda n: zo.at[n], gsem, 5)
    sqkv = Scatter(gqkv, lambda n: yqkv.at[n], lambda n: zqkv.at[n], gsem, 6)
    cgu = Columns(sgu, ogu, csem, 0, kept.at[0])
    cqkv = Columns(sqkv, oqkv, csem, 2, kept.at[1])
    h_out = Home(pb, out, l1, own, l2, homes, here.at[0], 0)
    h_in = Home(pc, igrad, l1b, ownb, l2c, homes, here.at[1], 6)
    order = [(sd, 0)] + [(sgu, n) for n in range(4)] + [(so, 0)] + [(sqkv, n) for n in range(4)]

    def y_send(j):
        which, n = order[j]
        which.y_send(n)

    def relay(j):
        which, n = order[j]
        which.relay(n)

    def step(j):
        which, n = order[j]
        which.z_step(n)
        if j + 2 < len(order):
            y_send(j + 2)
        if j > 0:
            relay(j - 1)

    pq, pg = yqkv.at[0], ggu.at[0, 0]
    for gain, dst, todo in (
        (ga, pq, ((w_query, 0, 512), (key_projection, 512, 256), (value_projection, 768, 256))),
        (gm, pg, ((w_gate, 0, 768), (w_up, 768, 768))),
    ):
        up = upright(gain[...].astype(F32))
        for w, first, width in todo:
            for t in range(4):
                v = w[:, t * width : (t + 1) * width].astype(F32) * up
                dst[t, :, first : first + width] = v.astype(BF)
    g = Gather((tok, cot, pos, pq, pg, po, pd), (xf, cf, of, wq, wg, wo, wd), sems)
    peers = [(2 * x_ + cc, mod(p + k, 8)) for k in range(1, 8) for cc in (0, 1)]
    peers += [(mod(q + k, 4), p) for k in (1, 2, 3)]
    greet(peers)
    g.pos_start()
    g.token_start(0)
    g.column_start(0)
    for n in range(4):
        g.own_copy(n).start()
    g.column_start(1)
    g.own_copy(0).wait()
    g.column_wait(0)
    g.begin(0)
    g.pos_finish()
    sort = pltpu.make_async_copy(of, rows_of_two, sorts_sem.at[0])
    sort.start()
    lse[...] = jnp.zeros_like(lse)
    g.step(0, 1)
    g.token_pass(0, 0, 2)
    g.step(0, 2)
    g.token_pass(0, 2, 4)
    g.token_start(1)
    g.step(0, 3)
    g.token_pass(0, 4, 8)
    g.own_copy(1).wait()
    g.column_wait(1)
    g.begin(2)
    g.own_copy(2).wait()
    g.begin(1, 3)
    g.own_copy(3).wait()
    sort.wait()
    slot = mod(z, 2)
    for j in range(16):
        sorts[0, j] = rows_of_two[slot, j]
        where = jnp.int32(0)
        for b in range(16):
            where = jnp.where(rows_of_two[slot, b] == j, b, where)
        sorts[1, j] = where
    g.y_wait(0)

    @pl.loop(0, 4)
    def _(n):
        rows = pl.ds(pl.multiple_of(n * 256, 256), 256)
        v = pieces(xf, sorts, 1, n * 4, 4).astype(F32)
        h = (v * unit(v)).astype(BF)

        @pl.when(n == 2)
        def _():
            g.token_pass(1, 0, 3)
            g.begin(4)

        raw = jnp.dot(h, wq[...].reshape(WIDTH, WIDTH), preferred_element_type=F32)
        raw_o[rows, :] = raw[:, :768]
        cosine, sine = turns(table[rows, :])
        for t in range(2):
            vb[t, rows, :] = raw[:, 768 + t * 128 : 896 + t * 128].astype(BF)
        for t in range(6):
            u = raw[:, t * 128 : (t + 1) * 128]
            n_ = u * unit(u) * (qg[...] if t < 4 else kg[...])
            r = rotate(n_, cosine, sine).astype(BF)
            if t < 4:
                qb[t, rows, :] = r
            else:
                kb[t - 4, rows, :] = r

    @pl.loop(0, 4)
    def _(h):
        @pl.when(h == 0)
        def _():
            g.step(1, 1)
            g.token_pass(1, 3, 6)

        @pl.when(h == 1)
        def _():
            g.step(1, 2)
            g.token_pass(1, 6, 8)
            g.begin(5)

        @pl.when(h == 2)
        def _():
            g.step(1, 3)
            g.step(2, 1)
            g.lines_begin()

        @pl.when(h == 3)
        def _():
            g.step(2, 2)
            g.step(2, 3)

        kv = h // 2
        for i in range(4):
            length = (i + 1) * 256
            rows = slice(i * 256, length)
            s = dims(qb[h, rows, :], kb[kv, :length, :], 1, 1) * (HEAD_SIZE**-0.5 * LOG2E)
            s = lower(s, NEGATIVE_FILL)
            top = jnp.max(s, axis=-1, keepdims=True)
            e = jnp.exp2(s - top)
            sum_e = jnp.sum(e, axis=-1, keepdims=True)
            o = jnp.dot(e.astype(BF), vb[kv, :length, :], preferred_element_type=F32) / sum_e
            ob[rows, pl.ds(pl.multiple_of(h * 128, 128), 128)] = o.astype(BF)
            lane = lax.broadcasted_iota(jnp.int32, (256, 128), 1)
            lse[rows, :] = jnp.where(lane == h, top + jnp.log2(sum_e), lse[rows, :])

    g.y_wait(1)
    s1 = Sum(pa, pb, l1, own, l2, sums, 0)
    s2 = Sum(pc, gqkv, l1b, ownb, l2b, sums, 6)

    @pl.loop(0, 4)
    def _(n):
        rows = pl.ds(pl.multiple_of(n * 256, 256), 256)
        out_w = wo[...].reshape(512, WIDTH)
        pa[rows, :] = jnp.dot(ob[rows, :], out_w, preferred_element_type=F32).astype(BF)
        s1.beside(n)

        @pl.when(n > 0)
        def _():
            s1.across(n - 1)

    s1.across(3)
    g.step(3, 1)
    g.step(3, 2)
    s1.back(0)
    g.step(3, 3)
    g.step(4, 1)
    s1.back(1)
    g.lines_turn()
    g.step(4, 2)
    g.step(4, 3)
    s1.back(2)
    g.step(5, 1)
    g.line_step(False, 1)
    g.step(5, 2)
    g.line_step(True, 1)
    s1.back(3)
    g.step(5, 3)
    g.line_step(False, 2)
    g.line_step(True, 2)
    g.line_step(False, 3)
    g.line_step(True, 3)
    g.y_wait(2, 3, 4, 5)
    s1.close(0)

    @pl.loop(0, 4)
    def _(n):
        s1.ready(n)
        rows = pl.ds(pl.multiple_of(n * 256, 256), 256)
        h = pieces(xf, sorts, 1, n * 4, 4).astype(F32) + pb[rows, :].astype(F32)
        hidden[pl.ds(n * 4, 4)] = h.reshape(4, BLK, WIDTH)
        a = (h * unit(h)).astype(BF)
        pa[rows, :] = a
        wgu = wg[...].reshape(WIDTH, 1536)
        gu = jnp.dot(a, wgu, preferred_element_type=F32)
        gate = gu[:, :768]
        up = gu[:, 768:]
        sig = 1.0 / (1.0 + jnp.exp2(gate * -LOG2E))
        silu = gate * sig
        mb[pl.ds(n * 4, 4)] = (silu * up).astype(BF).reshape(4, BLK, 768)
        cc = pieces(cf, sorts, 1, n * 4, 4)
        cs[rows, :] = cc
        dm = dims(cc, wd[...].reshape(768, WIDTH), 1, 1)
        dg = (dm * up * sig * (1.0 + gate * (1.0 - sig))).astype(BF)
        du = (dm * silu).astype(BF)
        both = jnp.concatenate([dg, du], axis=1)
        dgu[rows, :] = both
        pc[rows, :] = dims(both, wgu, 1, 1).astype(BF)
        s2.beside(n)

        @pl.when(n > 0)
        def _():
            s2.across(n - 1)

    s2.across(3)
    s1.close(1, 2)

    @pl.loop(0, 2)
    def _(n):
        m_all = mb[...].reshape(TOKENS, 768)
        for t in range(2):

            @pl.when(n == t)
            def _():
                v = dims(m_all[:, t * 384 : (t + 1) * 384], cs[...], 0, 0).astype(BF)
                v = v.reshape(2, 2, 96, WIDTH)
                for u in range(2):
                    gd[u, 0, 2 * t : 2 * t + 2] = v[:, u]

    @pl.loop(0, 4)
    def _(n):
        rows = pl.ds(pl.multiple_of(n * 256, 256), 256)
        m = pieces(mb, sorts, 0, n * 4, 4)
        pb[rows, :] = jnp.dot(m, wd[...].reshape(768, WIDTH), preferred_element_type=F32).astype(BF)
        rest[n] = pieces(hidden, sorts, 0, 4 * n + 2 * g.c, 2)

    g.close()
    near = [(q, 2 * z + 1 - y), (2 * x_ + 1 - c, p), (2 * (1 - x_) + c, p)]
    near += [(q, 2 * mod(z + k, 4) + y) for k in (1, 2, 3)]
    for peer in near:
        pl.semaphore_signal(free, inc=1, device_id=peer, device_id_type=MESH)
    s2.back(0)

    s2.back(1)
    pl.semaphore_wait(free, len(near))
    y_send(0)
    for n in range(4):
        h_out.beside(n)

    @pl.loop(0, 4)
    def _(n):
        v = dims(pa[:, pl.ds(pl.multiple_of(n * 256, 256), 256)], dgu[...], 0, 0).astype(BF)
        v = v.reshape(4, 2, 32, 1536)
        for t in range(2):
            ggu[t, n] = v[:, t]

        @pl.when(n == 0)
        def _():
            y_send(1)

        @pl.when(n < 2)
        def _():
            s2.back(n + 2)

    @pl.loop(0, 4)
    def _(n):
        rows = pl.ds(pl.multiple_of(n * 256, 256), 256)
        h = hidden[pl.ds(n * 4, 4)].reshape(256, WIDTH)
        r = unit(h)
        s2.ready(n)
        da = gqkv[n // 2, pl.ds(2 * (n % 2), 2)].reshape(256, WIDTH).astype(F32)
        back = r * da - h * (r * r * r * jnp.mean(h * da, axis=-1, keepdims=True))
        d = cs[rows, :].astype(F32) + back
        hidden[pl.ds(n * 4, 4)] = d.reshape(4, BLK, WIDTH)
        low = d.astype(BF)
        pa[rows, :] = low
        do = dims(low, wo[...].reshape(512, WIDTH), 1, 1).astype(BF)
        cs[rows, :512] = do
        h_out.across(n)

    @pl.loop(0, 2)
    def _(n):
        v = dims(ob[:, pl.ds(pl.multiple_of(n * 256, 256), 256)], pa[...], 0, 0).astype(BF)
        v = v.reshape(2, 2, 64, WIDTH)
        for t in range(2):
            go[t, 0, pl.ds(n * 2, 2)] = v[:, t]

    s2.close(0, 1, 2)
    heads[...] = jnp.zeros_like(heads)
    scale = HEAD_SIZE**-0.5

    def norm_back(dn, u, gain, rows):
        dn = rotate_back(dn, *turns(table[rows, :]))
        r = unit(u)
        gd_ = gain * dn
        du = r * gd_ - u * (r * r * r * jnp.mean(u * gd_, axis=-1, keepdims=True))
        return du.astype(BF), jnp.sum(dn * u * r, axis=0, keepdims=True)

    def result(n, s):
        return s + rest[n]

    def inward(n, s):
        v = xf[pl.ds(4 * n + 2 * c, 2)].reshape(128, WIDTH).astype(F32)
        r = unit(v)
        s = r * s - v * (r * r * r * jnp.mean(v * s, axis=-1, keepdims=True))
        return s + pieces(hidden, sorts, 0, 4 * n + 2 * c, 2)

    @pl.loop(0, 2)
    def _(g):
        dkv[...] = jnp.zeros_like(dkv)
        for t in range(2):
            if t == 0:

                @pl.when(g == 1)
                def _():
                    step(1)
                    h_out.finish(0, result)
                    h_out.finish(1, result)
            else:
                for turn in range(2):

                    @pl.when(g == turn)
                    def _():
                        step(2 * turn)
                        if turn == 1:
                            h_out.finish(2, result)
                            h_out.finish(3, result)

            h = g * 2 + t
            lanes = pl.ds(pl.multiple_of(h * 128, 128), 128)
            for i in range(4):
                length = (i + 1) * 256
                rows = slice(i * 256, length)
                qv = qb[h, rows, :]
                kv = kb[g, :length, :]
                dov = cs[rows, lanes]
                s = dims(qv, kv, 1, 1) * (scale * LOG2E)
                pr = lower(jnp.exp2(s - column(lse[rows, :], h)), 0.0)
                dp = dims(dov, vb[g, :length, :], 1, 1)
                delta = jnp.sum(dov.astype(F32) * ob[rows, lanes].astype(F32), axis=-1, keepdims=True)
                ds_ = lower(pr * (dp - delta), 0.0).astype(BF)
                dq = jnp.dot(ds_, kv, preferred_element_type=F32) * scale
                dkv[0, :length, :] += dims(ds_, qv, 0, 0)
                dkv[1, :length, :] += dims(pr.astype(BF), dov, 0, 0)
                du, dgain = norm_back(dq, raw_o[rows, lanes], qg[...], pl.ds(i * 256, 256))
                cf[i * 4 : i * 4 + 4, :, lanes] = du.reshape(4, BLK, 128)
                heads[0:1, :] += dgain
        lanes = pl.ds(pl.multiple_of(512 + g * 128, 128), 128)
        for i in range(4):
            rows = slice(i * 256, (i + 1) * 256)
            du, dgain = norm_back(dkv[0, rows, :] * scale, raw_o[rows, lanes], kg[...], pl.ds(i * 256, 256))
            cf[i * 4 : i * 4 + 4, :, lanes] = du.reshape(4, BLK, 128)
            heads[1:2, :] += dgain
        cf[:, :, pl.ds(pl.multiple_of(768 + g * 128, 128), 128)] = dkv[1].astype(BF).reshape(16, BLK, 128)

    step(3)
    hy_copy = remote(heads, hy, hs.at[0], hr.at[0], (q, 2 * z + 1 - y))
    hy_copy.start()

    @pl.loop(0, 4)
    def _(n):
        rows = pl.ds(pl.multiple_of(n * 256, 256), 256)
        d = pieces(cf, sorts, 0, n * 4, 4)
        pc[rows, :] = dims(d, wq[...].reshape(WIDTH, WIDTH), 1, 1).astype(BF)
        h_in.beside(n)

        @pl.when(n > 0)
        def _():
            h_in.across(n - 1)

    h_in.across(3)

    @pl.loop(0, 4)
    def _(n):
        rows = pl.ds(pl.multiple_of(n * 256, 256), 256)
        v = pieces(xf, sorts, 1, n * 4, 4).astype(F32)
        pa[rows, :] = (v * unit(v)).astype(BF)

    @pl.loop(0, 4)
    def _(n):
        v = dims(pa[:, pl.ds(pl.multiple_of(n * 256, 256), 256)], cf[...].reshape(TOKENS, WIDTH), 0, 0).astype(BF)
        v = v.reshape(4, 2, 32, WIDTH)
        for t in range(2):
            gqkv[t, n] = v[:, t]

    step(4)

    def z_heads(k):
        return remote(hz.at[z], hz.at[z], hs.at[k], hr.at[k], (q, 2 * mod(z + k, 4) + y))

    def dp_heads(k):
        return remote(hdp.at[q], hdp.at[q], hs.at[3 + k], hr.at[3 + k], (mod(q + k, 4), p))

    hy_copy.wait()
    hz[z] = heads[...] + hy[...]
    for k in (1, 2, 3):
        z_heads(k).start()
    sums_d[...] = sd.z_sum(0)
    to_d = pltpu.make_async_copy(sums_d, od, kept.at[2])
    to_d.start()
    for n in range(4):
        step(5 + n)
        cgu.step(n)
        if n == 3:
            h_in.finish(0, inward)
    step(9)
    relay(9)
    for n in (1, 2, 3):
        h_in.finish(n, inward)
    for k in (1, 2, 3):
        f = mod(z + 4 - k, 4)
        remote(hz.at[f], hz.at[f], hs.at[k], hr.at[k], (q, p)).wait_recv()
    hdp[q] = hz[0] + hz[1] + hz[2] + hz[3]
    for k in (1, 2, 3):
        dp_heads(k).start()
    sums_o[...] = so.z_sum(0)
    to_o = pltpu.make_async_copy(sums_o, oo, kept.at[3])
    to_o.start()

    @pl.loop(0, 4)
    def _(n):
        cqkv.step(n)

    cgu.close()
    for k in (1, 2, 3):
        f = mod(q + 4 - k, 4)
        remote(hdp.at[f], hdp.at[f], hs.at[3 + k], hr.at[3 + k], (q, p)).wait_recv()
    heads[...] = hdp[0] + hdp[1] + hdp[2] + hdp[3]
    to_h = pltpu.make_async_copy(heads, oheads, kept.at[4])
    to_h.start()
    cqkv.close()
    h_out.close()
    h_in.close()
    sd.close(1)
    sgu.close(4)
    so.close(1)
    sqkv.close(4)
    for cp in (to_d, to_o, to_h):
        cp.wait()
    for k in (1, 2, 3):
        z_heads(k).wait_send()
        dp_heads(k).wait_send()


def layer_call(tok, cot, pos, po, pd, table, qg, kg, *rest):
    sem = pltpu.SemaphoreType.DMA
    shape = jax.ShapeDtypeStruct
    vm = pltpu.VMEM
    full = (TOKENS, WIDTH)
    return pl.pallas_call(
        layer_kernel,
        out_shape=(
            shape((2, 128, WIDTH), BF),
            shape((2, 128, WIDTH), BF),
            shape((96, WIDTH), F32),
            shape((4, 32, 1536), BF),
            shape((64, WIDTH), F32),
            shape((4, 32, WIDTH), BF),
            shape((8, 128), F32),
            shape((8, 128), jnp.int32),
        ),
        in_specs=[ANY] * 5 + [VM] * 10,
        out_specs=(ANY,) * 8,
        scratch_shapes=[
            vm((16, BLK, WIDTH), BF), vm((16, BLK, WIDTH), BF),
            vm((4, 8, 32, WIDTH), BF), vm((4, 8, 32, 1536), BF),
            vm((8,) + po.shape, BF), vm((8,) + pd.shape, BF),
            vm((TOKENS, 768), F32),
            vm((4, TOKENS, 128), BF), vm((2, TOKENS, 128), BF), vm((2, TOKENS, 128), BF), vm((TOKENS, 512), BF),
            vm((TOKENS, 128), F32), vm((16, BLK, WIDTH), F32), vm((4, 128, WIDTH), F32),
            vm(full, BF), vm(full, BF), vm(full, BF), vm(full, BF),
            vm((16, BLK, 768), BF), vm((TOKENS, 1536), BF),
            vm((2, 1, 4, 96, WIDTH), BF), vm((2, 4, 4, 32, 1536), BF),
            vm((2, TOKENS, 128), F32),
            vm((2, 1, 4, 64, WIDTH), BF), vm((2, 4, 4, 32, WIDTH), BF),
            vm((1, 4, 64, WIDTH), BF), vm((4, 4, 32, WIDTH), BF),
            vm((1, 4, 64, WIDTH), BF), vm((4, 4, 32, WIDTH), BF),
            vm((96, WIDTH), F32), vm((64, WIDTH), F32), vm((8, 128), F32), vm((8, 128), F32), vm((4, 8, 128), F32), vm((4, 8, 128), F32),
        ]
        + [vm((4, 128, WIDTH), BF)] * 7
        + [
            pltpu.SMEM((8, 128), jnp.int32), pltpu.SMEM((2, 16), jnp.int32), sem((1,)), pltpu.SemaphoreType.REGULAR, sem((12, 4)),
            sem((10, 10)), sem((4, 4)), sem((7,)), sem((7,)), sem((12, 4)), sem((2,)), sem((5,)),
        ]
        + [sem(n) for n in GATHER_SEMS],
        compiler_params=pltpu.CompilerParams(
            collective_id=0, has_side_effects=True, vmem_limit_bytes=VMEM_BYTES
        ),
        name="layer_both_ways",
    )(tok, cot, pos, po, pd, table, qg, kg, *rest)


def whole_sequences(
    tokens, attn_gain, w_query, key_projection, value_projection, query_head_gain, key_gain, w_out,
    mlp_gain, w_gate, w_up, w_down, cotangent, span_order,
):
    pos = jnp.pad(span_order, ((0, 6), (0, 112)))
    gains = attn_gain[None, :], mlp_gain[None, :]
    weights = w_query, key_projection, value_projection, w_gate, w_up
    freqs = BASE ** (-np.arange(HEAD_SIZE // 2) * 2.0 / HEAD_SIZE)
    angles = np.arange(TOKENS)[:, None] * freqs.astype(np.float32)[None, :].astype(np.float64)
    table = np.concatenate([np.cos(angles), np.sin(angles)], axis=1).astype(np.float32)
    qg = query_head_gain.astype(F32)[None, :]
    kg = key_gain.astype(F32)[None, :]
    out, igrad, od, ogu, oo, oqkv, oheads, _ = layer_call(
        tokens.reshape(2, 2, BLK, WIDTH), cotangent.reshape(2, 2, BLK, WIDTH), pos, w_out, w_down,
        table, qg, kg, *gains, *weights,
    )
    return finish(out, igrad, od, ogu, oo, oqkv, oheads, *gains, *weights)


def diagonal(v):
    i = lax.broadcasted_iota(jnp.int32, (32, 32), 0)
    j = lax.broadcasted_iota(jnp.int32, (32, 32), 1)
    return jnp.where(i == j, jnp.broadcast_to(v, (32, 32)), 0.0)


def upright(row):
    return jnp.sum(diagonal(row), axis=1, keepdims=True)


def flat_row(col):
    return jnp.sum(diagonal(col), axis=0, keepdims=True)


def finish_kernel(
    out_i, igrad_i, od_i, ogu, oo_i, oqkv, oheads, ga, gm, w_query, key_projection, value_projection, w_gate, w_up,
    out, igrad, attn, query, key, value, qgain, kgain, oo, mlp, gate, up, od,
):
    out[...] = out_i[...]
    igrad[...] = igrad_i[...]
    od[...] = od_i[...]
    oo[...] = oo_i[...]
    qgain[...] = oheads[0:1, :]
    kgain[...] = oheads[1:2, :]
    for gain, grads, total, todo in (
        (ga, oqkv, attn, ((w_query, query, 0, 512), (key_projection, key, 512, 256), (value_projection, value, 768, 256))),
        (gm, ogu, mlp, ((w_gate, gate, 0, 768), (w_up, up, 768, 768))),
    ):
        g = upright(gain[...].astype(F32))
        dot = jnp.zeros((32, 1), F32)
        for w, o, first, width in todo:
            for t in range(4):
                h = grads[t, :, first : first + width].astype(F32)
                lanes = slice(t * width, (t + 1) * width)
                o[:, lanes] = g * h
                dot = dot + jnp.sum(w[:, lanes].astype(F32) * h, axis=1, keepdims=True)
        total[...] = flat_row(dot)


def finish(*args):
    shape = jax.ShapeDtypeStruct
    ws = args[9:]
    res = pl.pallas_call(
        finish_kernel,
        out_shape=(
            shape(args[0].shape, BF),
            shape(args[1].shape, BF),
            shape((1, 32), F32),
            *[shape(w.shape, F32) for w in ws[:3]],
            shape((1, 128), F32),
            shape((1, 128), F32),
            shape(args[4].shape, F32),
            shape((1, 32), F32),
            *[shape(w.shape, F32) for w in ws[3:]],
            shape(args[2].shape, F32),
        ),
        in_specs=[VM] * 14,
        out_specs=(VM,) * 13,
        name="gains_and_layout",
    )(*args)
    res = list(res)
    for i in (2, 6, 7, 9):
        res[i] = res[i].reshape(-1)
    return tuple(res)


def layer(tokens, *rest):
    whole = (
        lax.axis_size("dp") == 4
        and lax.axis_size("seq") == 8
        and tokens.shape == (2, 128, WIDTH)
        and rest[-1].shape == (2, 16)
    )
    return (whole_sequences if whole else shards)(tokens, *rest)


def solution(mesh):
    return jax.shard_map(
        layer,
        mesh=mesh,
        in_specs=(
            P("dp", "seq", None),
            P(("dp", "seq")),
            P(("dp", "seq"), None),
            P(("dp", "seq"), None),
            P(("dp", "seq"), None),
            P(),
            P(),
            P(("dp", "seq"), None),
            P(("dp", "seq")),
            P(("dp", "seq"), None),
            P(("dp", "seq"), None),
            P(("dp", "seq"), None),
            P("dp", "seq", None),
            P("dp", None),
        ),
        out_specs=(
            P("dp", "seq", None),
            P("dp", "seq", None),
            P(("dp", "seq")),
            P(("dp", "seq"), None),
            P(("dp", "seq"), None),
            P(("dp", "seq"), None),
            P(),
            P(),
            P(("dp", "seq"), None),
            P(("dp", "seq")),
            P(("dp", "seq"), None),
            P(("dp", "seq"), None),
            P(("dp", "seq"), None),
        ),
        check_vma=False,
    )
```
